32 devices in a mesh: dp: 8 (over z, x), tensor: 4 (over y, core).
Axes of the slice: x: 2, y: 2, z: 4, core: 2. Of those that a mesh axis runs over, the one named last changes fastest.
Arguments:
- layer_input: bfloat16 [1536, 2560], P('dp')
- segment_ids: int32 [1536], P('dp'), may hold values from 0 to 31, as said below
- valid_mask: int32 [1536], P('dp'), may hold values from 0 to 1, as said below
- cotangent: bfloat16 [1536, 2560], P('dp'), may hold values from -8 to 8
- attn_gain: bfloat16 [2560], P('dp'), may hold values from 0.25 to 1.75
- q_down: bfloat16 [2560, 768], P('dp'), may hold values from -0.125 to 0.125
- q_gain: bfloat16 [768], P('dp'), may hold values from 0.25 to 1.75
- q_up: bfloat16 [768, 3840], P('dp', 'tensor'), may hold values from -0.21875 to 0.21875
- kv_down: bfloat16 [2560, 288], P('dp'), may hold values from -0.125 to 0.125
- kv_gain: bfloat16 [256], P('dp'), may hold values from 0.25 to 1.75
- kv_up: bfloat16 [256, 5120], P('dp', 'tensor'), may hold values from -0.375 to 0.375
- o_proj: bfloat16 [2560, 2560], P('tensor', 'dp'), may hold values from -4 to 4
- mlp_gain: bfloat16 [2560], P('dp'), may hold values from 0.25 to 1.75
- w_gate: bfloat16 [2560, 6400], P('dp', 'tensor'), may hold values from -0.125 to 0.125
- w_up: bfloat16 [2560, 6400], P('dp', 'tensor'), may hold values from -0.125 to 0.125
- w_down: bfloat16 [6400, 2560], P('tensor', 'dp'), may hold values from -1.5 to 1.5
Outputs:
- block_out: float32 [1536, 2560], P('dp')
- grad_input: float32 [1536, 2560], P('dp')
- grad_attn_gain: float32 [2560], P('dp')
- grad_q_down: float32 [2560, 768], P('dp')
- grad_q_gain: float32 [768], P('dp')
- grad_q_up: float32 [768, 3840], P('dp', 'tensor')
- grad_kv_down: float32 [2560, 288], P('dp')
- grad_kv_gain: float32 [256], P('dp')
- grad_kv_up: float32 [256, 5120], P('dp', 'tensor')
- grad_o_proj: float32 [2560, 2560], P('tensor', 'dp')
- grad_mlp_gain: float32 [2560], P('dp')
- grad_w_gate: float32 [2560, 6400], P('dp', 'tensor')
- grad_w_up: float32 [2560, 6400], P('dp', 'tensor')
- grad_w_down: float32 [6400, 2560], P('tensor', 'dp')
- rms_stats: float32 [3], replicated
The draws below stay inside these ranges and needn't reach their ends.
Inputs may be any that keep to these rules, and one draw needn't show every extreme that they name: `segment_ids`: within each sequence of 192 tokens the ids start at 0 and never fall; a document is a run of equal ids, and padding tokens carry the id of their sequence's last document. `valid_mask`: within each sequence the valid tokens are a leading run, followed by padding; the last sequence has no padding.
All inputs are finite; a program needn't handle non-finite values.
Results may differ from the reference program's by a relative error of at most 0.024.
Values may be sent and summed in bfloat16 or wider, within the bound.
A program may use at most 192 MiB of HBM per device.

```python
import math
import jax
import jax.numpy as jnp
from jax import lax

D = 2560
QR = 768
KR = 256
H = 40
NOPE = 64
ROPE = 32
VD = 64
FF = 6400
LEN = 192
TOKENS = 1536
N_DP = 8


def draw_layer_input(key, part):
    first, second, third = jax.random.split(key, 3)
    column = jnp.exp(jax.random.uniform(second, (1, D), jnp.float32, math.log(0.3), math.log(3.0)))
    row_scale = jnp.exp(jax.random.uniform(third, (TOKENS, 1), jnp.float32, math.log(0.3), math.log(3.0)))
    base = jnp.clip(jax.random.normal(first, (TOKENS, D), jnp.float32), -6.0, 6.0)
    return (base * column * row_scale).astype(jnp.bfloat16)


def doc_layout(key):
    folded = jax.random.fold_in(key, 11)
    first, second, third = jax.random.split(folded, 3)
    count = TOKENS // LEN
    seq_index = jnp.arange(count)
    last_seq = seq_index == count - 1
    base_len = LEN // 3 + (LEN - LEN // 3) * seq_index // max(count - 1, 1)
    jitter = jax.random.randint(first, (count,), 0, LEN // 16 + 1)
    jitter = jnp.where(last_seq, 0, jitter)
    valid_len = base_len - jitter
    power = jax.random.randint(second, (count,), 0, 6)
    power = jnp.where(last_seq, 5, power)
    starts_count = jnp.left_shift(jnp.ones_like(power), power) - 1
    places = jax.random.randint(third, (count, 31), 1, valid_len[:, None])
    spaced = 1 + jnp.arange(31, dtype=jnp.int32) * ((LEN - 1) // 31)
    places = jnp.where(last_seq[:, None], spaced[None, :], places)
    in_use = jnp.arange(31)[None, :] < starts_count[:, None]
    position = jnp.arange(LEN)
    starts = jnp.any((places[:, :, None] == position[None, None, :]) & in_use[:, :, None], axis=1).astype(jnp.int32)
    segment = jnp.cumsum(starts, axis=1).astype(jnp.int32)
    valid_row = (position[None, :] < valid_len[:, None]).astype(jnp.int32)
    return (segment.reshape(TOKENS), valid_row.reshape(TOKENS))


def draw_segment_ids(key, part):
    return doc_layout(key)[0]


def draw_valid_mask(key, part):
    return doc_layout(key)[1]


def raised(drawn, rng, source, target, blocks, factor):
    owner, partner = [(jnp.arange(drawn.shape[axis_at]) // (drawn.shape[axis_at] // blocks)).reshape([-1 if axis == axis_at else 1 for axis in range(drawn.ndim)]) for axis_at in (source, target)]
    chosen = jax.random.permutation(rng, blocks)[partner]
    strong = (owner == chosen) | (owner == (partner + blocks // 2) % blocks)
    return jnp.where(strong, factor * drawn, drawn)


def block_scale(stream_key, dims, cuts, low, top_value):
    level, own = 1.0, jax.random.fold_in(stream_key, 6)
    for axis_at, shards_of in cuts:
        steps = jnp.exp(jax.random.uniform(jax.random.fold_in(own, axis_at), (shards_of,), jnp.float32, low / len(cuts), top_value / len(cuts)))
        level = level * jnp.repeat(steps, dims[axis_at] // shards_of).reshape([-1 if axis == axis_at else 1 for axis in range(len(dims))])
    return level


def scatter_about(stream_key, shape, deviation, bound, pieces=(), kind=jnp.bfloat16):
    drawn = deviation * jax.random.normal(stream_key, shape, jnp.float32)
    if pieces:
        drawn = drawn * block_scale(stream_key, shape, pieces, -0.22, 0.18)
    return jnp.clip(drawn, -bound, bound).astype(kind)


def noise_with(stream_key, dims, deviation, most, cuts, heavy, kind=jnp.bfloat16):
    array = deviation * jax.random.normal(stream_key, dims, jnp.float32)
    if cuts:
        array = array * block_scale(stream_key, dims, cuts, -0.22, 0.18)
    return jnp.clip(raised(array, jax.random.fold_in(stream_key, 3), *heavy), -most, most).astype(kind)


def setup_inputs(seed: int = 0) -> dict:
    keys = jax.random.split(jax.random.key(seed), 17)
    return {
        "layer_input": draw_layer_input(jax.random.fold_in(keys[16], 71), 0),
        "segment_ids": draw_segment_ids(jax.random.fold_in(keys[16], 71), 0),
        "valid_mask": draw_valid_mask(jax.random.fold_in(keys[16], 71), 0),
        "cotangent": noise_with(keys[3], (TOKENS, D), 1.0, 8.0, ((0, 8),), (0, 1, 8, 2.0)),
        "attn_gain": jnp.clip(1.0 + 0.15 * jax.random.normal(keys[4], (D,), jnp.float32), 0.25, 1.75).astype(jnp.bfloat16),
        "q_down": scatter_about(keys[5], (D, QR), D ** -0.5, 0.125, ((0, 8),)),
        "q_gain": jnp.clip(1.0 + 0.15 * jax.random.normal(keys[6], (QR,), jnp.float32), 0.25, 1.75).astype(jnp.bfloat16),
        "q_up": scatter_about(keys[7], (QR, H * (NOPE + ROPE)), QR ** -0.5, 0.21875, ((0, 8), (1, 4))),
        "kv_down": scatter_about(keys[8], (D, KR + ROPE), D ** -0.5, 0.125, ((0, 8),)),
        "kv_gain": jnp.clip(1.0 + 0.15 * jax.random.normal(keys[9], (KR,), jnp.float32), 0.25, 1.75).astype(jnp.bfloat16),
        "kv_up": scatter_about(keys[10], (KR, H * (NOPE + VD)), KR ** -0.5, 0.375, ((0, 8), (1, 4))),
        "o_proj": scatter_about(keys[11], (H * VD, D), (max(H * VD // 1280, 1)) ** -0.5, 4.0, ((0, 4), (1, 8))),
        "mlp_gain": jnp.clip(1.0 + 0.15 * jax.random.normal(keys[12], (D,), jnp.float32), 0.25, 1.75).astype(jnp.bfloat16),
        "w_gate": scatter_about(keys[13], (D, FF), D ** -0.5, 0.125, ((0, 8), (1, 4))),
        "w_up": scatter_about(keys[14], (D, FF), D ** -0.5, 0.125, ((0, 8), (1, 4))),
        "w_down": scatter_about(keys[15], (FF, D), (max(FF // 400, 1)) ** -0.5, 1.5, ((0, 4), (1, 8))),
    }


NORM_EPS = 1e-05
RESIDUAL_SCALE = 1.4 / math.sqrt(62.0)
ROPE_BASE = 10000.0
NEGATIVE = -1e+30
HIGHEST = lax.Precision.HIGHEST

@jax.custom_vjp
def low(v):
    return lax.optimization_barrier(v.astype(jnp.bfloat16)).astype(jnp.float32)

@jax.custom_vjp
def low_back(v):
    return v

def low_keep(v):
    return (low(v), None)

def low_pass(kept, grad):
    return (grad,)

def back_keep(v):
    return (v, None)

def back_low(kept, grad):
    return (low(grad),)
low.defvjp(low_keep, low_pass)
low_back.defvjp(back_keep, back_low)

def rope_tables(length, rot_dim):
    half_dim = rot_dim // 2
    position = jnp.arange(length, dtype=jnp.float32)
    frequency = jnp.exp(-math.log(ROPE_BASE) * 2.0 * jnp.arange(half_dim, dtype=jnp.float32) / rot_dim)
    phases = position[:, None] * frequency[None, :]
    return (jnp.cos(phases), jnp.sin(phases))

def rotate(values, cosine, sine_table):
    half_dim = values.shape[-1] // 2
    first_half = values[..., :half_dim]
    second_half = values[..., half_dim:]
    return jnp.concatenate([first_half * cosine - second_half * sine_table, second_half * cosine + first_half * sine_table], axis=-1)

def rms_normal(values, gain_row):
    return values * lax.rsqrt(lax.optimization_barrier(jnp.mean(values * values, axis=-1, keepdims=True)) + NORM_EPS) * gain_row

def matmul(left, right):
    return jnp.dot(left, right, precision=HIGHEST)

def attend(queries, key_rows, value_rows, allowed):
    inv_root = 1.0 / math.sqrt(queries.shape[-1])
    scores = low_back(jnp.einsum('qhd,khd->hqk', queries, key_rows, precision=HIGHEST) * inv_root)
    scores = jnp.where(allowed[None], scores, NEGATIVE)
    row_max = lax.optimization_barrier(jnp.max(scores, axis=-1, keepdims=True))
    weights = jnp.exp(scores - row_max)
    probs = low(weights / lax.optimization_barrier(jnp.sum(weights, axis=-1, keepdims=True)))
    mixed = jnp.einsum('hqk,khd->qhd', probs, value_rows, precision=HIGHEST)
    return mixed.reshape(mixed.shape[0], -1)

def block_forward(stream, segment, valid_row, params):
    attn_gain, q_down, q_gain, q_up, kv_down, kv_gain, kv_up, o_proj, mlp_gain, w_gate, w_up, w_down = params
    length = stream.shape[0]
    cosine, sine_table = rope_tables(length, ROPE)
    normed = low(rms_normal(stream, attn_gain))
    q_latent = low_back(matmul(normed, q_down))
    q_normed = low(rms_normal(q_latent, q_gain))
    q_heads = low_back(matmul(q_normed, q_up)).reshape(length, H, NOPE + ROPE)
    kv_joint = low_back(matmul(normed, kv_down))
    kv_normed = low(rms_normal(kv_joint[:, :KR], kv_gain))
    kv_heads = low_back(matmul(kv_normed, kv_up)).reshape(length, H, NOPE + VD)
    queries = low(jnp.concatenate([q_heads[..., :NOPE], rotate(q_heads[..., NOPE:], cosine[:, None, :], sine_table[:, None, :])], axis=-1))
    key_rot = rotate(kv_joint[:, KR:], cosine, sine_table)
    key_rows = low(jnp.concatenate([kv_heads[..., :NOPE], jnp.broadcast_to(key_rot[:, None, :], (length, H, ROPE))], axis=-1))
    value_rows = low(kv_heads[..., NOPE:])
    position = jnp.arange(length)
    allowed = (segment[:, None] == segment[None, :]) & (position[None, :] <= position[:, None]) & ((valid_row[None, :] == 1) | (position[None, :] == position[:, None]))
    attend_block = jax.checkpoint(lambda query_in, key_in, value_in: attend(query_in, key_in, value_in, allowed))
    mixed = low(low_back(attend_block(queries, key_rows, value_rows)))
    attn_out = low_back(matmul(mixed, o_proj))
    resid = stream + RESIDUAL_SCALE * attn_out
    normed_two = low(rms_normal(resid, mlp_gain))
    gate = low_back(matmul(normed_two, w_gate))
    upper = low_back(matmul(normed_two, w_up))
    hidden = low(gate * jax.nn.sigmoid(gate) * upper)
    mlp_out = low_back(matmul(hidden, w_down))
    return (resid + RESIDUAL_SCALE * mlp_out, (resid, attn_out, mlp_out))

def reference(layer_input, segment_ids, valid_mask, cotangent, attn_gain, q_down, q_gain, q_up, kv_down, kv_gain, kv_up, o_proj, mlp_gain, w_gate, w_up, w_down):
    params = tuple((weight.astype(jnp.float32) for weight in (attn_gain, q_down, q_gain, q_up, kv_down, kv_gain, kv_up, o_proj, mlp_gain, w_gate, w_up, w_down)))
    streams = layer_input.astype(jnp.float32).reshape(N_DP, LEN, D)
    segments = segment_ids.reshape(N_DP, LEN)
    valids = valid_mask.reshape(N_DP, LEN)
    cotangents = cotangent.astype(jnp.float32).reshape(N_DP, LEN, D)
    zero_grads = tuple((jnp.zeros(weight.shape, jnp.float32) for weight in params))
    zero_stats = jnp.zeros((4,), jnp.float32)

    def per_sequence(carry, sequence_item):
        totals, stat_sums = carry
        stream, segment, valid_row, cot_row = sequence_item

        def forward_fn(stream_in, *weights):
            return block_forward(stream_in, segment, valid_row, weights)
        result, pullback, extras = jax.vjp(forward_fn, stream, *params, has_aux=True)
        resid, attn_out, mlp_out = extras
        grads = pullback(cot_row)
        totals = tuple((total + part for total, part in zip(totals, grads[1:])))
        weight_rows = valid_row.astype(jnp.float32)[:, None]
        attn_branch = RESIDUAL_SCALE * attn_out
        mlp_branch = RESIDUAL_SCALE * mlp_out
        stat_sums = stat_sums + jnp.stack([jnp.sum(weight_rows * resid * resid), jnp.sum(weight_rows * attn_branch * attn_branch), jnp.sum(weight_rows * mlp_branch * mlp_branch), jnp.sum(weight_rows)])
        return ((totals, stat_sums), (result, grads[0]))
    (totals, stat_sums), (results, input_grads) = lax.scan(per_sequence, (zero_grads, zero_stats), (streams, segments, valids, cotangents))
    rms_stats = jnp.sqrt(stat_sums[:3] / (stat_sums[3] * D))
    return (results.reshape(TOKENS, D), input_grads.reshape(TOKENS, D), totals[0], totals[1], totals[2], totals[3], totals[4], totals[5], totals[6], totals[7], totals[8], totals[9], totals[10], totals[11], rms_stats)
```

```python
import math

import jax
import jax.numpy as jnp
from jax import lax
from jax.sharding import PartitionSpec as P

D = 2560
KR = 256
NOPE = 64
ROPE = 32
VD = 64


NORM_EPS = 1e-05
RESIDUAL_SCALE = 1.4 / math.sqrt(62.0)
ROPE_BASE = 10000.0
NEGATIVE = -1e30


def rope_tables(length, rot_dim):
    half_dim = rot_dim // 2
    position = jnp.arange(length, dtype=jnp.float32)
    frequency = jnp.exp(
        -math.log(ROPE_BASE) * 2.0 * jnp.arange(half_dim, dtype=jnp.float32) / rot_dim
    )
    phases = position[:, None] * frequency[None, :]
    return (jnp.cos(phases), jnp.sin(phases))


def rotate(values, cosine, sine_table):
    half_dim = values.shape[-1] // 2
    first_half = values[..., :half_dim]
    second_half = values[..., half_dim:]
    return jnp.concatenate(
        [
            first_half * cosine - second_half * sine_table,
            second_half * cosine + first_half * sine_table,
        ],
        axis=-1,
    )


def unrotate(grads, cosine, sine_table):
    half_dim = grads.shape[-1] // 2
    first_half = grads[..., :half_dim]
    second_half = grads[..., half_dim:]
    return jnp.concatenate(
        [
            first_half * cosine + second_half * sine_table,
            second_half * cosine - first_half * sine_table,
        ],
        axis=-1,
    )


def inverse_rms(values):
    return lax.rsqrt(jnp.mean(values * values, axis=-1, keepdims=True) + NORM_EPS)


def norm_back(grad_unit, unit, inv_rms):
    return inv_rms * (grad_unit - unit * jnp.mean(grad_unit * unit, axis=-1, keepdims=True))


def attend_forward(query_major, key_major, value_major, allowed):
    inv_root = 1.0 / math.sqrt(query_major.shape[-1])

    def one_head(operands):
        query_head, key_head, value_head = operands
        scores = (
            jnp.einsum("qd,kd->qk", query_head, key_head, preferred_element_type=jnp.float32)
            * inv_root
        )
        scores = jnp.where(allowed, scores, NEGATIVE)
        row_max = jnp.max(scores, axis=-1, keepdims=True)
        weights = jnp.exp(scores - row_max)
        totals = jnp.sum(weights, axis=-1, keepdims=True)
        probs_low = (weights / totals).astype(jnp.bfloat16)
        mixed_head = jnp.dot(probs_low, value_head, preferred_element_type=jnp.float32)
        return (mixed_head, row_max[:, 0] + jnp.log(totals[:, 0]))

    return lax.map(one_head, (query_major, key_major, value_major))


def attend_backward(query_major, key_major, value_major, grad_major, log_norm, allowed):
    inv_root = 1.0 / math.sqrt(query_major.shape[-1])

    def one_head(operands):
        query_head, key_head, value_head, grad_head, norm_head = operands
        scores = (
            jnp.einsum("qd,kd->qk", query_head, key_head, preferred_element_type=jnp.float32)
            * inv_root
        )
        scores = jnp.where(allowed, scores, NEGATIVE)
        probs = jnp.exp(scores - norm_head[:, None])
        probs_low = probs.astype(jnp.bfloat16)
        grad_value = jnp.einsum(
            "qk,qd->kd", probs_low, grad_head, preferred_element_type=jnp.float32
        )
        grad_probs = jnp.einsum(
            "qd,kd->qk", grad_head, value_head, preferred_element_type=jnp.float32
        )
        inner = jnp.sum(probs * grad_probs, axis=-1, keepdims=True)
        grad_scores = (probs * (grad_probs - inner)).astype(jnp.bfloat16)
        grad_query = jnp.dot(grad_scores, key_head, preferred_element_type=jnp.float32) * inv_root
        grad_key = (
            jnp.einsum("qk,qd->kd", grad_scores, query_head, preferred_element_type=jnp.float32)
            * inv_root
        )
        return (grad_query, grad_key, grad_value)

    return lax.map(one_head, (query_major, key_major, value_major, grad_major, log_norm))


BF = jnp.bfloat16
F32 = jnp.float32
EVERY = ("dp", "tensor")


def dot(left, right):
    return jnp.dot(left, right, preferred_element_type=F32)


def dot_nt(left, right):
    return jnp.einsum("ac,bc->ab", left, right, preferred_element_type=F32)


def dot_tn(left, right):
    return jnp.einsum("ca,cb->ab", left, right, preferred_element_type=F32)


def gather_dp(block):
    return lax.all_gather(block, "dp", axis=0, tiled=True)


def gather_tensor(block):
    return lax.all_gather(block, "tensor", axis=0, tiled=True)


def gather_every(block):
    return lax.all_gather(block, EVERY, axis=0, tiled=True)


def scatter_dp(part):
    return lax.psum_scatter(part, "dp", scatter_dimension=0, tiled=True).astype(F32)


def scatter_tensor(part):
    return lax.psum_scatter(part, "tensor", scatter_dimension=0, tiled=True).astype(F32)


def scatter_every(part):
    return lax.psum_scatter(part, EVERY, scatter_dimension=0, tiled=True).astype(F32)


def swap_dp(blocks):
    return lax.all_to_all(blocks, "dp", 0, 0, tiled=True)


def per_device(
    layer_input,
    segment_ids,
    valid_mask,
    cotangent,
    attn_gain,
    q_down,
    q_gain,
    q_up,
    kv_down,
    kv_gain,
    kv_up,
    o_proj,
    mlp_gain,
    w_gate,
    w_up,
    w_down,
):
    length = layer_input.shape[0]
    heads_local = q_up.shape[1] // (NOPE + ROPE)
    n_dp = lax.axis_size("dp")
    n_tensor = lax.axis_size("tensor")
    share = length // n_tensor
    me = lax.axis_index("tensor")
    width = w_gate.shape[0]
    slice_ff = w_gate.shape[1] // n_dp
    rows_down = width // n_tensor

    def rows_of(values, count):
        return lax.dynamic_slice_in_dim(values, me * count, count, 0)

    full_q_down = gather_every(rows_of(q_down, rows_down))
    full_kv_down = gather_every(rows_of(kv_down, rows_down))
    full_q_up = gather_dp(q_up)
    full_kv_up = gather_dp(kv_up)
    gain_attn = gather_dp(attn_gain).astype(F32)
    gain_q = gather_dp(q_gain).astype(F32)
    gain_kv = gather_dp(kv_gain).astype(F32)
    gain_mlp = gather_dp(mlp_gain).astype(F32)
    full_o = gather_dp(o_proj.T)

    packed = jnp.concatenate(
        [
            w_gate.reshape(width, n_dp, slice_ff),
            w_up.reshape(width, n_dp, slice_ff),
            w_down.T.reshape(width, n_dp, slice_ff),
        ],
        axis=2,
    ).transpose(1, 0, 2)
    mine = swap_dp(packed).reshape(n_dp * width, 3 * slice_ff)
    w_in = mine[:, : 2 * slice_ff]
    w_out = mine[:, 2 * slice_ff :]

    stream = layer_input.astype(F32)
    cosine, sine_table = rope_tables(length, ROPE)
    head_cos = cosine[:, None, :]
    head_sin = sine_table[:, None, :]
    inv_one = inverse_rms(stream)
    unit_one = stream * inv_one
    normed = (unit_one * gain_attn).astype(BF)
    q_latent = dot(normed, full_q_down)
    inv_q = inverse_rms(q_latent)
    unit_q = q_latent * inv_q
    q_normed = (unit_q * gain_q).astype(BF)
    q_heads = dot(q_normed, full_q_up).reshape(length, heads_local, NOPE + ROPE)
    kv_joint = dot(normed, full_kv_down)
    kv_latent = kv_joint[:, :KR]
    inv_kv = inverse_rms(kv_latent)
    unit_kv = kv_latent * inv_kv
    kv_normed = (unit_kv * gain_kv).astype(BF)
    kv_heads = dot(kv_normed, full_kv_up).reshape(length, heads_local, NOPE + VD)
    queries = jnp.concatenate(
        [q_heads[..., :NOPE], rotate(q_heads[..., NOPE:], head_cos, head_sin)], axis=-1
    ).astype(BF)
    key_rot = rotate(kv_joint[:, KR:], cosine, sine_table)
    key_rows = jnp.concatenate(
        [kv_heads[..., :NOPE], jnp.broadcast_to(key_rot[:, None, :], (length, heads_local, ROPE))],
        axis=-1,
    ).astype(BF)
    value_rows = kv_heads[..., NOPE:].astype(BF)
    position = jnp.arange(length)
    allowed = (
        (segment_ids[:, None] == segment_ids[None, :])
        & (position[None, :] <= position[:, None])
        & ((valid_mask[None, :] == 1) | (position[None, :] == position[:, None]))
    )
    query_major = queries.transpose(1, 0, 2)
    key_major = key_rows.transpose(1, 0, 2)
    value_major = value_rows.transpose(1, 0, 2)
    mixed_heads, log_norm = attend_forward(query_major, key_major, value_major, allowed)
    mixed = mixed_heads.transpose(1, 0, 2).reshape(length, heads_local * VD).astype(BF)
    attn_part = dot_nt(mixed, full_o)

    attn_rows = RESIDUAL_SCALE * scatter_tensor(attn_part.astype(BF))
    resid_rows = rows_of(layer_input, share).astype(F32) + attn_rows
    inv_two = inverse_rms(resid_rows)
    unit_two = resid_rows * inv_two
    normed_two = gather_every((unit_two * gain_mlp).astype(BF))
    cot_rows = rows_of(cotangent, share)
    grad_mlp = (RESIDUAL_SCALE * gather_every(cot_rows).astype(F32)).astype(BF)

    gate_upper = dot(normed_two, w_in)
    gate = gate_upper[:, :slice_ff]
    upper = gate_upper[:, slice_ff:]
    sigma = jax.nn.sigmoid(gate)
    swish = gate * sigma
    hidden = (swish * upper).astype(BF)
    mlp_rows = RESIDUAL_SCALE * scatter_every(dot_nt(hidden, w_out).astype(BF))
    grad_hidden = dot(grad_mlp, w_out)
    grad_both = jnp.concatenate(
        [
            grad_hidden * upper * (sigma * (1.0 + gate * (1.0 - sigma))),
            grad_hidden * swish,
        ],
        axis=1,
    ).astype(BF)
    grad_normed_two = scatter_every(dot_nt(grad_both, w_in).astype(BF))
    grad_packed = jnp.concatenate(
        [dot_tn(normed_two, grad_both), dot_tn(grad_mlp, hidden)], axis=1
    ).astype(BF)
    swapped = swap_dp(grad_packed.reshape(n_dp, width, 3 * slice_ff))

    def unpack(part):
        return part.transpose(1, 0, 2).reshape(width, n_dp * slice_ff).astype(F32)

    grad_w_gate = unpack(swapped[:, :, :slice_ff])
    grad_w_up = unpack(swapped[:, :, slice_ff : 2 * slice_ff])
    grad_w_down = unpack(swapped[:, :, 2 * slice_ff :]).T

    block_rows = resid_rows + mlp_rows
    block_full = gather_tensor(block_rows)
    weight_rows = rows_of(valid_mask.astype(F32)[:, None], share)
    grad_mlp_gain = jnp.sum(grad_normed_two * unit_two, axis=0)
    grad_resid_rows = cot_rows.astype(F32) + norm_back(
        grad_normed_two * gain_mlp, unit_two, inv_two
    )
    grad_attn = gather_tensor((RESIDUAL_SCALE * grad_resid_rows).astype(BF))

    grad_o = dot_tn(grad_attn, mixed)
    grad_mixed = dot(grad_attn, full_o).astype(BF)
    grad_major = grad_mixed.reshape(length, heads_local, VD).transpose(1, 0, 2)
    grad_q_major, grad_k_major, grad_v_major = attend_backward(
        query_major, key_major, value_major, grad_major, log_norm, allowed
    )
    grad_queries = grad_q_major.transpose(1, 0, 2)
    grad_keys = grad_k_major.transpose(1, 0, 2)
    grad_values = grad_v_major.transpose(1, 0, 2)
    grad_q_heads = (
        jnp.concatenate(
            [grad_queries[..., :NOPE], unrotate(grad_queries[..., NOPE:], head_cos, head_sin)],
            axis=-1,
        )
        .reshape(length, heads_local * (NOPE + ROPE))
        .astype(BF)
    )
    grad_kv_heads = (
        jnp.concatenate([grad_keys[..., :NOPE], grad_values], axis=-1)
        .reshape(length, heads_local * (NOPE + VD))
        .astype(BF)
    )
    grad_key_rot = unrotate(jnp.sum(grad_keys[..., NOPE:], axis=1), cosine, sine_table)
    grad_q_up = dot_tn(q_normed, grad_q_heads)
    grad_kv_up = dot_tn(kv_normed, grad_kv_heads)
    grad_latents = lax.psum(
        jnp.concatenate(
            [
                dot_nt(grad_q_heads, full_q_up),
                dot_nt(grad_kv_heads, full_kv_up),
                grad_key_rot,
            ],
            axis=1,
        ).astype(BF),
        "tensor",
    ).astype(F32)
    rank_q = q_latent.shape[1]
    grad_q_normed = grad_latents[:, :rank_q]
    grad_kv_normed = grad_latents[:, rank_q : rank_q + KR]
    grad_kv_rot = grad_latents[:, rank_q + KR :]
    grad_q_gain = jnp.sum(grad_q_normed * unit_q, axis=0)
    grad_kv_gain = jnp.sum(grad_kv_normed * unit_kv, axis=0)
    grad_q_latent = norm_back(grad_q_normed * gain_q, unit_q, inv_q).astype(BF)
    grad_kv_joint = jnp.concatenate(
        [norm_back(grad_kv_normed * gain_kv, unit_kv, inv_kv), grad_kv_rot], axis=-1
    ).astype(BF)
    grad_normed = dot_nt(grad_q_latent, full_q_down) + dot_nt(grad_kv_joint, full_kv_down)
    grad_attn_gain = jnp.sum(grad_normed * unit_one, axis=0)
    grad_input = grad_attn.astype(F32) * (1.0 / RESIDUAL_SCALE) + norm_back(
        grad_normed * gain_attn, unit_one, inv_one
    )

    quarter = lax.dynamic_index_in_dim(
        normed.reshape(length, n_dp, n_tensor, rows_down), me, 2, keepdims=False
    ).reshape(length, n_dp * rows_down)
    grad_q_down = gather_tensor(scatter_dp(dot_tn(quarter, grad_q_latent).astype(BF)).astype(BF))
    grad_kv_down = gather_tensor(scatter_dp(dot_tn(quarter, grad_kv_joint).astype(BF)).astype(BF))

    stat_sums = lax.psum(
        (
            jnp.sum(weight_rows * resid_rows * resid_rows),
            jnp.sum(weight_rows * attn_rows * attn_rows),
            jnp.sum(weight_rows * mlp_rows * mlp_rows),
            jnp.sum(weight_rows),
        ),
        EVERY,
    )
    rms_stats = jnp.sqrt(jnp.stack(stat_sums[:3]) / (stat_sums[3] * D))
    return (
        block_full,
        grad_input,
        scatter_dp(grad_attn_gain),
        grad_q_down.astype(F32),
        scatter_dp(grad_q_gain),
        scatter_dp(grad_q_up.astype(BF)),
        grad_kv_down.astype(F32),
        scatter_dp(grad_kv_gain),
        scatter_dp(grad_kv_up.astype(BF)),
        scatter_dp(grad_o.astype(BF)).T,
        scatter_dp(lax.psum(grad_mlp_gain, "tensor")),
        grad_w_gate,
        grad_w_up,
        grad_w_down,
        rms_stats,
    )


def solution(mesh):
    placed = (
        P("dp", None),
        P("dp"),
        P("dp"),
        P("dp", None),
        P("dp"),
        P("dp", None),
        P("dp"),
        P("dp", "tensor"),
        P("dp", None),
        P("dp"),
        P("dp", "tensor"),
        P("tensor", "dp"),
        P("dp"),
        P("dp", "tensor"),
        P("dp", "tensor"),
        P("tensor", "dp"),
    )
    return jax.shard_map(
        per_device,
        mesh=mesh,
        in_specs=placed,
        out_specs=(
            P("dp", None),
            P("dp", None),
            P("dp"),
            P("dp", None),
            P("dp"),
            P("dp", "tensor"),
            P("dp", None),
            P("dp"),
            P("dp", "tensor"),
            P("tensor", "dp"),
            P("dp"),
            P("dp", "tensor"),
            P("dp", "tensor"),
            P("tensor", "dp"),
            P(),
        ),
        check_vma=False,
    )
```

```python
import functools
import math

import jax
import jax.numpy as jnp
from jax import lax
from jax.experimental import pallas as pl
from jax.experimental.pallas import tpu as pltpu
from jax.sharding import PartitionSpec as P

D = 2560
KR = 256
NOPE = 64
ROPE = 32
VD = 64


NORM_EPS = 1e-05
RESIDUAL_SCALE = 1.4 / math.sqrt(62.0)
ROPE_BASE = 10000.0
NEGATIVE = -1e30


def rope_tables(length, rot_dim):
    half_dim = rot_dim // 2
    position = jnp.arange(length, dtype=jnp.float32)
    frequency = jnp.exp(
        -math.log(ROPE_BASE) * 2.0 * jnp.arange(half_dim, dtype=jnp.float32) / rot_dim
    )
    phases = position[:, None] * frequency[None, :]
    return (jnp.cos(phases), jnp.sin(phases))


def rotate(values, cosine, sine_table):
    half_dim = values.shape[-1] // 2
    first_half = values[..., :half_dim]
    second_half = values[..., half_dim:]
    return jnp.concatenate(
        [
            first_half * cosine - second_half * sine_table,
            second_half * cosine + first_half * sine_table,
        ],
        axis=-1,
    )


def unrotate(grads, cosine, sine_table):
    half_dim = grads.shape[-1] // 2
    first_half = grads[..., :half_dim]
    second_half = grads[..., half_dim:]
    return jnp.concatenate(
        [
            first_half * cosine + second_half * sine_table,
            second_half * cosine - first_half * sine_table,
        ],
        axis=-1,
    )


def inverse_rms(values):
    return lax.rsqrt(jnp.mean(values * values, axis=-1, keepdims=True) + NORM_EPS)


def norm_back(grad_unit, unit, inv_rms):
    return inv_rms * (grad_unit - unit * jnp.mean(grad_unit * unit, axis=-1, keepdims=True))


def attend_forward(query_major, key_major, value_major, allowed):
    inv_root = 1.0 / math.sqrt(query_major.shape[-1])

    def one_head(operands):
        query_head, key_head, value_head = operands
        scores = (
            jnp.einsum("qd,kd->qk", query_head, key_head, preferred_element_type=jnp.float32)
            * inv_root
        )
        scores = jnp.where(allowed, scores, NEGATIVE)
        row_max = jnp.max(scores, axis=-1, keepdims=True)
        weights = jnp.exp(scores - row_max)
        totals = jnp.sum(weights, axis=-1, keepdims=True)
        probs_low = (weights / totals).astype(jnp.bfloat16)
        mixed_head = jnp.dot(probs_low, value_head, preferred_element_type=jnp.float32)
        return (mixed_head, row_max[:, 0] + jnp.log(totals[:, 0]))

    return lax.map(one_head, (query_major, key_major, value_major))


def attend_backward(query_major, key_major, value_major, grad_major, log_norm, allowed):
    inv_root = 1.0 / math.sqrt(query_major.shape[-1])

    def one_head(operands):
        query_head, key_head, value_head, grad_head, norm_head = operands
        scores = (
            jnp.einsum("qd,kd->qk", query_head, key_head, preferred_element_type=jnp.float32)
            * inv_root
        )
        scores = jnp.where(allowed, scores, NEGATIVE)
        probs = jnp.exp(scores - norm_head[:, None])
        probs_low = probs.astype(jnp.bfloat16)
        grad_value = jnp.einsum(
            "qk,qd->kd", probs_low, grad_head, preferred_element_type=jnp.float32
        )
        grad_probs = jnp.einsum(
            "qd,kd->qk", grad_head, value_head, preferred_element_type=jnp.float32
        )
        inner = jnp.sum(probs * grad_probs, axis=-1, keepdims=True)
        grad_scores = (probs * (grad_probs - inner)).astype(jnp.bfloat16)
        grad_query = jnp.dot(grad_scores, key_head, preferred_element_type=jnp.float32) * inv_root
        grad_key = (
            jnp.einsum("qk,qd->kd", grad_scores, query_head, preferred_element_type=jnp.float32)
            * inv_root
        )
        return (grad_query, grad_key, grad_value)

    return lax.map(one_head, (query_major, key_major, value_major, grad_major, log_norm))


BF = jnp.bfloat16
F32 = jnp.float32


def dot(left, right):
    return jnp.dot(left, right, preferred_element_type=F32)


def dot_nt(left, right):
    return jnp.einsum("ac,bc->ab", left, right, preferred_element_type=F32)


def dot_tn(left, right):
    return jnp.einsum("ca,cb->ab", left, right, preferred_element_type=F32)


def swap_dp(blocks):
    return lax.all_to_all(blocks, "dp", 0, 0, tiled=True)


MESH = pl.DeviceIdType.MESH
ANY = pl.BlockSpec(memory_space=pl.ANY)
VMEM = pl.BlockSpec(memory_space=pltpu.VMEM)
VMEM_BYTES = 60 * 1024 * 1024


class Links:
    def __init__(self, n_dp):
        self.n_high = n_dp // 2
        dp = lax.axis_index("dp")
        tensor = lax.axis_index("tensor")
        self.high, self.low = dp // 2, dp % 2
        self.side, self.core = tensor // 2, tensor % 2

    def device(self, high=None, low=None, side=None, core=None):
        high = self.high if high is None else high
        low = self.low if low is None else low
        side = self.side if side is None else side
        core = self.core if core is None else core
        return {"dp": high * 2 + low, "tensor": side * 2 + core}

    def behind(self, step):
        return (self.high + self.n_high - step) % self.n_high

    def ahead(self, step):
        return (self.high + step) % self.n_high

    def over_low(self):
        return self.device(low=1 - self.low)

    def over_side(self):
        return self.device(side=1 - self.side)

    def over_core(self):
        return self.device(core=1 - self.core)

    def meet(self, high=True, low=True, side=True, core=True):
        barrier = pltpu.get_barrier_semaphore()
        partners = []
        if high:
            partners += [self.device(high=self.ahead(k)) for k in range(1, self.n_high)]
        if low:
            partners.append(self.over_low())
        if side:
            partners.append(self.over_side())
        if core:
            partners.append(self.over_core())
        for partner in partners:
            pl.semaphore_signal(barrier, inc=1, device_id=partner, device_id_type=MESH)
        pl.semaphore_wait(barrier, len(partners))


class Copies:
    def __init__(self, send, recv, local):
        self.send, self.recv, self.local = send, recv, local
        self.count = self.local_count = 0
        self.started = []
        self.local_started = []

    def go(self, source, target, device):
        copy = pltpu.make_async_remote_copy(
            src_ref=source,
            dst_ref=target,
            send_sem=self.send.at[self.count],
            recv_sem=self.recv.at[self.count],
            device_id=device,
            device_id_type=MESH,
        )
        self.count += 1
        copy.start()
        self.started.append(copy)
        return copy

    def near(self, source, target):
        copy = pltpu.make_async_copy(source, target, self.local.at[self.local_count])
        self.local_count += 1
        copy.start()
        self.local_started.append(copy)
        return copy

    def finish(self):
        for copy in self.started:
            copy.wait_send()


def take_turns(*streams):
    streams = list(streams)
    while streams:
        for stream in list(streams):
            try:
                next(stream)
            except StopIteration:
                streams.remove(stream)


def steps_by_distance(count):
    order, k = [], 1
    while len(order) < count - 1:
        order.append(k)
        if len(order) < count - 1:
            order.append(count - k)
        k += 1
    return order


def every_gather(links, copies, block, out):
    n_high = links.n_high
    cut = out.shape[-1] // 256 * 128
    halves = (pl.ds(0, cut), pl.ds(cut, out.shape[-1] - cut))

    def slot(high, low, side):
        return out.at[high * 2 + low, side * 2 + links.core]

    mine = slot(links.high, links.low, links.side)
    own = copies.near(block, mine)
    arrive = {}
    for k in steps_by_distance(n_high):
        arrive[k] = copies.go(block, mine, links.device(high=links.ahead(k)))
    yield
    order = [0] + steps_by_distance(n_high)
    last, over_low, over_side, corner_a, corner_b = [], {}, {}, {}, {}

    def first(k):
        here = slot(links.behind(k), links.low, links.side)
        if k:
            arrive[k].wait_recv()
        source = here if k else block
        over_low[k] = copies.go(source, here, links.over_low())
        over_side[k] = copies.go(source, here, links.over_side())
        last.append(copies.go(source, here, links.over_core()))

    def second(k):
        over_low[k].wait_recv()
        here = slot(links.behind(k), 1 - links.low, links.side)
        part = here.at[:, halves[0]]
        corner_a[k] = copies.go(part, part, links.over_side())
        last.append(copies.go(here, here, links.over_core()))
        over_side[k].wait_recv()
        here = slot(links.behind(k), links.low, 1 - links.side)
        part = here.at[:, halves[1]]
        corner_b[k] = copies.go(part, part, links.over_low())
        last.append(copies.go(here, here, links.over_core()))

    def third(k):
        here = slot(links.behind(k), 1 - links.low, 1 - links.side)
        for corner, half in ((corner_a, halves[0]), (corner_b, halves[1])):
            corner[k].wait_recv()
            part = here.at[:, half]
            last.append(copies.go(part, part, links.over_core()))

    for i in range(n_high + 2):
        if i < n_high:
            first(order[i])
            yield
        if 0 <= i - 1 < n_high:
            second(order[i - 1])
            yield
        if 0 <= i - 2:
            third(order[i - 2])
            yield
    for copy in last:
        copy.wait_recv()
    own.wait()


def dp_gather(links, copies, block, out):
    mine = out.at[links.high * 2 + links.low]
    own = copies.near(block, mine)
    arrive, last = {}, []
    for k in steps_by_distance(links.n_high):
        arrive[k] = copies.go(block, mine, links.device(high=links.ahead(k)))
    last.append(copies.go(block, mine, links.over_low()))
    yield
    for k in steps_by_distance(links.n_high):
        arrive[k].wait_recv()
        here = out.at[links.behind(k) * 2 + links.low]
        last.append(copies.go(here, here, links.over_low()))
        yield
    for copy in last:
        copy.wait_recv()
    own.wait()


def tensor_gather(links, copies, block, out):
    mine = out.at[links.side * 2 + links.core]
    own = copies.near(block, mine)
    last = [copies.go(block, mine, links.over_core())]
    across = copies.go(block, mine, links.over_side())
    yield
    across.wait_recv()
    here = out.at[(1 - links.side) * 2 + links.core]
    last.append(copies.go(here, here, links.over_core()))
    yield
    for copy in last:
        copy.wait_recv()
    own.wait()


def every_scatter(links, copies, part, bufs, result):
    own, from_core, low_a, side_b, side_a, low_b, done, from_high = bufs
    n_high = links.n_high
    columns = part.shape[-1]
    cut = columns // 256 * 128
    half_a, half_b = pl.ds(0, cut), pl.ds(cut, columns - cut)
    order = steps_by_distance(n_high) + [0]
    loads, core_in, a_in, b_in, a_last, b_last, high_in = {}, {}, {}, {}, {}, {}, {}
    for k in order:
        there = links.ahead(k)
        core_in[k] = copies.go(
            part.at[there, :, :, 1 - links.core], from_core.at[k], links.over_core()
        )
        loads[k] = copies.near(part.at[there, :, :, links.core], own.at[k])
    yield

    def first(k):
        core_in[k].wait_recv()
        loads[k].wait()
        for low in range(2):
            for side in range(2):
                own[k, low, side] = (
                    own[k, low, side].astype(F32) + from_core[k, low, side].astype(F32)
                ).astype(BF)
        a_in[k] = copies.go(
            own.at[k, 1 - links.low, :, :, half_a], low_a.at[k], links.over_low()
        )
        b_in[k] = copies.go(
            own.at[k, :, 1 - links.side, :, half_b], side_b.at[k], links.over_side()
        )

    def second(k):
        a_in[k].wait_recv()
        for side in range(2):
            low_a[k, side] = (
                low_a[k, side].astype(F32) + own[k, links.low, side, :, half_a].astype(F32)
            ).astype(BF)
        a_last[k] = copies.go(low_a.at[k, 1 - links.side], side_a.at[k], links.over_side())
        b_in[k].wait_recv()
        for low in range(2):
            side_b[k, low] = (
                side_b[k, low].astype(F32) + own[k, low, links.side, :, half_b].astype(F32)
            ).astype(BF)
        b_last[k] = copies.go(side_b.at[k, 1 - links.low], low_b.at[k], links.over_low())

    def third(k):
        a_last[k].wait_recv()
        done[k, :, half_a] = (
            side_a[k].astype(F32) + low_a[k, links.side].astype(F32)
        ).astype(BF)
        b_last[k].wait_recv()
        done[k, :, half_b] = (
            low_b[k].astype(F32) + side_b[k, links.low].astype(F32)
        ).astype(BF)
        if k:
            high_in[k] = copies.go(
                done.at[k], from_high.at[k - 1], links.device(high=links.ahead(k))
            )

    for i in range(n_high + 2):
        if i < n_high:
            first(order[i])
            yield
        if 0 <= i - 1 < n_high:
            second(order[i - 1])
            yield
        if 0 <= i - 2:
            third(order[i - 2])
            yield
    total = done[0].astype(F32)
    for k in steps_by_distance(n_high):
        high_in[k].wait_recv()
        total = total + from_high[k - 1].astype(F32)
    result[...] = total


def every_scatter_scratch(n_high, rows, columns):
    cut = columns // 256 * 128
    return [
        pltpu.VMEM((n_high, 2, 2, rows, columns), BF),
        pltpu.VMEM((n_high, 2, 2, rows, columns), BF),
        pltpu.VMEM((n_high, 2, rows, cut), BF),
        pltpu.VMEM((n_high, 2, rows, columns - cut), BF),
        pltpu.VMEM((n_high, rows, cut), BF),
        pltpu.VMEM((n_high, rows, columns - cut), BF),
        pltpu.VMEM((n_high, rows, columns), BF),
        pltpu.VMEM((n_high - 1, rows, columns), BF),
    ]


def dp_scatter(links, copies, part, bufs, result):
    from_low, done, from_high = bufs
    order = steps_by_distance(links.n_high) + [0]
    low_in, high_in = {}, {}
    for k in order:
        low_in[k] = copies.go(
            part.at[links.ahead(k), 1 - links.low], from_low.at[k], links.over_low()
        )
    yield
    for k in order:
        low_in[k].wait_recv()
        done[k] = (
            part[links.ahead(k), links.low].astype(F32) + from_low[k].astype(F32)
        ).astype(BF)
        if k:
            high_in[k] = copies.go(
                done.at[k], from_high.at[k - 1], links.device(high=links.ahead(k))
            )
        yield
    total = done[0].astype(F32)
    for k in steps_by_distance(links.n_high):
        high_in[k].wait_recv()
        total = total + from_high[k - 1].astype(F32)
    result[...] = total.astype(result.dtype)
    yield


def dp_scatter_scratch(n_high, shape):
    return [
        pltpu.VMEM((n_high, *shape), BF),
        pltpu.VMEM((n_high, *shape), BF),
        pltpu.VMEM((n_high - 1, *shape), BF),
    ]


def semaphores(count, local):
    return [
        pltpu.SemaphoreType.DMA((count,)),
        pltpu.SemaphoreType.DMA((count,)),
        pltpu.SemaphoreType.DMA((local,)),
    ]


def params(number):
    return pltpu.CompilerParams(
        collective_id=number, has_side_effects=True, vmem_limit_bytes=VMEM_BYTES
    )


def count_every_gather(n_high):
    return n_high - 1 + 9 * n_high


def weights_kernel(n_dp, down, o_t, q_up, kv_up, gains, cot, f_down, f_o, f_q, f_kv, f_g, f_cot, send, recv, local):
    links = Links(n_dp)
    copies = Copies(send, recv, local)
    links.meet()
    take_turns(
        every_gather(links, copies, down, f_down),
        dp_gather(links, copies, gains, f_g),
        dp_gather(links, copies, q_up, f_q),
        dp_gather(links, copies, kv_up, f_kv),
        dp_gather(links, copies, o_t, f_o),
        every_gather(links, copies, cot, f_cot),
    )
    copies.finish()


def gather_weights(n_dp, n_tensor, down, o_t, q_up, kv_up, gains, cot):
    n_high = n_dp // 2
    count = 2 * count_every_gather(n_high) + 4 * (2 * n_high - 1)

    def over(block, *lead):
        return jax.ShapeDtypeStruct((*lead, *block.shape), block.dtype)

    return pl.pallas_call(
        functools.partial(weights_kernel, n_dp),
        out_shape=(
            over(down, n_dp, n_tensor),
            over(o_t, n_dp),
            over(q_up, n_dp),
            over(kv_up, n_dp),
            over(gains, n_dp),
            over(cot, n_dp, n_tensor),
        ),
        in_specs=[ANY] * 6,
        out_specs=[ANY] * 6,
        scratch_shapes=semaphores(count, 6),
        compiler_params=params(1),
        name="gather_weights",
    )(down, o_t, q_up, kv_up, gains, cot)


def resid_kernel(n_dp, part, x_rows, gain, full, resid, branch, from_core, out_side, from_side, block, send, recv, local):
    links = Links(n_dp)
    copies = Copies(send, recv, local)
    links.meet()
    arrive = copies.go(part.at[:, 1 - links.core], from_core, links.over_core())
    arrive.wait_recv()
    out_side[...] = (
        part[1 - links.side, links.core].astype(F32) + from_core[1 - links.side].astype(F32)
    ).astype(BF)
    arrive = copies.go(out_side, from_side, links.over_side())
    mine = part[links.side, links.core].astype(F32) + from_core[links.side].astype(F32)
    arrive.wait_recv()
    attn = RESIDUAL_SCALE * (mine + from_side[...].astype(F32))
    stream = x_rows[...].astype(F32) + attn
    branch[...] = attn
    resid[...] = stream
    block[...] = (stream * inverse_rms(stream) * gain[...]).astype(BF)
    take_turns(every_gather(links, copies, block, full))
    copies.finish()


def attention_residual(n_dp, part, x_rows, gain):
    n_tensor = 4
    rows, columns = x_rows.shape
    block = (rows, columns)
    return pl.pallas_call(
        functools.partial(resid_kernel, n_dp),
        out_shape=(
            jax.ShapeDtypeStruct((n_dp, n_tensor, rows, columns), BF),
            jax.ShapeDtypeStruct(block, F32),
            jax.ShapeDtypeStruct(block, F32),
        ),
        in_specs=[VMEM] * 3,
        out_specs=[ANY, VMEM, VMEM],
        scratch_shapes=[
            pltpu.VMEM((2, *block), BF),
            pltpu.VMEM(block, BF),
            pltpu.VMEM(block, BF),
            pltpu.VMEM(block, BF),
            *semaphores(2 + count_every_gather(n_dp // 2), 1),
        ],
        compiler_params=params(2),
        name="attention_residual",
    )(part.reshape(2, 2, rows, columns), x_rows, gain)


def grad_rows_kernel(n_dp, both, *refs):
    links = Links(n_dp)
    copies = Copies(*refs[-3:])
    g_part, resid, cot, gain = refs[:4]
    if both:
        m_part, attn_full, g_rows, block_full, m_rows = refs[4:9]
        scratch = refs[9:-3]
    else:
        attn_full, g_rows = refs[4:6]
        scratch = refs[6:-3]
    links.meet()

    def grad_stream():
        grad_rows = scratch[0]
        yield from every_scatter(links, copies, g_part, scratch[1:9], g_rows)
        stream = resid[...]
        inv = inverse_rms(stream)
        grad = cot[...].astype(F32) + norm_back(g_rows[...] * gain[...], stream * inv, inv)
        grad_rows[...] = (RESIDUAL_SCALE * grad).astype(BF)
        yield from tensor_gather(links, copies, grad_rows, attn_full)

    if both:
        block = block_stream(links, copies, m_part, resid, block_full, m_rows, scratch[9:])
        take_turns(grad_stream(), block)
    else:
        take_turns(grad_stream())
    copies.finish()


def block_stream(links, copies, m_part, resid, block_full, m_rows, scratch):
    block_rows = scratch[0]
    yield from every_scatter(links, copies, m_part, scratch[1:9], m_rows)
    m_rows[...] = RESIDUAL_SCALE * m_rows[...]
    block_rows[...] = resid[...] + m_rows[...]
    yield from tensor_gather(links, copies, block_rows, block_full)


def block_rows_kernel(n_dp, m_part, resid, block_full, m_rows, *rest):
    links = Links(n_dp)
    copies = Copies(*rest[-3:])
    links.meet()
    take_turns(block_stream(links, copies, m_part, resid, block_full, m_rows, rest[:-3]))
    copies.finish()


def residual_grads(n_dp, g_part, m_part, resid, cot, gain):
    n_high = n_dp // 2
    rows, columns = resid.shape
    shape = (n_high, 2, 2, 2, rows, columns)
    g_part, m_part = g_part.reshape(shape), m_part.reshape(shape)
    both = n_high <= 4
    one = jax.ShapeDtypeStruct((rows, columns), F32)
    grad_out = (jax.ShapeDtypeStruct((4, rows, columns), BF), one)
    block_out = (jax.ShapeDtypeStruct((4, rows, columns), F32), one)
    grad_scratch = [
        pltpu.VMEM((rows, columns), BF),
        *every_scatter_scratch(n_high, rows, columns),
    ]
    block_scratch = [
        pltpu.VMEM((rows, columns), F32),
        *every_scatter_scratch(n_high, rows, columns),
    ]
    count, local = 6 * n_high - 1 + 3, n_high + 1
    if both:
        return pl.pallas_call(
            functools.partial(grad_rows_kernel, n_dp, True),
            out_shape=grad_out + block_out,
            in_specs=[ANY, VMEM, VMEM, VMEM, ANY],
            out_specs=[ANY, VMEM, ANY, VMEM],
            scratch_shapes=[*grad_scratch, *block_scratch, *semaphores(2 * count, 2 * local)],
            compiler_params=params(3),
            name="residual_grads",
        )(g_part, resid, cot, gain, m_part)
    grads = pl.pallas_call(
        functools.partial(grad_rows_kernel, n_dp, False),
        out_shape=grad_out,
        in_specs=[ANY, VMEM, VMEM, VMEM],
        out_specs=[ANY, VMEM],
        scratch_shapes=[*grad_scratch, *semaphores(count, local)],
        compiler_params=params(3),
        name="residual_grads",
    )(g_part, resid, cot, gain)
    block = pl.pallas_call(
        functools.partial(block_rows_kernel, n_dp),
        out_shape=block_out,
        in_specs=[ANY, VMEM],
        out_specs=[ANY, VMEM],
        scratch_shapes=[*block_scratch, *semaphores(count, local)],
        compiler_params=params(6),
        name="block_rows",
    )(m_part, resid)
    return (*grads, *block)


def latent_kernel(n_dp, part, full, from_core, half, from_side, send, recv, local):
    links = Links(n_dp)
    copies = Copies(send, recv, local)
    links.meet(high=False, low=False)
    arrive = copies.go(part.at[1 - links.core], from_core, links.over_core())
    arrive.wait_recv()
    half[...] = (part[links.core].astype(F32) + from_core[...].astype(F32)).astype(BF)
    arrive = copies.go(half, from_side, links.over_side())
    arrive.wait_recv()
    full[links.core] = (half[...].astype(F32) + from_side[...].astype(F32)).astype(BF)
    arrive = copies.go(full.at[links.core], full.at[links.core], links.over_core())
    arrive.wait_recv()
    copies.finish()


def sum_latents(n_dp, part):
    rows, columns = part.shape
    half = (rows // 2, columns)
    return pl.pallas_call(
        functools.partial(latent_kernel, n_dp),
        out_shape=jax.ShapeDtypeStruct((2, *half), BF),
        in_specs=[VMEM],
        out_specs=VMEM,
        scratch_shapes=[pltpu.VMEM(half, BF)] * 3 + semaphores(3, 1),
        compiler_params=params(4),
        name="sum_latents",
    )(part.reshape(2, *half)).reshape(rows, columns)


def weight_grads_kernel(n_dp, d_part, o_part, q_part, kv_part, small, stats, d_full, o_sum, q_sum, kv_sum, small_full, *rest):
    d_block, small_block, stats_block = rest[:3]
    bufs = rest[3:15]
    small_in, stats_in = rest[15:17]
    send, recv, local = rest[17:]
    links = Links(n_dp)
    copies = Copies(send, recv, local)
    links.meet()

    def small_stream():
        n_high = links.n_high
        low_in = copies.go(
            small.at[:, 1 - links.low], small_in.at[pl.ds(0, n_high)], links.over_low()
        )
        stats_low = copies.go(stats, stats_in.at[0], links.over_low())
        yield
        low_in.wait_recv()
        stats_low.wait_recv()
        for k in range(n_high):
            small_in[k] = small_in[k] + small[k, links.low]
        stats_block[...] = stats[...] + stats_in[0]
        waits = []
        for k in range(1, n_high):
            there = links.ahead(k)
            waits.append(
                copies.go(
                    small_in.at[there], small_in.at[n_high + k - 1], links.device(high=there)
                )
            )
            waits.append(copies.go(stats_block, stats_in.at[k], links.device(high=there)))
        yield
        for wait in waits:
            wait.wait_recv()
        total = small_in[links.high]
        everything = stats_block[...]
        for k in range(1, n_high):
            total = total + small_in[n_high + k - 1]
            everything = everything + stats_in[k]
        small_block[0] = total
        small_block[1] = everything
        yield from tensor_gather(links, copies, small_block, small_full)

    def down_stream():
        yield from dp_scatter(links, copies, d_part, bufs[:3], d_block)
        yield from tensor_gather(links, copies, d_block, d_full)

    take_turns(
        down_stream(),
        dp_scatter(links, copies, q_part, bufs[6:9], q_sum),
        dp_scatter(links, copies, kv_part, bufs[9:12], kv_sum),
        dp_scatter(links, copies, o_part, bufs[3:6], o_sum),
        small_stream(),
    )
    copies.finish()


def sum_weight_grads(n_dp, down, o_t, q_up, kv_up, small, stats):
    n_high = n_dp // 2

    def parts(array):
        return array.reshape(n_high, 2, array.shape[0] // n_dp, *array.shape[1:])

    down, o_t, q_up, kv_up = parts(down), parts(o_t), parts(q_up), parts(kv_up)
    small = small.reshape(n_high, 2, *small.shape[1:])
    count = 4 * (2 * n_high - 1) + 2 * n_high + 6
    d_shape, o_shape, q_shape, kv_shape = (a.shape[2:] for a in (down, o_t, q_up, kv_up))
    one = stats.shape
    return pl.pallas_call(
        functools.partial(weight_grads_kernel, n_dp),
        out_shape=(
            jax.ShapeDtypeStruct((4, *d_shape), BF),
            jax.ShapeDtypeStruct(o_shape, F32),
            jax.ShapeDtypeStruct(q_shape, F32),
            jax.ShapeDtypeStruct(kv_shape, F32),
            jax.ShapeDtypeStruct((4, 2, *one), F32),
        ),
        in_specs=[VMEM] * 6,
        out_specs=[VMEM] * 5,
        scratch_shapes=[
            pltpu.VMEM(d_shape, BF),
            pltpu.VMEM((2, *one), F32),
            pltpu.VMEM(one, F32),
            *dp_scatter_scratch(n_high, d_shape),
            *dp_scatter_scratch(n_high, o_shape),
            *dp_scatter_scratch(n_high, q_shape),
            *dp_scatter_scratch(n_high, kv_shape),
            pltpu.VMEM((2 * n_high - 1, *one), F32),
            pltpu.VMEM((n_high, *one), F32),
            *semaphores(count, 2),
        ],
        compiler_params=params(5),
        name="sum_weight_grads",
    )(down, o_t, q_up, kv_up, small, stats)


def per_device(
    layer_input,
    segment_ids,
    valid_mask,
    cotangent,
    attn_gain,
    q_down,
    q_gain,
    q_up,
    kv_down,
    kv_gain,
    kv_up,
    o_proj,
    mlp_gain,
    w_gate,
    w_up,
    w_down,
):
    length = layer_input.shape[0]
    heads_local = q_up.shape[1] // (NOPE + ROPE)
    n_dp = lax.axis_size("dp")
    n_tensor = lax.axis_size("tensor")
    share = length // n_tensor
    me = lax.axis_index("tensor")
    width = w_gate.shape[0]
    slice_ff = w_gate.shape[1] // n_dp
    rows_down = width // n_tensor

    def rows_of(values, count):
        return lax.dynamic_slice_in_dim(values, me * count, count, 0)

    rank_q = q_down.shape[1]
    columns_down = rank_q + kv_down.shape[1]
    pad_down = -columns_down % 128
    down_rows = jnp.concatenate(
        [
            rows_of(q_down, rows_down),
            rows_of(kv_down, rows_down),
            jnp.zeros((rows_down, pad_down), BF),
        ],
        axis=1,
    )
    lanes = -(-width // 128) * 128

    def lane_rows(rows, count, kind):
        padded = [jnp.pad(row.astype(kind), (0, lanes - row.shape[0])) for row in rows]
        return jnp.stack(padded + [jnp.zeros((lanes,), kind)] * (count - len(padded)))

    cot_rows = rows_of(cotangent, share)
    f_down, f_o, f_q, f_kv, f_g, f_cot = gather_weights(
        n_dp,
        n_tensor,
        down_rows,
        o_proj.T,
        q_up,
        kv_up,
        lane_rows([attn_gain, q_gain, kv_gain, mlp_gain], 16, BF),
        cot_rows,
    )
    full_down = f_down.reshape(n_dp * width, columns_down + pad_down)
    full_o = f_o.reshape(n_dp * width, -1)
    full_kv_up = f_kv.reshape(-1, kv_up.shape[1])

    def gain_of(row, gain):
        return f_g[:, row, : gain.shape[0]].reshape(-1).astype(F32)

    gain_attn = gain_of(0, attn_gain)
    gain_q = gain_of(1, q_gain)
    gain_kv = gain_of(2, kv_gain)
    gain_mlp = gain_of(3, mlp_gain)

    packed = jnp.concatenate(
        [
            w_gate.reshape(width, n_dp, slice_ff),
            w_up.reshape(width, n_dp, slice_ff),
            w_down.T.reshape(width, n_dp, slice_ff),
        ],
        axis=2,
    ).transpose(1, 0, 2)
    packed, f_q = lax.optimization_barrier((packed, f_q))
    mine = swap_dp(packed).reshape(n_dp * width, 3 * slice_ff)
    full_q_up = f_q.reshape(-1, q_up.shape[1])
    w_in = mine[:, : 2 * slice_ff]
    w_out = mine[:, 2 * slice_ff :]

    stream = layer_input.astype(F32)
    cosine, sine_table = rope_tables(length, ROPE)
    head_cos = cosine[:, None, :]
    head_sin = sine_table[:, None, :]
    inv_one = inverse_rms(stream)
    unit_one = stream * inv_one
    normed = (unit_one * gain_attn).astype(BF)
    latents = dot(normed, full_down)
    q_latent = latents[:, :rank_q]
    inv_q = inverse_rms(q_latent)
    unit_q = q_latent * inv_q
    q_normed = (unit_q * gain_q).astype(BF)
    q_heads = dot(q_normed, full_q_up).reshape(length, heads_local, NOPE + ROPE)
    kv_joint = latents[:, rank_q:columns_down]
    kv_latent = kv_joint[:, :KR]
    inv_kv = inverse_rms(kv_latent)
    unit_kv = kv_latent * inv_kv
    kv_normed = (unit_kv * gain_kv).astype(BF)
    kv_heads = dot(kv_normed, full_kv_up).reshape(length, heads_local, NOPE + VD)
    queries = jnp.concatenate(
        [q_heads[..., :NOPE], rotate(q_heads[..., NOPE:], head_cos, head_sin)], axis=-1
    ).astype(BF)
    key_rot = rotate(kv_joint[:, KR:], cosine, sine_table)
    key_rows = jnp.concatenate(
        [kv_heads[..., :NOPE], jnp.broadcast_to(key_rot[:, None, :], (length, heads_local, ROPE))],
        axis=-1,
    ).astype(BF)
    value_rows = kv_heads[..., NOPE:].astype(BF)
    position = jnp.arange(length)
    allowed = (
        (segment_ids[:, None] == segment_ids[None, :])
        & (position[None, :] <= position[:, None])
        & ((valid_mask[None, :] == 1) | (position[None, :] == position[:, None]))
    )
    query_major = queries.transpose(1, 0, 2)
    key_major = key_rows.transpose(1, 0, 2)
    value_major = value_rows.transpose(1, 0, 2)
    mixed_heads, log_norm = attend_forward(query_major, key_major, value_major, allowed)
    mixed = mixed_heads.transpose(1, 0, 2).reshape(length, heads_local * VD).astype(BF)
    attn_part = dot_nt(mixed, full_o)

    x_rows = rows_of(layer_input, share)
    f_normed, resid_rows, attn_rows = attention_residual(
        n_dp, attn_part.astype(BF), x_rows, gain_mlp[None, :]
    )
    normed_two = f_normed.reshape(n_dp * length, -1)
    inv_two = inverse_rms(resid_rows)
    unit_two = resid_rows * inv_two
    grad_mlp = (RESIDUAL_SCALE * f_cot.reshape(n_dp * length, -1).astype(F32)).astype(BF)

    gate_upper = dot(normed_two, w_in)
    gate = gate_upper[:, :slice_ff]
    upper = gate_upper[:, slice_ff:]
    sigma = jax.nn.sigmoid(gate)
    swish = gate * sigma
    hidden = (swish * upper).astype(BF)
    mlp_part = dot_nt(hidden, w_out).astype(BF)
    grad_hidden = dot(grad_mlp, w_out)
    grad_both = jnp.concatenate(
        [
            grad_hidden * upper * (sigma * (1.0 + gate * (1.0 - sigma))),
            grad_hidden * swish,
        ],
        axis=1,
    ).astype(BF)
    normed_part = dot_nt(grad_both, w_in).astype(BF)
    grad_packed = jnp.concatenate(
        [dot_tn(normed_two, grad_both), dot_tn(grad_mlp, hidden)], axis=1
    ).astype(BF)
    swapped = swap_dp(grad_packed.reshape(n_dp, width, 3 * slice_ff))
    normed_part, grad_packed = lax.optimization_barrier((normed_part, grad_packed))
    f_attn, grad_normed_two, f_block, mlp_rows = residual_grads(
        n_dp, normed_part, mlp_part, resid_rows, cot_rows, gain_mlp[None, :]
    )
    grad_attn = f_attn.reshape(length, -1)
    block_full = f_block.reshape(length, -1)

    def unpack(part):
        return part.transpose(1, 0, 2).reshape(width, n_dp * slice_ff).astype(F32)

    weight_rows = rows_of(valid_mask.astype(F32)[:, None], share)
    grad_mlp_gain = jnp.sum(grad_normed_two * unit_two, axis=0)

    grad_o = dot_tn(grad_attn, mixed)
    grad_mixed = dot(grad_attn, full_o).astype(BF)
    grad_major = grad_mixed.reshape(length, heads_local, VD).transpose(1, 0, 2)
    grad_q_major, grad_k_major, grad_v_major = attend_backward(
        query_major, key_major, value_major, grad_major, log_norm, allowed
    )
    grad_queries = grad_q_major.transpose(1, 0, 2)
    grad_keys = grad_k_major.transpose(1, 0, 2)
    grad_values = grad_v_major.transpose(1, 0, 2)
    grad_q_heads = (
        jnp.concatenate(
            [grad_queries[..., :NOPE], unrotate(grad_queries[..., NOPE:], head_cos, head_sin)],
            axis=-1,
        )
        .reshape(length, heads_local * (NOPE + ROPE))
        .astype(BF)
    )
    grad_kv_heads = (
        jnp.concatenate([grad_keys[..., :NOPE], grad_values], axis=-1)
        .reshape(length, heads_local * (NOPE + VD))
        .astype(BF)
    )
    grad_key_rot = unrotate(jnp.sum(grad_keys[..., NOPE:], axis=1), cosine, sine_table)
    grad_q_heads, swapped = lax.optimization_barrier((grad_q_heads, swapped))
    grad_q_up = dot_tn(q_normed, grad_q_heads)
    grad_kv_up = dot_tn(kv_normed, grad_kv_heads)
    grad_latents = sum_latents(
        n_dp,
        jnp.concatenate(
            [
                dot_nt(grad_q_heads, full_q_up),
                dot_nt(grad_kv_heads, full_kv_up),
                grad_key_rot,
                jnp.zeros((length, pad_down), F32),
            ],
            axis=1,
        ).astype(BF),
    ).astype(F32)
    grad_q_normed = grad_latents[:, :rank_q]
    grad_kv_normed = grad_latents[:, rank_q : rank_q + KR]
    grad_kv_rot = grad_latents[:, rank_q + KR : columns_down]
    grad_q_gain = jnp.sum(grad_q_normed * unit_q, axis=0)
    grad_kv_gain = jnp.sum(grad_kv_normed * unit_kv, axis=0)
    grad_down = jnp.concatenate(
        [
            norm_back(grad_q_normed * gain_q, unit_q, inv_q),
            norm_back(grad_kv_normed * gain_kv, unit_kv, inv_kv),
            grad_kv_rot,
            jnp.zeros((length, pad_down), F32),
        ],
        axis=-1,
    ).astype(BF)
    grad_normed = dot_nt(grad_down, full_down)
    grad_attn_gain = jnp.sum(grad_normed * unit_one, axis=0)
    grad_input = grad_attn.astype(F32) * (1.0 / RESIDUAL_SCALE) + norm_back(
        grad_normed * gain_attn, unit_one, inv_one
    )

    quarter = lax.dynamic_index_in_dim(
        normed.reshape(length, n_dp, n_tensor, rows_down), me, 2, keepdims=False
    ).reshape(length, n_dp * rows_down)
    def by_dp(vector):
        return vector.reshape(n_dp, -1)

    def small_rows(vectors):
        return jnp.stack(
            [jnp.pad(by_dp(v), ((0, 0), (0, lanes - v.shape[0] // n_dp))) for v in vectors]
            + [jnp.zeros((n_dp, lanes), F32)] * (8 - len(vectors)),
            axis=1,
        )

    stats = jnp.stack(
        [
            jnp.sum(weight_rows * resid_rows * resid_rows),
            jnp.sum(weight_rows * attn_rows * attn_rows),
            jnp.sum(weight_rows * mlp_rows * mlp_rows),
            jnp.sum(weight_rows),
        ]
    )
    s_down, s_o, s_q, s_kv, s_small = sum_weight_grads(
        n_dp,
        dot_tn(quarter, grad_down).astype(BF),
        grad_o.astype(BF),
        grad_q_up.astype(BF),
        grad_kv_up.astype(BF),
        small_rows([grad_attn_gain, grad_q_gain, grad_kv_gain, grad_mlp_gain]),
        lane_rows([stats], 8, F32),
    )
    grad_w_gate = unpack(swapped[:, :, :slice_ff])
    grad_w_up = unpack(swapped[:, :, slice_ff : 2 * slice_ff])
    grad_w_down = unpack(swapped[:, :, 2 * slice_ff :]).T

    d_down = s_down.reshape(width, -1).astype(F32)
    gains = s_small[me, 0]
    stat_sums = jnp.sum(s_small[:, 1, 0, :4], axis=0)
    rms_stats = jnp.sqrt(stat_sums[:3] / (stat_sums[3] * D))
    return (
        block_full,
        grad_input,
        gains[0, : attn_gain.shape[0]],
        d_down[:, :rank_q],
        gains[1, : q_gain.shape[0]],
        s_q,
        d_down[:, rank_q:columns_down],
        gains[2, : kv_gain.shape[0]],
        s_kv,
        s_o.T,
        jnp.sum(s_small[:, 0, 3], axis=0)[: mlp_gain.shape[0]],
        grad_w_gate,
        grad_w_up,
        grad_w_down,
        rms_stats,
    )


def solution(mesh):
    placed = (
        P("dp", None),
        P("dp"),
        P("dp"),
        P("dp", None),
        P("dp"),
        P("dp", None),
        P("dp"),
        P("dp", "tensor"),
        P("dp", None),
        P("dp"),
        P("dp", "tensor"),
        P("tensor", "dp"),
        P("dp"),
        P("dp", "tensor"),
        P("dp", "tensor"),
        P("tensor", "dp"),
    )
    return jax.shard_map(
        per_device,
        mesh=mesh,
        in_specs=placed,
        out_specs=(
            P("dp", None),
            P("dp", None),
            P("dp"),
            P("dp", None),
            P("dp"),
            P("dp", "tensor"),
            P("dp", None),
            P("dp"),
            P("dp", "tensor"),
            P("tensor", "dp"),
            P("dp"),
            P("dp", "tensor"),
            P("dp", "tensor"),
            P("tensor", "dp"),
            P(),
        ),
        check_vma=False,
    )
```

```python
import functools
import itertools
import math

import jax
import jax.numpy as jnp
from jax import lax
from jax.experimental import pallas as pl
from jax.experimental.pallas import tpu as pltpu
from jax.sharding import PartitionSpec as P

D = 2560
KR = 256
NOPE = 64
ROPE = 32
VD = 64


NORM_EPS = 1e-05
RESIDUAL_SCALE = 1.4 / math.sqrt(62.0)
ROPE_BASE = 10000.0
NEGATIVE = -1e30


def rope_tables(length, rot_dim):
    half_dim = rot_dim // 2
    position = jnp.arange(length, dtype=jnp.float32)
    frequency = jnp.exp(
        -math.log(ROPE_BASE) * 2.0 * jnp.arange(half_dim, dtype=jnp.float32) / rot_dim
    )
    phases = position[:, None] * frequency[None, :]
    return (jnp.cos(phases), jnp.sin(phases))


def inverse_rms(values):
    return lax.rsqrt(jnp.mean(values * values, axis=-1, keepdims=True) + NORM_EPS)


def norm_back(grad_unit, unit, inv_rms):
    return inv_rms * (grad_unit - unit * jnp.mean(grad_unit * unit, axis=-1, keepdims=True))


BF = jnp.bfloat16
F32 = jnp.float32


def dot(left, right):
    return jnp.dot(left, right, preferred_element_type=F32)


def dot_nt(left, right):
    return jnp.einsum("ac,bc->ab", left, right, preferred_element_type=F32)


def dot_tn(left, right):
    return jnp.einsum("ca,cb->ab", left, right, preferred_element_type=F32)


def swap_dp(blocks):
    return lax.all_to_all(blocks, "dp", 0, 0, tiled=True)


MESH = pl.DeviceIdType.MESH
ANY = pl.BlockSpec(memory_space=pl.ANY)
VMEM = pl.BlockSpec(memory_space=pltpu.VMEM)
VMEM_BYTES = 60 * 1024 * 1024


class Links:
    def __init__(self, n_dp):
        self.n_high = n_dp // 2
        dp = lax.axis_index("dp")
        tensor = lax.axis_index("tensor")
        self.high, self.low = dp // 2, dp % 2
        self.side, self.core = tensor // 2, tensor % 2

    def device(self, high=None, low=None, side=None, core=None):
        high = self.high if high is None else high
        low = self.low if low is None else low
        side = self.side if side is None else side
        core = self.core if core is None else core
        return {"dp": high * 2 + low, "tensor": side * 2 + core}

    def behind(self, step):
        return (self.high + self.n_high - step) % self.n_high

    def ahead(self, step):
        return (self.high + step) % self.n_high

    def over_low(self):
        return self.device(low=1 - self.low)

    def over_side(self):
        return self.device(side=1 - self.side)

    def over_core(self):
        return self.device(core=1 - self.core)

    def meet(self, high=True, low=True, side=True, core=True, swap=False):
        barrier = pltpu.get_barrier_semaphore()
        partners = []
        if swap:
            partners += [
                self.device(high=self.ahead(k), low=1 - self.low) for k in range(1, self.n_high)
            ]
        if high:
            partners += [self.device(high=self.ahead(k)) for k in range(1, self.n_high)]
        if low:
            partners.append(self.over_low())
        if side:
            partners.append(self.over_side())
        if core:
            partners.append(self.over_core())
        for partner in partners:
            pl.semaphore_signal(barrier, inc=1, device_id=partner, device_id_type=MESH)
        pl.semaphore_wait(barrier, len(partners))


class Copies:
    def __init__(self, send, recv, local):
        self.send, self.recv, self.local = send, recv, local
        self.count = self.local_count = 0
        self.started = []
        self.local_started = []

    def go(self, source, target, device):
        copy = pltpu.make_async_remote_copy(
            src_ref=source,
            dst_ref=target,
            send_sem=self.send.at[self.count],
            recv_sem=self.recv.at[self.count],
            device_id=device,
            device_id_type=MESH,
        )
        self.count += 1
        copy.start()
        self.started.append(copy)
        return copy

    def near(self, source, target):
        copy = pltpu.make_async_copy(source, target, self.local.at[self.local_count])
        self.local_count += 1
        copy.start()
        self.local_started.append(copy)
        return copy

    def finish(self):
        for copy in self.started:
            copy.wait_send()


def take_turns(*streams):
    streams = list(streams)
    while streams:
        for stream in list(streams):
            try:
                next(stream)
            except StopIteration:
                streams.remove(stream)


def steps_by_distance(count):
    order, k = [], 1
    while len(order) < count - 1:
        order.append(k)
        if len(order) < count - 1:
            order.append(count - k)
        k += 1
    return order


def every_gather(links, copies, block, out):
    n_high = links.n_high
    cut = out.shape[-1] // 256 * 128
    halves = (pl.ds(0, cut), pl.ds(cut, out.shape[-1] - cut))

    def slot(high, low, side):
        return out.at[high * 2 + low, side * 2 + links.core]

    mine = slot(links.high, links.low, links.side)
    own = copies.near(block, mine)
    arrive = {}
    for k in steps_by_distance(n_high):
        arrive[k] = copies.go(block, mine, links.device(high=links.ahead(k)))
    yield
    order = [0] + steps_by_distance(n_high)
    last, over_low, over_side, corner_a, corner_b = [], {}, {}, {}, {}

    def first(k):
        here = slot(links.behind(k), links.low, links.side)
        if k:
            arrive[k].wait_recv()
        source = here if k else block
        over_low[k] = copies.go(source, here, links.over_low())
        over_side[k] = copies.go(source, here, links.over_side())
        last.append(copies.go(source, here, links.over_core()))

    def second(k):
        over_low[k].wait_recv()
        here = slot(links.behind(k), 1 - links.low, links.side)
        part = here.at[:, halves[0]]
        corner_a[k] = copies.go(part, part, links.over_side())
        last.append(copies.go(here, here, links.over_core()))
        over_side[k].wait_recv()
        here = slot(links.behind(k), links.low, 1 - links.side)
        part = here.at[:, halves[1]]
        corner_b[k] = copies.go(part, part, links.over_low())
        last.append(copies.go(here, here, links.over_core()))

    def third(k):
        here = slot(links.behind(k), 1 - links.low, 1 - links.side)
        for corner, half in ((corner_a, halves[0]), (corner_b, halves[1])):
            corner[k].wait_recv()
            part = here.at[:, half]
            last.append(copies.go(part, part, links.over_core()))

    for i in range(n_high + 2):
        if i < n_high:
            first(order[i])
            yield
        if 0 <= i - 1 < n_high:
            second(order[i - 1])
            yield
        if 0 <= i - 2:
            third(order[i - 2])
            yield
    for copy in last:
        copy.wait_recv()
    own.wait()


def dp_gather(links, copies, block, out):
    mine = out.at[links.high * 2 + links.low]
    own = copies.near(block, mine)
    arrive, last = {}, []
    for k in steps_by_distance(links.n_high):
        arrive[k] = copies.go(block, mine, links.device(high=links.ahead(k)))
    last.append(copies.go(block, mine, links.over_low()))
    yield
    for k in steps_by_distance(links.n_high):
        arrive[k].wait_recv()
        here = out.at[links.behind(k) * 2 + links.low]
        last.append(copies.go(here, here, links.over_low()))
        yield
    for copy in last:
        copy.wait_recv()
    own.wait()


def tensor_gather(links, copies, block, out):
    mine = out.at[links.side * 2 + links.core]
    own = copies.near(block, mine)
    last = [copies.go(block, mine, links.over_core())]
    across = copies.go(block, mine, links.over_side())
    yield
    across.wait_recv()
    here = out.at[(1 - links.side) * 2 + links.core]
    last.append(copies.go(here, here, links.over_core()))
    yield
    for copy in last:
        copy.wait_recv()
    own.wait()


def every_scatter(links, copies, part, bufs, result):
    own, from_core, low_a, side_b, side_a, low_b, done, from_high = bufs
    n_high = links.n_high
    columns = part.shape[-1]
    cut = columns // 256 * 128
    half_a, half_b = pl.ds(0, cut), pl.ds(cut, columns - cut)
    order = steps_by_distance(n_high) + [0]
    loads, core_in, a_in, b_in, a_last, b_last, high_in = {}, {}, {}, {}, {}, {}, {}
    for k in order:
        there = links.ahead(k)
        core_in[k] = copies.go(
            part.at[there, :, :, 1 - links.core], from_core.at[k], links.over_core()
        )
        loads[k] = copies.near(part.at[there, :, :, links.core], own.at[k])
    yield

    def first(k):
        core_in[k].wait_recv()
        loads[k].wait()
        for low in range(2):
            for side in range(2):
                own[k, low, side] = (
                    own[k, low, side].astype(F32) + from_core[k, low, side].astype(F32)
                ).astype(BF)
        a_in[k] = copies.go(
            own.at[k, 1 - links.low, :, :, half_a], low_a.at[k], links.over_low()
        )
        b_in[k] = copies.go(
            own.at[k, :, 1 - links.side, :, half_b], side_b.at[k], links.over_side()
        )

    def second(k):
        a_in[k].wait_recv()
        for side in range(2):
            low_a[k, side] = (
                low_a[k, side].astype(F32) + own[k, links.low, side, :, half_a].astype(F32)
            ).astype(BF)
        a_last[k] = copies.go(low_a.at[k, 1 - links.side], side_a.at[k], links.over_side())
        b_in[k].wait_recv()
        for low in range(2):
            side_b[k, low] = (
                side_b[k, low].astype(F32) + own[k, low, links.side, :, half_b].astype(F32)
            ).astype(BF)
        b_last[k] = copies.go(side_b.at[k, 1 - links.low], low_b.at[k], links.over_low())

    def third(k):
        a_last[k].wait_recv()
        done[k, :, half_a] = (
            side_a[k].astype(F32) + low_a[k, links.side].astype(F32)
        ).astype(BF)
        b_last[k].wait_recv()
        done[k, :, half_b] = (
            low_b[k].astype(F32) + side_b[k, links.low].astype(F32)
        ).astype(BF)
        if k:
            high_in[k] = copies.go(
                done.at[k], from_high.at[k - 1], links.device(high=links.ahead(k))
            )

    for i in range(n_high + 2):
        if i < n_high:
            first(order[i])
            yield
        if 0 <= i - 1 < n_high:
            second(order[i - 1])
            yield
        if 0 <= i - 2:
            third(order[i - 2])
            yield
    total = done[0].astype(F32)
    for k in steps_by_distance(n_high):
        high_in[k].wait_recv()
        total = total + from_high[k - 1].astype(F32)
    result[...] = total


def every_scatter_scratch(n_high, rows, columns):
    cut = columns // 256 * 128
    return [
        pltpu.VMEM((n_high, 2, 2, rows, columns), BF),
        pltpu.VMEM((n_high, 2, 2, rows, columns), BF),
        pltpu.VMEM((n_high, 2, rows, cut), BF),
        pltpu.VMEM((n_high, 2, rows, columns - cut), BF),
        pltpu.VMEM((n_high, rows, cut), BF),
        pltpu.VMEM((n_high, rows, columns - cut), BF),
        pltpu.VMEM((n_high, rows, columns), BF),
        pltpu.VMEM((n_high - 1, rows, columns), BF),
    ]


def dp_scatter(links, copies, part, bufs, result):
    from_low, done, from_high = bufs
    order = steps_by_distance(links.n_high) + [0]
    low_in, high_in = {}, {}
    for k in order:
        low_in[k] = copies.go(
            part.at[links.ahead(k), 1 - links.low], from_low.at[k], links.over_low()
        )
    yield
    for k in order:
        low_in[k].wait_recv()
        done[k] = (
            part[links.ahead(k), links.low].astype(F32) + from_low[k].astype(F32)
        ).astype(BF)
        if k:
            high_in[k] = copies.go(
                done.at[k], from_high.at[k - 1], links.device(high=links.ahead(k))
            )
        yield
    total = done[0].astype(F32)
    for k in steps_by_distance(links.n_high):
        high_in[k].wait_recv()
        total = total + from_high[k - 1].astype(F32)
    result[...] = total.astype(result.dtype)
    yield


def dp_scatter_scratch(n_high, shape):
    return [
        pltpu.VMEM((n_high, *shape), BF),
        pltpu.VMEM((n_high, *shape), BF),
        pltpu.VMEM((n_high - 1, *shape), BF),
    ]


def semaphores(count, local):
    return [
        pltpu.SemaphoreType.DMA((count,)),
        pltpu.SemaphoreType.DMA((count,)),
        pltpu.SemaphoreType.DMA((local,)),
    ]


def params(number):
    return pltpu.CompilerParams(
        collective_id=number, has_side_effects=True, vmem_limit_bytes=VMEM_BYTES
    )


def count_every_gather(n_high):
    return n_high - 1 + 9 * n_high


def weights_kernel(n_dp, down, o_t, q_up, kv_up, gains, cot, f_down, f_o, f_q, f_kv, f_g, f_cot, send, recv, local):
    links = Links(n_dp)
    copies = Copies(send, recv, local)
    links.meet()
    take_turns(
        every_gather(links, copies, down, f_down),
        dp_gather(links, copies, gains, f_g),
        dp_gather(links, copies, q_up, f_q),
        dp_gather(links, copies, kv_up, f_kv),
        dp_gather(links, copies, o_t, f_o),
        every_gather(links, copies, cot, f_cot),
    )
    copies.finish()


def gather_weights(n_dp, n_tensor, down, o_t, q_up, kv_up, gains, cot):
    n_high = n_dp // 2
    count = 2 * count_every_gather(n_high) + 4 * (2 * n_high - 1)

    def over(block, *lead):
        return jax.ShapeDtypeStruct((*lead, *block.shape), block.dtype)

    return pl.pallas_call(
        functools.partial(weights_kernel, n_dp),
        out_shape=(
            over(down, n_dp, n_tensor),
            over(o_t, n_dp),
            over(q_up, n_dp),
            over(kv_up, n_dp),
            over(gains, n_dp),
            over(cot, n_dp, n_tensor),
        ),
        in_specs=[ANY] * 6,
        out_specs=[ANY] * 6,
        scratch_shapes=semaphores(count, 6),
        compiler_params=params(1),
        name="gather_weights",
    )(down, o_t, q_up, kv_up, gains, cot)


def resid_kernel(n_dp, part, x_rows, gain, full, resid, branch, from_core, out_side, from_side, block, send, recv, local):
    links = Links(n_dp)
    copies = Copies(send, recv, local)
    links.meet()
    arrive = copies.go(part.at[:, 1 - links.core], from_core, links.over_core())
    arrive.wait_recv()
    out_side[...] = (
        part[1 - links.side, links.core].astype(F32) + from_core[1 - links.side].astype(F32)
    ).astype(BF)
    arrive = copies.go(out_side, from_side, links.over_side())
    mine = part[links.side, links.core].astype(F32) + from_core[links.side].astype(F32)
    arrive.wait_recv()
    attn = RESIDUAL_SCALE * (mine + from_side[...].astype(F32))
    stream = x_rows[...].astype(F32) + attn
    branch[...] = attn
    resid[...] = stream
    block[...] = (stream * inverse_rms(stream) * gain[...]).astype(BF)
    take_turns(every_gather(links, copies, block, full))
    copies.finish()


def attention_residual(n_dp, part, x_rows, gain):
    n_tensor = 4
    rows, columns = x_rows.shape
    block = (rows, columns)
    return pl.pallas_call(
        functools.partial(resid_kernel, n_dp),
        out_shape=(
            jax.ShapeDtypeStruct((n_dp, n_tensor, rows, columns), BF),
            jax.ShapeDtypeStruct(block, F32),
            jax.ShapeDtypeStruct(block, F32),
        ),
        in_specs=[VMEM] * 3,
        out_specs=[ANY, VMEM, VMEM],
        scratch_shapes=[
            pltpu.VMEM((2, *block), BF),
            pltpu.VMEM(block, BF),
            pltpu.VMEM(block, BF),
            pltpu.VMEM(block, BF),
            *semaphores(2 + count_every_gather(n_dp // 2), 1),
        ],
        compiler_params=params(2),
        name="attention_residual",
    )(part.reshape(2, 2, rows, columns), x_rows, gain)


def grad_rows_kernel(n_dp, both, *refs):
    links = Links(n_dp)
    copies = Copies(*refs[-3:])
    g_part, resid, cot, gain = refs[:4]
    if both:
        m_part, attn_full, g_rows, block_full, m_rows = refs[4:9]
        scratch = refs[9:-3]
    else:
        attn_full, g_rows = refs[4:6]
        scratch = refs[6:-3]
    links.meet()

    def grad_stream():
        grad_rows = scratch[0]
        yield from every_scatter(links, copies, g_part, scratch[1:9], g_rows)
        stream = resid[...]
        inv = inverse_rms(stream)
        grad = cot[...].astype(F32) + norm_back(g_rows[...] * gain[...], stream * inv, inv)
        grad_rows[...] = (RESIDUAL_SCALE * grad).astype(BF)
        yield from tensor_gather(links, copies, grad_rows, attn_full)

    if both:
        block = block_stream(links, copies, m_part, resid, block_full, m_rows, scratch[9:])
        take_turns(grad_stream(), block)
    else:
        take_turns(grad_stream())
    copies.finish()


def block_stream(links, copies, m_part, resid, block_full, m_rows, scratch):
    block_rows = scratch[0]
    yield from every_scatter(links, copies, m_part, scratch[1:9], m_rows)
    m_rows[...] = RESIDUAL_SCALE * m_rows[...]
    block_rows[...] = resid[...] + m_rows[...]
    yield from tensor_gather(links, copies, block_rows, block_full)


def block_rows_kernel(n_dp, m_part, resid, block_full, m_rows, *rest):
    links = Links(n_dp)
    copies = Copies(*rest[-3:])
    links.meet()
    take_turns(block_stream(links, copies, m_part, resid, block_full, m_rows, rest[:-3]))
    copies.finish()


def residual_grads(n_dp, g_part, m_part, resid, cot, gain):
    n_high = n_dp // 2
    rows, columns = resid.shape
    shape = (n_high, 2, 2, 2, rows, columns)
    g_part, m_part = g_part.reshape(shape), m_part.reshape(shape)
    both = n_high <= 4
    one = jax.ShapeDtypeStruct((rows, columns), F32)
    grad_out = (jax.ShapeDtypeStruct((4, rows, columns), BF), one)
    block_out = (jax.ShapeDtypeStruct((4, rows, columns), F32), one)
    grad_scratch = [
        pltpu.VMEM((rows, columns), BF),
        *every_scatter_scratch(n_high, rows, columns),
    ]
    block_scratch = [
        pltpu.VMEM((rows, columns), F32),
        *every_scatter_scratch(n_high, rows, columns),
    ]
    count, local = 6 * n_high - 1 + 3, n_high + 1
    if both:
        return pl.pallas_call(
            functools.partial(grad_rows_kernel, n_dp, True),
            out_shape=grad_out + block_out,
            in_specs=[ANY, VMEM, VMEM, VMEM, ANY],
            out_specs=[ANY, VMEM, ANY, VMEM],
            scratch_shapes=[*grad_scratch, *block_scratch, *semaphores(2 * count, 2 * local)],
            compiler_params=params(3),
            name="residual_grads",
        )(g_part, resid, cot, gain, m_part)
    grads = pl.pallas_call(
        functools.partial(grad_rows_kernel, n_dp, False),
        out_shape=grad_out,
        in_specs=[ANY, VMEM, VMEM, VMEM],
        out_specs=[ANY, VMEM],
        scratch_shapes=[*grad_scratch, *semaphores(count, local)],
        compiler_params=params(3),
        name="residual_grads",
    )(g_part, resid, cot, gain)
    block = pl.pallas_call(
        functools.partial(block_rows_kernel, n_dp),
        out_shape=block_out,
        in_specs=[ANY, VMEM],
        out_specs=[ANY, VMEM],
        scratch_shapes=[*block_scratch, *semaphores(count, local)],
        compiler_params=params(6),
        name="block_rows",
    )(m_part, resid)
    return (*grads, *block)


def latent_kernel(n_dp, part, full, from_core, half, from_side, send, recv, local):
    links = Links(n_dp)
    copies = Copies(send, recv, local)
    links.meet(high=False, low=False)
    arrive = copies.go(part.at[1 - links.core], from_core, links.over_core())
    arrive.wait_recv()
    half[...] = (part[links.core].astype(F32) + from_core[...].astype(F32)).astype(BF)
    arrive = copies.go(half, from_side, links.over_side())
    arrive.wait_recv()
    full[links.core] = (half[...].astype(F32) + from_side[...].astype(F32)).astype(BF)
    arrive = copies.go(full.at[links.core], full.at[links.core], links.over_core())
    arrive.wait_recv()
    copies.finish()


def sum_latents(n_dp, part):
    rows, columns = part.shape
    half = (rows // 2, columns)
    return pl.pallas_call(
        functools.partial(latent_kernel, n_dp),
        out_shape=jax.ShapeDtypeStruct((2, *half), BF),
        in_specs=[VMEM],
        out_specs=VMEM,
        scratch_shapes=[pltpu.VMEM(half, BF)] * 3 + semaphores(3, 1),
        compiler_params=params(4),
        name="sum_latents",
    )(part.reshape(2, *half)).reshape(rows, columns)


def weight_grads_kernel(n_dp, d_part, o_part, q_part, kv_part, small, stats, d_full, o_sum, q_sum, kv_sum, small_full, *rest):
    d_block, small_block, stats_block = rest[:3]
    bufs = rest[3:15]
    small_in, stats_in = rest[15:17]
    send, recv, local = rest[17:]
    links = Links(n_dp)
    copies = Copies(send, recv, local)
    links.meet()

    def small_stream():
        n_high = links.n_high
        low_in = copies.go(
            small.at[:, 1 - links.low], small_in.at[pl.ds(0, n_high)], links.over_low()
        )
        stats_low = copies.go(stats, stats_in.at[0], links.over_low())
        yield
        low_in.wait_recv()
        stats_low.wait_recv()
        for k in range(n_high):
            small_in[k] = small_in[k] + small[k, links.low]
        stats_block[...] = stats[...] + stats_in[0]
        waits = []
        for k in range(1, n_high):
            there = links.ahead(k)
            waits.append(
                copies.go(
                    small_in.at[there], small_in.at[n_high + k - 1], links.device(high=there)
                )
            )
            waits.append(copies.go(stats_block, stats_in.at[k], links.device(high=there)))
        yield
        for wait in waits:
            wait.wait_recv()
        total = small_in[links.high]
        everything = stats_block[...]
        for k in range(1, n_high):
            total = total + small_in[n_high + k - 1]
            everything = everything + stats_in[k]
        small_block[0] = total
        small_block[1] = everything
        yield from tensor_gather(links, copies, small_block, small_full)

    def down_stream():
        yield from dp_scatter(links, copies, d_part, bufs[:3], d_block)
        yield from tensor_gather(links, copies, d_block, d_full)

    take_turns(
        down_stream(),
        dp_scatter(links, copies, q_part, bufs[6:9], q_sum),
        dp_scatter(links, copies, kv_part, bufs[9:12], kv_sum),
        dp_scatter(links, copies, o_part, bufs[3:6], o_sum),
        small_stream(),
    )
    copies.finish()


def sum_weight_grads(n_dp, down, o_t, q_up, kv_up, small, stats):
    n_high = n_dp // 2

    def parts(array):
        return array.reshape(n_high, 2, array.shape[0] // n_dp, *array.shape[1:])

    down, o_t, q_up, kv_up = parts(down), parts(o_t), parts(q_up), parts(kv_up)
    small = small.reshape(n_high, 2, *small.shape[1:])
    count = 4 * (2 * n_high - 1) + 2 * n_high + 6
    d_shape, o_shape, q_shape, kv_shape = (a.shape[2:] for a in (down, o_t, q_up, kv_up))
    one = stats.shape
    return pl.pallas_call(
        functools.partial(weight_grads_kernel, n_dp),
        out_shape=(
            jax.ShapeDtypeStruct((4, *d_shape), BF),
            jax.ShapeDtypeStruct(o_shape, F32),
            jax.ShapeDtypeStruct(q_shape, F32),
            jax.ShapeDtypeStruct(kv_shape, F32),
            jax.ShapeDtypeStruct((4, 2, *one), F32),
        ),
        in_specs=[VMEM] * 6,
        out_specs=[VMEM] * 5,
        scratch_shapes=[
            pltpu.VMEM(d_shape, BF),
            pltpu.VMEM((2, *one), F32),
            pltpu.VMEM(one, F32),
            *dp_scatter_scratch(n_high, d_shape),
            *dp_scatter_scratch(n_high, o_shape),
            *dp_scatter_scratch(n_high, q_shape),
            *dp_scatter_scratch(n_high, kv_shape),
            pltpu.VMEM((2 * n_high - 1, *one), F32),
            pltpu.VMEM((n_high, *one), F32),
            *semaphores(count, 2),
        ],
        compiler_params=params(5),
        name="sum_weight_grads",
    )(down, o_t, q_up, kv_up, small, stats)


def attention_mask(seg_col, seg_row, valid_row):
    length = seg_col.shape[0]
    row = lax.broadcasted_iota(jnp.int32, (length, length), 0)
    column = lax.broadcasted_iota(jnp.int32, (length, length), 1)
    allowed = (
        (seg_col[...] == seg_row[...])
        & (column <= row)
        & ((valid_row[...] == 1) | (column == row))
    )
    return jnp.where(allowed, 0.0, NEGATIVE)


def swap_halves(values):
    half = values.shape[1] // 2
    return jnp.concatenate([values[:, half:], values[:, :half]], axis=1)


def turn(values, cos_full, sin_full):
    return values * cos_full + swap_halves(values) * sin_full


def head_probs(query, key, bias, inv_root):
    scores = dot_nt(query, key) * inv_root + bias
    weights = jnp.exp(scores - jnp.max(scores, axis=-1, keepdims=True))
    return weights / jnp.sum(weights, axis=-1, keepdims=True)


def attend_rows(
    x, gain_attn, gain_q, gain_kv, down, q_up, kv_up, bias, cos_full, sin_full,
    normed, latents, q_normed, kv_normed, q_rows, kv_rows, key_rot, mixed,
):
    rank_q = gain_q.shape[1]
    stream = x[...].astype(F32)
    normed[...] = (stream * inverse_rms(stream) * gain_attn).astype(BF)
    latents[...] = dot(normed[...], down)
    q_latent = latents[:, :rank_q]
    q_normed[...] = (q_latent * inverse_rms(q_latent) * gain_q).astype(BF)
    kv_latent = latents[:, rank_q : rank_q + KR]
    kv_normed[...] = (kv_latent * inverse_rms(kv_latent) * gain_kv).astype(BF)
    turned = turn(latents[:, rank_q + KR : rank_q + KR + ROPE], cos_full[...], sin_full[...])
    key_rot[...] = turned.astype(BF)
    kv_rows[...] = dot(kv_normed[...], kv_up).astype(BF)
    q_heads = dot(q_normed[...], q_up)
    inv_root = 1.0 / math.sqrt(NOPE + ROPE)
    for head in range(q_rows.shape[1] // (NOPE + ROPE)):
        base = head * (NOPE + ROPE)
        query = jnp.concatenate(
            [
                q_heads[:, base : base + NOPE],
                turn(
                    q_heads[:, base + NOPE : base + NOPE + ROPE], cos_full[...], sin_full[...]
                ),
            ],
            axis=1,
        ).astype(BF)
        q_rows[:, base : base + NOPE + ROPE] = query
        start = head * (NOPE + VD)
        key = jnp.concatenate([kv_rows[:, start : start + NOPE], key_rot[...]], axis=1)
        value = kv_rows[:, start + NOPE : start + NOPE + VD]
        probs = head_probs(query, key, bias, inv_root).astype(BF)
        mixed[:, head * VD : head * VD + VD] = dot(probs, value).astype(BF)


def attend_kernel(
    x, gain_attn, gain_q, gain_kv, down, q_up, kv_up, seg_col, seg_row, valid_row, cos_full, sin_full,
    *outs,
):
    attend_rows(
        x, gain_attn[...], gain_q[...], gain_kv[...], down[...], q_up[...], kv_up[...],
        attention_mask(seg_col, seg_row, valid_row), cos_full, sin_full, *outs,
    )


def attend(x, gain_attn, gain_q, gain_kv, down, q_up, kv_up, segments, valid, cos_full, sin_full):
    length = x.shape[0]
    heads = q_up.shape[1] // (NOPE + ROPE)

    def rows(columns, kind):
        return jax.ShapeDtypeStruct((length, columns), kind)

    return pl.pallas_call(
        attend_kernel,
        out_shape=(
            rows(x.shape[1], BF),
            rows(down.shape[1], F32),
            rows(q_up.shape[0], BF),
            rows(kv_up.shape[0], BF),
            rows(q_up.shape[1], BF),
            rows(kv_up.shape[1], BF),
            rows(ROPE, BF),
            rows(heads * VD, BF),
        ),
        in_specs=[VMEM] * 12,
        out_specs=[VMEM] * 8,
        compiler_params=pltpu.CompilerParams(vmem_limit_bytes=VMEM_BYTES),
        name="attend",
    )(
        x,
        gain_attn[None, :],
        gain_q[None, :],
        gain_kv[None, :],
        down,
        q_up,
        kv_up,
        segments[:, None],
        segments[None, :],
        valid[None, :],
        cos_full,
        sin_full,
    )


def later(stream, turns):
    for _ in range(turns):
        yield
    yield from stream


def swap_start(links, copies, blocks, out, n_dp):
    me = links.high * 2 + links.low
    own = copies.near(blocks.at[me], out.at[me])
    arrive = []
    for k in range(1, n_dp):
        there = (me + k) % n_dp
        arrive.append(copies.go(blocks.at[there], out.at[me], {"dp": there}))
    return own, arrive


def pack_stream(w_gate, w_up, w_down, packed):
    n_dp, width, lanes = packed.shape
    slice_ff = w_gate.shape[1] // n_dp
    for k in range(n_dp):
        at = k * slice_ff
        packed[k] = jnp.concatenate(
            [
                w_gate[:, at : at + slice_ff],
                w_up[:, at : at + slice_ff],
                w_down[at : at + slice_ff, :].T,
                jnp.zeros((width, lanes - 3 * slice_ff), BF),
            ],
            axis=1,
        )
        yield


def front_kernel(
    n_dp, x, x_rows, cot, down, gains, q_up, kv_up, o_t, w_gate, w_up, w_down,
    seg_col, seg_row, valid_row, cos_full, sin_full,
    f_down, f_o, f_q, f_kv, f_g, f_cot, f_w, f_normed,
    normed, latents, q_normed, kv_normed, q_rows, kv_rows, key_rot, mixed, resid, branch, gain_mlp,
    packed, part, from_core, out_side, from_side, block, send, recv, local,
):
    links = Links(n_dp)
    copies = Copies(send, recv, local)
    links.meet(swap=True)
    o_stream = dp_gather(links, copies, o_t, f_o)
    take_turns(
        every_gather(links, copies, down, f_down),
        dp_gather(links, copies, gains, f_g),
        dp_gather(links, copies, q_up, f_q),
        dp_gather(links, copies, kv_up, f_kv),
        pack_stream(w_gate, w_up, w_down, packed),
        later(itertools.islice(o_stream, 1), 7),
    )

    def gain_of(row, count):
        return jnp.concatenate(
            [f_g[k].astype(F32)[row : row + 1, :count] for k in range(n_dp)], axis=1
        )

    width = down.shape[0] * 4
    full_down = f_down[...].reshape(n_dp * width, down.shape[1])
    full_q = f_q[...].reshape(n_dp * q_up.shape[0], q_up.shape[1])
    full_kv = f_kv[...].reshape(n_dp * kv_up.shape[0], kv_up.shape[1])
    attend_rows(
        x, gain_of(0, width), gain_of(1, q_up.shape[0]), gain_of(2, kv_up.shape[0]),
        full_down, full_q, full_kv, attention_mask(seg_col, seg_row, valid_row), cos_full, sin_full,
        normed, latents, q_normed, kv_normed, q_rows, kv_rows, key_rot, mixed,
    )
    for _ in range(links.n_high - 1):
        next(o_stream)
    own, arrive = swap_start(links, copies, packed, f_w, n_dp)
    cot_stream = every_gather(links, copies, cot, f_cot)
    next(cot_stream)
    next(cot_stream)
    take_turns(o_stream)
    gain_mlp[...] = gain_of(3, width)
    full_o = f_o[...].reshape(n_dp * width, o_t.shape[1])
    rows = block.shape[0]
    attn_part = dot_nt(mixed[...], full_o).astype(BF)
    for side in range(2):
        for core in range(2):
            at = (side * 2 + core) * rows
            part[side, core] = attn_part[at : at + rows]

    def resid_stream():
        over = copies.go(part.at[:, 1 - links.core], from_core, links.over_core())
        over.wait_recv()
        out_side[...] = (
            part[1 - links.side, links.core].astype(F32) + from_core[1 - links.side].astype(F32)
        ).astype(BF)
        over = copies.go(out_side, from_side, links.over_side())
        mine = part[links.side, links.core].astype(F32) + from_core[links.side].astype(F32)
        over.wait_recv()
        attn = RESIDUAL_SCALE * (mine + from_side[...].astype(F32))
        stream = x_rows[...].astype(F32) + attn
        branch[...] = attn
        resid[...] = stream
        block[...] = (stream * inverse_rms(stream) * gain_mlp[...]).astype(BF)
        yield from every_gather(links, copies, block, f_normed)

    take_turns(resid_stream(), cot_stream)
    for copy in arrive:
        copy.wait_recv()
    own.wait()
    copies.finish()


def front(n_dp, x, x_rows, cot, down, gains, q_up, kv_up, o_t, w_gate, w_up, w_down, segments, valid, cos_full, sin_full):
    n_high = n_dp // 2
    length, columns = x.shape
    rows = x_rows.shape[0]
    lanes = -(-3 * (w_gate.shape[1] // n_dp) // 128) * 128
    heads = q_up.shape[1] // (NOPE + ROPE)
    count = 3 * count_every_gather(n_high) + 4 * (2 * n_high - 1) + n_dp + 1

    def over(block, *lead, kind=BF):
        return jax.ShapeDtypeStruct((*lead, *block), kind)

    return pl.pallas_call(
        functools.partial(front_kernel, n_dp),
        out_shape=(
            over(down.shape, n_dp, 4),
            over(o_t.shape, n_dp),
            over(q_up.shape, n_dp),
            over(kv_up.shape, n_dp),
            over(gains.shape, n_dp),
            over(cot.shape, n_dp, 4),
            over((w_gate.shape[0], lanes), n_dp),
            over(cot.shape, n_dp, 4),
            over((columns,), length),
            over((down.shape[1],), length, kind=F32),
            over((q_up.shape[0] * n_dp,), length),
            over((kv_up.shape[0] * n_dp,), length),
            over((q_up.shape[1],), length),
            over((kv_up.shape[1],), length),
            over((ROPE,), length),
            over((heads * VD,), length),
            over((columns,), rows, kind=F32),
            over((columns,), rows, kind=F32),
            over((columns,), 1, kind=F32),
        ),
        in_specs=[VMEM] * 16,
        out_specs=[VMEM] * 5 + [ANY] * 3 + [VMEM] * 11,
        scratch_shapes=[
            pltpu.VMEM((n_dp, w_gate.shape[0], lanes), BF),
            pltpu.VMEM((2, 2, rows, columns), BF),
            pltpu.VMEM((2, rows, columns), BF),
            pltpu.VMEM((rows, columns), BF),
            pltpu.VMEM((rows, columns), BF),
            pltpu.VMEM((rows, columns), BF),
            *semaphores(count, 8),
        ],
        compiler_params=params(7),
        name="front",
    )(
        x, x_rows, cot, down, gains, q_up, kv_up, o_t, w_gate, w_up, w_down,
        segments[:, None], segments[None, :], valid[None, :], cos_full, sin_full,
    )


def feed_forward_kernel(slice_ff, normed, cot, weights, m_part, g_part, grads, sum_in, sum_out):
    step = pl.program_id(0)
    cut = slice_ff * 2 // 128 * 128
    pad = slice_ff * 2 - cut
    w_in, w_out = weights[:, : sum_in.shape[0]], weights[:, cut:]
    rows = normed.shape[0]
    both = dot(normed[...], w_in)
    gate, upper = both[:, :slice_ff], both[:, slice_ff : 2 * slice_ff]
    sigma = jax.nn.sigmoid(gate)
    swish = gate * sigma

    def zeros(count):
        return jnp.zeros((rows, count), F32)

    def placed(hidden):
        rest = w_out.shape[1] - pad - slice_ff
        return jnp.concatenate([zeros(pad), hidden, zeros(rest)], axis=1).astype(BF)

    hidden = placed(swish * upper)
    m_part[...] = dot_nt(hidden, w_out).astype(BF)
    grad_mlp = (RESIDUAL_SCALE * cot[...].astype(F32)).astype(BF)
    grad_hidden = dot(grad_mlp, w_out)[:, pad : pad + slice_ff]
    grad_both = jnp.concatenate(
        [
            grad_hidden * upper * (sigma * (1.0 + gate * (1.0 - sigma))),
            grad_hidden * swish,
            zeros(w_in.shape[1] - 2 * slice_ff),
        ],
        axis=1,
    ).astype(BF)
    g_part[...] = dot_nt(grad_both, w_in).astype(BF)

    @pl.when(step == 0)
    def _():
        sum_in[...] = dot_tn(grad_both, normed[...])
        sum_out[...] = dot_tn(hidden, grad_mlp)

    @pl.when(step > 0)
    def _():
        sum_in[...] += dot_tn(grad_both, normed[...])
        sum_out[...] += dot_tn(hidden, grad_mlp)

    @pl.when(step == pl.num_programs(0) - 1)
    def _():
        mid = sum_in.shape[0]
        if cut:
            grads[:, :cut] = sum_in[:cut].T.astype(BF)
        grads[:, cut:mid] = (sum_in[cut:] + sum_out[: mid - cut]).T.astype(BF)
        grads[:, mid:] = sum_out[mid - cut :].T.astype(BF)


def feed_forward(normed, cot, weights, slice_ff, rows):
    tokens, columns = normed.shape
    lanes = weights.shape[1]
    cut = slice_ff * 2 // 128 * 128
    wide = -(-slice_ff * 2 // 128) * 128
    token_block = pl.BlockSpec((rows, columns), lambda i: (i, 0))
    whole = pl.BlockSpec((columns, lanes), lambda i: (0, 0))
    part = jax.ShapeDtypeStruct((tokens, columns), BF)
    return pl.pallas_call(
        functools.partial(feed_forward_kernel, slice_ff),
        grid=(tokens // rows,),
        out_shape=(part, part, jax.ShapeDtypeStruct((columns, lanes), BF)),
        in_specs=[token_block, token_block, whole],
        out_specs=[token_block, token_block, whole],
        scratch_shapes=[
            pltpu.VMEM((wide, columns), F32),
            pltpu.VMEM((lanes - cut, columns), F32),
        ],
        compiler_params=pltpu.CompilerParams(vmem_limit_bytes=VMEM_BYTES),
        name="feed_forward",
    )(normed, cot, weights)


def attend_back_kernel(
    grad_attn, mixed, o_t, q_rows, kv_rows, key_rot, q_normed, kv_normed, q_up, kv_up,
    seg_col, seg_row, valid_row, cos_full, sin_full,
    grad_latents, grad_o, grad_q_up, grad_kv_up, grad_q, grad_kv,
):
    rank_q = q_up.shape[0]
    grad_o[...] = dot_tn(grad_attn[...], mixed[...]).astype(BF)
    grad_mixed = dot(grad_attn[...], o_t[...]).astype(BF)
    bias = attention_mask(seg_col, seg_row, valid_row)
    inv_root = 1.0 / math.sqrt(NOPE + ROPE)
    grad_rot = jnp.zeros((grad_attn.shape[0], ROPE), F32)
    for head in range(q_rows.shape[1] // (NOPE + ROPE)):
        base = head * (NOPE + ROPE)
        start = head * (NOPE + VD)
        query = q_rows[:, base : base + NOPE + ROPE]
        key = jnp.concatenate([kv_rows[:, start : start + NOPE], key_rot[...]], axis=1)
        value = kv_rows[:, start + NOPE : start + NOPE + VD]
        grad = grad_mixed[:, head * VD : head * VD + VD]
        probs = head_probs(query, key, bias, inv_root)
        grad_value = dot_tn(probs.astype(BF), grad)
        grad_probs = dot_nt(grad, value)
        inner = jnp.sum(probs * grad_probs, axis=-1, keepdims=True)
        grad_scores = (probs * (grad_probs - inner)).astype(BF)
        grad_query = dot(grad_scores, key) * inv_root
        grad_key = dot_tn(grad_scores, query) * inv_root
        grad_q[:, base : base + NOPE + ROPE] = jnp.concatenate(
            [grad_query[:, :NOPE], turn(grad_query[:, NOPE:], cos_full[...], -sin_full[...])],
            axis=1,
        ).astype(BF)
        grad_kv[:, start : start + NOPE + VD] = jnp.concatenate(
            [grad_key[:, :NOPE], grad_value], axis=1
        ).astype(BF)
        grad_rot = grad_rot + grad_key[:, NOPE:]
    grad_latents[...] = jnp.zeros_like(grad_latents)
    grad_latents[:, :rank_q] = dot_nt(grad_q[...], q_up[...]).astype(BF)
    grad_latents[:, rank_q : rank_q + KR] = dot_nt(grad_kv[...], kv_up[...]).astype(BF)
    grad_latents[:, rank_q + KR : rank_q + KR + ROPE] = turn(
        grad_rot, cos_full[...], -sin_full[...]
    ).astype(BF)
    grad_q_up[...] = dot_tn(q_normed[...], grad_q[...]).astype(BF)
    grad_kv_up[...] = dot_tn(kv_normed[...], grad_kv[...]).astype(BF)


def attend_back(
    grad_attn, mixed, o_t, q_rows, kv_rows, key_rot, q_normed, kv_normed, q_up, kv_up,
    segments, valid, cos_full, sin_full, columns_down,
):
    length = grad_attn.shape[0]

    def out(shape):
        return jax.ShapeDtypeStruct(shape, BF)

    return pl.pallas_call(
        attend_back_kernel,
        out_shape=(
            out((length, columns_down)),
            out(o_t.shape),
            out(q_up.shape),
            out(kv_up.shape),
        ),
        in_specs=[VMEM] * 15,
        out_specs=[VMEM] * 4,
        scratch_shapes=[pltpu.VMEM(q_rows.shape, BF), pltpu.VMEM(kv_rows.shape, BF)],
        compiler_params=pltpu.CompilerParams(vmem_limit_bytes=VMEM_BYTES),
        name="attend_back",
    )(
        grad_attn, mixed, o_t, q_rows, kv_rows, key_rot, q_normed, kv_normed, q_up, kv_up,
        segments[:, None], segments[None, :], valid[None, :], cos_full, sin_full,
    )


def per_device(
    layer_input,
    segment_ids,
    valid_mask,
    cotangent,
    attn_gain,
    q_down,
    q_gain,
    q_up,
    kv_down,
    kv_gain,
    kv_up,
    o_proj,
    mlp_gain,
    w_gate,
    w_up,
    w_down,
):
    length = layer_input.shape[0]
    n_dp = lax.axis_size("dp")
    n_tensor = lax.axis_size("tensor")
    share = length // n_tensor
    me = lax.axis_index("tensor")
    width = w_gate.shape[0]
    slice_ff = w_gate.shape[1] // n_dp
    rows_down = width // n_tensor

    def rows_of(values, count):
        return lax.dynamic_slice_in_dim(values, me * count, count, 0)

    rank_q = q_down.shape[1]
    columns_down = rank_q + kv_down.shape[1]
    pad_down = -columns_down % 128
    down_rows = jnp.concatenate(
        [
            rows_of(q_down, rows_down),
            rows_of(kv_down, rows_down),
            jnp.zeros((rows_down, pad_down), BF),
        ],
        axis=1,
    )
    lanes = -(-width // 128) * 128

    def lane_rows(rows, count, kind):
        padded = [jnp.pad(row.astype(kind), (0, lanes - row.shape[0])) for row in rows]
        return jnp.stack(padded + [jnp.zeros((lanes,), kind)] * (count - len(padded)))

    cot_rows = rows_of(cotangent, share)
    x_rows = rows_of(layer_input, share)
    gains_block = lane_rows([attn_gain, q_gain, kv_gain, mlp_gain], 16, BF)
    cosine, sine_table = rope_tables(length, ROPE)
    cos_full = jnp.concatenate([cosine, cosine], axis=1)
    sin_full = jnp.concatenate([-sine_table, sine_table], axis=1)
    fused = n_dp == 8 and rows_down % 16 == 0 and q_up.shape[0] % 16 == 0
    if fused:
        (
            f_down, f_o, f_q, f_kv, f_g, f_cot, f_w, f_normed,
            normed, latents, q_normed, kv_normed, q_rows, kv_rows, key_rot, mixed,
            resid_rows, attn_rows, _,
        ) = front(
            n_dp, layer_input, x_rows, cot_rows, down_rows, gains_block, q_up, kv_up, o_proj.T,
            w_gate, w_up, w_down, segment_ids, valid_mask, cos_full, sin_full,
        )
    else:
        f_down, f_o, f_q, f_kv, f_g, f_cot = gather_weights(
            n_dp, n_tensor, down_rows, o_proj.T, q_up, kv_up, gains_block, cot_rows
        )
    full_down = f_down.reshape(n_dp * width, columns_down + pad_down)
    full_o = f_o.reshape(n_dp * width, -1)

    def gain_of(row, gain):
        return f_g[:, row, : gain.shape[0]].reshape(-1).astype(F32)

    gain_attn = gain_of(0, attn_gain)
    gain_q = gain_of(1, q_gain)
    gain_kv = gain_of(2, kv_gain)
    gain_mlp = gain_of(3, mlp_gain)
    if not fused:
        packed = jnp.concatenate(
            [
                w_gate.reshape(width, n_dp, slice_ff),
                w_up.reshape(width, n_dp, slice_ff),
                w_down.T.reshape(width, n_dp, slice_ff),
                jnp.zeros((width, n_dp, -3 * slice_ff % 128), BF),
            ],
            axis=2,
        ).transpose(1, 0, 2)
        packed, f_q = lax.optimization_barrier((packed, f_q))
        f_w = swap_dp(packed)
    full_q_up = f_q.reshape(-1, q_up.shape[1])
    full_kv_up = f_kv.reshape(-1, kv_up.shape[1])
    if not fused:
        normed, latents, q_normed, kv_normed, q_rows, kv_rows, key_rot, mixed = attend(
            layer_input, gain_attn, gain_q, gain_kv, full_down, full_q_up, full_kv_up,
            segment_ids, valid_mask, cos_full, sin_full,
        )
        f_normed, resid_rows, attn_rows = attention_residual(
            n_dp, dot_nt(mixed, full_o).astype(BF), x_rows, gain_mlp[None, :]
        )
    inv_two = inverse_rms(resid_rows)
    unit_two = resid_rows * inv_two

    mlp_part, normed_part, grad_packed = feed_forward(
        f_normed.reshape(n_dp * length, -1),
        f_cot.reshape(n_dp * length, -1),
        f_w.reshape(n_dp * width, -1),
        slice_ff,
        length,
    )
    swapped = swap_dp(grad_packed.reshape(n_dp, width, -1))
    normed_part, grad_packed = lax.optimization_barrier((normed_part, grad_packed))
    f_attn, grad_normed_two, f_block, mlp_rows = residual_grads(
        n_dp, normed_part, mlp_part, resid_rows, cot_rows, gain_mlp[None, :]
    )
    grad_attn = f_attn.reshape(length, -1)
    block_full = f_block.reshape(length, -1)

    def unpack(part):
        return part.transpose(1, 0, 2).reshape(width, n_dp * slice_ff).astype(F32)

    weight_rows = rows_of(valid_mask.astype(F32)[:, None], share)
    grad_mlp_gain = jnp.sum(grad_normed_two * unit_two, axis=0)

    grad_part, grad_o, grad_q_up, grad_kv_up = attend_back(
        grad_attn, mixed, full_o, q_rows, kv_rows, key_rot, q_normed, kv_normed,
        full_q_up, full_kv_up, segment_ids, valid_mask, cos_full, sin_full,
        columns_down + pad_down,
    )
    grad_part, swapped = lax.optimization_barrier((grad_part, swapped))
    grad_latents = sum_latents(n_dp, grad_part).astype(F32)
    stream = layer_input.astype(F32)
    inv_one = inverse_rms(stream)
    unit_one = stream * inv_one
    q_latent = latents[:, :rank_q]
    inv_q = inverse_rms(q_latent)
    unit_q = q_latent * inv_q
    kv_latent = latents[:, rank_q : rank_q + KR]
    inv_kv = inverse_rms(kv_latent)
    unit_kv = kv_latent * inv_kv
    grad_q_normed = grad_latents[:, :rank_q]
    grad_kv_normed = grad_latents[:, rank_q : rank_q + KR]
    grad_kv_rot = grad_latents[:, rank_q + KR : columns_down]
    grad_q_gain = jnp.sum(grad_q_normed * unit_q, axis=0)
    grad_kv_gain = jnp.sum(grad_kv_normed * unit_kv, axis=0)
    grad_down = jnp.concatenate(
        [
            norm_back(grad_q_normed * gain_q, unit_q, inv_q),
            norm_back(grad_kv_normed * gain_kv, unit_kv, inv_kv),
            grad_kv_rot,
            jnp.zeros((length, pad_down), F32),
        ],
        axis=-1,
    ).astype(BF)
    grad_normed = dot_nt(grad_down, full_down)
    grad_attn_gain = jnp.sum(grad_normed * unit_one, axis=0)
    grad_input = grad_attn.astype(F32) * (1.0 / RESIDUAL_SCALE) + norm_back(
        grad_normed * gain_attn, unit_one, inv_one
    )

    quarter = lax.dynamic_index_in_dim(
        normed.reshape(length, n_dp, n_tensor, rows_down), me, 2, keepdims=False
    ).reshape(length, n_dp * rows_down)
    def by_dp(vector):
        return vector.reshape(n_dp, -1)

    def small_rows(vectors):
        return jnp.stack(
            [jnp.pad(by_dp(v), ((0, 0), (0, lanes - v.shape[0] // n_dp))) for v in vectors]
            + [jnp.zeros((n_dp, lanes), F32)] * (8 - len(vectors)),
            axis=1,
        )

    stats = jnp.stack(
        [
            jnp.sum(weight_rows * resid_rows * resid_rows),
            jnp.sum(weight_rows * attn_rows * attn_rows),
            jnp.sum(weight_rows * mlp_rows * mlp_rows),
            jnp.sum(weight_rows),
        ]
    )
    s_down, s_o, s_q, s_kv, s_small = sum_weight_grads(
        n_dp,
        dot_tn(quarter, grad_down).astype(BF),
        grad_o,
        grad_q_up,
        grad_kv_up,
        small_rows([grad_attn_gain, grad_q_gain, grad_kv_gain, grad_mlp_gain]),
        lane_rows([stats], 8, F32),
    )
    grad_w_gate = unpack(swapped[:, :, :slice_ff])
    grad_w_up = unpack(swapped[:, :, slice_ff : 2 * slice_ff])
    grad_w_down = unpack(swapped[:, :, 2 * slice_ff : 3 * slice_ff]).T

    d_down = s_down.reshape(width, -1).astype(F32)
    gains = s_small[me, 0]
    stat_sums = jnp.sum(s_small[:, 1, 0, :4], axis=0)
    rms_stats = jnp.sqrt(stat_sums[:3] / (stat_sums[3] * D))
    return (
        block_full,
        grad_input,
        gains[0, : attn_gain.shape[0]],
        d_down[:, :rank_q],
        gains[1, : q_gain.shape[0]],
        s_q,
        d_down[:, rank_q:columns_down],
        gains[2, : kv_gain.shape[0]],
        s_kv,
        s_o.T,
        jnp.sum(s_small[:, 0, 3], axis=0)[: mlp_gain.shape[0]],
        grad_w_gate,
        grad_w_up,
        grad_w_down,
        rms_stats,
    )


def solution(mesh):
    placed = (
        P("dp", None),
        P("dp"),
        P("dp"),
        P("dp", None),
        P("dp"),
        P("dp", None),
        P("dp"),
        P("dp", "tensor"),
        P("dp", None),
        P("dp"),
        P("dp", "tensor"),
        P("tensor", "dp"),
        P("dp"),
        P("dp", "tensor"),
        P("dp", "tensor"),
        P("tensor", "dp"),
    )
    return jax.shard_map(
        per_device,
        mesh=mesh,
        in_specs=placed,
        out_specs=(
            P("dp", None),
            P("dp", None),
            P("dp"),
            P("dp", None),
            P("dp"),
            P("dp", "tensor"),
            P("dp", None),
            P("dp"),
            P("dp", "tensor"),
            P("tensor", "dp"),
            P("dp"),
            P("dp", "tensor"),
            P("dp", "tensor"),
            P("tensor", "dp"),
            P(),
        ),
        check_vma=False,
    )
```

```python
import functools
import itertools
import math

import jax
import jax.numpy as jnp
from jax import lax
from jax.experimental import pallas as pl
from jax.experimental.pallas import tpu as pltpu
from jax.sharding import PartitionSpec as P

D = 2560
KR = 256
NOPE = 64
ROPE = 32
VD = 64


NORM_EPS = 1e-05
RESIDUAL_SCALE = 1.4 / math.sqrt(62.0)
ROPE_BASE = 10000.0
NEGATIVE = -1e30


def rope_tables(length, rot_dim):
    half_dim = rot_dim // 2
    position = jnp.arange(length, dtype=jnp.float32)
    frequency = jnp.exp(
        -math.log(ROPE_BASE) * 2.0 * jnp.arange(half_dim, dtype=jnp.float32) / rot_dim
    )
    phases = position[:, None] * frequency[None, :]
    return (jnp.cos(phases), jnp.sin(phases))


def inverse_rms(values):
    return lax.rsqrt(jnp.mean(values * values, axis=-1, keepdims=True) + NORM_EPS)


def norm_back(grad_unit, unit, inv_rms):
    return inv_rms * (grad_unit - unit * jnp.mean(grad_unit * unit, axis=-1, keepdims=True))


BF = jnp.bfloat16
F32 = jnp.float32


def dot(left, right):
    return jnp.dot(left, right, preferred_element_type=F32)


def dot_nt(left, right):
    return jnp.einsum("ac,bc->ab", left, right, preferred_element_type=F32)


def dot_tn(left, right):
    return jnp.einsum("ca,cb->ab", left, right, preferred_element_type=F32)


def swap_dp(blocks):
    return lax.all_to_all(blocks, "dp", 0, 0, tiled=True)


MESH = pl.DeviceIdType.MESH
ANY = pl.BlockSpec(memory_space=pl.ANY)
VMEM = pl.BlockSpec(memory_space=pltpu.VMEM)
VMEM_BYTES = 60 * 1024 * 1024


class Links:
    def __init__(self, n_dp):
        self.n_high = n_dp // 2
        dp = lax.axis_index("dp")
        tensor = lax.axis_index("tensor")
        self.high, self.low = dp // 2, dp % 2
        self.side, self.core = tensor // 2, tensor % 2

    def device(self, high=None, low=None, side=None, core=None):
        high = self.high if high is None else high
        low = self.low if low is None else low
        side = self.side if side is None else side
        core = self.core if core is None else core
        return {"dp": high * 2 + low, "tensor": side * 2 + core}

    def behind(self, step):
        return (self.high + self.n_high - step) % self.n_high

    def ahead(self, step):
        return (self.high + step) % self.n_high

    def over_low(self):
        return self.device(low=1 - self.low)

    def over_side(self):
        return self.device(side=1 - self.side)

    def over_core(self):
        return self.device(core=1 - self.core)

    def meet(self, high=True, low=True, side=True, core=True, swap=False):
        barrier = pltpu.get_barrier_semaphore()
        partners = []
        if swap:
            partners += [
                self.device(high=self.ahead(k), low=1 - self.low) for k in range(1, self.n_high)
            ]
        if high:
            partners += [self.device(high=self.ahead(k)) for k in range(1, self.n_high)]
        if low:
            partners.append(self.over_low())
        if side:
            partners.append(self.over_side())
        if core:
            partners.append(self.over_core())
        for partner in partners:
            pl.semaphore_signal(barrier, inc=1, device_id=partner, device_id_type=MESH)
        pl.semaphore_wait(barrier, len(partners))


class Copies:
    def __init__(self, send, recv, local):
        self.send, self.recv, self.local = send, recv, local
        self.count = self.local_count = 0
        self.started = []
        self.local_started = []

    def go(self, source, target, device):
        copy = pltpu.make_async_remote_copy(
            src_ref=source,
            dst_ref=target,
            send_sem=self.send.at[self.count],
            recv_sem=self.recv.at[self.count],
            device_id=device,
            device_id_type=MESH,
        )
        self.count += 1
        copy.start()
        self.started.append(copy)
        return copy

    def near(self, source, target):
        copy = pltpu.make_async_copy(source, target, self.local.at[self.local_count])
        self.local_count += 1
        copy.start()
        self.local_started.append(copy)
        return copy

    def finish(self):
        for copy in self.started:
            copy.wait_send()


def take_turns(*streams):
    streams = list(streams)
    while streams:
        for stream in list(streams):
            try:
                next(stream)
            except StopIteration:
                streams.remove(stream)


def steps_by_distance(count):
    order, k = [], 1
    while len(order) < count - 1:
        order.append(k)
        if len(order) < count - 1:
            order.append(count - k)
        k += 1
    return order


def every_gather(links, copies, block, out, cut=None):
    n_high = links.n_high
    columns = out.shape[-1]
    cut = columns // 256 * 128 if cut is None else cut
    halves = (pl.ds(0, cut), pl.ds(cut, columns - cut))

    def slot(high, low, side):
        return out.at[high * 2 + low, side * 2 + links.core]

    mine = slot(links.high, links.low, links.side)
    own = copies.near(block, mine)
    arrive = {}
    for k in steps_by_distance(n_high):
        arrive[k] = copies.go(block, mine, links.device(high=links.ahead(k)))
    yield
    order = [0] + steps_by_distance(n_high)
    last, over_low, over_side, corner_a, corner_b = [], {}, {}, {}, {}

    def first(k):
        here = slot(links.behind(k), links.low, links.side)
        if k:
            arrive[k].wait_recv()
        source = here if k else block
        over_low[k] = copies.go(source, here, links.over_low())
        over_side[k] = copies.go(source, here, links.over_side())
        last.append(copies.go(source, here, links.over_core()))

    def second(k):
        over_low[k].wait_recv()
        here = slot(links.behind(k), 1 - links.low, links.side)
        part = here.at[:, halves[0]]
        corner_a[k] = copies.go(part, part, links.over_side())
        last.append(copies.go(here, here, links.over_core()))
        over_side[k].wait_recv()
        here = slot(links.behind(k), links.low, 1 - links.side)
        if cut < columns:
            part = here.at[:, halves[1]]
            corner_b[k] = copies.go(part, part, links.over_low())
        last.append(copies.go(here, here, links.over_core()))

    def third(k):
        here = slot(links.behind(k), 1 - links.low, 1 - links.side)
        for corner, half in ((corner_a, halves[0]), (corner_b, halves[1])):
            if k not in corner:
                continue
            corner[k].wait_recv()
            part = here.at[:, half]
            last.append(copies.go(part, part, links.over_core()))

    for i in range(n_high + 2):
        if i < n_high:
            first(order[i])
            yield
        if 0 <= i - 1 < n_high:
            second(order[i - 1])
            yield
        if 0 <= i - 2:
            third(order[i - 2])
            yield
    for copy in last:
        copy.wait_recv()
    own.wait()


def dp_gather(links, copies, block, out):
    mine = out.at[links.high * 2 + links.low]
    own = copies.near(block, mine)
    arrive, last = {}, []
    for k in steps_by_distance(links.n_high):
        arrive[k] = copies.go(block, mine, links.device(high=links.ahead(k)))
    yield
    last.append(copies.go(block, mine, links.over_low()))
    yield
    for k in steps_by_distance(links.n_high):
        arrive[k].wait_recv()
        here = out.at[links.behind(k) * 2 + links.low]
        last.append(copies.go(here, here, links.over_low()))
        yield
    for copy in last:
        copy.wait_recv()
    own.wait()


def tensor_gather(links, copies, block, out):
    mine = out.at[links.side * 2 + links.core]
    own = copies.near(block, mine)
    last = [copies.go(block, mine, links.over_core())]
    across = copies.go(block, mine, links.over_side())
    yield
    across.wait_recv()
    here = out.at[(1 - links.side) * 2 + links.core]
    last.append(copies.go(here, here, links.over_core()))
    yield
    for copy in last:
        copy.wait_recv()
    own.wait()


class EveryScatter:
    def __init__(self, links, copies, part, bufs, result, cut):
        self.links, self.copies, self.part, self.result = links, copies, part, result
        self.own, self.chip, *bufs = bufs
        self.low_a, self.side_a = (bufs.pop(0), bufs.pop(0)) if cut else (None, None)
        self.side_b, self.low_b, self.done, self.from_high = bufs
        self.cut = cut
        self.half_a, self.half_b = pl.ds(0, cut), pl.ds(cut, part.shape[-1] - cut)
        self.order = steps_by_distance(links.n_high) + [0]
        self.loads, self.core_in, self.a_in, self.b_in = {}, {}, {}, {}
        self.a_last, self.b_last, self.high_in = {}, {}, {}

    def load(self, i):
        there = self.links.ahead(self.order[i])
        self.loads[i] = self.copies.near(
            self.part.at[there, :, :, self.links.core], self.own.at[i % 2]
        )

    def start(self):
        for i, k in enumerate(self.order):
            self.core_in[k] = self.copies.go(
                self.part.at[self.links.ahead(k), :, :, 1 - self.links.core],
                self.chip.at[k],
                self.links.over_core(),
            )
            if i < 2:
                self.load(i)

    def first(self, i):
        links, copies, chip, k = self.links, self.copies, self.chip, self.order[i]
        self.core_in[k].wait_recv()
        self.loads[i].wait()
        for low in range(2):
            for side in range(2):
                chip[k, low, side] = (
                    self.own[i % 2, low, side].astype(F32) + chip[k, low, side].astype(F32)
                ).astype(BF)
        if i + 2 < links.n_high:
            self.load(i + 2)
        if self.cut:
            self.a_in[k] = copies.go(
                chip.at[k, 1 - links.low, :, :, self.half_a], self.low_a.at[k], links.over_low()
            )
        self.b_in[k] = copies.go(
            chip.at[k, :, 1 - links.side, :, self.half_b], self.side_b.at[k], links.over_side()
        )

    def second(self, i):
        links, copies, chip, k = self.links, self.copies, self.chip, self.order[i]
        low_a, side_b = self.low_a, self.side_b
        if self.cut:
            self.a_in[k].wait_recv()
            for side in range(2):
                low_a[k, side] = (
                    low_a[k, side].astype(F32)
                    + chip[k, links.low, side, :, self.half_a].astype(F32)
                ).astype(BF)
            self.a_last[k] = copies.go(
                low_a.at[k, 1 - links.side], self.side_a.at[k], links.over_side()
            )
        self.b_in[k].wait_recv()
        for low in range(2):
            side_b[k, low] = (
                side_b[k, low].astype(F32) + chip[k, low, links.side, :, self.half_b].astype(F32)
            ).astype(BF)
        self.b_last[k] = copies.go(side_b.at[k, 1 - links.low], self.low_b.at[k], links.over_low())

    def third(self, i):
        links, k = self.links, self.order[i]
        if self.cut:
            self.a_last[k].wait_recv()
            self.done[k, :, self.half_a] = (
                self.side_a[k].astype(F32) + self.low_a[k, links.side].astype(F32)
            ).astype(BF)
        self.b_last[k].wait_recv()
        self.done[k, :, self.half_b] = (
            self.low_b[k].astype(F32) + self.side_b[k, links.low].astype(F32)
        ).astype(BF)
        if k:
            self.high_in[k] = self.copies.go(
                self.done.at[k], self.from_high.at[k - 1], links.device(high=links.ahead(k))
            )

    def finish(self):
        total = self.done[0].astype(F32)
        for k in steps_by_distance(self.links.n_high):
            self.high_in[k].wait_recv()
            total = total + self.from_high[k - 1].astype(F32)
        self.result[...] = total


def every_scatter(links, copies, part, bufs, result):
    work = EveryScatter(links, copies, part, bufs, result, part.shape[-1] // 256 * 128)
    work.start()
    yield
    for i in range(links.n_high + 2):
        if i < links.n_high:
            work.first(i)
            yield
        if 0 <= i - 1 < links.n_high:
            work.second(i - 1)
            yield
        if 0 <= i - 2:
            work.third(i - 2)
            yield
    work.finish()


def every_scatter_scratch(n_high, rows, columns, cut=None):
    cut = columns // 256 * 128 if cut is None else cut
    over_low = [
        pltpu.VMEM((n_high, 2, rows, cut), BF),
        pltpu.VMEM((n_high, rows, cut), BF),
    ]
    return [
        pltpu.VMEM((2, 2, 2, rows, columns), BF),
        pltpu.VMEM((n_high, 2, 2, rows, columns), BF),
        *(over_low if cut else []),
        pltpu.VMEM((n_high, 2, rows, columns - cut), BF),
        pltpu.VMEM((n_high, rows, columns - cut), BF),
        pltpu.VMEM((n_high, rows, columns), BF),
        pltpu.VMEM((n_high - 1, rows, columns), BF),
    ]


def dp_scatter(links, copies, part, bufs, result):
    from_low, done, from_high = bufs
    order = steps_by_distance(links.n_high) + [0]
    low_in, high_in = {}, {}
    for k in order:
        low_in[k] = copies.go(
            part.at[links.ahead(k), 1 - links.low], from_low.at[k], links.over_low()
        )
    yield
    for k in order:
        low_in[k].wait_recv()
        done[k] = (
            part[links.ahead(k), links.low].astype(F32) + from_low[k].astype(F32)
        ).astype(BF)
        if k:
            high_in[k] = copies.go(
                done.at[k], from_high.at[k - 1], links.device(high=links.ahead(k))
            )
        yield
    total = done[0].astype(F32)
    for k in steps_by_distance(links.n_high):
        high_in[k].wait_recv()
        total = total + from_high[k - 1].astype(F32)
    result[...] = total.astype(result.dtype)
    yield


def dp_scatter_scratch(n_high, shape):
    return [
        pltpu.VMEM((n_high, *shape), BF),
        pltpu.VMEM((n_high, *shape), BF),
        pltpu.VMEM((n_high - 1, *shape), BF),
    ]


def semaphores(count, local):
    return [
        pltpu.SemaphoreType.DMA((count,)),
        pltpu.SemaphoreType.DMA((count,)),
        pltpu.SemaphoreType.DMA((local,)),
    ]


def params(number, mebibytes=60):
    return pltpu.CompilerParams(
        collective_id=number, has_side_effects=True, vmem_limit_bytes=mebibytes * 1024 * 1024
    )


def count_every_gather(n_high):
    return n_high - 1 + 9 * n_high


def weights_kernel(n_dp, down, o_t, q_up, kv_up, gains, cot, f_down, f_o, f_q, f_kv, f_g, f_cot, send, recv, local):
    links = Links(n_dp)
    copies = Copies(send, recv, local)
    links.meet()
    take_turns(
        every_gather(links, copies, down, f_down),
        dp_gather(links, copies, gains, f_g),
        dp_gather(links, copies, q_up, f_q),
        dp_gather(links, copies, kv_up, f_kv),
        dp_gather(links, copies, o_t, f_o),
        every_gather(links, copies, cot, f_cot),
    )
    copies.finish()


def gather_weights(n_dp, n_tensor, down, o_t, q_up, kv_up, gains, cot):
    n_high = n_dp // 2
    count = 2 * count_every_gather(n_high) + 4 * (2 * n_high - 1)

    def over(block, *lead):
        return jax.ShapeDtypeStruct((*lead, *block.shape), block.dtype)

    return pl.pallas_call(
        functools.partial(weights_kernel, n_dp),
        out_shape=(
            over(down, n_dp, n_tensor),
            over(o_t, n_dp),
            over(q_up, n_dp),
            over(kv_up, n_dp),
            over(gains, n_dp),
            over(cot, n_dp, n_tensor),
        ),
        in_specs=[ANY] * 6,
        out_specs=[ANY] * 6,
        scratch_shapes=semaphores(count, 6),
        compiler_params=params(1),
        name="gather_weights",
    )(down, o_t, q_up, kv_up, gains, cot)


def resid_kernel(n_dp, part, x_rows, gain, full, resid, branch, from_core, out_side, from_side, block, send, recv, local):
    links = Links(n_dp)
    copies = Copies(send, recv, local)
    links.meet()
    arrive = copies.go(part.at[:, 1 - links.core], from_core, links.over_core())
    arrive.wait_recv()
    out_side[...] = (
        part[1 - links.side, links.core].astype(F32) + from_core[1 - links.side].astype(F32)
    ).astype(BF)
    arrive = copies.go(out_side, from_side, links.over_side())
    mine = part[links.side, links.core].astype(F32) + from_core[links.side].astype(F32)
    arrive.wait_recv()
    attn = RESIDUAL_SCALE * (mine + from_side[...].astype(F32))
    stream = x_rows[...].astype(F32) + attn
    branch[...] = attn
    resid[...] = stream
    block[...] = (stream * inverse_rms(stream) * gain[...]).astype(BF)
    take_turns(every_gather(links, copies, block, full))
    copies.finish()


def attention_residual(n_dp, part, x_rows, gain):
    n_tensor = 4
    rows, columns = x_rows.shape
    block = (rows, columns)
    return pl.pallas_call(
        functools.partial(resid_kernel, n_dp),
        out_shape=(
            jax.ShapeDtypeStruct((n_dp, n_tensor, rows, columns), BF),
            jax.ShapeDtypeStruct(block, F32),
            jax.ShapeDtypeStruct(block, F32),
        ),
        in_specs=[VMEM] * 3,
        out_specs=[ANY, VMEM, VMEM],
        scratch_shapes=[
            pltpu.VMEM((2, *block), BF),
            pltpu.VMEM(block, BF),
            pltpu.VMEM(block, BF),
            pltpu.VMEM(block, BF),
            *semaphores(2 + count_every_gather(n_dp // 2), 1),
        ],
        compiler_params=params(2),
        name="attention_residual",
    )(part.reshape(2, 2, rows, columns), x_rows, gain)


def grad_rows_kernel(n_dp, both, *refs):
    links = Links(n_dp)
    copies = Copies(*refs[-3:])
    g_part, resid, cot, gain = refs[:4]
    if both:
        m_part, attn_full, g_rows, block_full, m_rows = refs[4:9]
        scratch = refs[9:-3]
    else:
        attn_full, g_rows = refs[4:6]
        scratch = refs[6:-3]
    links.meet()

    def grad_stream():
        grad_rows = scratch[0]
        yield from every_scatter(links, copies, g_part, scratch[1:9], g_rows)
        stream = resid[...]
        inv = inverse_rms(stream)
        grad = cot[...].astype(F32) + norm_back(g_rows[...] * gain[...], stream * inv, inv)
        grad_rows[...] = (RESIDUAL_SCALE * grad).astype(BF)
        yield from tensor_gather(links, copies, grad_rows, attn_full)

    if both:
        block = block_stream(links, copies, m_part, resid, block_full, m_rows, scratch[9:])
        take_turns(grad_stream(), block)
    else:
        take_turns(grad_stream())
    copies.finish()


def block_stream(links, copies, m_part, resid, block_full, m_rows, scratch):
    block_rows = scratch[0]
    yield from every_scatter(links, copies, m_part, scratch[1:9], m_rows)
    m_rows[...] = RESIDUAL_SCALE * m_rows[...]
    block_rows[...] = resid[...] + m_rows[...]
    yield from tensor_gather(links, copies, block_rows, block_full)


def block_rows_kernel(n_dp, m_part, resid, block_full, m_rows, *rest):
    links = Links(n_dp)
    copies = Copies(*rest[-3:])
    links.meet()
    take_turns(block_stream(links, copies, m_part, resid, block_full, m_rows, rest[:-3]))
    copies.finish()


def residual_grads(n_dp, g_part, m_part, resid, cot, gain):
    n_high = n_dp // 2
    rows, columns = resid.shape
    shape = (n_high, 2, 2, 2, rows, columns)
    g_part, m_part = g_part.reshape(shape), m_part.reshape(shape)
    both = n_high <= 4
    one = jax.ShapeDtypeStruct((rows, columns), F32)
    grad_out = (jax.ShapeDtypeStruct((4, rows, columns), BF), one)
    block_out = (jax.ShapeDtypeStruct((4, rows, columns), F32), one)
    grad_scratch = [
        pltpu.VMEM((rows, columns), BF),
        *every_scatter_scratch(n_high, rows, columns),
    ]
    block_scratch = [
        pltpu.VMEM((rows, columns), F32),
        *every_scatter_scratch(n_high, rows, columns),
    ]
    count, local = 6 * n_high - 1 + 3, n_high + 1
    if both:
        return pl.pallas_call(
            functools.partial(grad_rows_kernel, n_dp, True),
            out_shape=grad_out + block_out,
            in_specs=[ANY, VMEM, VMEM, VMEM, ANY],
            out_specs=[ANY, VMEM, ANY, VMEM],
            scratch_shapes=[*grad_scratch, *block_scratch, *semaphores(2 * count, 2 * local)],
            compiler_params=params(3),
            name="residual_grads",
        )(g_part, resid, cot, gain, m_part)
    grads = pl.pallas_call(
        functools.partial(grad_rows_kernel, n_dp, False),
        out_shape=grad_out,
        in_specs=[ANY, VMEM, VMEM, VMEM],
        out_specs=[ANY, VMEM],
        scratch_shapes=[*grad_scratch, *semaphores(count, local)],
        compiler_params=params(3),
        name="residual_grads",
    )(g_part, resid, cot, gain)
    block = pl.pallas_call(
        functools.partial(block_rows_kernel, n_dp),
        out_shape=block_out,
        in_specs=[ANY, VMEM],
        out_specs=[ANY, VMEM],
        scratch_shapes=[*block_scratch, *semaphores(count, local)],
        compiler_params=params(6),
        name="block_rows",
    )(m_part, resid)
    return (*grads, *block)


def latent_kernel(n_dp, part, full, from_core, half, from_side, send, recv, local):
    links = Links(n_dp)
    copies = Copies(send, recv, local)
    links.meet(high=False, low=False)
    arrive = copies.go(part.at[1 - links.core], from_core, links.over_core())
    arrive.wait_recv()
    half[...] = (part[links.core].astype(F32) + from_core[...].astype(F32)).astype(BF)
    arrive = copies.go(half, from_side, links.over_side())
    arrive.wait_recv()
    full[links.core] = (half[...].astype(F32) + from_side[...].astype(F32)).astype(BF)
    arrive = copies.go(full.at[links.core], full.at[links.core], links.over_core())
    arrive.wait_recv()
    copies.finish()


def sum_latents(n_dp, part):
    rows, columns = part.shape
    half = (rows // 2, columns)
    return pl.pallas_call(
        functools.partial(latent_kernel, n_dp),
        out_shape=jax.ShapeDtypeStruct((2, *half), BF),
        in_specs=[VMEM],
        out_specs=VMEM,
        scratch_shapes=[pltpu.VMEM(half, BF)] * 3 + semaphores(3, 1),
        compiler_params=params(4),
        name="sum_latents",
    )(part.reshape(2, *half)).reshape(rows, columns)


def weight_grads_kernel(n_dp, d_part, o_part, q_part, kv_part, small, stats, d_full, o_sum, q_sum, kv_sum, small_full, *rest):
    d_block, small_block, stats_block = rest[:3]
    bufs = rest[3:15]
    small_in, stats_in = rest[15:17]
    send, recv, local = rest[17:]
    links = Links(n_dp)
    copies = Copies(send, recv, local)
    links.meet()

    def small_stream():
        n_high = links.n_high
        low_in = copies.go(
            small.at[:, 1 - links.low], small_in.at[pl.ds(0, n_high)], links.over_low()
        )
        stats_low = copies.go(stats, stats_in.at[0], links.over_low())
        yield
        low_in.wait_recv()
        stats_low.wait_recv()
        for k in range(n_high):
            small_in[k] = small_in[k] + small[k, links.low]
        stats_block[...] = stats[...] + stats_in[0]
        waits = []
        for k in range(1, n_high):
            there = links.ahead(k)
            waits.append(
                copies.go(
                    small_in.at[there], small_in.at[n_high + k - 1], links.device(high=there)
                )
            )
            waits.append(copies.go(stats_block, stats_in.at[k], links.device(high=there)))
        yield
        for wait in waits:
            wait.wait_recv()
        total = small_in[links.high]
        everything = stats_block[...]
        for k in range(1, n_high):
            total = total + small_in[n_high + k - 1]
            everything = everything + stats_in[k]
        small_block[0] = total
        small_block[1] = everything
        yield from tensor_gather(links, copies, small_block, small_full)

    def down_stream():
        yield from dp_scatter(links, copies, d_part, bufs[:3], d_block)
        yield from tensor_gather(links, copies, d_block, d_full)

    take_turns(
        down_stream(),
        dp_scatter(links, copies, q_part, bufs[6:9], q_sum),
        dp_scatter(links, copies, kv_part, bufs[9:12], kv_sum),
        dp_scatter(links, copies, o_part, bufs[3:6], o_sum),
        small_stream(),
    )
    copies.finish()


def sum_weight_grads(n_dp, down, o_t, q_up, kv_up, small, stats):
    n_high = n_dp // 2

    def parts(array):
        return array.reshape(n_high, 2, array.shape[0] // n_dp, *array.shape[1:])

    down, o_t, q_up, kv_up = parts(down), parts(o_t), parts(q_up), parts(kv_up)
    small = small.reshape(n_high, 2, *small.shape[1:])
    count = 4 * (2 * n_high - 1) + 2 * n_high + 6
    d_shape, o_shape, q_shape, kv_shape = (a.shape[2:] for a in (down, o_t, q_up, kv_up))
    one = stats.shape
    return pl.pallas_call(
        functools.partial(weight_grads_kernel, n_dp),
        out_shape=(
            jax.ShapeDtypeStruct((4, *d_shape), BF),
            jax.ShapeDtypeStruct(o_shape, F32),
            jax.ShapeDtypeStruct(q_shape, F32),
            jax.ShapeDtypeStruct(kv_shape, F32),
            jax.ShapeDtypeStruct((4, 2, *one), F32),
        ),
        in_specs=[VMEM] * 6,
        out_specs=[VMEM] * 5,
        scratch_shapes=[
            pltpu.VMEM(d_shape, BF),
            pltpu.VMEM((2, *one), F32),
            pltpu.VMEM(one, F32),
            *dp_scatter_scratch(n_high, d_shape),
            *dp_scatter_scratch(n_high, o_shape),
            *dp_scatter_scratch(n_high, q_shape),
            *dp_scatter_scratch(n_high, kv_shape),
            pltpu.VMEM((2 * n_high - 1, *one), F32),
            pltpu.VMEM((n_high, *one), F32),
            *semaphores(count, 2),
        ],
        compiler_params=params(5),
        name="sum_weight_grads",
    )(down, o_t, q_up, kv_up, small, stats)


def attention_mask(seg_col, seg_row, valid_row):
    length = seg_col.shape[0]
    row = lax.broadcasted_iota(jnp.int32, (length, length), 0)
    column = lax.broadcasted_iota(jnp.int32, (length, length), 1)
    allowed = (
        (seg_col[...] == seg_row[...])
        & (column <= row)
        & ((valid_row[...] == 1) | (column == row))
    )
    return jnp.where(allowed, 0.0, NEGATIVE)


def swap_halves(values):
    half = values.shape[1] // 2
    return jnp.concatenate([values[:, half:], values[:, :half]], axis=1)


def turn(values, cos_full, sin_full):
    return values * cos_full + swap_halves(values) * sin_full


def head_probs(query, key, bias, inv_root):
    scores = dot_nt(query, key) * inv_root + bias
    weights = jnp.exp(scores - jnp.max(scores, axis=-1, keepdims=True))
    return weights / jnp.sum(weights, axis=-1, keepdims=True)


def attend_rows(
    x, gain_attn, gain_q, gain_kv, down, q_up, kv_up, bias, cos_full, sin_full,
    normed, latents, q_normed, kv_normed, q_rows, kv_rows, key_rot, mixed,
):
    rank_q = gain_q.shape[1]
    stream = x[...].astype(F32)
    normed[...] = (stream * inverse_rms(stream) * gain_attn).astype(BF)
    latents[...] = dot(normed[...], down)
    q_latent = latents[:, :rank_q]
    q_normed[...] = (q_latent * inverse_rms(q_latent) * gain_q).astype(BF)
    kv_latent = latents[:, rank_q : rank_q + KR]
    kv_normed[...] = (kv_latent * inverse_rms(kv_latent) * gain_kv).astype(BF)
    turned = turn(latents[:, rank_q + KR : rank_q + KR + ROPE], cos_full[...], sin_full[...])
    key_rot[...] = turned.astype(BF)
    kv_rows[...] = dot(kv_normed[...], kv_up).astype(BF)
    q_heads = dot(q_normed[...], q_up)
    inv_root = 1.0 / math.sqrt(NOPE + ROPE)
    for head in range(q_rows.shape[1] // (NOPE + ROPE)):
        base = head * (NOPE + ROPE)
        query = jnp.concatenate(
            [
                q_heads[:, base : base + NOPE],
                turn(
                    q_heads[:, base + NOPE : base + NOPE + ROPE], cos_full[...], sin_full[...]
                ),
            ],
            axis=1,
        ).astype(BF)
        q_rows[:, base : base + NOPE + ROPE] = query
        start = head * (NOPE + VD)
        key = jnp.concatenate([kv_rows[:, start : start + NOPE], key_rot[...]], axis=1)
        value = kv_rows[:, start + NOPE : start + NOPE + VD]
        probs = head_probs(query, key, bias, inv_root).astype(BF)
        mixed[:, head * VD : head * VD + VD] = dot(probs, value).astype(BF)


def attend_kernel(
    x, gain_attn, gain_q, gain_kv, down, q_up, kv_up, seg_col, seg_row, valid_row, cos_full, sin_full,
    *outs,
):
    attend_rows(
        x, gain_attn[...], gain_q[...], gain_kv[...], down[...], q_up[...], kv_up[...],
        attention_mask(seg_col, seg_row, valid_row), cos_full, sin_full, *outs,
    )


def attend(x, gain_attn, gain_q, gain_kv, down, q_up, kv_up, segments, valid, cos_full, sin_full):
    length = x.shape[0]
    heads = q_up.shape[1] // (NOPE + ROPE)

    def rows(columns, kind):
        return jax.ShapeDtypeStruct((length, columns), kind)

    return pl.pallas_call(
        attend_kernel,
        out_shape=(
            rows(x.shape[1], BF),
            rows(down.shape[1], F32),
            rows(q_up.shape[0], BF),
            rows(kv_up.shape[0], BF),
            rows(q_up.shape[1], BF),
            rows(kv_up.shape[1], BF),
            rows(ROPE, BF),
            rows(heads * VD, BF),
        ),
        in_specs=[VMEM] * 12,
        out_specs=[VMEM] * 8,
        compiler_params=pltpu.CompilerParams(vmem_limit_bytes=VMEM_BYTES),
        name="attend",
    )(
        x,
        gain_attn[None, :],
        gain_q[None, :],
        gain_kv[None, :],
        down,
        q_up,
        kv_up,
        segments[:, None],
        segments[None, :],
        valid[None, :],
        cos_full,
        sin_full,
    )


def later(stream, turns):
    for _ in range(turns):
        yield
    yield from stream


class Swap:
    def __init__(self, links, copies, blocks, out):
        self.me = links.high * 2 + links.low
        self.copies, self.blocks, self.out = copies, blocks, out
        self.own = copies.near(blocks.at[self.me], out.at[self.me])
        self.arrive = []

    def send(self, steps):
        n_dp = self.blocks.shape[0]
        for k in steps:
            there = (self.me + k) % n_dp
            self.arrive.append(
                self.copies.go(self.blocks.at[there], self.out.at[self.me], {"dp": there})
            )

    def finish(self):
        for copy in self.arrive:
            copy.wait_recv()
        self.own.wait()


def pack_stream(w_gate, w_up, w_down, packed):
    n_dp, width, lanes = packed.shape
    slice_ff = w_gate.shape[1] // n_dp
    for k in range(n_dp):
        at = k * slice_ff
        packed[k] = jnp.concatenate(
            [
                w_gate[:, at : at + slice_ff],
                w_up[:, at : at + slice_ff],
                w_down[at : at + slice_ff, :].T,
                jnp.zeros((width, lanes - 3 * slice_ff), BF),
            ],
            axis=1,
        )
        yield


def front_kernel(
    n_dp, x, x_rows, cot, down, gains, q_up, kv_up, o_t, w_gate, w_up, w_down,
    seg_col, seg_row, valid_row, cos_full, sin_full,
    f_down, f_o, f_q, f_kv, f_g, f_cot, f_w, f_normed,
    normed, latents, q_normed, kv_normed, q_rows, kv_rows, key_rot, mixed, resid, branch, gain_mlp,
    packed, part, from_core, out_side, from_side, block, send, recv, local,
):
    links = Links(n_dp)
    copies = Copies(send, recv, local)
    links.meet(swap=True)
    o_stream = dp_gather(links, copies, o_t, f_o)
    take_turns(
        every_gather(links, copies, down, f_down),
        dp_gather(links, copies, gains, f_g),
        dp_gather(links, copies, q_up, f_q),
        dp_gather(links, copies, kv_up, f_kv),
        pack_stream(w_gate, w_up, w_down, packed),
        later(itertools.islice(o_stream, 1), 1),
    )

    def gain_of(row, count):
        return jnp.concatenate(
            [f_g[k].astype(F32)[row : row + 1, :count] for k in range(n_dp)], axis=1
        )

    swap = Swap(links, copies, packed, f_w)
    swap.send(range(2, n_dp, 2))
    next(o_stream)
    width = down.shape[0] * 4
    full_down = f_down[...].reshape(n_dp * width, down.shape[1])
    full_q = f_q[...].reshape(n_dp * q_up.shape[0], q_up.shape[1])
    full_kv = f_kv[...].reshape(n_dp * kv_up.shape[0], kv_up.shape[1])
    attend_rows(
        x, gain_of(0, width), gain_of(1, q_up.shape[0]), gain_of(2, kv_up.shape[0]),
        full_down, full_q, full_kv, attention_mask(seg_col, seg_row, valid_row), cos_full, sin_full,
        normed, latents, q_normed, kv_normed, q_rows, kv_rows, key_rot, mixed,
    )
    for _ in range(links.n_high - 1):
        next(o_stream)
    cot_stream = every_gather(links, copies, cot, f_cot, cot.shape[-1])
    next(cot_stream)
    next(cot_stream)
    take_turns(o_stream)
    gain_mlp[...] = gain_of(3, width)
    full_o = f_o[...].reshape(n_dp * width, o_t.shape[1])
    rows = block.shape[0]
    attn_part = dot_nt(mixed[...], full_o).astype(BF)
    for side in range(2):
        for core in range(2):
            at = (side * 2 + core) * rows
            part[side, core] = attn_part[at : at + rows]

    def resid_stream():
        over = copies.go(part.at[:, 1 - links.core], from_core, links.over_core())
        over.wait_recv()
        out_side[...] = (
            part[1 - links.side, links.core].astype(F32) + from_core[1 - links.side].astype(F32)
        ).astype(BF)
        over = copies.go(out_side, from_side, links.over_side())
        mine = part[links.side, links.core].astype(F32) + from_core[links.side].astype(F32)
        over.wait_recv()
        attn = RESIDUAL_SCALE * (mine + from_side[...].astype(F32))
        stream = x_rows[...].astype(F32) + attn
        branch[...] = attn
        resid[...] = stream
        block[...] = (stream * inverse_rms(stream) * gain_mlp[...]).astype(BF)
        yield from every_gather(links, copies, block, f_normed)

    normed_stream = resid_stream()
    next(normed_stream)
    swap.send(range(1, n_dp, 2))
    take_turns(normed_stream, cot_stream)
    swap.finish()
    copies.finish()


def front(n_dp, x, x_rows, cot, down, gains, q_up, kv_up, o_t, w_gate, w_up, w_down, segments, valid, cos_full, sin_full):
    n_high = n_dp // 2
    length, columns = x.shape
    rows = x_rows.shape[0]
    lanes = -(-3 * (w_gate.shape[1] // n_dp) // 128) * 128
    heads = q_up.shape[1] // (NOPE + ROPE)
    count = 3 * count_every_gather(n_high) + 4 * (2 * n_high - 1) + n_dp + 1

    def over(block, *lead, kind=BF):
        return jax.ShapeDtypeStruct((*lead, *block), kind)

    return pl.pallas_call(
        functools.partial(front_kernel, n_dp),
        out_shape=(
            over(down.shape, n_dp, 4),
            over(o_t.shape, n_dp),
            over(q_up.shape, n_dp),
            over(kv_up.shape, n_dp),
            over(gains.shape, n_dp),
            over(cot.shape, n_dp, 4),
            over((w_gate.shape[0], lanes), n_dp),
            over(cot.shape, n_dp, 4),
            over((columns,), length),
            over((down.shape[1],), length, kind=F32),
            over((q_up.shape[0] * n_dp,), length),
            over((kv_up.shape[0] * n_dp,), length),
            over((q_up.shape[1],), length),
            over((kv_up.shape[1],), length),
            over((ROPE,), length),
            over((heads * VD,), length),
            over((columns,), rows, kind=F32),
            over((columns,), rows, kind=F32),
            over((columns,), 1, kind=F32),
        ),
        in_specs=[VMEM] * 16,
        out_specs=[VMEM] * 5 + [ANY] * 3 + [VMEM] * 11,
        scratch_shapes=[
            pltpu.VMEM((n_dp, w_gate.shape[0], lanes), BF),
            pltpu.VMEM((2, 2, rows, columns), BF),
            pltpu.VMEM((2, rows, columns), BF),
            pltpu.VMEM((rows, columns), BF),
            pltpu.VMEM((rows, columns), BF),
            pltpu.VMEM((rows, columns), BF),
            *semaphores(count, 8),
        ],
        compiler_params=params(7),
        name="front",
    )(
        x, x_rows, cot, down, gains, q_up, kv_up, o_t, w_gate, w_up, w_down,
        segments[:, None], segments[None, :], valid[None, :], cos_full, sin_full,
    )


def feed_forward_kernel(slice_ff, normed, cot, weights, m_part, g_part, grads, sum_in, sum_out):
    step = pl.program_id(0)
    cut = slice_ff * 2 // 128 * 128
    pad = slice_ff * 2 - cut
    w_in, w_out = weights[:, : sum_in.shape[0]], weights[:, cut:]
    rows = normed.shape[0]
    both = dot(normed[...], w_in)
    gate, upper = both[:, :slice_ff], both[:, slice_ff : 2 * slice_ff]
    sigma = jax.nn.sigmoid(gate)
    swish = gate * sigma

    def zeros(count):
        return jnp.zeros((rows, count), F32)

    def placed(hidden):
        rest = w_out.shape[1] - pad - slice_ff
        return jnp.concatenate([zeros(pad), hidden, zeros(rest)], axis=1).astype(BF)

    hidden = placed(swish * upper)
    m_part[...] = dot_nt(hidden, w_out).astype(BF)
    grad_mlp = (RESIDUAL_SCALE * cot[...].astype(F32)).astype(BF)
    grad_hidden = dot(grad_mlp, w_out)[:, pad : pad + slice_ff]
    grad_both = jnp.concatenate(
        [
            grad_hidden * upper * (sigma * (1.0 + gate * (1.0 - sigma))),
            grad_hidden * swish,
            zeros(w_in.shape[1] - 2 * slice_ff),
        ],
        axis=1,
    ).astype(BF)
    g_part[...] = dot_nt(grad_both, w_in).astype(BF)

    @pl.when(step == 0)
    def _():
        sum_in[...] = dot_tn(grad_both, normed[...])
        sum_out[...] = dot_tn(hidden, grad_mlp)

    @pl.when(step > 0)
    def _():
        sum_in[...] += dot_tn(grad_both, normed[...])
        sum_out[...] += dot_tn(hidden, grad_mlp)

    @pl.when(step == pl.num_programs(0) - 1)
    def _():
        mid = sum_in.shape[0]
        if cut:
            grads[:, :cut] = sum_in[:cut].T.astype(BF)
        grads[:, cut:mid] = (sum_in[cut:] + sum_out[: mid - cut]).T.astype(BF)
        grads[:, mid:] = sum_out[mid - cut :].T.astype(BF)


def feed_forward(normed, cot, weights, slice_ff, rows):
    tokens, columns = normed.shape
    lanes = weights.shape[1]
    cut = slice_ff * 2 // 128 * 128
    wide = -(-slice_ff * 2 // 128) * 128
    token_block = pl.BlockSpec((rows, columns), lambda i: (i, 0))
    whole = pl.BlockSpec((columns, lanes), lambda i: (0, 0))
    part = jax.ShapeDtypeStruct((tokens, columns), BF)
    return pl.pallas_call(
        functools.partial(feed_forward_kernel, slice_ff),
        grid=(tokens // rows,),
        out_shape=(part, part, jax.ShapeDtypeStruct((columns, lanes), BF)),
        in_specs=[token_block, token_block, whole],
        out_specs=[token_block, token_block, whole],
        scratch_shapes=[
            pltpu.VMEM((wide, columns), F32),
            pltpu.VMEM((lanes - cut, columns), F32),
        ],
        compiler_params=pltpu.CompilerParams(vmem_limit_bytes=VMEM_BYTES),
        name="feed_forward",
    )(normed, cot, weights)


def attend_back_kernel(
    grad_attn, mixed, o_t, q_rows, kv_rows, key_rot, q_normed, kv_normed, q_up, kv_up,
    seg_col, seg_row, valid_row, cos_full, sin_full,
    grad_latents, grad_o, grad_q_up, grad_kv_up, grad_q, grad_kv,
):
    rank_q = q_up.shape[0]
    grad_o[...] = dot_tn(grad_attn[...], mixed[...]).astype(BF)
    grad_mixed = dot(grad_attn[...], o_t[...]).astype(BF)
    bias = attention_mask(seg_col, seg_row, valid_row)
    inv_root = 1.0 / math.sqrt(NOPE + ROPE)
    grad_rot = jnp.zeros((grad_attn.shape[0], ROPE), F32)
    for head in range(q_rows.shape[1] // (NOPE + ROPE)):
        base = head * (NOPE + ROPE)
        start = head * (NOPE + VD)
        query = q_rows[:, base : base + NOPE + ROPE]
        key = jnp.concatenate([kv_rows[:, start : start + NOPE], key_rot[...]], axis=1)
        value = kv_rows[:, start + NOPE : start + NOPE + VD]
        grad = grad_mixed[:, head * VD : head * VD + VD]
        probs = head_probs(query, key, bias, inv_root)
        grad_value = dot_tn(probs.astype(BF), grad)
        grad_probs = dot_nt(grad, value)
        inner = jnp.sum(probs * grad_probs, axis=-1, keepdims=True)
        grad_scores = (probs * (grad_probs - inner)).astype(BF)
        grad_query = dot(grad_scores, key) * inv_root
        grad_key = dot_tn(grad_scores, query) * inv_root
        grad_q[:, base : base + NOPE + ROPE] = jnp.concatenate(
            [grad_query[:, :NOPE], turn(grad_query[:, NOPE:], cos_full[...], -sin_full[...])],
            axis=1,
        ).astype(BF)
        grad_kv[:, start : start + NOPE + VD] = jnp.concatenate(
            [grad_key[:, :NOPE], grad_value], axis=1
        ).astype(BF)
        grad_rot = grad_rot + grad_key[:, NOPE:]
    grad_latents[...] = jnp.zeros_like(grad_latents)
    grad_latents[:, :rank_q] = dot_nt(grad_q[...], q_up[...]).astype(BF)
    grad_latents[:, rank_q : rank_q + KR] = dot_nt(grad_kv[...], kv_up[...]).astype(BF)
    grad_latents[:, rank_q + KR : rank_q + KR + ROPE] = turn(
        grad_rot, cos_full[...], -sin_full[...]
    ).astype(BF)
    grad_q_up[...] = dot_tn(q_normed[...], grad_q[...]).astype(BF)
    grad_kv_up[...] = dot_tn(kv_normed[...], grad_kv[...]).astype(BF)


def attend_back(
    grad_attn, mixed, o_t, q_rows, kv_rows, key_rot, q_normed, kv_normed, q_up, kv_up,
    segments, valid, cos_full, sin_full, columns_down,
):
    length = grad_attn.shape[0]

    def out(shape):
        return jax.ShapeDtypeStruct(shape, BF)

    return pl.pallas_call(
        attend_back_kernel,
        out_shape=(
            out((length, columns_down)),
            out(o_t.shape),
            out(q_up.shape),
            out(kv_up.shape),
        ),
        in_specs=[VMEM] * 15,
        out_specs=[VMEM] * 4,
        scratch_shapes=[pltpu.VMEM(q_rows.shape, BF), pltpu.VMEM(kv_rows.shape, BF)],
        compiler_params=pltpu.CompilerParams(vmem_limit_bytes=VMEM_BYTES),
        name="attend_back",
    )(
        grad_attn, mixed, o_t, q_rows, kv_rows, key_rot, q_normed, kv_normed, q_up, kv_up,
        segments[:, None], segments[None, :], valid[None, :], cos_full, sin_full,
    )


class ScatterInto:
    def __init__(self, links, copies, bufs, result):
        self.links, self.copies, self.result = links, copies, result
        self.part, self.from_low, self.from_high = bufs
        self.order = steps_by_distance(links.n_high) + [0]
        self.low_in, self.high_in = {}, {}

    def start(self):
        for k in self.order:
            self.low_in[k] = self.copies.go(
                self.part.at[self.links.ahead(k), 1 - self.links.low],
                self.from_low.at[k],
                self.links.over_low(),
            )

    def steps(self):
        links, part = self.links, self.part
        for k in self.order:
            there = links.ahead(k)
            self.low_in[k].wait_recv()
            part[there, links.low] = (
                part[there, links.low].astype(F32) + self.from_low[k].astype(F32)
            ).astype(BF)
            if k:
                self.high_in[k] = self.copies.go(
                    part.at[there, links.low], self.from_high.at[k - 1], links.device(high=there)
                )

    def finish(self):
        total = self.part[self.links.high, self.links.low].astype(F32)
        for k in steps_by_distance(self.links.n_high):
            self.high_in[k].wait_recv()
            total = total + self.from_high[k - 1].astype(F32)
        self.result[...] = total.astype(self.result.dtype)


def scatter_into_scratch(n_high, shape):
    return [
        pltpu.VMEM((n_high, 2, *shape), BF),
        pltpu.VMEM((n_high, *shape), BF),
        pltpu.VMEM((n_high - 1, *shape), BF),
    ]


def small_stream(links, copies, small, small_in, stats, stats_in, stats_block, small_block, small_full):
    n_high = links.n_high
    low_in = copies.go(
        small.at[:, 1 - links.low], small_in.at[pl.ds(0, n_high)], links.over_low()
    )
    stats_low = copies.go(stats, stats_in.at[0], links.over_low())
    yield
    low_in.wait_recv()
    stats_low.wait_recv()
    for k in range(n_high):
        small_in[k] = small_in[k] + small[k, links.low]
    stats_block[...] = stats[...] + stats_in[0]
    waits = []
    for k in range(1, n_high):
        there = links.ahead(k)
        waits.append(
            copies.go(small_in.at[there], small_in.at[n_high + k - 1], links.device(high=there))
        )
        waits.append(copies.go(stats_block, stats_in.at[k], links.device(high=there)))
    yield
    for wait in waits:
        wait.wait_recv()
    total = small_in[links.high]
    everything = stats_block[...]
    for k in range(1, n_high):
        total = total + small_in[n_high + k - 1]
        everything = everything + stats_in[k]
    small_block[0] = total
    small_block[1] = everything
    yield from tensor_gather(links, copies, small_block, small_full)


def back_kernel(
    n_dp, g_part, m_part, w_part, resid, branch, cot, weight, x, normed, latents, q_normed, kv_normed,
    q_rows, kv_rows, key_rot, mixed, f_down, f_o, f_q, f_kv, f_g, seg_col, seg_row, valid_row,
    cos_full, sin_full,
    block_full, grad_input, d_full, o_sum, q_sum, kv_sum, small_full, w_full,
    attn_full, grad_rows, g_rows, m_rows, grad_q, grad_kv, lat, lat_in, lat_half, lat_side,
    lat_full, d_block, small, small_in, stats, stats_in, stats_block, small_block, *rest,
):
    g_bufs, m_bufs = rest[:8], (rest[0], *rest[8:13])
    d_bufs, o_bufs, q_bufs, kv_bufs = rest[13:16], rest[16:19], rest[19:22], rest[22:25]
    links = Links(n_dp)
    copies = Copies(*rest[25:])
    links.meet(swap=True)
    length = x.shape[0]
    rank_q, rank_kv = q_normed.shape[1], kv_normed.shape[1]
    width = o_sum.shape[0]

    def gain_of(row, count):
        return jnp.concatenate(
            [f_g[k].astype(F32)[row : row + 1, :count] for k in range(n_dp)], axis=1
        )

    half_columns = x.shape[1] // 256 * 128
    g = EveryScatter(links, copies, g_part, g_bufs, g_rows, half_columns)
    m = EveryScatter(links, copies, m_part, m_bufs, m_rows, 0)
    swap = Swap(links, copies, w_part, w_full)
    high = range(links.n_high)
    g.start()
    swap.send(range(2, n_dp, 2))
    for i in range(links.n_high + 1):
        if i in high:
            g.first(i)
        if i - 1 in high:
            g.second(i - 1)
        if i - 2 in high:
            g.third(i - 2)
    m.start()
    swap.send(range(1, n_dp, 2))
    g.third(links.n_high - 1)
    m.first(0)
    m.first(1)
    g.finish()
    stream = resid[...]
    inv_two = inverse_rms(stream)
    unit_two = stream * inv_two
    gain_mlp = gain_of(3, width)
    grad = cot[...].astype(F32) + norm_back(g_rows[...] * gain_mlp, unit_two, inv_two)
    grad_rows[...] = (RESIDUAL_SCALE * grad).astype(BF)
    t_stream = tensor_gather(links, copies, grad_rows, attn_full)
    next(t_stream)
    m.first(2)
    m.first(3)
    mlp_gain = jnp.sum(g_rows[...] * unit_two, axis=0, keepdims=True)
    bias = attention_mask(seg_col, seg_row, valid_row)
    for _ in t_stream:
        pass

    grad_attn = attn_full[...].reshape(length, x.shape[1])
    for k in range(n_dp):
        o_bufs[0][k // 2, k % 2] = dot_tn(
            grad_attn[:, k * width : k * width + width], mixed[...]
        ).astype(BF)
    o = ScatterInto(links, copies, o_bufs, o_sum)
    o.start()

    grad_mixed = dot(grad_attn, f_o[...].reshape(n_dp * width, mixed.shape[1])).astype(BF)
    inv_root = 1.0 / math.sqrt(NOPE + ROPE)
    grad_rot = jnp.zeros((length, ROPE), F32)
    for head in range(q_rows.shape[1] // (NOPE + ROPE)):
        base = head * (NOPE + ROPE)
        start = head * (NOPE + VD)
        query = q_rows[:, base : base + NOPE + ROPE]
        key = jnp.concatenate([kv_rows[:, start : start + NOPE], key_rot[...]], axis=1)
        value = kv_rows[:, start + NOPE : start + NOPE + VD]
        grad_head = grad_mixed[:, head * VD : head * VD + VD]
        probs = head_probs(query, key, bias, inv_root)
        grad_value = dot_tn(probs.astype(BF), grad_head)
        grad_probs = dot_nt(grad_head, value)
        inner = jnp.sum(probs * grad_probs, axis=-1, keepdims=True)
        grad_scores = (probs * (grad_probs - inner)).astype(BF)
        grad_query = dot(grad_scores, key) * inv_root
        grad_key = dot_tn(grad_scores, query) * inv_root
        grad_q[:, base : base + NOPE + ROPE] = jnp.concatenate(
            [grad_query[:, :NOPE], turn(grad_query[:, NOPE:], cos_full[...], -sin_full[...])],
            axis=1,
        ).astype(BF)
        grad_kv[:, start : start + NOPE + VD] = jnp.concatenate(
            [grad_key[:, :NOPE], grad_value], axis=1
        ).astype(BF)
        grad_rot = grad_rot + grad_key[:, NOPE:]

    half = length // 2
    lat[...] = jnp.zeros_like(lat)
    full_q = f_q[...].reshape(rank_q, q_rows.shape[1])
    full_kv = f_kv[...].reshape(rank_kv, kv_rows.shape[1])
    grad_turned = turn(grad_rot, cos_full[...], -sin_full[...]).astype(BF)
    for core in range(2):
        at = core * half
        lat[core, :, :rank_q] = dot_nt(grad_q[at : at + half], full_q).astype(BF)
        lat[core, :, rank_q : rank_q + rank_kv] = dot_nt(
            grad_kv[at : at + half], full_kv
        ).astype(BF)
        lat[core, :, rank_q + rank_kv : rank_q + rank_kv + ROPE] = grad_turned[at : at + half]
    over = copies.go(lat.at[1 - links.core], lat_in, links.over_core())
    rows_q = q_sum.shape[0]
    for k in range(n_dp):
        q_bufs[0][k // 2, k % 2] = dot_tn(
            q_normed[:, k * rows_q : k * rows_q + rows_q], grad_q[...]
        ).astype(BF)
    q = ScatterInto(links, copies, q_bufs, q_sum)
    q.start()
    over.wait_recv()
    lat_half[...] = (lat[links.core].astype(F32) + lat_in[...].astype(F32)).astype(BF)
    over = copies.go(lat_half, lat_side, links.over_side())
    rows_kv = kv_sum.shape[0]
    for k in range(n_dp):
        kv_bufs[0][k // 2, k % 2] = dot_tn(
            kv_normed[:, k * rows_kv : k * rows_kv + rows_kv], grad_kv[...]
        ).astype(BF)
    kv = ScatterInto(links, copies, kv_bufs, kv_sum)
    kv.start()
    over.wait_recv()
    lat_full[links.core] = (lat_half[...].astype(F32) + lat_side[...].astype(F32)).astype(BF)
    mine = lat_full.at[links.core]
    over = copies.go(mine, mine, links.over_core())
    q_latent = latents[:, :rank_q]
    inv_q = inverse_rms(q_latent)
    unit_q = q_latent * inv_q
    kv_latent = latents[:, rank_q : rank_q + rank_kv]
    inv_kv = inverse_rms(kv_latent)
    unit_kv = kv_latent * inv_kv
    over.wait_recv()
    lat_sum = lat_full[...].reshape(length, lat.shape[2]).astype(F32)
    grad_q_latent, grad_kv_latent = lat_sum[:, :rank_q], lat_sum[:, rank_q : rank_q + rank_kv]
    q_gain = jnp.sum(grad_q_latent * unit_q, axis=0, keepdims=True)
    kv_gain = jnp.sum(grad_kv_latent * unit_kv, axis=0, keepdims=True)
    grad_down = jnp.concatenate(
        [
            norm_back(grad_q_latent * gain_of(1, rows_q), unit_q, inv_q),
            norm_back(grad_kv_latent * gain_of(2, rows_kv), unit_kv, inv_kv),
            lat_sum[:, rank_q + rank_kv :],
        ],
        axis=1,
    ).astype(BF)

    rows_down = d_block.shape[0]
    m.second(0)
    m.second(1)
    copies.near(normed, g_bufs[0].at[0]).wait()
    normed_rows = g_bufs[0][0].reshape(length, x.shape[1])
    rank = links.side * 2 + links.core
    for k in range(n_dp):
        rows_all = dot_tn(normed_rows[:, k * width : k * width + width], grad_down)
        mine = rows_all[:rows_down]
        for quarter in range(1, 4):
            at = quarter * rows_down
            mine = jnp.where(rank == quarter, rows_all[at : at + rows_down], mine)
        d_bufs[0][k // 2, k % 2] = mine.astype(BF)

    d = ScatterInto(links, copies, d_bufs, d_block)
    d.start()
    o.steps()
    m.second(2)
    m.second(3)
    grad_input[...] = dot_nt(grad_down, f_down[...].reshape(n_dp * width, grad_down.shape[1]))
    q.steps()
    kv.steps()
    for i in high:
        m.third(i)
    d.steps()
    m.finish()
    mlp = RESIDUAL_SCALE * m_rows[...]
    g_rows[...] = resid[...] + mlp
    block_gather = tensor_gather(links, copies, g_rows, block_full)
    next(block_gather)
    weights = weight[...]
    lane = lax.broadcasted_iota(jnp.int32, stats.shape, 1)
    sums = [
        jnp.sum(jnp.sum(weights * rows * rows, axis=1, keepdims=True), axis=0, keepdims=True)
        for rows in (resid[...], branch[...], mlp)
    ] + [jnp.sum(weights, axis=0, keepdims=True)]
    packed = jnp.zeros(stats.shape, F32)
    for index, value in enumerate(sums):
        packed = jnp.where(lane == index, value, packed)
    stats[...] = packed
    stream = x[...].astype(F32)
    inv_one = inverse_rms(stream)
    unit_one = stream * inv_one
    attn_gain = jnp.sum(grad_input[...] * unit_one, axis=0, keepdims=True)
    grad_input[...] = grad_attn.astype(F32) * (1.0 / RESIDUAL_SCALE) + norm_back(
        grad_input[...] * gain_of(0, width), unit_one, inv_one
    )

    def piece(vector, k):
        count = vector.shape[1] // n_dp
        cut = vector[:, k * count : k * count + count]
        return jnp.concatenate([cut, jnp.zeros((1, small.shape[3] - count), F32)], axis=1)

    for k in range(n_dp):
        small[k // 2, k % 2] = jnp.concatenate(
            [piece(v, k) for v in (attn_gain, q_gain, kv_gain, mlp_gain)]
            + [jnp.zeros((4, small.shape[3]), F32)],
            axis=0,
        )
    small_rows = small_stream(
        links, copies, small, small_in, stats, stats_in, stats_block, small_block, small_full
    )
    next(small_rows)
    d.finish()
    down_gather = tensor_gather(links, copies, d_block, d_full)
    take_turns(small_rows, down_gather, block_gather)
    o.finish()
    q.finish()
    kv.finish()
    swap.finish()
    copies.finish()


def back(
    n_dp, g_part, m_part, w_part, resid, branch, cot, weight, x, normed, latents, q_normed, kv_normed,
    q_rows, kv_rows, key_rot, mixed, f_down, f_o, f_q, f_kv, f_g, segments, valid, cos_full, sin_full,
):
    n_high = n_dp // 2
    rows, columns = resid.shape
    length = x.shape[0]
    lanes = f_g.shape[2]
    half = (length // 2, latents.shape[1])
    shape = (n_high, 2, 2, 2, rows, columns)
    d_shape, o_shape, q_shape, kv_shape = f_down.shape[2:], f_o.shape[1:], f_q.shape[1:], f_kv.shape[1:]
    one = (8, lanes)
    count = 2 * (6 * n_high - 1) + 4 * (2 * n_high - 1) + 4 * 3 + (n_dp - 1) + 2 * n_high + 3

    def out(shape, kind=F32):
        return jax.ShapeDtypeStruct(shape, kind)

    return pl.pallas_call(
        functools.partial(back_kernel, n_dp),
        out_shape=(
            out((4, rows, columns)),
            out((length, columns)),
            out((4, *d_shape), BF),
            out(o_shape),
            out(q_shape),
            out(kv_shape),
            out((4, 2, *one)),
            out(w_part.shape, BF),
        ),
        in_specs=[ANY] * 3 + [VMEM] * 5 + [ANY] + [VMEM] * 17,
        out_specs=[ANY] + [VMEM] * 6 + [ANY],
        scratch_shapes=[
            pltpu.VMEM((4, rows, columns), BF),
            pltpu.VMEM((rows, columns), BF),
            pltpu.VMEM((rows, columns), F32),
            pltpu.VMEM((rows, columns), F32),
            pltpu.VMEM(q_rows.shape, BF),
            pltpu.VMEM(kv_rows.shape, BF),
            pltpu.VMEM((2, *half), BF),
            pltpu.VMEM(half, BF),
            pltpu.VMEM(half, BF),
            pltpu.VMEM(half, BF),
            pltpu.VMEM((2, *half), BF),
            pltpu.VMEM(d_shape, BF),
            pltpu.VMEM((n_high, 2, *one), F32),
            pltpu.VMEM((2 * n_high - 1, *one), F32),
            pltpu.VMEM(one, F32),
            pltpu.VMEM((n_high, *one), F32),
            pltpu.VMEM(one, F32),
            pltpu.VMEM((2, *one), F32),
            *every_scatter_scratch(n_high, rows, columns),
            *every_scatter_scratch(n_high, rows, columns, 0)[1:],
            *scatter_into_scratch(n_high, d_shape),
            *scatter_into_scratch(n_high, o_shape),
            *scatter_into_scratch(n_high, q_shape),
            *scatter_into_scratch(n_high, kv_shape),
            *semaphores(count, 2 * n_high + 6),
        ],
        compiler_params=params(8, 62),
        name="back",
    )(
        g_part.reshape(shape), m_part.reshape(shape), w_part, resid, branch, cot, weight, x,
        normed.reshape(2, 2, rows, columns), latents, q_normed, kv_normed, q_rows, kv_rows, key_rot, mixed, f_down, f_o, f_q, f_kv, f_g,
        segments[:, None], segments[None, :], valid[None, :], cos_full, sin_full,
    )


def per_device(
    layer_input,
    segment_ids,
    valid_mask,
    cotangent,
    attn_gain,
    q_down,
    q_gain,
    q_up,
    kv_down,
    kv_gain,
    kv_up,
    o_proj,
    mlp_gain,
    w_gate,
    w_up,
    w_down,
):
    length = layer_input.shape[0]
    n_dp = lax.axis_size("dp")
    n_tensor = lax.axis_size("tensor")
    share = length // n_tensor
    me = lax.axis_index("tensor")
    width = w_gate.shape[0]
    slice_ff = w_gate.shape[1] // n_dp
    rows_down = width // n_tensor

    def rows_of(values, count):
        return lax.dynamic_slice_in_dim(values, me * count, count, 0)

    rank_q = q_down.shape[1]
    columns_down = rank_q + kv_down.shape[1]
    pad_down = -columns_down % 128
    down_rows = jnp.concatenate(
        [
            rows_of(q_down, rows_down),
            rows_of(kv_down, rows_down),
            jnp.zeros((rows_down, pad_down), BF),
        ],
        axis=1,
    )
    lanes = -(-width // 128) * 128

    def lane_rows(rows, count, kind):
        padded = [jnp.pad(row.astype(kind), (0, lanes - row.shape[0])) for row in rows]
        return jnp.stack(padded + [jnp.zeros((lanes,), kind)] * (count - len(padded)))

    cot_rows = rows_of(cotangent, share)
    x_rows = rows_of(layer_input, share)
    gains_block = lane_rows([attn_gain, q_gain, kv_gain, mlp_gain], 16, BF)
    cosine, sine_table = rope_tables(length, ROPE)
    cos_full = jnp.concatenate([cosine, cosine], axis=1)
    sin_full = jnp.concatenate([-sine_table, sine_table], axis=1)
    fused = n_dp == 8 and rows_down % 16 == 0 and q_up.shape[0] % 16 == 0
    if fused:
        (
            f_down, f_o, f_q, f_kv, f_g, f_cot, f_w, f_normed,
            normed, latents, q_normed, kv_normed, q_rows, kv_rows, key_rot, mixed,
            resid_rows, attn_rows, _,
        ) = front(
            n_dp, layer_input, x_rows, cot_rows, down_rows, gains_block, q_up, kv_up, o_proj.T,
            w_gate, w_up, w_down, segment_ids, valid_mask, cos_full, sin_full,
        )
    else:
        f_down, f_o, f_q, f_kv, f_g, f_cot = gather_weights(
            n_dp, n_tensor, down_rows, o_proj.T, q_up, kv_up, gains_block, cot_rows
        )
    full_down = f_down.reshape(n_dp * width, columns_down + pad_down)
    full_o = f_o.reshape(n_dp * width, -1)

    def gain_of(row, gain):
        return f_g[:, row, : gain.shape[0]].reshape(-1).astype(F32)

    gain_attn = gain_of(0, attn_gain)
    gain_q = gain_of(1, q_gain)
    gain_kv = gain_of(2, kv_gain)
    gain_mlp = gain_of(3, mlp_gain)
    if not fused:
        packed = jnp.concatenate(
            [
                w_gate.reshape(width, n_dp, slice_ff),
                w_up.reshape(width, n_dp, slice_ff),
                w_down.T.reshape(width, n_dp, slice_ff),
                jnp.zeros((width, n_dp, -3 * slice_ff % 128), BF),
            ],
            axis=2,
        ).transpose(1, 0, 2)
        packed, f_q = lax.optimization_barrier((packed, f_q))
        f_w = swap_dp(packed)
    full_q_up = f_q.reshape(-1, q_up.shape[1])
    full_kv_up = f_kv.reshape(-1, kv_up.shape[1])
    if not fused:
        normed, latents, q_normed, kv_normed, q_rows, kv_rows, key_rot, mixed = attend(
            layer_input, gain_attn, gain_q, gain_kv, full_down, full_q_up, full_kv_up,
            segment_ids, valid_mask, cos_full, sin_full,
        )
        f_normed, resid_rows, attn_rows = attention_residual(
            n_dp, dot_nt(mixed, full_o).astype(BF), x_rows, gain_mlp[None, :]
        )
    mlp_part, normed_part, grad_packed = feed_forward(
        f_normed.reshape(n_dp * length, -1),
        f_cot.reshape(n_dp * length, -1),
        f_w.reshape(n_dp * width, -1),
        slice_ff,
        length,
    )
    weight_rows = rows_of(valid_mask.astype(F32)[:, None], share)
    if fused:
        f_block, grad_input, s_down, s_o, s_q, s_kv, s_small, swapped = back(
            n_dp, normed_part, mlp_part, grad_packed.reshape(n_dp, width, -1), resid_rows, attn_rows,
            cot_rows, weight_rows, layer_input, normed, latents, q_normed, kv_normed, q_rows, kv_rows,
            key_rot, mixed, f_down, f_o, f_q, f_kv, f_g, segment_ids, valid_mask, cos_full, sin_full,
        )
        block_full = f_block.reshape(length, -1)
    else:
        inv_two = inverse_rms(resid_rows)
        unit_two = resid_rows * inv_two
        swapped = swap_dp(grad_packed.reshape(n_dp, width, -1))
        normed_part, grad_packed = lax.optimization_barrier((normed_part, grad_packed))
        f_attn, grad_normed_two, f_block, mlp_rows = residual_grads(
            n_dp, normed_part, mlp_part, resid_rows, cot_rows, gain_mlp[None, :]
        )
        grad_attn = f_attn.reshape(length, -1)
        block_full = f_block.reshape(length, -1)

        grad_mlp_gain = jnp.sum(grad_normed_two * unit_two, axis=0)

        grad_part, grad_o, grad_q_up, grad_kv_up = attend_back(
            grad_attn, mixed, full_o, q_rows, kv_rows, key_rot, q_normed, kv_normed,
            full_q_up, full_kv_up, segment_ids, valid_mask, cos_full, sin_full,
            columns_down + pad_down,
        )
        grad_part, swapped = lax.optimization_barrier((grad_part, swapped))
        grad_latents = sum_latents(n_dp, grad_part).astype(F32)
        stream = layer_input.astype(F32)
        inv_one = inverse_rms(stream)
        unit_one = stream * inv_one
        q_latent = latents[:, :rank_q]
        inv_q = inverse_rms(q_latent)
        unit_q = q_latent * inv_q
        kv_latent = latents[:, rank_q : rank_q + KR]
        inv_kv = inverse_rms(kv_latent)
        unit_kv = kv_latent * inv_kv
        grad_q_normed = grad_latents[:, :rank_q]
        grad_kv_normed = grad_latents[:, rank_q : rank_q + KR]
        grad_kv_rot = grad_latents[:, rank_q + KR : columns_down]
        grad_q_gain = jnp.sum(grad_q_normed * unit_q, axis=0)
        grad_kv_gain = jnp.sum(grad_kv_normed * unit_kv, axis=0)
        grad_down = jnp.concatenate(
            [
                norm_back(grad_q_normed * gain_q, unit_q, inv_q),
                norm_back(grad_kv_normed * gain_kv, unit_kv, inv_kv),
                grad_kv_rot,
                jnp.zeros((length, pad_down), F32),
            ],
            axis=-1,
        ).astype(BF)
        grad_normed = dot_nt(grad_down, full_down)
        grad_attn_gain = jnp.sum(grad_normed * unit_one, axis=0)
        grad_input = grad_attn.astype(F32) * (1.0 / RESIDUAL_SCALE) + norm_back(
            grad_normed * gain_attn, unit_one, inv_one
        )

        quarter = lax.dynamic_index_in_dim(
            normed.reshape(length, n_dp, n_tensor, rows_down), me, 2, keepdims=False
        ).reshape(length, n_dp * rows_down)
        def by_dp(vector):
            return vector.reshape(n_dp, -1)

        def small_rows(vectors):
            return jnp.stack(
                [jnp.pad(by_dp(v), ((0, 0), (0, lanes - v.shape[0] // n_dp))) for v in vectors]
                + [jnp.zeros((n_dp, lanes), F32)] * (8 - len(vectors)),
                axis=1,
            )

        stats = jnp.stack(
            [
                jnp.sum(weight_rows * resid_rows * resid_rows),
                jnp.sum(weight_rows * attn_rows * attn_rows),
                jnp.sum(weight_rows * mlp_rows * mlp_rows),
                jnp.sum(weight_rows),
            ]
        )
        s_down, s_o, s_q, s_kv, s_small = sum_weight_grads(
            n_dp,
            dot_tn(quarter, grad_down).astype(BF),
            grad_o,
            grad_q_up,
            grad_kv_up,
            small_rows([grad_attn_gain, grad_q_gain, grad_kv_gain, grad_mlp_gain]),
            lane_rows([stats], 8, F32),
        )

    def unpack(part):
        return part.transpose(1, 0, 2).reshape(width, n_dp * slice_ff).astype(F32)

    grad_w_gate = unpack(swapped[:, :, :slice_ff])
    grad_w_up = unpack(swapped[:, :, slice_ff : 2 * slice_ff])
    grad_w_down = unpack(swapped[:, :, 2 * slice_ff : 3 * slice_ff]).T

    d_down = s_down.reshape(width, -1).astype(F32)
    gains = s_small[me, 0]
    stat_sums = jnp.sum(s_small[:, 1, 0, :4], axis=0)
    rms_stats = jnp.sqrt(stat_sums[:3] / (stat_sums[3] * D))
    return (
        block_full,
        grad_input,
        gains[0, : attn_gain.shape[0]],
        d_down[:, :rank_q],
        gains[1, : q_gain.shape[0]],
        s_q,
        d_down[:, rank_q:columns_down],
        gains[2, : kv_gain.shape[0]],
        s_kv,
        s_o.T,
        jnp.sum(s_small[:, 0, 3], axis=0)[: mlp_gain.shape[0]],
        grad_w_gate,
        grad_w_up,
        grad_w_down,
        rms_stats,
    )


def solution(mesh):
    placed = (
        P("dp", None),
        P("dp"),
        P("dp"),
        P("dp", None),
        P("dp"),
        P("dp", None),
        P("dp"),
        P("dp", "tensor"),
        P("dp", None),
        P("dp"),
        P("dp", "tensor"),
        P("tensor", "dp"),
        P("dp"),
        P("dp", "tensor"),
        P("dp", "tensor"),
        P("tensor", "dp"),
    )
    return jax.shard_map(
        per_device,
        mesh=mesh,
        in_specs=placed,
        out_specs=(
            P("dp", None),
            P("dp", None),
            P("dp"),
            P("dp", None),
            P("dp"),
            P("dp", "tensor"),
            P("dp", None),
            P("dp"),
            P("dp", "tensor"),
            P("tensor", "dp"),
            P("dp"),
            P("dp", "tensor"),
            P("dp", "tensor"),
            P("tensor", "dp"),
            P(),
        ),
        check_vma=False,
    )
```

```python
import functools
import itertools
import math

import jax
import jax.numpy as jnp
from jax import lax
from jax.experimental import pallas as pl
from jax.experimental.pallas import tpu as pltpu
from jax.sharding import PartitionSpec as P

D = 2560
KR = 256
NOPE = 64
ROPE = 32
VD = 64


NORM_EPS = 1e-05
RESIDUAL_SCALE = 1.4 / math.sqrt(62.0)
ROPE_BASE = 10000.0
NEGATIVE = -1e30


def rope_tables(length, rot_dim):
    half_dim = rot_dim // 2
    position = jnp.arange(length, dtype=jnp.float32)
    frequency = jnp.exp(
        -math.log(ROPE_BASE) * 2.0 * jnp.arange(half_dim, dtype=jnp.float32) / rot_dim
    )
    phases = position[:, None] * frequency[None, :]
    return (jnp.cos(phases), jnp.sin(phases))


def inverse_rms(values):
    return lax.rsqrt(jnp.mean(values * values, axis=-1, keepdims=True) + NORM_EPS)


def norm_back(grad_unit, unit, inv_rms):
    return inv_rms * (grad_unit - unit * jnp.mean(grad_unit * unit, axis=-1, keepdims=True))


BF = jnp.bfloat16
F32 = jnp.float32


def dot(left, right):
    return jnp.dot(left, right, preferred_element_type=F32)


def dot_nt(left, right):
    return jnp.einsum("ac,bc->ab", left, right, preferred_element_type=F32)


def dot_tn(left, right):
    return jnp.einsum("ca,cb->ab", left, right, preferred_element_type=F32)


def swap_dp(blocks):
    return lax.all_to_all(blocks, "dp", 0, 0, tiled=True)


MESH = pl.DeviceIdType.MESH
ANY = pl.BlockSpec(memory_space=pl.ANY)
VMEM = pl.BlockSpec(memory_space=pltpu.VMEM)
VMEM_BYTES = 60 * 1024 * 1024


class Links:
    def __init__(self, n_dp):
        self.n_high = n_dp // 2
        dp = lax.axis_index("dp")
        tensor = lax.axis_index("tensor")
        self.high, self.low = dp // 2, dp % 2
        self.side, self.core = tensor // 2, tensor % 2

    def device(self, high=None, low=None, side=None, core=None):
        high = self.high if high is None else high
        low = self.low if low is None else low
        side = self.side if side is None else side
        core = self.core if core is None else core
        return {"dp": high * 2 + low, "tensor": side * 2 + core}

    def behind(self, step):
        return (self.high + self.n_high - step) % self.n_high

    def ahead(self, step):
        return (self.high + step) % self.n_high

    def over_low(self):
        return self.device(low=1 - self.low)

    def over_side(self):
        return self.device(side=1 - self.side)

    def over_core(self):
        return self.device(core=1 - self.core)

    def meet(self, high=True, low=True, side=True, core=True, swap=False):
        barrier = pltpu.get_barrier_semaphore()
        partners = []
        if swap:
            partners += [
                self.device(high=self.ahead(k), low=1 - self.low) for k in range(1, self.n_high)
            ]
        if high:
            partners += [self.device(high=self.ahead(k)) for k in range(1, self.n_high)]
        if low:
            partners.append(self.over_low())
        if side:
            partners.append(self.over_side())
        if core:
            partners.append(self.over_core())
        for partner in partners:
            pl.semaphore_signal(barrier, inc=1, device_id=partner, device_id_type=MESH)
        pl.semaphore_wait(barrier, len(partners))


class Copies:
    def __init__(self, send, recv, local):
        self.send, self.recv, self.local = send, recv, local
        self.count = self.local_count = 0
        self.started = []
        self.local_started = []

    def go(self, source, target, device):
        copy = pltpu.make_async_remote_copy(
            src_ref=source,
            dst_ref=target,
            send_sem=self.send.at[self.count],
            recv_sem=self.recv.at[self.count],
            device_id=device,
            device_id_type=MESH,
        )
        self.count += 1
        copy.start()
        self.started.append(copy)
        return copy

    def near(self, source, target):
        copy = pltpu.make_async_copy(source, target, self.local.at[self.local_count])
        self.local_count += 1
        copy.start()
        self.local_started.append(copy)
        return copy

    def sent(self, copy):
        copy.wait_send()
        self.started = [other for other in self.started if other is not copy]

    def finish(self):
        for copy in self.started:
            copy.wait_send()


def take_turns(*streams):
    streams = list(streams)
    while streams:
        for stream in list(streams):
            try:
                next(stream)
            except StopIteration:
                streams.remove(stream)


def steps_by_distance(count):
    order, k = [], 1
    while len(order) < count - 1:
        order.append(k)
        if len(order) < count - 1:
            order.append(count - k)
        k += 1
    return order


class EveryGather:
    def __init__(self, links, copies, block, out, cut=None):
        self.links, self.copies, self.block, self.out = links, copies, block, out
        self.columns = out.shape[-1]
        self.cut = self.columns // 256 * 128 if cut is None else cut
        self.order = [0] + steps_by_distance(links.n_high)
        self.arrive, self.over_low, self.over_side = {}, {}, {}
        self.corners = {k: [] for k in self.order}
        self.last = {k: [] for k in self.order}

    def slot(self, high, low, side):
        return self.out.at[high * 2 + low, side * 2 + self.links.core]

    def start(self):
        links = self.links
        mine = self.slot(links.high, links.low, links.side)
        self.own = self.copies.near(self.block, mine)
        for k in self.order[1:]:
            self.arrive[k] = self.copies.go(
                self.block, mine, links.device(high=links.ahead(k))
            )

    def to_core(self, k, source, target):
        self.last[k].append(self.copies.go(source, target, self.links.over_core()))

    def first(self, i):
        links, k = self.links, self.order[i]
        here = self.slot(links.behind(k), links.low, links.side)
        if k:
            self.arrive[k].wait_recv()
        source = here if k else self.block
        self.over_low[k] = self.copies.go(source, here, links.over_low())
        self.over_side[k] = self.copies.go(source, here, links.over_side())
        self.to_core(k, source, here)

    def second(self, i):
        links, k = self.links, self.order[i]
        self.over_low[k].wait_recv()
        here = self.slot(links.behind(k), 1 - links.low, links.side)
        if self.cut:
            half = pl.ds(0, self.cut)
            part = here.at[:, half]
            self.corners[k].append((self.copies.go(part, part, links.over_side()), half))
        self.to_core(k, here, here)
        self.over_side[k].wait_recv()
        here = self.slot(links.behind(k), links.low, 1 - links.side)
        if self.cut < self.columns:
            half = pl.ds(self.cut, self.columns - self.cut)
            part = here.at[:, half]
            self.corners[k].append((self.copies.go(part, part, links.over_low()), half))
        self.to_core(k, here, here)

    def third(self, i):
        links, k = self.links, self.order[i]
        here = self.slot(links.behind(k), 1 - links.low, 1 - links.side)
        for corner, half in self.corners[k]:
            corner.wait_recv()
            part = here.at[:, half]
            self.to_core(k, part, part)

    def fourth(self, i):
        k = self.order[i]
        for copy in self.last[k]:
            copy.wait_recv()
        if k == 0:
            self.own.wait()

    def sent(self):
        copies = [*self.arrive.values(), *self.over_low.values(), *self.over_side.values()]
        copies += [corner for pairs in self.corners.values() for corner, _ in pairs]
        copies += [copy for last in self.last.values() for copy in last]
        for copy in copies:
            self.copies.sent(copy)


def every_gather(links, copies, block, out, cut=None):
    work = EveryGather(links, copies, block, out, cut)
    work.start()
    yield
    for i in range(links.n_high + 2):
        if i < links.n_high:
            work.first(i)
            yield
        if 0 <= i - 1 < links.n_high:
            work.second(i - 1)
            yield
        if 0 <= i - 2:
            work.third(i - 2)
            yield
    for i in range(links.n_high):
        work.fourth(i)


def dp_gather(links, copies, block, out):
    mine = out.at[links.high * 2 + links.low]
    own = copies.near(block, mine)
    arrive, last = {}, []
    for k in steps_by_distance(links.n_high):
        arrive[k] = copies.go(block, mine, links.device(high=links.ahead(k)))
    yield
    last.append(copies.go(block, mine, links.over_low()))
    yield
    for k in steps_by_distance(links.n_high):
        arrive[k].wait_recv()
        here = out.at[links.behind(k) * 2 + links.low]
        last.append(copies.go(here, here, links.over_low()))
        yield
    for copy in last:
        copy.wait_recv()
    own.wait()


def tensor_gather(links, copies, block, out):
    mine = out.at[links.side * 2 + links.core]
    own = copies.near(block, mine)
    last = [copies.go(block, mine, links.over_core())]
    across = copies.go(block, mine, links.over_side())
    yield
    across.wait_recv()
    here = out.at[(1 - links.side) * 2 + links.core]
    last.append(copies.go(here, here, links.over_core()))
    yield
    for copy in last:
        copy.wait_recv()
    own.wait()


class EveryScatter:
    def __init__(self, links, copies, part, bufs, result, cut):
        self.links, self.copies, self.part, self.result = links, copies, part, result
        self.own, self.chip, *bufs = bufs
        self.low_a, self.side_a = (bufs.pop(0), bufs.pop(0)) if cut else (None, None)
        self.side_b, self.low_b, self.done, self.from_high = bufs
        self.cut = cut
        self.half_a, self.half_b = pl.ds(0, cut), pl.ds(cut, part.shape[-1] - cut)
        self.order = steps_by_distance(links.n_high) + [0]
        self.loads, self.core_in, self.a_in, self.b_in = {}, {}, {}, {}
        self.a_last, self.b_last, self.high_in = {}, {}, {}

    def load(self, i):
        there = self.links.ahead(self.order[i])
        self.loads[i] = self.copies.near(
            self.part.at[there, :, :, self.links.core], self.own.at[i % 2]
        )

    def start(self):
        for i, k in enumerate(self.order):
            self.core_in[k] = self.copies.go(
                self.part.at[self.links.ahead(k), :, :, 1 - self.links.core],
                self.chip.at[k],
                self.links.over_core(),
            )
            if i < 2:
                self.load(i)

    def first(self, i):
        links, copies, chip, k = self.links, self.copies, self.chip, self.order[i]
        self.core_in[k].wait_recv()
        self.loads[i].wait()
        for low in range(2):
            for side in range(2):
                chip[k, low, side] = (
                    self.own[i % 2, low, side].astype(F32) + chip[k, low, side].astype(F32)
                ).astype(BF)
        if i + 2 < links.n_high:
            self.load(i + 2)
        if self.cut:
            self.a_in[k] = copies.go(
                chip.at[k, 1 - links.low, :, :, self.half_a], self.low_a.at[k], links.over_low()
            )
        self.b_in[k] = copies.go(
            chip.at[k, :, 1 - links.side, :, self.half_b], self.side_b.at[k], links.over_side()
        )

    def second(self, i):
        links, copies, chip, k = self.links, self.copies, self.chip, self.order[i]
        low_a, side_b = self.low_a, self.side_b
        if self.cut:
            self.a_in[k].wait_recv()
            for side in range(2):
                low_a[k, side] = (
                    low_a[k, side].astype(F32)
                    + chip[k, links.low, side, :, self.half_a].astype(F32)
                ).astype(BF)
            self.a_last[k] = copies.go(
                low_a.at[k, 1 - links.side], self.side_a.at[k], links.over_side()
            )
        self.b_in[k].wait_recv()
        for low in range(2):
            side_b[k, low] = (
                side_b[k, low].astype(F32) + chip[k, low, links.side, :, self.half_b].astype(F32)
            ).astype(BF)
        self.b_last[k] = copies.go(side_b.at[k, 1 - links.low], self.low_b.at[k], links.over_low())

    def third(self, i):
        links, k = self.links, self.order[i]
        if self.cut:
            self.a_last[k].wait_recv()
            self.done[k, :, self.half_a] = (
                self.side_a[k].astype(F32) + self.low_a[k, links.side].astype(F32)
            ).astype(BF)
        self.b_last[k].wait_recv()
        self.done[k, :, self.half_b] = (
            self.low_b[k].astype(F32) + self.side_b[k, links.low].astype(F32)
        ).astype(BF)
        if k:
            self.high_in[k] = self.copies.go(
                self.done.at[k], self.from_high.at[k - 1], links.device(high=links.ahead(k))
            )

    def finish(self):
        total = self.done[0].astype(F32)
        for k in steps_by_distance(self.links.n_high):
            self.high_in[k].wait_recv()
            total = total + self.from_high[k - 1].astype(F32)
        self.result[...] = total


def every_scatter(links, copies, part, bufs, result):
    work = EveryScatter(links, copies, part, bufs, result, part.shape[-1] // 256 * 128)
    work.start()
    yield
    for i in range(links.n_high + 2):
        if i < links.n_high:
            work.first(i)
            yield
        if 0 <= i - 1 < links.n_high:
            work.second(i - 1)
            yield
        if 0 <= i - 2:
            work.third(i - 2)
            yield
    work.finish()


def every_scatter_scratch(n_high, rows, columns, cut=None):
    cut = columns // 256 * 128 if cut is None else cut
    over_low = [
        pltpu.VMEM((n_high, 2, rows, cut), BF),
        pltpu.VMEM((n_high, rows, cut), BF),
    ]
    return [
        pltpu.VMEM((2, 2, 2, rows, columns), BF),
        pltpu.VMEM((n_high, 2, 2, rows, columns), BF),
        *(over_low if cut else []),
        pltpu.VMEM((n_high, 2, rows, columns - cut), BF),
        pltpu.VMEM((n_high, rows, columns - cut), BF),
        pltpu.VMEM((n_high, rows, columns), BF),
        pltpu.VMEM((n_high - 1, rows, columns), BF),
    ]


def dp_scatter(links, copies, part, bufs, result):
    from_low, done, from_high = bufs
    order = steps_by_distance(links.n_high) + [0]
    low_in, high_in = {}, {}
    for k in order:
        low_in[k] = copies.go(
            part.at[links.ahead(k), 1 - links.low], from_low.at[k], links.over_low()
        )
    yield
    for k in order:
        low_in[k].wait_recv()
        done[k] = (
            part[links.ahead(k), links.low].astype(F32) + from_low[k].astype(F32)
        ).astype(BF)
        if k:
            high_in[k] = copies.go(
                done.at[k], from_high.at[k - 1], links.device(high=links.ahead(k))
            )
        yield
    total = done[0].astype(F32)
    for k in steps_by_distance(links.n_high):
        high_in[k].wait_recv()
        total = total + from_high[k - 1].astype(F32)
    result[...] = total.astype(result.dtype)
    yield


def dp_scatter_scratch(n_high, shape):
    return [
        pltpu.VMEM((n_high, *shape), BF),
        pltpu.VMEM((n_high, *shape), BF),
        pltpu.VMEM((n_high - 1, *shape), BF),
    ]


def semaphores(count, local):
    return [
        pltpu.SemaphoreType.DMA((count,)),
        pltpu.SemaphoreType.DMA((count,)),
        pltpu.SemaphoreType.DMA((local,)),
    ]


def params(number, mebibytes=60):
    return pltpu.CompilerParams(
        collective_id=number, has_side_effects=True, vmem_limit_bytes=mebibytes * 1024 * 1024
    )


def count_every_gather(n_high):
    return n_high - 1 + 9 * n_high


def weights_kernel(n_dp, down, o_t, q_up, kv_up, gains, cot, f_down, f_o, f_q, f_kv, f_g, f_cot, send, recv, local):
    links = Links(n_dp)
    copies = Copies(send, recv, local)
    links.meet()
    take_turns(
        every_gather(links, copies, down, f_down),
        dp_gather(links, copies, gains, f_g),
        dp_gather(links, copies, q_up, f_q),
        dp_gather(links, copies, kv_up, f_kv),
        dp_gather(links, copies, o_t, f_o),
        every_gather(links, copies, cot, f_cot),
    )
    copies.finish()


def gather_weights(n_dp, n_tensor, down, o_t, q_up, kv_up, gains, cot):
    n_high = n_dp // 2
    count = 2 * count_every_gather(n_high) + 4 * (2 * n_high - 1)

    def over(block, *lead):
        return jax.ShapeDtypeStruct((*lead, *block.shape), block.dtype)

    return pl.pallas_call(
        functools.partial(weights_kernel, n_dp),
        out_shape=(
            over(down, n_dp, n_tensor),
            over(o_t, n_dp),
            over(q_up, n_dp),
            over(kv_up, n_dp),
            over(gains, n_dp),
            over(cot, n_dp, n_tensor),
        ),
        in_specs=[ANY] * 6,
        out_specs=[ANY] * 6,
        scratch_shapes=semaphores(count, 6),
        compiler_params=params(1),
        name="gather_weights",
    )(down, o_t, q_up, kv_up, gains, cot)


def resid_kernel(n_dp, part, x_rows, gain, full, resid, branch, from_core, out_side, from_side, block, send, recv, local):
    links = Links(n_dp)
    copies = Copies(send, recv, local)
    links.meet()
    arrive = copies.go(part.at[:, 1 - links.core], from_core, links.over_core())
    arrive.wait_recv()
    out_side[...] = (
        part[1 - links.side, links.core].astype(F32) + from_core[1 - links.side].astype(F32)
    ).astype(BF)
    arrive = copies.go(out_side, from_side, links.over_side())
    mine = part[links.side, links.core].astype(F32) + from_core[links.side].astype(F32)
    arrive.wait_recv()
    attn = RESIDUAL_SCALE * (mine + from_side[...].astype(F32))
    stream = x_rows[...].astype(F32) + attn
    branch[...] = attn
    resid[...] = stream
    block[...] = (stream * inverse_rms(stream) * gain[...]).astype(BF)
    take_turns(every_gather(links, copies, block, full))
    copies.finish()


def attention_residual(n_dp, part, x_rows, gain):
    n_tensor = 4
    rows, columns = x_rows.shape
    block = (rows, columns)
    return pl.pallas_call(
        functools.partial(resid_kernel, n_dp),
        out_shape=(
            jax.ShapeDtypeStruct((n_dp, n_tensor, rows, columns), BF),
            jax.ShapeDtypeStruct(block, F32),
            jax.ShapeDtypeStruct(block, F32),
        ),
        in_specs=[VMEM] * 3,
        out_specs=[ANY, VMEM, VMEM],
        scratch_shapes=[
            pltpu.VMEM((2, *block), BF),
            pltpu.VMEM(block, BF),
            pltpu.VMEM(block, BF),
            pltpu.VMEM(block, BF),
            *semaphores(2 + count_every_gather(n_dp // 2), 1),
        ],
        compiler_params=params(2),
        name="attention_residual",
    )(part.reshape(2, 2, rows, columns), x_rows, gain)


def grad_rows_kernel(n_dp, both, *refs):
    links = Links(n_dp)
    copies = Copies(*refs[-3:])
    g_part, resid, cot, gain = refs[:4]
    if both:
        m_part, attn_full, g_rows, block_full, m_rows = refs[4:9]
        scratch = refs[9:-3]
    else:
        attn_full, g_rows = refs[4:6]
        scratch = refs[6:-3]
    links.meet()

    def grad_stream():
        grad_rows = scratch[0]
        yield from every_scatter(links, copies, g_part, scratch[1:9], g_rows)
        stream = resid[...]
        inv = inverse_rms(stream)
        grad = cot[...].astype(F32) + norm_back(g_rows[...] * gain[...], stream * inv, inv)
        grad_rows[...] = (RESIDUAL_SCALE * grad).astype(BF)
        yield from tensor_gather(links, copies, grad_rows, attn_full)

    if both:
        block = block_stream(links, copies, m_part, resid, block_full, m_rows, scratch[9:])
        take_turns(grad_stream(), block)
    else:
        take_turns(grad_stream())
    copies.finish()


def block_stream(links, copies, m_part, resid, block_full, m_rows, scratch):
    block_rows = scratch[0]
    yield from every_scatter(links, copies, m_part, scratch[1:9], m_rows)
    m_rows[...] = RESIDUAL_SCALE * m_rows[...]
    block_rows[...] = resid[...] + m_rows[...]
    yield from tensor_gather(links, copies, block_rows, block_full)


def block_rows_kernel(n_dp, m_part, resid, block_full, m_rows, *rest):
    links = Links(n_dp)
    copies = Copies(*rest[-3:])
    links.meet()
    take_turns(block_stream(links, copies, m_part, resid, block_full, m_rows, rest[:-3]))
    copies.finish()


def residual_grads(n_dp, g_part, m_part, resid, cot, gain):
    n_high = n_dp // 2
    rows, columns = resid.shape
    shape = (n_high, 2, 2, 2, rows, columns)
    g_part, m_part = g_part.reshape(shape), m_part.reshape(shape)
    both = n_high <= 4
    one = jax.ShapeDtypeStruct((rows, columns), F32)
    grad_out = (jax.ShapeDtypeStruct((4, rows, columns), BF), one)
    block_out = (jax.ShapeDtypeStruct((4, rows, columns), F32), one)
    grad_scratch = [
        pltpu.VMEM((rows, columns), BF),
        *every_scatter_scratch(n_high, rows, columns),
    ]
    block_scratch = [
        pltpu.VMEM((rows, columns), F32),
        *every_scatter_scratch(n_high, rows, columns),
    ]
    count, local = 6 * n_high - 1 + 3, n_high + 1
    if both:
        return pl.pallas_call(
            functools.partial(grad_rows_kernel, n_dp, True),
            out_shape=grad_out + block_out,
            in_specs=[ANY, VMEM, VMEM, VMEM, ANY],
            out_specs=[ANY, VMEM, ANY, VMEM],
            scratch_shapes=[*grad_scratch, *block_scratch, *semaphores(2 * count, 2 * local)],
            compiler_params=params(3),
            name="residual_grads",
        )(g_part, resid, cot, gain, m_part)
    grads = pl.pallas_call(
        functools.partial(grad_rows_kernel, n_dp, False),
        out_shape=grad_out,
        in_specs=[ANY, VMEM, VMEM, VMEM],
        out_specs=[ANY, VMEM],
        scratch_shapes=[*grad_scratch, *semaphores(count, local)],
        compiler_params=params(3),
        name="residual_grads",
    )(g_part, resid, cot, gain)
    block = pl.pallas_call(
        functools.partial(block_rows_kernel, n_dp),
        out_shape=block_out,
        in_specs=[ANY, VMEM],
        out_specs=[ANY, VMEM],
        scratch_shapes=[*block_scratch, *semaphores(count, local)],
        compiler_params=params(6),
        name="block_rows",
    )(m_part, resid)
    return (*grads, *block)


def latent_kernel(n_dp, part, full, from_core, half, from_side, send, recv, local):
    links = Links(n_dp)
    copies = Copies(send, recv, local)
    links.meet(high=False, low=False)
    arrive = copies.go(part.at[1 - links.core], from_core, links.over_core())
    arrive.wait_recv()
    half[...] = (part[links.core].astype(F32) + from_core[...].astype(F32)).astype(BF)
    arrive = copies.go(half, from_side, links.over_side())
    arrive.wait_recv()
    full[links.core] = (half[...].astype(F32) + from_side[...].astype(F32)).astype(BF)
    arrive = copies.go(full.at[links.core], full.at[links.core], links.over_core())
    arrive.wait_recv()
    copies.finish()


def sum_latents(n_dp, part):
    rows, columns = part.shape
    half = (rows // 2, columns)
    return pl.pallas_call(
        functools.partial(latent_kernel, n_dp),
        out_shape=jax.ShapeDtypeStruct((2, *half), BF),
        in_specs=[VMEM],
        out_specs=VMEM,
        scratch_shapes=[pltpu.VMEM(half, BF)] * 3 + semaphores(3, 1),
        compiler_params=params(4),
        name="sum_latents",
    )(part.reshape(2, *half)).reshape(rows, columns)


def weight_grads_kernel(n_dp, d_part, o_part, q_part, kv_part, small, stats, d_full, o_sum, q_sum, kv_sum, small_full, *rest):
    d_block, small_block, stats_block = rest[:3]
    bufs = rest[3:15]
    small_in, stats_in = rest[15:17]
    send, recv, local = rest[17:]
    links = Links(n_dp)
    copies = Copies(send, recv, local)
    links.meet()

    def small_stream():
        n_high = links.n_high
        low_in = copies.go(
            small.at[:, 1 - links.low], small_in.at[pl.ds(0, n_high)], links.over_low()
        )
        stats_low = copies.go(stats, stats_in.at[0], links.over_low())
        yield
        low_in.wait_recv()
        stats_low.wait_recv()
        for k in range(n_high):
            small_in[k] = small_in[k] + small[k, links.low]
        stats_block[...] = stats[...] + stats_in[0]
        waits = []
        for k in range(1, n_high):
            there = links.ahead(k)
            waits.append(
                copies.go(
                    small_in.at[there], small_in.at[n_high + k - 1], links.device(high=there)
                )
            )
            waits.append(copies.go(stats_block, stats_in.at[k], links.device(high=there)))
        yield
        for wait in waits:
            wait.wait_recv()
        total = small_in[links.high]
        everything = stats_block[...]
        for k in range(1, n_high):
            total = total + small_in[n_high + k - 1]
            everything = everything + stats_in[k]
        small_block[0] = total
        small_block[1] = everything
        yield from tensor_gather(links, copies, small_block, small_full)

    def down_stream():
        yield from dp_scatter(links, copies, d_part, bufs[:3], d_block)
        yield from tensor_gather(links, copies, d_block, d_full)

    take_turns(
        down_stream(),
        dp_scatter(links, copies, q_part, bufs[6:9], q_sum),
        dp_scatter(links, copies, kv_part, bufs[9:12], kv_sum),
        dp_scatter(links, copies, o_part, bufs[3:6], o_sum),
        small_stream(),
    )
    copies.finish()


def sum_weight_grads(n_dp, down, o_t, q_up, kv_up, small, stats):
    n_high = n_dp // 2

    def parts(array):
        return array.reshape(n_high, 2, array.shape[0] // n_dp, *array.shape[1:])

    down, o_t, q_up, kv_up = parts(down), parts(o_t), parts(q_up), parts(kv_up)
    small = small.reshape(n_high, 2, *small.shape[1:])
    count = 4 * (2 * n_high - 1) + 2 * n_high + 6
    d_shape, o_shape, q_shape, kv_shape = (a.shape[2:] for a in (down, o_t, q_up, kv_up))
    one = stats.shape
    return pl.pallas_call(
        functools.partial(weight_grads_kernel, n_dp),
        out_shape=(
            jax.ShapeDtypeStruct((4, *d_shape), BF),
            jax.ShapeDtypeStruct(o_shape, F32),
            jax.ShapeDtypeStruct(q_shape, F32),
            jax.ShapeDtypeStruct(kv_shape, F32),
            jax.ShapeDtypeStruct((4, 2, *one), F32),
        ),
        in_specs=[VMEM] * 6,
        out_specs=[VMEM] * 5,
        scratch_shapes=[
            pltpu.VMEM(d_shape, BF),
            pltpu.VMEM((2, *one), F32),
            pltpu.VMEM(one, F32),
            *dp_scatter_scratch(n_high, d_shape),
            *dp_scatter_scratch(n_high, o_shape),
            *dp_scatter_scratch(n_high, q_shape),
            *dp_scatter_scratch(n_high, kv_shape),
            pltpu.VMEM((2 * n_high - 1, *one), F32),
            pltpu.VMEM((n_high, *one), F32),
            *semaphores(count, 2),
        ],
        compiler_params=params(5),
        name="sum_weight_grads",
    )(down, o_t, q_up, kv_up, small, stats)


def attention_mask(seg_row, valid_row):
    length = seg_row.shape[1]
    row = lax.broadcasted_iota(jnp.int32, (length, length), 0)
    column = lax.broadcasted_iota(jnp.int32, (length, length), 1)
    segments = jnp.broadcast_to(seg_row[...].astype(F32), (length, length))
    allowed = (
        (segments == segments.T)
        & (column <= row)
        & ((valid_row[...] == 1) | (column == row))
    )
    return jnp.where(allowed, 0.0, NEGATIVE)


def swap_halves(values):
    half = values.shape[1] // 2
    return jnp.concatenate([values[:, half:], values[:, :half]], axis=1)


def turn(values, cos_full, sin_full):
    return values * cos_full + swap_halves(values) * sin_full


def head_probs(query, key, bias, inv_root):
    scores = dot_nt(query, key) * inv_root + bias
    weights = jnp.exp(scores - jnp.max(scores, axis=-1, keepdims=True))
    return weights / jnp.sum(weights, axis=-1, keepdims=True)


def attend_rows(
    x, gain_attn, gain_q, gain_kv, down, q_up, kv_up, bias, cos_full, sin_full,
    normed, latents, q_normed, kv_normed, q_rows, kv_rows, key_rot, mixed,
):
    rank_q = gain_q.shape[1]
    stream = x[...].astype(F32)
    normed[...] = (stream * inverse_rms(stream) * gain_attn).astype(BF)
    latents[...] = dot(normed[...], down)
    q_latent = latents[:, :rank_q]
    q_normed[...] = (q_latent * inverse_rms(q_latent) * gain_q).astype(BF)
    kv_latent = latents[:, rank_q : rank_q + KR]
    kv_normed[...] = (kv_latent * inverse_rms(kv_latent) * gain_kv).astype(BF)
    turned = turn(latents[:, rank_q + KR : rank_q + KR + ROPE], cos_full[...], sin_full[...])
    key_rot[...] = turned.astype(BF)
    kv_rows[...] = dot(kv_normed[...], kv_up).astype(BF)
    q_heads = dot(q_normed[...], q_up)
    inv_root = 1.0 / math.sqrt(NOPE + ROPE)
    for head in range(q_rows.shape[1] // (NOPE + ROPE)):
        base = head * (NOPE + ROPE)
        query = jnp.concatenate(
            [
                q_heads[:, base : base + NOPE],
                turn(
                    q_heads[:, base + NOPE : base + NOPE + ROPE], cos_full[...], sin_full[...]
                ),
            ],
            axis=1,
        ).astype(BF)
        q_rows[:, base : base + NOPE + ROPE] = query
        start = head * (NOPE + VD)
        key = jnp.concatenate([kv_rows[:, start : start + NOPE], key_rot[...]], axis=1)
        value = kv_rows[:, start + NOPE : start + NOPE + VD]
        probs = head_probs(query, key, bias, inv_root).astype(BF)
        mixed[:, head * VD : head * VD + VD] = dot(probs, value).astype(BF)


def attend_kernel(
    x, gain_attn, gain_q, gain_kv, down, q_up, kv_up, seg_row, valid_row, cos_full, sin_full,
    *outs,
):
    attend_rows(
        x, gain_attn[...], gain_q[...], gain_kv[...], down[...], q_up[...], kv_up[...],
        attention_mask(seg_row, valid_row), cos_full, sin_full, *outs,
    )


def attend(x, gain_attn, gain_q, gain_kv, down, q_up, kv_up, segments, valid, cos_full, sin_full):
    length = x.shape[0]
    heads = q_up.shape[1] // (NOPE + ROPE)

    def rows(columns, kind):
        return jax.ShapeDtypeStruct((length, columns), kind)

    return pl.pallas_call(
        attend_kernel,
        out_shape=(
            rows(x.shape[1], BF),
            rows(down.shape[1], F32),
            rows(q_up.shape[0], BF),
            rows(kv_up.shape[0], BF),
            rows(q_up.shape[1], BF),
            rows(kv_up.shape[1], BF),
            rows(ROPE, BF),
            rows(heads * VD, BF),
        ),
        in_specs=[VMEM] * 11,
        out_specs=[VMEM] * 8,
        compiler_params=pltpu.CompilerParams(vmem_limit_bytes=VMEM_BYTES),
        name="attend",
    )(
        x,
        gain_attn[None, :],
        gain_q[None, :],
        gain_kv[None, :],
        down,
        q_up,
        kv_up,
        segments[None, :],
        valid[None, :],
        cos_full,
        sin_full,
    )


def later(stream, turns):
    for _ in range(turns):
        yield
    yield from stream


class Swap:
    def __init__(self, links, copies, blocks, out):
        self.me = links.high * 2 + links.low
        self.copies, self.blocks, self.out = copies, blocks, out
        self.own = copies.near(blocks.at[self.me], out.at[self.me])
        self.arrive = []

    def send(self, steps):
        n_dp = self.blocks.shape[0]
        for k in steps:
            there = (self.me + k) % n_dp
            self.arrive.append(
                self.copies.go(self.blocks.at[there], self.out.at[self.me], {"dp": there})
            )

    def finish(self):
        for copy in self.arrive:
            copy.wait_recv()
        self.own.wait()

    def sent(self):
        for copy in self.arrive:
            self.copies.sent(copy)


def pack_stream(w_gate, w_up, w_down_t, packed):
    n_dp, width, lanes = packed.shape
    slice_ff = w_gate.shape[1] // n_dp
    for k in range(n_dp):
        at = k * slice_ff
        packed[k] = jnp.concatenate(
            [
                w_gate[:, at : at + slice_ff],
                w_up[:, at : at + slice_ff],
                w_down_t[:, at : at + slice_ff],
                jnp.zeros((width, lanes - 3 * slice_ff), BF),
            ],
            axis=1,
        )
        yield


def quarter_of(values, rank):
    rows = values.shape[0] // 4
    mine = values[:rows]
    for other in range(1, 4):
        mine = jnp.where(rank == other, values[other * rows : other * rows + rows], mine)
    return mine


def forward_kernel(
    n_dp, x, cotangent, q_down, kv_down_t, gain_attn, gain_q, gain_kv, gain_mlp, q_up, kv_up, o_t,
    w_gate, w_up, w_down_t, seg_row, valid_row, turns,
    f_down, f_o, f_q, f_kv, f_g, m_part, g_part, w_grads,
    normed, latents, q_normed, kv_normed, q_rows, kv_rows, key_rot, mixed, resid, branch, cot,
    down, gains, packed, f_w, f_cot, f_normed, hidden_all, both_all, m_block, g_block,
    part, from_core, out_side, from_side, block, send, recv, local,
):
    links = Links(n_dp)
    copies = Copies(send, recv, local)
    cos_full, sin_full = turns[:, :ROPE], turns[:, ROPE:]
    rank = links.side * 2 + links.core
    rows_down, rank_q = down.shape[0], q_down.shape[1]
    quarter = pl.ds(pl.multiple_of(rank * rows_down, 16), rows_down)
    down[:, :rank_q] = q_down[quarter, :]
    kv_rows_down = quarter_of(kv_down_t[...].T, rank)
    pad = down.shape[1] - rank_q - kv_rows_down.shape[1]
    down[:, rank_q:] = jnp.concatenate([kv_rows_down, jnp.zeros((rows_down, pad), BF)], axis=1)
    lanes = gains.shape[1]
    gain_rows = [
        jnp.concatenate([g[...].astype(F32), jnp.zeros((1, lanes - g.shape[1]), F32)], axis=1)
        for g in (gain_attn, gain_q, gain_kv, gain_mlp)
    ]
    gains[...] = jnp.concatenate(gain_rows + [jnp.zeros((12, lanes), F32)], axis=0).astype(BF)
    rows = block.shape[0]
    own_rows = pl.ds(pl.multiple_of(rank * rows, 16), rows)
    cot[...] = cotangent[own_rows, :]
    links.meet(swap=True)
    o_stream = dp_gather(links, copies, o_t, f_o)
    take_turns(
        every_gather(links, copies, down, f_down),
        dp_gather(links, copies, gains, f_g),
        dp_gather(links, copies, q_up, f_q),
        dp_gather(links, copies, kv_up, f_kv),
        pack_stream(w_gate, w_up, w_down_t, packed),
        later(itertools.islice(o_stream, 1), 1),
    )

    def gain_of(row, count):
        return jnp.concatenate(
            [f_g[k].astype(F32)[row : row + 1, :count] for k in range(n_dp)], axis=1
        )

    swap = Swap(links, copies, packed, f_w)
    swap.send(range(2, n_dp, 2))
    next(o_stream)
    width = o_t.shape[0]
    full_down = f_down[...].reshape(n_dp * width, down.shape[1])
    full_q = f_q[...].reshape(n_dp * q_up.shape[0], q_up.shape[1])
    full_kv = f_kv[...].reshape(n_dp * kv_up.shape[0], kv_up.shape[1])
    attend_rows(
        x, gain_of(0, width), gain_of(1, q_up.shape[0]), gain_of(2, kv_up.shape[0]),
        full_down, full_q, full_kv, attention_mask(seg_row, valid_row), cos_full, sin_full,
        normed, latents, q_normed, kv_normed, q_rows, kv_rows, key_rot, mixed,
    )
    for _ in range(links.n_high - 1):
        next(o_stream)
    cots = EveryGather(links, copies, cot, f_cot, cot.shape[-1])
    cots.start()
    cots.first(0)
    swap.send(range(1, n_dp, 2))
    take_turns(o_stream)
    full_o = f_o[...].reshape(n_dp * width, o_t.shape[1])
    attn_part = dot_nt(mixed[...], full_o).astype(BF)
    for side in range(2):
        for core in range(2):
            at = (side * 2 + core) * rows
            part[side, core] = attn_part[at : at + rows]
    over = copies.go(part.at[:, 1 - links.core], from_core, links.over_core())
    over.wait_recv()
    out_side[...] = (
        part[1 - links.side, links.core].astype(F32) + from_core[1 - links.side].astype(F32)
    ).astype(BF)
    over = copies.go(out_side, from_side, links.over_side())
    mine = part[links.side, links.core].astype(F32) + from_core[links.side].astype(F32)
    over.wait_recv()
    attn = RESIDUAL_SCALE * (mine + from_side[...].astype(F32))
    stream = x[own_rows, :].astype(F32) + attn
    branch[...] = attn
    resid[...] = stream
    block[...] = (stream * inverse_rms(stream) * gain_of(3, width)).astype(BF)
    normeds = EveryGather(links, copies, block, f_normed)
    normeds.start()
    normeds.first(0)
    n_high = links.n_high
    for i in range(n_high + 2):
        if 1 <= i < n_high:
            cots.first(i)
        if 0 <= i - 1 < n_high:
            cots.second(i - 1)
        if 0 <= i - 2:
            cots.third(i - 2)
    normeds.second(0)
    for i in range(n_high):
        cots.fourth(i)
    swap.finish()
    cots.sent()
    normeds.third(0)
    normeds.fourth(0)

    lanes = f_w.shape[2]
    slice_ff = w_gate.shape[1] // n_dp
    wide = both_all.shape[1]
    cut = lanes - hidden_all.shape[1]
    before = 2 * slice_ff - cut
    columns = x.shape[1]
    tokens = 2 * x.shape[0]
    stores = []

    def zeros(count):
        return jnp.zeros((tokens, count), F32)

    def feed_forward_of(high):
        pair = pl.ds(high * 2, 2)
        at = pl.ds(pl.multiple_of(high * tokens, 128), tokens)
        w_in = f_w[:, :, :wide].reshape(columns, wide)
        w_out = f_w[:, :, cut:].reshape(columns, lanes - cut)
        grad_mlp = (RESIDUAL_SCALE * f_cot[pair].astype(F32)).astype(BF)
        f_cot[pair] = grad_mlp
        both = dot(f_normed[pair].reshape(tokens, columns), w_in)
        gate, upper = both[:, :slice_ff], both[:, slice_ff : 2 * slice_ff]
        sigma = jax.nn.sigmoid(gate)
        swish = gate * sigma
        after = lanes - cut - before - slice_ff
        hidden = jnp.concatenate([zeros(before), swish * upper, zeros(after)], axis=1).astype(BF)
        grad_hidden = dot(grad_mlp.reshape(tokens, columns), w_out)[:, before : before + slice_ff]
        grad_both = jnp.concatenate(
            [
                grad_hidden * upper * (sigma * (1.0 + gate * (1.0 - sigma))),
                grad_hidden * swish,
                zeros(wide - 2 * slice_ff),
            ],
            axis=1,
        ).astype(BF)
        hidden_all[at, :] = hidden
        both_all[at, :] = grad_both
        while stores:
            stores.pop().wait()
        m_block[...] = dot_nt(hidden, w_out).astype(BF).reshape(m_block.shape)
        stores.append(copies.near(m_block, m_part.at[pair]))
        g_block[...] = dot_nt(grad_both, w_in).astype(BF).reshape(g_block.shape)
        stores.append(copies.near(g_block, g_part.at[pair]))

    for i in range(1, n_high):
        normeds.first(i)
        if i == 1:
            feed_forward_of(links.behind(normeds.order[0]))
        normeds.second(i)
        normeds.third(i)
        if i > 1:
            feed_forward_of(links.behind(normeds.order[i - 1]))
        normeds.fourth(i)
    feed_forward_of(links.behind(normeds.order[n_high - 1]))
    swap.sent()
    all_tokens = n_dp * x.shape[0]
    for k in range(n_dp):
        at = k * width
        slab_in = dot_tn(
            f_normed[:, :, :, at : at + width].reshape(all_tokens, width), both_all[...]
        )
        slab_out = dot_tn(
            f_cot[:, :, :, at : at + width].reshape(all_tokens, width), hidden_all[...]
        )
        packed[k, :, :cut] = slab_in[:, :cut].astype(BF)
        packed[k, :, cut:wide] = (slab_in[:, cut:] + slab_out[:, : wide - cut]).astype(BF)
        packed[k, :, wide:] = slab_out[:, wide - cut :].astype(BF)
        stores.append(copies.near(packed.at[k], w_grads.at[k]))
    while stores:
        stores.pop().wait()
    copies.finish()


def forward(
    n_dp, x, cotangent, q_down, kv_down_t, gains, q_up, kv_up, o_t, w_gate, w_up, w_down_t,
    segments, valid, turns, down_shape, gain_lanes,
):
    n_high = n_dp // 2
    length, columns = x.shape
    rows = length // 4
    slice_ff = w_gate.shape[1] // n_dp
    lanes = -(-3 * slice_ff // 128) * 128
    wide = -(-2 * slice_ff // 128) * 128
    cut = 2 * slice_ff // 128 * 128
    heads = q_up.shape[1] // (NOPE + ROPE)
    count = 3 * count_every_gather(n_high) + 4 * (2 * n_high - 1) + n_dp + 1
    block = (rows, columns)

    def over(block, *lead, kind=BF):
        return jax.ShapeDtypeStruct((*lead, *block), kind)

    return pl.pallas_call(
        functools.partial(forward_kernel, n_dp),
        out_shape=(
            over(down_shape, n_dp, 4),
            over(o_t.shape, n_dp),
            over(q_up.shape, n_dp),
            over(kv_up.shape, n_dp),
            over((16, gain_lanes), n_dp),
            over(block, n_dp, 4),
            over(block, n_dp, 4),
            over((w_gate.shape[0], lanes), n_dp),
            over((columns,), length),
            over((down_shape[1],), length, kind=F32),
            over((q_up.shape[0] * n_dp,), length),
            over((kv_up.shape[0] * n_dp,), length),
            over((q_up.shape[1],), length),
            over((kv_up.shape[1],), length),
            over((ROPE,), length),
            over((heads * VD,), length),
            over(block, kind=F32),
            over(block, kind=F32),
            over(block),
        ),
        in_specs=[VMEM] * 17,
        out_specs=[VMEM] * 5 + [ANY] * 3 + [VMEM] * 11,
        scratch_shapes=[
            pltpu.VMEM(down_shape, BF),
            pltpu.VMEM((16, gain_lanes), BF),
            pltpu.VMEM((n_dp, w_gate.shape[0], lanes), BF),
            pltpu.VMEM((n_dp, w_gate.shape[0], lanes), BF),
            pltpu.VMEM((n_dp, 4, *block), BF),
            pltpu.VMEM((n_dp, 4, *block), BF),
            pltpu.VMEM((n_dp * length, lanes - cut), BF),
            pltpu.VMEM((n_dp * length, wide), BF),
            pltpu.VMEM((2, 4, *block), BF),
            pltpu.VMEM((2, 4, *block), BF),
            pltpu.VMEM((2, 2, *block), BF),
            pltpu.VMEM((2, *block), BF),
            pltpu.VMEM(block, BF),
            pltpu.VMEM(block, BF),
            pltpu.VMEM(block, BF),
            *semaphores(count, 8 + 2 * n_high + n_dp),
        ],
        compiler_params=params(7, 62),
        name="forward",
    )(
        x, cotangent, q_down, kv_down_t, *(g[None, :] for g in gains), q_up, kv_up, o_t,
        w_gate, w_up, w_down_t, segments[None, :], valid[None, :], turns,
    )


def feed_forward_kernel(slice_ff, normed, cot, weights, m_part, g_part, grads, sum_in, sum_out):
    step = pl.program_id(0)
    cut = slice_ff * 2 // 128 * 128
    pad = slice_ff * 2 - cut
    w_in, w_out = weights[:, : sum_in.shape[0]], weights[:, cut:]
    rows = normed.shape[0]
    both = dot(normed[...], w_in)
    gate, upper = both[:, :slice_ff], both[:, slice_ff : 2 * slice_ff]
    sigma = jax.nn.sigmoid(gate)
    swish = gate * sigma

    def zeros(count):
        return jnp.zeros((rows, count), F32)

    def placed(hidden):
        rest = w_out.shape[1] - pad - slice_ff
        return jnp.concatenate([zeros(pad), hidden, zeros(rest)], axis=1).astype(BF)

    hidden = placed(swish * upper)
    m_part[...] = dot_nt(hidden, w_out).astype(BF)
    grad_mlp = (RESIDUAL_SCALE * cot[...].astype(F32)).astype(BF)
    grad_hidden = dot(grad_mlp, w_out)[:, pad : pad + slice_ff]
    grad_both = jnp.concatenate(
        [
            grad_hidden * upper * (sigma * (1.0 + gate * (1.0 - sigma))),
            grad_hidden * swish,
            zeros(w_in.shape[1] - 2 * slice_ff),
        ],
        axis=1,
    ).astype(BF)
    g_part[...] = dot_nt(grad_both, w_in).astype(BF)

    @pl.when(step == 0)
    def _():
        sum_in[...] = dot_tn(grad_both, normed[...])
        sum_out[...] = dot_tn(hidden, grad_mlp)

    @pl.when(step > 0)
    def _():
        sum_in[...] += dot_tn(grad_both, normed[...])
        sum_out[...] += dot_tn(hidden, grad_mlp)

    @pl.when(step == pl.num_programs(0) - 1)
    def _():
        mid = sum_in.shape[0]
        if cut:
            grads[:, :cut] = sum_in[:cut].T.astype(BF)
        grads[:, cut:mid] = (sum_in[cut:] + sum_out[: mid - cut]).T.astype(BF)
        grads[:, mid:] = sum_out[mid - cut :].T.astype(BF)


def feed_forward(normed, cot, weights, slice_ff, rows):
    tokens, columns = normed.shape
    lanes = weights.shape[1]
    cut = slice_ff * 2 // 128 * 128
    wide = -(-slice_ff * 2 // 128) * 128
    token_block = pl.BlockSpec((rows, columns), lambda i: (i, 0))
    whole = pl.BlockSpec((columns, lanes), lambda i: (0, 0))
    part = jax.ShapeDtypeStruct((tokens, columns), BF)
    return pl.pallas_call(
        functools.partial(feed_forward_kernel, slice_ff),
        grid=(tokens // rows,),
        out_shape=(part, part, jax.ShapeDtypeStruct((columns, lanes), BF)),
        in_specs=[token_block, token_block, whole],
        out_specs=[token_block, token_block, whole],
        scratch_shapes=[
            pltpu.VMEM((wide, columns), F32),
            pltpu.VMEM((lanes - cut, columns), F32),
        ],
        compiler_params=pltpu.CompilerParams(vmem_limit_bytes=VMEM_BYTES),
        name="feed_forward",
    )(normed, cot, weights)


def attend_back_kernel(
    grad_attn, mixed, o_t, q_rows, kv_rows, key_rot, q_normed, kv_normed, q_up, kv_up,
    seg_row, valid_row, cos_full, sin_full,
    grad_latents, grad_o, grad_q_up, grad_kv_up, grad_q, grad_kv,
):
    rank_q = q_up.shape[0]
    grad_o[...] = dot_tn(grad_attn[...], mixed[...]).astype(BF)
    grad_mixed = dot(grad_attn[...], o_t[...]).astype(BF)
    bias = attention_mask(seg_row, valid_row)
    inv_root = 1.0 / math.sqrt(NOPE + ROPE)
    grad_rot = jnp.zeros((grad_attn.shape[0], ROPE), F32)
    for head in range(q_rows.shape[1] // (NOPE + ROPE)):
        base = head * (NOPE + ROPE)
        start = head * (NOPE + VD)
        query = q_rows[:, base : base + NOPE + ROPE]
        key = jnp.concatenate([kv_rows[:, start : start + NOPE], key_rot[...]], axis=1)
        value = kv_rows[:, start + NOPE : start + NOPE + VD]
        grad = grad_mixed[:, head * VD : head * VD + VD]
        probs = head_probs(query, key, bias, inv_root)
        grad_value = dot_tn(probs.astype(BF), grad)
        grad_probs = dot_nt(grad, value)
        inner = jnp.sum(probs * grad_probs, axis=-1, keepdims=True)
        grad_scores = (probs * (grad_probs - inner)).astype(BF)
        grad_query = dot(grad_scores, key) * inv_root
        grad_key = dot_tn(grad_scores, query) * inv_root
        grad_q[:, base : base + NOPE + ROPE] = jnp.concatenate(
            [grad_query[:, :NOPE], turn(grad_query[:, NOPE:], cos_full[...], -sin_full[...])],
            axis=1,
        ).astype(BF)
        grad_kv[:, start : start + NOPE + VD] = jnp.concatenate(
            [grad_key[:, :NOPE], grad_value], axis=1
        ).astype(BF)
        grad_rot = grad_rot + grad_key[:, NOPE:]
    grad_latents[...] = jnp.zeros_like(grad_latents)
    grad_latents[:, :rank_q] = dot_nt(grad_q[...], q_up[...]).astype(BF)
    grad_latents[:, rank_q : rank_q + KR] = dot_nt(grad_kv[...], kv_up[...]).astype(BF)
    grad_latents[:, rank_q + KR : rank_q + KR + ROPE] = turn(
        grad_rot, cos_full[...], -sin_full[...]
    ).astype(BF)
    grad_q_up[...] = dot_tn(q_normed[...], grad_q[...]).astype(BF)
    grad_kv_up[...] = dot_tn(kv_normed[...], grad_kv[...]).astype(BF)


def attend_back(
    grad_attn, mixed, o_t, q_rows, kv_rows, key_rot, q_normed, kv_normed, q_up, kv_up,
    segments, valid, cos_full, sin_full, columns_down,
):
    length = grad_attn.shape[0]

    def out(shape):
        return jax.ShapeDtypeStruct(shape, BF)

    return pl.pallas_call(
        attend_back_kernel,
        out_shape=(
            out((length, columns_down)),
            out(o_t.shape),
            out(q_up.shape),
            out(kv_up.shape),
        ),
        in_specs=[VMEM] * 14,
        out_specs=[VMEM] * 4,
        scratch_shapes=[pltpu.VMEM(q_rows.shape, BF), pltpu.VMEM(kv_rows.shape, BF)],
        compiler_params=pltpu.CompilerParams(vmem_limit_bytes=VMEM_BYTES),
        name="attend_back",
    )(
        grad_attn, mixed, o_t, q_rows, kv_rows, key_rot, q_normed, kv_normed, q_up, kv_up,
        segments[None, :], valid[None, :], cos_full, sin_full,
    )


class ScatterInto:
    def __init__(self, links, copies, bufs, result):
        self.links, self.copies, self.result = links, copies, result
        self.part, self.from_low, self.from_high = bufs
        self.order = steps_by_distance(links.n_high) + [0]
        self.low_in, self.high_in = {}, {}

    def start(self):
        for k in self.order:
            self.low_in[k] = self.copies.go(
                self.part.at[self.links.ahead(k), 1 - self.links.low],
                self.from_low.at[k],
                self.links.over_low(),
            )

    def steps(self):
        links, part = self.links, self.part
        for k in self.order:
            there = links.ahead(k)
            self.low_in[k].wait_recv()
            part[there, links.low] = (
                part[there, links.low].astype(F32) + self.from_low[k].astype(F32)
            ).astype(BF)
            if k:
                self.high_in[k] = self.copies.go(
                    part.at[there, links.low], self.from_high.at[k - 1], links.device(high=there)
                )

    def finish(self):
        total = self.part[self.links.high, self.links.low].astype(F32)
        for k in steps_by_distance(self.links.n_high):
            self.high_in[k].wait_recv()
            total = total + self.from_high[k - 1].astype(F32)
        self.result[...] = total.astype(self.result.dtype)


def scatter_into_scratch(n_high, shape):
    return [
        pltpu.VMEM((n_high, 2, *shape), BF),
        pltpu.VMEM((n_high, *shape), BF),
        pltpu.VMEM((n_high - 1, *shape), BF),
    ]


def small_stream(links, copies, small, small_in, stats, stats_in, stats_block, small_block, small_full):
    n_high = links.n_high
    low_in = copies.go(
        small.at[:, 1 - links.low], small_in.at[pl.ds(0, n_high)], links.over_low()
    )
    stats_low = copies.go(stats, stats_in.at[0], links.over_low())
    yield
    low_in.wait_recv()
    stats_low.wait_recv()
    for k in range(n_high):
        small_in[k] = small_in[k] + small[k, links.low]
    stats_block[...] = stats[...] + stats_in[0]
    waits = []
    for k in range(1, n_high):
        there = links.ahead(k)
        waits.append(
            copies.go(small_in.at[there], small_in.at[n_high + k - 1], links.device(high=there))
        )
        waits.append(copies.go(stats_block, stats_in.at[k], links.device(high=there)))
    yield
    for wait in waits:
        wait.wait_recv()
    total = small_in[links.high]
    everything = stats_block[...]
    for k in range(1, n_high):
        total = total + small_in[n_high + k - 1]
        everything = everything + stats_in[k]
    small_block[0] = total
    small_block[1] = everything
    yield from tensor_gather(links, copies, small_block, small_full)


def back_kernel(
    n_dp, g_part, m_part, w_part, resid, branch, cot, x, normed, latents, q_normed, kv_normed,
    q_rows, kv_rows, key_rot, mixed, f_down, f_o, f_q, f_kv, f_g, seg_row, valid_row,
    turns,
    block_full, grad_input, d_full, o_sum, q_sum, kv_sum, small_full, w_full,
    attn_full, grad_rows, g_rows, m_rows, grad_q, grad_kv, lat, lat_in, lat_half, lat_side,
    lat_full, d_block, small, small_in, stats, stats_in, stats_block, small_block, *rest,
):
    g_bufs, m_bufs = rest[:8], (rest[0], *rest[8:13])
    d_bufs, o_bufs, q_bufs, kv_bufs = rest[13:16], rest[16:19], rest[19:22], rest[22:25]
    links = Links(n_dp)
    copies = Copies(*rest[25:])
    links.meet(swap=True)
    cos_full, sin_full = turns[:, :ROPE], turns[:, ROPE:]
    length = x.shape[0]
    rank_q, rank_kv = q_normed.shape[1], kv_normed.shape[1]
    width = o_sum.shape[0]

    def gain_of(row, count):
        return jnp.concatenate(
            [f_g[k].astype(F32)[row : row + 1, :count] for k in range(n_dp)], axis=1
        )

    half_columns = x.shape[1] // 256 * 128
    g = EveryScatter(links, copies, g_part, g_bufs, g_rows, half_columns)
    m = EveryScatter(links, copies, m_part, m_bufs, m_rows, 0)
    swap = Swap(links, copies, w_part, w_full)
    high = range(links.n_high)
    g.start()
    swap.send(range(2, n_dp, 2))
    for i in range(links.n_high + 1):
        if i in high:
            g.first(i)
        if i - 1 in high:
            g.second(i - 1)
        if i - 2 in high:
            g.third(i - 2)
    m.start()
    swap.send(range(1, n_dp, 2))
    g.third(links.n_high - 1)
    m.first(0)
    m.first(1)
    g.finish()
    stream = resid[...]
    inv_two = inverse_rms(stream)
    unit_two = stream * inv_two
    gain_mlp = gain_of(3, width)
    grad = cot[...].astype(F32) + norm_back(g_rows[...] * gain_mlp, unit_two, inv_two)
    grad_rows[...] = (RESIDUAL_SCALE * grad).astype(BF)
    t_stream = tensor_gather(links, copies, grad_rows, attn_full)
    next(t_stream)
    m.first(2)
    m.first(3)
    mlp_gain = jnp.sum(g_rows[...] * unit_two, axis=0, keepdims=True)
    bias = attention_mask(seg_row, valid_row)
    for _ in t_stream:
        pass

    grad_attn = attn_full[...].reshape(length, x.shape[1])
    for k in range(n_dp):
        o_bufs[0][k // 2, k % 2] = dot_tn(
            grad_attn[:, k * width : k * width + width], mixed[...]
        ).astype(BF)
    o = ScatterInto(links, copies, o_bufs, o_sum)
    o.start()

    grad_mixed = dot(grad_attn, f_o[...].reshape(n_dp * width, mixed.shape[1])).astype(BF)
    inv_root = 1.0 / math.sqrt(NOPE + ROPE)
    grad_rot = jnp.zeros((length, ROPE), F32)
    for head in range(q_rows.shape[1] // (NOPE + ROPE)):
        base = head * (NOPE + ROPE)
        start = head * (NOPE + VD)
        query = q_rows[:, base : base + NOPE + ROPE]
        key = jnp.concatenate([kv_rows[:, start : start + NOPE], key_rot[...]], axis=1)
        value = kv_rows[:, start + NOPE : start + NOPE + VD]
        grad_head = grad_mixed[:, head * VD : head * VD + VD]
        probs = head_probs(query, key, bias, inv_root)
        grad_value = dot_tn(probs.astype(BF), grad_head)
        grad_probs = dot_nt(grad_head, value)
        inner = jnp.sum(probs * grad_probs, axis=-1, keepdims=True)
        grad_scores = (probs * (grad_probs - inner)).astype(BF)
        grad_query = dot(grad_scores, key) * inv_root
        grad_key = dot_tn(grad_scores, query) * inv_root
        grad_q[:, base : base + NOPE + ROPE] = jnp.concatenate(
            [grad_query[:, :NOPE], turn(grad_query[:, NOPE:], cos_full[...], -sin_full[...])],
            axis=1,
        ).astype(BF)
        grad_kv[:, start : start + NOPE + VD] = jnp.concatenate(
            [grad_key[:, :NOPE], grad_value], axis=1
        ).astype(BF)
        grad_rot = grad_rot + grad_key[:, NOPE:]

    half = length // 2
    lat[...] = jnp.zeros_like(lat)
    full_q = f_q[...].reshape(rank_q, q_rows.shape[1])
    full_kv = f_kv[...].reshape(rank_kv, kv_rows.shape[1])
    grad_turned = turn(grad_rot, cos_full[...], -sin_full[...]).astype(BF)
    for core in range(2):
        at = core * half
        lat[core, :, :rank_q] = dot_nt(grad_q[at : at + half], full_q).astype(BF)
        lat[core, :, rank_q : rank_q + rank_kv] = dot_nt(
            grad_kv[at : at + half], full_kv
        ).astype(BF)
        lat[core, :, rank_q + rank_kv : rank_q + rank_kv + ROPE] = grad_turned[at : at + half]
    over = copies.go(lat.at[1 - links.core], lat_in, links.over_core())
    rows_q = q_sum.shape[0]
    for k in range(n_dp):
        q_bufs[0][k // 2, k % 2] = dot_tn(
            q_normed[:, k * rows_q : k * rows_q + rows_q], grad_q[...]
        ).astype(BF)
    q = ScatterInto(links, copies, q_bufs, q_sum)
    q.start()
    over.wait_recv()
    lat_half[...] = (lat[links.core].astype(F32) + lat_in[...].astype(F32)).astype(BF)
    over = copies.go(lat_half, lat_side, links.over_side())
    rows_kv = kv_sum.shape[0]
    for k in range(n_dp):
        kv_bufs[0][k // 2, k % 2] = dot_tn(
            kv_normed[:, k * rows_kv : k * rows_kv + rows_kv], grad_kv[...]
        ).astype(BF)
    kv = ScatterInto(links, copies, kv_bufs, kv_sum)
    kv.start()
    over.wait_recv()
    lat_full[links.core] = (lat_half[...].astype(F32) + lat_side[...].astype(F32)).astype(BF)
    mine = lat_full.at[links.core]
    over = copies.go(mine, mine, links.over_core())
    q_latent = latents[:, :rank_q]
    inv_q = inverse_rms(q_latent)
    unit_q = q_latent * inv_q
    kv_latent = latents[:, rank_q : rank_q + rank_kv]
    inv_kv = inverse_rms(kv_latent)
    unit_kv = kv_latent * inv_kv
    over.wait_recv()
    lat_sum = lat_full[...].reshape(length, lat.shape[2]).astype(F32)
    grad_q_latent, grad_kv_latent = lat_sum[:, :rank_q], lat_sum[:, rank_q : rank_q + rank_kv]
    q_gain = jnp.sum(grad_q_latent * unit_q, axis=0, keepdims=True)
    kv_gain = jnp.sum(grad_kv_latent * unit_kv, axis=0, keepdims=True)
    grad_down = jnp.concatenate(
        [
            norm_back(grad_q_latent * gain_of(1, rows_q), unit_q, inv_q),
            norm_back(grad_kv_latent * gain_of(2, rows_kv), unit_kv, inv_kv),
            lat_sum[:, rank_q + rank_kv :],
        ],
        axis=1,
    ).astype(BF)

    rows_down = d_block.shape[0]
    m.second(0)
    m.second(1)
    copies.near(normed, g_bufs[0].at[0]).wait()
    normed_rows = g_bufs[0][0].reshape(length, x.shape[1])
    rank = links.side * 2 + links.core
    for k in range(n_dp):
        rows_all = dot_tn(normed_rows[:, k * width : k * width + width], grad_down)
        d_bufs[0][k // 2, k % 2] = quarter_of(rows_all, rank).astype(BF)

    d = ScatterInto(links, copies, d_bufs, d_block)
    d.start()
    o.steps()
    m.second(2)
    m.second(3)
    grad_input[...] = dot_nt(grad_down, f_down[...].reshape(n_dp * width, grad_down.shape[1]))
    q.steps()
    kv.steps()
    for i in high:
        m.third(i)
    d.steps()
    m.finish()
    mlp = RESIDUAL_SCALE * m_rows[...]
    g_rows[...] = resid[...] + mlp
    block_gather = tensor_gather(links, copies, g_rows, block_full)
    next(block_gather)
    valid = jnp.broadcast_to((valid_row[...] == 1).astype(F32), (length, length)).T
    weights = quarter_of(valid, rank)[:, :1]
    lane = lax.broadcasted_iota(jnp.int32, stats.shape, 1)
    sums = [
        jnp.sum(jnp.sum(weights * rows * rows, axis=1, keepdims=True), axis=0, keepdims=True)
        for rows in (resid[...], branch[...], mlp)
    ] + [jnp.sum(weights, axis=0, keepdims=True)]
    packed = jnp.zeros(stats.shape, F32)
    for index, value in enumerate(sums):
        packed = jnp.where(lane == index, value, packed)
    stats[...] = packed
    stream = x[...].astype(F32)
    inv_one = inverse_rms(stream)
    unit_one = stream * inv_one
    attn_gain = jnp.sum(grad_input[...] * unit_one, axis=0, keepdims=True)
    grad_input[...] = grad_attn.astype(F32) * (1.0 / RESIDUAL_SCALE) + norm_back(
        grad_input[...] * gain_of(0, width), unit_one, inv_one
    )

    def piece(vector, k):
        count = vector.shape[1] // n_dp
        cut = vector[:, k * count : k * count + count]
        return jnp.concatenate([cut, jnp.zeros((1, small.shape[3] - count), F32)], axis=1)

    for k in range(n_dp):
        small[k // 2, k % 2] = jnp.concatenate(
            [piece(v, k) for v in (attn_gain, q_gain, kv_gain, mlp_gain)]
            + [jnp.zeros((4, small.shape[3]), F32)],
            axis=0,
        )
    small_rows = small_stream(
        links, copies, small, small_in, stats, stats_in, stats_block, small_block, small_full
    )
    next(small_rows)
    d.finish()
    down_gather = tensor_gather(links, copies, d_block, d_full)
    take_turns(small_rows, down_gather, block_gather)
    o.finish()
    q.finish()
    kv.finish()
    swap.finish()
    copies.finish()


def back(
    n_dp, g_part, m_part, w_part, resid, branch, cot, x, normed, latents, q_normed, kv_normed,
    q_rows, kv_rows, key_rot, mixed, f_down, f_o, f_q, f_kv, f_g, segments, valid, turns,
):
    n_high = n_dp // 2
    rows, columns = resid.shape
    length = x.shape[0]
    lanes = f_g.shape[2]
    half = (length // 2, latents.shape[1])
    shape = (n_high, 2, 2, 2, rows, columns)
    d_shape, o_shape, q_shape, kv_shape = f_down.shape[2:], f_o.shape[1:], f_q.shape[1:], f_kv.shape[1:]
    one = (8, lanes)
    count = 2 * (6 * n_high - 1) + 4 * (2 * n_high - 1) + 4 * 3 + (n_dp - 1) + 2 * n_high + 3

    def out(shape, kind=F32):
        return jax.ShapeDtypeStruct(shape, kind)

    return pl.pallas_call(
        functools.partial(back_kernel, n_dp),
        out_shape=(
            out((4, rows, columns)),
            out((length, columns)),
            out((4, *d_shape), BF),
            out(o_shape),
            out(q_shape),
            out(kv_shape),
            out((4, 2, *one)),
            out(w_part.shape, BF),
        ),
        in_specs=[ANY] * 3 + [VMEM] * 4 + [ANY] + [VMEM] * 15,
        out_specs=[ANY] + [VMEM] * 6 + [ANY],
        scratch_shapes=[
            pltpu.VMEM((4, rows, columns), BF),
            pltpu.VMEM((rows, columns), BF),
            pltpu.VMEM((rows, columns), F32),
            pltpu.VMEM((rows, columns), F32),
            pltpu.VMEM(q_rows.shape, BF),
            pltpu.VMEM(kv_rows.shape, BF),
            pltpu.VMEM((2, *half), BF),
            pltpu.VMEM(half, BF),
            pltpu.VMEM(half, BF),
            pltpu.VMEM(half, BF),
            pltpu.VMEM((2, *half), BF),
            pltpu.VMEM(d_shape, BF),
            pltpu.VMEM((n_high, 2, *one), F32),
            pltpu.VMEM((2 * n_high - 1, *one), F32),
            pltpu.VMEM(one, F32),
            pltpu.VMEM((n_high, *one), F32),
            pltpu.VMEM(one, F32),
            pltpu.VMEM((2, *one), F32),
            *every_scatter_scratch(n_high, rows, columns),
            *every_scatter_scratch(n_high, rows, columns, 0)[1:],
            *scatter_into_scratch(n_high, d_shape),
            *scatter_into_scratch(n_high, o_shape),
            *scatter_into_scratch(n_high, q_shape),
            *scatter_into_scratch(n_high, kv_shape),
            *semaphores(count, 2 * n_high + 6),
        ],
        compiler_params=params(8, 62),
        name="back",
    )(
        g_part.reshape(shape), m_part.reshape(shape), w_part, resid, branch, cot, x,
        normed.reshape(2, 2, rows, columns), latents, q_normed, kv_normed, q_rows, kv_rows, key_rot, mixed, f_down, f_o, f_q, f_kv, f_g,
        segments[None, :], valid[None, :], turns,
    )


def unpack_kernel(
    slice_ff, rank_q, swapped, down, o_in, q_in, kv_in, block_in, input_in, small,
    grad_gate, grad_upper, grad_down_t, grad_o_t, grad_q_down, grad_kv_down_t, grad_q_up, grad_kv_up,
    block_out, grad_input,
    attn_gain, q_gain, kv_gain, mlp_gain, stats,
):
    n_dp = swapped.shape[0]

    def pieces(start):
        return jnp.concatenate(
            [swapped[k, :, start : start + slice_ff] for k in range(n_dp)], axis=1
        ).astype(F32)

    grad_gate[...] = pieces(0)
    grad_upper[...] = pieces(slice_ff)
    grad_down_t[...] = pieces(2 * slice_ff)
    for target, source in (
        (grad_o_t, o_in), (grad_q_up, q_in), (grad_kv_up, kv_in), (block_out, block_in), (grad_input, input_in),
    ):
        target[...] = source[...]
    rows = down[...].reshape(grad_q_down.shape[0], down.shape[2]).astype(F32)
    grad_q_down[...] = rows[:, :rank_q]
    grad_kv_down_t[...] = rows[:, rank_q : rank_q + grad_kv_down_t.shape[0]].T
    gains = small[0, 0]
    for row, gain in ((0, attn_gain), (1, q_gain), (2, kv_gain)):
        gain[...] = gains[row : row + 1, : gain.shape[1]]
    total = small[0, 0] + small[1, 0] + small[2, 0] + small[3, 0]
    mlp_gain[...] = total[3:4, : mlp_gain.shape[1]]
    sums = (small[0, 1] + small[1, 1] + small[2, 1] + small[3, 1])[0:1]
    stats[...] = jnp.sqrt(sums[:, :3] / (sums[:, 3:4] * D))


def unpack(swapped, down, o_t, q_up, kv_up, block, grad_input, small, slice_ff, rank_q, columns_down, gains):
    n_dp, width, _ = swapped.shape

    def out(*shape):
        return jax.ShapeDtypeStruct(shape, F32)

    return pl.pallas_call(
        functools.partial(unpack_kernel, slice_ff, rank_q),
        out_shape=(
            out(width, n_dp * slice_ff),
            out(width, n_dp * slice_ff),
            out(width, n_dp * slice_ff),
            out(*o_t.shape),
            out(width, rank_q),
            out(columns_down - rank_q, width),
            out(*q_up.shape),
            out(*kv_up.shape),
            out(*block.shape),
            out(*grad_input.shape),
            *(out(1, gain.shape[0]) for gain in gains),
            out(1, 3),
        ),
        in_specs=[VMEM] * 8,
        out_specs=[VMEM] * 15,
        compiler_params=pltpu.CompilerParams(vmem_limit_bytes=VMEM_BYTES),
        name="unpack",
    )(swapped, down, o_t, q_up, kv_up, block, grad_input, small)


def per_device(
    layer_input,
    segment_ids,
    valid_mask,
    cotangent,
    attn_gain,
    q_down,
    q_gain,
    q_up,
    kv_down,
    kv_gain,
    kv_up,
    o_proj,
    mlp_gain,
    w_gate,
    w_up,
    w_down,
):
    length = layer_input.shape[0]
    n_dp = lax.axis_size("dp")
    n_tensor = lax.axis_size("tensor")
    share = length // n_tensor
    me = lax.axis_index("tensor")
    width = w_gate.shape[0]
    slice_ff = w_gate.shape[1] // n_dp
    rows_down = width // n_tensor

    def rows_of(values, count):
        return lax.dynamic_slice_in_dim(values, me * count, count, 0)

    rank_q = q_down.shape[1]
    columns_down = rank_q + kv_down.shape[1]
    pad_down = -columns_down % 128
    down_rows = jnp.concatenate(
        [
            rows_of(q_down, rows_down),
            rows_of(kv_down, rows_down),
            jnp.zeros((rows_down, pad_down), BF),
        ],
        axis=1,
    )
    lanes = -(-width // 128) * 128

    def lane_rows(rows, count, kind):
        padded = [jnp.pad(row.astype(kind), (0, lanes - row.shape[0])) for row in rows]
        return jnp.stack(padded + [jnp.zeros((lanes,), kind)] * (count - len(padded)))

    cot_rows = rows_of(cotangent, share)
    x_rows = rows_of(layer_input, share)
    gains_block = lane_rows([attn_gain, q_gain, kv_gain, mlp_gain], 16, BF)
    cosine, sine_table = rope_tables(length, ROPE)
    cos_full = jnp.concatenate([cosine, cosine], axis=1)
    sin_full = jnp.concatenate([-sine_table, sine_table], axis=1)
    fused = n_dp == 8 and rows_down % 16 == 0 and q_up.shape[0] % 16 == 0
    if fused:
        (
            f_down, f_o, f_q, f_kv, f_g, mlp_part, normed_part, grad_packed,
            normed, latents, q_normed, kv_normed, q_rows, kv_rows, key_rot, mixed,
            resid_rows, attn_rows, cot_rows,
        ) = forward(
            n_dp, layer_input, cotangent, q_down, kv_down.T, (attn_gain, q_gain, kv_gain, mlp_gain),
            q_up, kv_up, o_proj.T, w_gate, w_up, w_down.T, segment_ids, valid_mask,
            jnp.concatenate([cos_full, sin_full], axis=1), down_rows.shape, lanes,
        )
    else:
        f_down, f_o, f_q, f_kv, f_g, f_cot = gather_weights(
            n_dp, n_tensor, down_rows, o_proj.T, q_up, kv_up, gains_block, cot_rows
        )
    full_down = f_down.reshape(n_dp * width, columns_down + pad_down)
    full_o = f_o.reshape(n_dp * width, -1)

    def gain_of(row, gain):
        return f_g[:, row, : gain.shape[0]].reshape(-1).astype(F32)

    gain_attn = gain_of(0, attn_gain)
    gain_q = gain_of(1, q_gain)
    gain_kv = gain_of(2, kv_gain)
    gain_mlp = gain_of(3, mlp_gain)
    if not fused:
        packed = jnp.concatenate(
            [
                w_gate.reshape(width, n_dp, slice_ff),
                w_up.reshape(width, n_dp, slice_ff),
                w_down.T.reshape(width, n_dp, slice_ff),
                jnp.zeros((width, n_dp, -3 * slice_ff % 128), BF),
            ],
            axis=2,
        ).transpose(1, 0, 2)
        packed, f_q = lax.optimization_barrier((packed, f_q))
        f_w = swap_dp(packed)
    full_q_up = f_q.reshape(-1, q_up.shape[1])
    full_kv_up = f_kv.reshape(-1, kv_up.shape[1])
    if not fused:
        normed, latents, q_normed, kv_normed, q_rows, kv_rows, key_rot, mixed = attend(
            layer_input, gain_attn, gain_q, gain_kv, full_down, full_q_up, full_kv_up,
            segment_ids, valid_mask, cos_full, sin_full,
        )
        f_normed, resid_rows, attn_rows = attention_residual(
            n_dp, dot_nt(mixed, full_o).astype(BF), x_rows, gain_mlp[None, :]
        )
    if not fused:
        mlp_part, normed_part, grad_packed = feed_forward(
            f_normed.reshape(n_dp * length, -1),
            f_cot.reshape(n_dp * length, -1),
            f_w.reshape(n_dp * width, -1),
            slice_ff,
            length,
        )
    weight_rows = rows_of(valid_mask.astype(F32)[:, None], share)
    if fused:
        f_block, grad_input, s_down, s_o, s_q, s_kv, s_small, swapped = back(
            n_dp, normed_part, mlp_part, grad_packed.reshape(n_dp, width, -1), resid_rows, attn_rows,
            cot_rows, layer_input, normed, latents, q_normed, kv_normed, q_rows, kv_rows,
            key_rot, mixed, f_down, f_o, f_q, f_kv, f_g, segment_ids, valid_mask,
            jnp.concatenate([cos_full, sin_full], axis=1),
        )
        (
            grad_w_gate, grad_w_up, grad_down_t, grad_o_t, grad_q_down, grad_kv_down_t, grad_q_up,
            grad_kv_up, block_full, grad_input, grad_attn_gain, grad_q_gain, grad_kv_gain, grad_mlp_gain, rms_stats,
        ) = unpack(
            swapped, s_down, s_o, s_q, s_kv, f_block.reshape(length, -1), grad_input, s_small,
            slice_ff, rank_q, columns_down,
            (attn_gain, q_gain, kv_gain, mlp_gain),
        )
        return (
            block_full,
            grad_input,
            grad_attn_gain.reshape(-1),
            grad_q_down,
            grad_q_gain.reshape(-1),
            grad_q_up,
            grad_kv_down_t.T,
            grad_kv_gain.reshape(-1),
            grad_kv_up,
            grad_o_t.T,
            grad_mlp_gain.reshape(-1),
            grad_w_gate,
            grad_w_up,
            grad_down_t.T,
            rms_stats.reshape(-1),
        )
    else:
        inv_two = inverse_rms(resid_rows)
        unit_two = resid_rows * inv_two
        swapped = swap_dp(grad_packed.reshape(n_dp, width, -1))
        normed_part, grad_packed = lax.optimization_barrier((normed_part, grad_packed))
        f_attn, grad_normed_two, f_block, mlp_rows = residual_grads(
            n_dp, normed_part, mlp_part, resid_rows, cot_rows, gain_mlp[None, :]
        )
        grad_attn = f_attn.reshape(length, -1)
        block_full = f_block.reshape(length, -1)

        grad_mlp_gain = jnp.sum(grad_normed_two * unit_two, axis=0)

        grad_part, grad_o, grad_q_up, grad_kv_up = attend_back(
            grad_attn, mixed, full_o, q_rows, kv_rows, key_rot, q_normed, kv_normed,
            full_q_up, full_kv_up, segment_ids, valid_mask, cos_full, sin_full,
            columns_down + pad_down,
        )
        grad_part, swapped = lax.optimization_barrier((grad_part, swapped))
        grad_latents = sum_latents(n_dp, grad_part).astype(F32)
        stream = layer_input.astype(F32)
        inv_one = inverse_rms(stream)
        unit_one = stream * inv_one
        q_latent = latents[:, :rank_q]
        inv_q = inverse_rms(q_latent)
        unit_q = q_latent * inv_q
        kv_latent = latents[:, rank_q : rank_q + KR]
        inv_kv = inverse_rms(kv_latent)
        unit_kv = kv_latent * inv_kv
        grad_q_normed = grad_latents[:, :rank_q]
        grad_kv_normed = grad_latents[:, rank_q : rank_q + KR]
        grad_kv_rot = grad_latents[:, rank_q + KR : columns_down]
        grad_q_gain = jnp.sum(grad_q_normed * unit_q, axis=0)
        grad_kv_gain = jnp.sum(grad_kv_normed * unit_kv, axis=0)
        grad_down = jnp.concatenate(
            [
                norm_back(grad_q_normed * gain_q, unit_q, inv_q),
                norm_back(grad_kv_normed * gain_kv, unit_kv, inv_kv),
                grad_kv_rot,
                jnp.zeros((length, pad_down), F32),
            ],
            axis=-1,
        ).astype(BF)
        grad_normed = dot_nt(grad_down, full_down)
        grad_attn_gain = jnp.sum(grad_normed * unit_one, axis=0)
        grad_input = grad_attn.astype(F32) * (1.0 / RESIDUAL_SCALE) + norm_back(
            grad_normed * gain_attn, unit_one, inv_one
        )

        quarter = lax.dynamic_index_in_dim(
            normed.reshape(length, n_dp, n_tensor, rows_down), me, 2, keepdims=False
        ).reshape(length, n_dp * rows_down)
        def by_dp(vector):
            return vector.reshape(n_dp, -1)

        def small_rows(vectors):
            return jnp.stack(
                [jnp.pad(by_dp(v), ((0, 0), (0, lanes - v.shape[0] // n_dp))) for v in vectors]
                + [jnp.zeros((n_dp, lanes), F32)] * (8 - len(vectors)),
                axis=1,
            )

        stats = jnp.stack(
            [
                jnp.sum(weight_rows * resid_rows * resid_rows),
                jnp.sum(weight_rows * attn_rows * attn_rows),
                jnp.sum(weight_rows * mlp_rows * mlp_rows),
                jnp.sum(weight_rows),
            ]
        )
        s_down, s_o, s_q, s_kv, s_small = sum_weight_grads(
            n_dp,
            dot_tn(quarter, grad_down).astype(BF),
            grad_o,
            grad_q_up,
            grad_kv_up,
            small_rows([grad_attn_gain, grad_q_gain, grad_kv_gain, grad_mlp_gain]),
            lane_rows([stats], 8, F32),
        )

    def columns_of(part):
        return part.transpose(1, 0, 2).reshape(width, n_dp * slice_ff).astype(F32)

    grad_w_gate = columns_of(swapped[:, :, :slice_ff])
    grad_w_up = columns_of(swapped[:, :, slice_ff : 2 * slice_ff])
    grad_w_down = columns_of(swapped[:, :, 2 * slice_ff : 3 * slice_ff]).T

    d_down = s_down.reshape(width, -1).astype(F32)
    gains = s_small[me, 0]
    stat_sums = jnp.sum(s_small[:, 1, 0, :4], axis=0)
    rms_stats = jnp.sqrt(stat_sums[:3] / (stat_sums[3] * D))
    return (
        block_full,
        grad_input,
        gains[0, : attn_gain.shape[0]],
        d_down[:, :rank_q],
        gains[1, : q_gain.shape[0]],
        s_q,
        d_down[:, rank_q:columns_down],
        gains[2, : kv_gain.shape[0]],
        s_kv,
        s_o.T,
        jnp.sum(s_small[:, 0, 3], axis=0)[: mlp_gain.shape[0]],
        grad_w_gate,
        grad_w_up,
        grad_w_down,
        rms_stats,
    )


def solution(mesh):
    placed = (
        P("dp", None),
        P("dp"),
        P("dp"),
        P("dp", None),
        P("dp"),
        P("dp", None),
        P("dp"),
        P("dp", "tensor"),
        P("dp", None),
        P("dp"),
        P("dp", "tensor"),
        P("tensor", "dp"),
        P("dp"),
        P("dp", "tensor"),
        P("dp", "tensor"),
        P("tensor", "dp"),
    )
    return jax.shard_map(
        per_device,
        mesh=mesh,
        in_specs=placed,
        out_specs=(
            P("dp", None),
            P("dp", None),
            P("dp"),
            P("dp", None),
            P("dp"),
            P("dp", "tensor"),
            P("dp", None),
            P("dp"),
            P("dp", "tensor"),
            P("tensor", "dp"),
            P("dp"),
            P("dp", "tensor"),
            P("dp", "tensor"),
            P("tensor", "dp"),
            P(),
        ),
        check_vma=False,
    )
```

```python
import functools
import itertools
import math

import jax
import jax.numpy as jnp
from jax import lax
from jax.experimental import pallas as pl
from jax.experimental.pallas import tpu as pltpu
from jax.sharding import PartitionSpec as P

D = 2560
KR = 256
NOPE = 64
ROPE = 32
VD = 64


NORM_EPS = 1e-05
RESIDUAL_SCALE = 1.4 / math.sqrt(62.0)
ROPE_BASE = 10000.0
NEGATIVE = -1e30


def rope_tables(length, rot_dim):
    half_dim = rot_dim // 2
    position = jnp.arange(length, dtype=jnp.float32)
    frequency = jnp.exp(
        -math.log(ROPE_BASE) * 2.0 * jnp.arange(half_dim, dtype=jnp.float32) / rot_dim
    )
    phases = position[:, None] * frequency[None, :]
    return (jnp.cos(phases), jnp.sin(phases))


def inverse_rms(values):
    return lax.rsqrt(jnp.mean(values * values, axis=-1, keepdims=True) + NORM_EPS)


def norm_back(grad_unit, unit, inv_rms):
    return inv_rms * (grad_unit - unit * jnp.mean(grad_unit * unit, axis=-1, keepdims=True))


BF = jnp.bfloat16
F32 = jnp.float32


def dot(left, right):
    return jnp.dot(left, right, preferred_element_type=F32)


def dot_nt(left, right):
    return jnp.einsum("ac,bc->ab", left, right, preferred_element_type=F32)


def dot_tn(left, right):
    return jnp.einsum("ca,cb->ab", left, right, preferred_element_type=F32)


def swap_dp(blocks):
    return lax.all_to_all(blocks, "dp", 0, 0, tiled=True)


MESH = pl.DeviceIdType.MESH
ANY = pl.BlockSpec(memory_space=pl.ANY)
VMEM = pl.BlockSpec(memory_space=pltpu.VMEM)
VMEM_BYTES = 60 * 1024 * 1024


class Links:
    def __init__(self, n_dp):
        self.n_high = n_dp // 2
        dp = lax.axis_index("dp")
        tensor = lax.axis_index("tensor")
        self.high, self.low = dp // 2, dp % 2
        self.side, self.core = tensor // 2, tensor % 2

    def device(self, high=None, low=None, side=None, core=None):
        high = self.high if high is None else high
        low = self.low if low is None else low
        side = self.side if side is None else side
        core = self.core if core is None else core
        return {"dp": high * 2 + low, "tensor": side * 2 + core}

    def behind(self, step):
        return (self.high + self.n_high - step) % self.n_high

    def ahead(self, step):
        return (self.high + step) % self.n_high

    def over_low(self):
        return self.device(low=1 - self.low)

    def over_side(self):
        return self.device(side=1 - self.side)

    def over_core(self):
        return self.device(core=1 - self.core)

    def meet(self, high=True, low=True, side=True, core=True, swap=False):
        barrier = pltpu.get_barrier_semaphore()
        partners = []
        if swap:
            partners += [
                self.device(high=self.ahead(k), low=1 - self.low) for k in range(1, self.n_high)
            ]
        if high:
            partners += [self.device(high=self.ahead(k)) for k in range(1, self.n_high)]
        if low:
            partners.append(self.over_low())
        if side:
            partners.append(self.over_side())
        if core:
            partners.append(self.over_core())
        for partner in partners:
            pl.semaphore_signal(barrier, inc=1, device_id=partner, device_id_type=MESH)
        pl.semaphore_wait(barrier, len(partners))


class Copies:
    def __init__(self, send, recv, local):
        self.send, self.recv, self.local = send, recv, local
        self.count = self.local_count = 0
        self.started = []
        self.maybe = []

    def go(self, source, target, device):
        copy = pltpu.make_async_remote_copy(
            src_ref=source,
            dst_ref=target,
            send_sem=self.send.at[self.count],
            recv_sem=self.recv.at[self.count],
            device_id=device,
            device_id_type=MESH,
        )
        self.count += 1
        copy.start()
        self.started.append(copy)
        return copy

    def sent_maybe(self):
        for condition, copy in self.maybe:
            pl.when(condition)(copy.wait_send)
        self.maybe = []

    def near(self, source, target):
        copy = pltpu.make_async_copy(source, target, self.local.at[self.local_count])
        self.local_count += 1
        copy.start()
        return copy

    def sent(self, copy):
        copy.wait_send()
        self.started = [other for other in self.started if other is not copy]

    def finish(self):
        for copy in self.started:
            copy.wait_send()
        for condition, copy in self.maybe:
            pl.when(condition)(copy.wait_send)


def take_turns(*streams):
    streams = list(streams)
    while streams:
        for stream in list(streams):
            try:
                next(stream)
            except StopIteration:
                streams.remove(stream)


def steps_by_distance(count):
    order, k = [], 1
    while len(order) < count - 1:
        order.append(k)
        if len(order) < count - 1:
            order.append(count - k)
        k += 1
    return order


class Line:
    def __init__(self, links, copies, block, target):
        self.links, self.copies, self.block, self.target = links, copies, block, target
        self.count = links.n_high
        self.first_tag = copies.count
        copies.count += self.count
        inner = steps_by_distance(self.count)
        at_start = (self.count - 1 - links.high) // (self.count - 1)
        at_end = links.high // (self.count - 1)
        self.tags = [0] + [
            at_start * (self.count - i) + at_end * i + (1 - at_start - at_end) * inner[i - 1]
            for i in range(1, self.count)
        ]

    def source(self, i):
        return (self.links.high + self.count - self.tags[i]) % self.count

    def send(self, condition, source, to, tag):
        copy = pltpu.make_async_remote_copy(
            src_ref=source,
            dst_ref=source if source is not self.block else self.target(self.links.high),
            send_sem=self.copies.send.at[self.copies.count],
            recv_sem=self.copies.recv.at[self.first_tag + tag],
            device_id=self.links.device(high=to),
            device_id_type=MESH,
        )
        self.copies.count += 1
        pl.when(condition)(copy.start)
        self.copies.maybe.append((condition, copy))

    def start(self):
        high = self.links.high
        self.send(high < self.count - 1, self.block, (high + 1) % self.count, 1)
        self.send(
            high > 0, self.block, (high + self.count - 1) % self.count, self.count - 1
        )

    def arrived(self, i):
        high, tag = self.links.high, self.tags[i]
        here = self.target(self.source(i))
        pltpu.make_async_remote_copy(
            src_ref=here,
            dst_ref=here,
            send_sem=self.copies.send.at[self.first_tag],
            recv_sem=self.copies.recv.at[self.first_tag + tag],
            device_id=self.links.over_low(),
            device_id_type=MESH,
        ).wait_recv()
        from_left = high >= tag
        onward = (from_left & (high < self.count - 1)) | ((high < tag) & (high > 0))
        way = jnp.where(from_left, 1, self.count - 1)
        self.send(onward, here, (high + way) % self.count, (tag + way) % self.count)


class Direct:
    def __init__(self, links, copies, block, target):
        self.links, self.copies, self.block, self.target = links, copies, block, target
        self.order = [0] + steps_by_distance(links.n_high)

    def source(self, i):
        return self.links.behind(self.order[i])

    def start(self):
        mine = self.target(self.links.high)
        self.arrive = [None] + [
            self.copies.go(self.block, mine, self.links.device(high=self.links.ahead(k)))
            for k in self.order[1:]
        ]

    def arrived(self, i):
        self.arrive[i].wait_recv()


def along_high(links, copies, block, target):
    return (Line if links.n_high == 4 else Direct)(links, copies, block, target)


class EveryGather:
    def __init__(self, links, copies, block, out, cut=None):
        self.links, self.copies, self.block, self.out = links, copies, block, out
        self.columns = out.shape[-1]
        self.cut = self.columns // 256 * 128 if cut is None else cut
        self.line = along_high(
            links, copies, block, lambda high: self.slot(high, links.low, links.side)
        )
        self.over_low, self.over_side = {}, {}
        self.corners = {i: [] for i in range(links.n_high)}
        self.last = {i: [] for i in range(links.n_high)}

    def slot(self, high, low, side):
        return self.out.at[high * 2 + low, side * 2 + self.links.core]

    def start(self):
        links = self.links
        self.own = self.copies.near(self.block, self.slot(links.high, links.low, links.side))
        self.line.start()

    def to_core(self, i, source, target):
        self.last[i].append(self.copies.go(source, target, self.links.over_core()))

    def first(self, i):
        links = self.links
        here = self.slot(self.line.source(i), links.low, links.side)
        if i:
            self.line.arrived(i)
        source = here if i else self.block
        self.over_low[i] = self.copies.go(source, here, links.over_low())
        self.over_side[i] = self.copies.go(source, here, links.over_side())
        self.to_core(i, source, here)

    def second(self, i):
        links, high = self.links, self.line.source(i)
        self.over_low[i].wait_recv()
        here = self.slot(high, 1 - links.low, links.side)
        if self.cut:
            half = pl.ds(0, self.cut)
            part = here.at[:, half]
            self.corners[i].append((self.copies.go(part, part, links.over_side()), half))
        self.to_core(i, here, here)
        self.over_side[i].wait_recv()
        here = self.slot(high, links.low, 1 - links.side)
        if self.cut < self.columns:
            half = pl.ds(self.cut, self.columns - self.cut)
            part = here.at[:, half]
            self.corners[i].append((self.copies.go(part, part, links.over_low()), half))
        self.to_core(i, here, here)

    def third(self, i):
        links = self.links
        here = self.slot(self.line.source(i), 1 - links.low, 1 - links.side)
        for corner, half in self.corners[i]:
            corner.wait_recv()
            part = here.at[:, half]
            self.to_core(i, part, part)

    def fourth(self, i):
        for copy in self.last[i]:
            copy.wait_recv()
        if i == 0:
            self.own.wait()

    def sent(self):
        copies = [*self.over_low.values(), *self.over_side.values()]
        copies += [corner for pairs in self.corners.values() for corner, _ in pairs]
        copies += [copy for last in self.last.values() for copy in last]
        for copy in copies:
            self.copies.sent(copy)
        self.copies.sent_maybe()


def every_gather(links, copies, block, out, cut=None):
    work = EveryGather(links, copies, block, out, cut)
    work.start()
    yield
    for i in range(links.n_high + 2):
        if i < links.n_high:
            work.first(i)
            yield
        if 0 <= i - 1 < links.n_high:
            work.second(i - 1)
            yield
        if 0 <= i - 2:
            work.third(i - 2)
            yield
    for i in range(links.n_high):
        work.fourth(i)


class DpGather:
    def __init__(self, links, copies, block, out):
        self.links, self.copies, self.block, self.out = links, copies, block, out
        self.line = along_high(links, copies, block, lambda high: out.at[high * 2 + links.low])
        self.last = []
        self.mine = out.at[links.high * 2 + links.low]

    def start(self):
        self.own = self.copies.near(self.block, self.mine)
        self.line.start()

    def own_low(self):
        self.last.append(self.copies.go(self.block, self.mine, self.links.over_low()))

    def step(self, i):
        self.line.arrived(i + 1)
        here = self.out.at[self.line.source(i + 1) * 2 + self.links.low]
        self.last.append(self.copies.go(here, here, self.links.over_low()))

    def finish(self):
        for copy in self.last:
            copy.wait_recv()
        self.own.wait()


def dp_gather(links, copies, block, out):
    work = DpGather(links, copies, block, out)
    work.start()
    yield
    work.own_low()
    yield
    for i in range(links.n_high - 1):
        work.step(i)
        yield
    work.finish()


def tensor_gather(links, copies, block, out):
    mine = out.at[links.side * 2 + links.core]
    own = copies.near(block, mine)
    last = [copies.go(block, mine, links.over_core())]
    across = copies.go(block, mine, links.over_side())
    yield
    across.wait_recv()
    here = out.at[(1 - links.side) * 2 + links.core]
    last.append(copies.go(here, here, links.over_core()))
    yield
    for copy in last:
        copy.wait_recv()
    own.wait()


class EveryScatter:
    def __init__(self, links, copies, part, bufs, result, cut):
        self.links, self.copies, self.part, self.result = links, copies, part, result
        self.own, self.chip, *bufs = bufs
        self.low_a, self.side_a = (bufs.pop(0), bufs.pop(0)) if cut else (None, None)
        self.side_b, self.low_b, self.done, self.from_high = bufs
        self.cut = cut
        self.half_a, self.half_b = pl.ds(0, cut), pl.ds(cut, part.shape[-1] - cut)
        self.order = steps_by_distance(links.n_high) + [0]
        self.loads, self.core_in, self.a_in, self.b_in = {}, {}, {}, {}
        self.a_last, self.b_last, self.high_in = {}, {}, {}

    def load(self, i):
        there = self.links.ahead(self.order[i])
        self.loads[i] = self.copies.near(
            self.part.at[there, :, :, self.links.core], self.own.at[i % 2]
        )

    def start(self):
        for i, k in enumerate(self.order):
            self.core_in[k] = self.copies.go(
                self.part.at[self.links.ahead(k), :, :, 1 - self.links.core],
                self.chip.at[k],
                self.links.over_core(),
            )
            if i < 2:
                self.load(i)

    def first(self, i):
        links, copies, chip, k = self.links, self.copies, self.chip, self.order[i]
        self.core_in[k].wait_recv()
        self.loads[i].wait()
        for low in range(2):
            for side in range(2):
                chip[k, low, side] = (
                    self.own[i % 2, low, side].astype(F32) + chip[k, low, side].astype(F32)
                ).astype(BF)
        if i + 2 < links.n_high:
            self.load(i + 2)
        if self.cut:
            self.a_in[k] = copies.go(
                chip.at[k, 1 - links.low, :, :, self.half_a], self.low_a.at[k], links.over_low()
            )
        self.b_in[k] = copies.go(
            chip.at[k, :, 1 - links.side, :, self.half_b], self.side_b.at[k], links.over_side()
        )

    def second(self, i):
        links, copies, chip, k = self.links, self.copies, self.chip, self.order[i]
        low_a, side_b = self.low_a, self.side_b
        if self.cut:
            self.a_in[k].wait_recv()
            for side in range(2):
                low_a[k, side] = (
                    low_a[k, side].astype(F32)
                    + chip[k, links.low, side, :, self.half_a].astype(F32)
                ).astype(BF)
            self.a_last[k] = copies.go(
                low_a.at[k, 1 - links.side], self.side_a.at[k], links.over_side()
            )
        self.b_in[k].wait_recv()
        for low in range(2):
            side_b[k, low] = (
                side_b[k, low].astype(F32) + chip[k, low, links.side, :, self.half_b].astype(F32)
            ).astype(BF)
        self.b_last[k] = copies.go(side_b.at[k, 1 - links.low], self.low_b.at[k], links.over_low())

    def third(self, i):
        links, k = self.links, self.order[i]
        if self.cut:
            self.a_last[k].wait_recv()
            self.done[k, :, self.half_a] = (
                self.side_a[k].astype(F32) + self.low_a[k, links.side].astype(F32)
            ).astype(BF)
        self.b_last[k].wait_recv()
        self.done[k, :, self.half_b] = (
            self.low_b[k].astype(F32) + self.side_b[k, links.low].astype(F32)
        ).astype(BF)
        if k:
            self.high_in[k] = self.copies.go(
                self.done.at[k], self.from_high.at[k - 1], links.device(high=links.ahead(k))
            )

    def finish(self):
        total = self.done[0].astype(F32)
        for k in steps_by_distance(self.links.n_high):
            self.high_in[k].wait_recv()
            total = total + self.from_high[k - 1].astype(F32)
        self.result[...] = total


def every_scatter(links, copies, part, bufs, result):
    work = EveryScatter(links, copies, part, bufs, result, part.shape[-1] // 256 * 128)
    work.start()
    yield
    for i in range(links.n_high + 2):
        if i < links.n_high:
            work.first(i)
            yield
        if 0 <= i - 1 < links.n_high:
            work.second(i - 1)
            yield
        if 0 <= i - 2:
            work.third(i - 2)
            yield
    work.finish()


def every_scatter_scratch(n_high, rows, columns, cut=None):
    cut = columns // 256 * 128 if cut is None else cut
    over_low = [
        pltpu.VMEM((n_high, 2, rows, cut), BF),
        pltpu.VMEM((n_high, rows, cut), BF),
    ]
    return [
        pltpu.VMEM((2, 2, 2, rows, columns), BF),
        pltpu.VMEM((n_high, 2, 2, rows, columns), BF),
        *(over_low if cut else []),
        pltpu.VMEM((n_high, 2, rows, columns - cut), BF),
        pltpu.VMEM((n_high, rows, columns - cut), BF),
        pltpu.VMEM((n_high, rows, columns), BF),
        pltpu.VMEM((n_high - 1, rows, columns), BF),
    ]


def dp_scatter(links, copies, part, bufs, result):
    from_low, done, from_high = bufs
    order = steps_by_distance(links.n_high) + [0]
    low_in, high_in = {}, {}
    for k in order:
        low_in[k] = copies.go(
            part.at[links.ahead(k), 1 - links.low], from_low.at[k], links.over_low()
        )
    yield
    for k in order:
        low_in[k].wait_recv()
        done[k] = (
            part[links.ahead(k), links.low].astype(F32) + from_low[k].astype(F32)
        ).astype(BF)
        if k:
            high_in[k] = copies.go(
                done.at[k], from_high.at[k - 1], links.device(high=links.ahead(k))
            )
        yield
    total = done[0].astype(F32)
    for k in steps_by_distance(links.n_high):
        high_in[k].wait_recv()
        total = total + from_high[k - 1].astype(F32)
    result[...] = total.astype(result.dtype)
    yield


def dp_scatter_scratch(n_high, shape):
    return [
        pltpu.VMEM((n_high, *shape), BF),
        pltpu.VMEM((n_high, *shape), BF),
        pltpu.VMEM((n_high - 1, *shape), BF),
    ]


def semaphores(count, local):
    return [
        pltpu.SemaphoreType.DMA((count,)),
        pltpu.SemaphoreType.DMA((count,)),
        pltpu.SemaphoreType.DMA((local,)),
    ]


def params(number, mebibytes=60):
    return pltpu.CompilerParams(
        collective_id=number, has_side_effects=True, vmem_limit_bytes=mebibytes * 1024 * 1024
    )


def count_every_gather(n_high):
    return 11 * n_high + 1


def count_dp_gather(n_high):
    return 3 * n_high + 1


def weights_kernel(n_dp, down, o_t, q_up, kv_up, gains, cot, f_down, f_o, f_q, f_kv, f_g, f_cot, send, recv, local):
    links = Links(n_dp)
    copies = Copies(send, recv, local)
    links.meet()
    take_turns(
        every_gather(links, copies, down, f_down),
        dp_gather(links, copies, gains, f_g),
        dp_gather(links, copies, q_up, f_q),
        dp_gather(links, copies, kv_up, f_kv),
        dp_gather(links, copies, o_t, f_o),
        every_gather(links, copies, cot, f_cot),
    )
    copies.finish()


def gather_weights(n_dp, n_tensor, down, o_t, q_up, kv_up, gains, cot):
    n_high = n_dp // 2
    count = 2 * count_every_gather(n_high) + 4 * count_dp_gather(n_high)

    def over(block, *lead):
        return jax.ShapeDtypeStruct((*lead, *block.shape), block.dtype)

    return pl.pallas_call(
        functools.partial(weights_kernel, n_dp),
        out_shape=(
            over(down, n_dp, n_tensor),
            over(o_t, n_dp),
            over(q_up, n_dp),
            over(kv_up, n_dp),
            over(gains, n_dp),
            over(cot, n_dp, n_tensor),
        ),
        in_specs=[ANY] * 6,
        out_specs=[ANY] * 6,
        scratch_shapes=semaphores(count, 6),
        compiler_params=params(1),
        name="gather_weights",
    )(down, o_t, q_up, kv_up, gains, cot)


def resid_kernel(n_dp, part, x_rows, gain, full, resid, branch, from_core, out_side, from_side, block, send, recv, local):
    links = Links(n_dp)
    copies = Copies(send, recv, local)
    links.meet()
    arrive = copies.go(part.at[:, 1 - links.core], from_core, links.over_core())
    arrive.wait_recv()
    out_side[...] = (
        part[1 - links.side, links.core].astype(F32) + from_core[1 - links.side].astype(F32)
    ).astype(BF)
    arrive = copies.go(out_side, from_side, links.over_side())
    mine = part[links.side, links.core].astype(F32) + from_core[links.side].astype(F32)
    arrive.wait_recv()
    attn = RESIDUAL_SCALE * (mine + from_side[...].astype(F32))
    stream = x_rows[...].astype(F32) + attn
    branch[...] = attn
    resid[...] = stream
    block[...] = (stream * inverse_rms(stream) * gain[...]).astype(BF)
    take_turns(every_gather(links, copies, block, full))
    copies.finish()


def attention_residual(n_dp, part, x_rows, gain):
    n_tensor = 4
    rows, columns = x_rows.shape
    block = (rows, columns)
    return pl.pallas_call(
        functools.partial(resid_kernel, n_dp),
        out_shape=(
            jax.ShapeDtypeStruct((n_dp, n_tensor, rows, columns), BF),
            jax.ShapeDtypeStruct(block, F32),
            jax.ShapeDtypeStruct(block, F32),
        ),
        in_specs=[VMEM] * 3,
        out_specs=[ANY, VMEM, VMEM],
        scratch_shapes=[
            pltpu.VMEM((2, *block), BF),
            pltpu.VMEM(block, BF),
            pltpu.VMEM(block, BF),
            pltpu.VMEM(block, BF),
            *semaphores(2 + count_every_gather(n_dp // 2), 1),
        ],
        compiler_params=params(2),
        name="attention_residual",
    )(part.reshape(2, 2, rows, columns), x_rows, gain)


def grad_rows_kernel(n_dp, both, *refs):
    links = Links(n_dp)
    copies = Copies(*refs[-3:])
    g_part, resid, cot, gain = refs[:4]
    if both:
        m_part, attn_full, g_rows, block_full, m_rows = refs[4:9]
        scratch = refs[9:-3]
    else:
        attn_full, g_rows = refs[4:6]
        scratch = refs[6:-3]
    links.meet()

    def grad_stream():
        grad_rows = scratch[0]
        yield from every_scatter(links, copies, g_part, scratch[1:9], g_rows)
        stream = resid[...]
        inv = inverse_rms(stream)
        grad = cot[...].astype(F32) + norm_back(g_rows[...] * gain[...], stream * inv, inv)
        grad_rows[...] = (RESIDUAL_SCALE * grad).astype(BF)
        yield from tensor_gather(links, copies, grad_rows, attn_full)

    if both:
        block = block_stream(links, copies, m_part, resid, block_full, m_rows, scratch[9:])
        take_turns(grad_stream(), block)
    else:
        take_turns(grad_stream())
    copies.finish()


def block_stream(links, copies, m_part, resid, block_full, m_rows, scratch):
    block_rows = scratch[0]
    yield from every_scatter(links, copies, m_part, scratch[1:9], m_rows)
    m_rows[...] = RESIDUAL_SCALE * m_rows[...]
    block_rows[...] = resid[...] + m_rows[...]
    yield from tensor_gather(links, copies, block_rows, block_full)


def block_rows_kernel(n_dp, m_part, resid, block_full, m_rows, *rest):
    links = Links(n_dp)
    copies = Copies(*rest[-3:])
    links.meet()
    take_turns(block_stream(links, copies, m_part, resid, block_full, m_rows, rest[:-3]))
    copies.finish()


def residual_grads(n_dp, g_part, m_part, resid, cot, gain):
    n_high = n_dp // 2
    rows, columns = resid.shape
    shape = (n_high, 2, 2, 2, rows, columns)
    g_part, m_part = g_part.reshape(shape), m_part.reshape(shape)
    both = n_high <= 4
    one = jax.ShapeDtypeStruct((rows, columns), F32)
    grad_out = (jax.ShapeDtypeStruct((4, rows, columns), BF), one)
    block_out = (jax.ShapeDtypeStruct((4, rows, columns), F32), one)
    grad_scratch = [
        pltpu.VMEM((rows, columns), BF),
        *every_scatter_scratch(n_high, rows, columns),
    ]
    block_scratch = [
        pltpu.VMEM((rows, columns), F32),
        *every_scatter_scratch(n_high, rows, columns),
    ]
    count, local = 6 * n_high - 1 + 3, n_high + 1
    if both:
        return pl.pallas_call(
            functools.partial(grad_rows_kernel, n_dp, True),
            out_shape=grad_out + block_out,
            in_specs=[ANY, VMEM, VMEM, VMEM, ANY],
            out_specs=[ANY, VMEM, ANY, VMEM],
            scratch_shapes=[*grad_scratch, *block_scratch, *semaphores(2 * count, 2 * local)],
            compiler_params=params(3),
            name="residual_grads",
        )(g_part, resid, cot, gain, m_part)
    grads = pl.pallas_call(
        functools.partial(grad_rows_kernel, n_dp, False),
        out_shape=grad_out,
        in_specs=[ANY, VMEM, VMEM, VMEM],
        out_specs=[ANY, VMEM],
        scratch_shapes=[*grad_scratch, *semaphores(count, local)],
        compiler_params=params(3),
        name="residual_grads",
    )(g_part, resid, cot, gain)
    block = pl.pallas_call(
        functools.partial(block_rows_kernel, n_dp),
        out_shape=block_out,
        in_specs=[ANY, VMEM],
        out_specs=[ANY, VMEM],
        scratch_shapes=[*block_scratch, *semaphores(count, local)],
        compiler_params=params(6),
        name="block_rows",
    )(m_part, resid)
    return (*grads, *block)


def latent_kernel(n_dp, part, full, from_core, half, from_side, send, recv, local):
    links = Links(n_dp)
    copies = Copies(send, recv, local)
    links.meet(high=False, low=False)
    arrive = copies.go(part.at[1 - links.core], from_core, links.over_core())
    arrive.wait_recv()
    half[...] = (part[links.core].astype(F32) + from_core[...].astype(F32)).astype(BF)
    arrive = copies.go(half, from_side, links.over_side())
    arrive.wait_recv()
    full[links.core] = (half[...].astype(F32) + from_side[...].astype(F32)).astype(BF)
    arrive = copies.go(full.at[links.core], full.at[links.core], links.over_core())
    arrive.wait_recv()
    copies.finish()


def sum_latents(n_dp, part):
    rows, columns = part.shape
    half = (rows // 2, columns)
    return pl.pallas_call(
        functools.partial(latent_kernel, n_dp),
        out_shape=jax.ShapeDtypeStruct((2, *half), BF),
        in_specs=[VMEM],
        out_specs=VMEM,
        scratch_shapes=[pltpu.VMEM(half, BF)] * 3 + semaphores(3, 1),
        compiler_params=params(4),
        name="sum_latents",
    )(part.reshape(2, *half)).reshape(rows, columns)


def weight_grads_kernel(n_dp, d_part, o_part, q_part, kv_part, small, stats, d_full, o_sum, q_sum, kv_sum, small_full, *rest):
    d_block, small_block, stats_block = rest[:3]
    bufs = rest[3:15]
    small_in, stats_in = rest[15:17]
    send, recv, local = rest[17:]
    links = Links(n_dp)
    copies = Copies(send, recv, local)
    links.meet()

    def small_stream():
        n_high = links.n_high
        low_in = copies.go(
            small.at[:, 1 - links.low], small_in.at[pl.ds(0, n_high)], links.over_low()
        )
        stats_low = copies.go(stats, stats_in.at[0], links.over_low())
        yield
        low_in.wait_recv()
        stats_low.wait_recv()
        for k in range(n_high):
            small_in[k] = small_in[k] + small[k, links.low]
        stats_block[...] = stats[...] + stats_in[0]
        waits = []
        for k in range(1, n_high):
            there = links.ahead(k)
            waits.append(
                copies.go(
                    small_in.at[there], small_in.at[n_high + k - 1], links.device(high=there)
                )
            )
            waits.append(copies.go(stats_block, stats_in.at[k], links.device(high=there)))
        yield
        for wait in waits:
            wait.wait_recv()
        total = small_in[links.high]
        everything = stats_block[...]
        for k in range(1, n_high):
            total = total + small_in[n_high + k - 1]
            everything = everything + stats_in[k]
        small_block[0] = total
        small_block[1] = everything
        yield from tensor_gather(links, copies, small_block, small_full)

    def down_stream():
        yield from dp_scatter(links, copies, d_part, bufs[:3], d_block)
        yield from tensor_gather(links, copies, d_block, d_full)

    take_turns(
        down_stream(),
        dp_scatter(links, copies, q_part, bufs[6:9], q_sum),
        dp_scatter(links, copies, kv_part, bufs[9:12], kv_sum),
        dp_scatter(links, copies, o_part, bufs[3:6], o_sum),
        small_stream(),
    )
    copies.finish()


def sum_weight_grads(n_dp, down, o_t, q_up, kv_up, small, stats):
    n_high = n_dp // 2

    def parts(array):
        return array.reshape(n_high, 2, array.shape[0] // n_dp, *array.shape[1:])

    down, o_t, q_up, kv_up = parts(down), parts(o_t), parts(q_up), parts(kv_up)
    small = small.reshape(n_high, 2, *small.shape[1:])
    count = 4 * (2 * n_high - 1) + 2 * n_high + 6
    d_shape, o_shape, q_shape, kv_shape = (a.shape[2:] for a in (down, o_t, q_up, kv_up))
    one = stats.shape
    return pl.pallas_call(
        functools.partial(weight_grads_kernel, n_dp),
        out_shape=(
            jax.ShapeDtypeStruct((4, *d_shape), BF),
            jax.ShapeDtypeStruct(o_shape, F32),
            jax.ShapeDtypeStruct(q_shape, F32),
            jax.ShapeDtypeStruct(kv_shape, F32),
            jax.ShapeDtypeStruct((4, 2, *one), F32),
        ),
        in_specs=[VMEM] * 6,
        out_specs=[VMEM] * 5,
        scratch_shapes=[
            pltpu.VMEM(d_shape, BF),
            pltpu.VMEM((2, *one), F32),
            pltpu.VMEM(one, F32),
            *dp_scatter_scratch(n_high, d_shape),
            *dp_scatter_scratch(n_high, o_shape),
            *dp_scatter_scratch(n_high, q_shape),
            *dp_scatter_scratch(n_high, kv_shape),
            pltpu.VMEM((2 * n_high - 1, *one), F32),
            pltpu.VMEM((n_high, *one), F32),
            *semaphores(count, 2),
        ],
        compiler_params=params(5),
        name="sum_weight_grads",
    )(down, o_t, q_up, kv_up, small, stats)


def attention_mask(seg_row, valid_row):
    length = seg_row.shape[1]
    row = lax.broadcasted_iota(jnp.int32, (length, length), 0)
    column = lax.broadcasted_iota(jnp.int32, (length, length), 1)
    segments = jnp.broadcast_to(seg_row[...].astype(F32), (length, length))
    allowed = (
        (segments == segments.T)
        & (column <= row)
        & ((valid_row[...] == 1) | (column == row))
    )
    return jnp.where(allowed, 0.0, NEGATIVE)


def swap_halves(values):
    half = values.shape[1] // 2
    return jnp.concatenate([values[:, half:], values[:, :half]], axis=1)


def turn(values, cos_full, sin_full):
    return values * cos_full + swap_halves(values) * sin_full


def head_probs(query, key, bias, inv_root):
    scores = dot_nt(query, key) * inv_root + bias
    weights = jnp.exp(scores - jnp.max(scores, axis=-1, keepdims=True))
    return weights / jnp.sum(weights, axis=-1, keepdims=True)


def latent_rows(x, gain_attn, down, normed, latents):
    stream = x[...].astype(F32)
    normed[...] = (stream * inverse_rms(stream) * gain_attn).astype(BF)
    latents[...] = dot(normed[...], down)


def attend_rows(
    gain_q, gain_kv, q_up, kv_up, bias, cos_full, sin_full, latents, q_normed, kv_normed, q_rows, kv_rows, key_rot, mixed,
):
    rank_q = gain_q.shape[1]
    q_latent = latents[:, :rank_q]
    q_normed[...] = (q_latent * inverse_rms(q_latent) * gain_q).astype(BF)
    kv_latent = latents[:, rank_q : rank_q + KR]
    kv_normed[...] = (kv_latent * inverse_rms(kv_latent) * gain_kv).astype(BF)
    turned = turn(latents[:, rank_q + KR : rank_q + KR + ROPE], cos_full[...], sin_full[...])
    key_rot[...] = turned.astype(BF)
    kv_rows[...] = dot(kv_normed[...], kv_up).astype(BF)
    q_heads = dot(q_normed[...], q_up)
    inv_root = 1.0 / math.sqrt(NOPE + ROPE)
    for head in range(q_rows.shape[1] // (NOPE + ROPE)):
        base = head * (NOPE + ROPE)
        query = jnp.concatenate(
            [
                q_heads[:, base : base + NOPE],
                turn(
                    q_heads[:, base + NOPE : base + NOPE + ROPE], cos_full[...], sin_full[...]
                ),
            ],
            axis=1,
        ).astype(BF)
        q_rows[:, base : base + NOPE + ROPE] = query
        start = head * (NOPE + VD)
        key = jnp.concatenate([kv_rows[:, start : start + NOPE], key_rot[...]], axis=1)
        value = kv_rows[:, start + NOPE : start + NOPE + VD]
        probs = head_probs(query, key, bias, inv_root).astype(BF)
        mixed[:, head * VD : head * VD + VD] = dot(probs, value).astype(BF)


def attend_kernel(
    x, gain_attn, gain_q, gain_kv, down, q_up, kv_up, seg_row, valid_row, cos_full, sin_full,
    normed, *outs,
):
    latent_rows(x, gain_attn[...], down[...], normed, outs[0])
    attend_rows(
        gain_q[...], gain_kv[...], q_up[...], kv_up[...], attention_mask(seg_row, valid_row),
        cos_full, sin_full, *outs,
    )


def attend(x, gain_attn, gain_q, gain_kv, down, q_up, kv_up, segments, valid, cos_full, sin_full):
    length = x.shape[0]
    heads = q_up.shape[1] // (NOPE + ROPE)

    def rows(columns, kind):
        return jax.ShapeDtypeStruct((length, columns), kind)

    return pl.pallas_call(
        attend_kernel,
        out_shape=(
            rows(x.shape[1], BF),
            rows(down.shape[1], F32),
            rows(q_up.shape[0], BF),
            rows(kv_up.shape[0], BF),
            rows(q_up.shape[1], BF),
            rows(kv_up.shape[1], BF),
            rows(ROPE, BF),
            rows(heads * VD, BF),
        ),
        in_specs=[VMEM] * 11,
        out_specs=[VMEM] * 8,
        compiler_params=pltpu.CompilerParams(vmem_limit_bytes=VMEM_BYTES),
        name="attend",
    )(
        x,
        gain_attn[None, :],
        gain_q[None, :],
        gain_kv[None, :],
        down,
        q_up,
        kv_up,
        segments[None, :],
        valid[None, :],
        cos_full,
        sin_full,
    )


def later(stream, turns):
    for _ in range(turns):
        yield
    yield from stream


class Swap:
    def __init__(self, links, copies, blocks, out):
        self.me = links.high * 2 + links.low
        self.copies, self.blocks, self.out = copies, blocks, out
        self.own = copies.near(blocks.at[self.me], out.at[self.me])
        self.arrive = []

    def send(self, steps):
        n_dp = self.blocks.shape[0]
        for k in steps:
            there = (self.me + k) % n_dp
            self.arrive.append(
                self.copies.go(self.blocks.at[there], self.out.at[self.me], {"dp": there})
            )

    def finish(self):
        for copy in self.arrive:
            copy.wait_recv()
        self.own.wait()

    def sent(self):
        for copy in self.arrive:
            self.copies.sent(copy)


def pack_stream(w_gate, w_up, w_down_t, packed):
    n_dp, width, lanes = packed.shape
    slice_ff = w_gate.shape[1] // n_dp
    for k in range(n_dp):
        at = k * slice_ff
        packed[k] = jnp.concatenate(
            [
                w_gate[:, at : at + slice_ff],
                w_up[:, at : at + slice_ff],
                w_down_t[:, at : at + slice_ff],
                jnp.zeros((width, lanes - 3 * slice_ff), BF),
            ],
            axis=1,
        )
        yield


def quarter_of(values, rank):
    rows = values.shape[0] // 4
    mine = values[:rows]
    for other in range(1, 4):
        mine = jnp.where(rank == other, values[other * rows : other * rows + rows], mine)
    return mine


def forward_kernel(
    n_dp, x, cotangent, q_down, kv_down_t, gain_attn, gain_q, gain_kv, gain_mlp, q_up, kv_up, o_t,
    w_gate, w_up, w_down_t, seg_row, valid_row, turns,
    f_down, f_o, f_q, f_kv, f_g, m_part, g_part, w_grads,
    normed, latents, q_normed, kv_normed, q_rows, kv_rows, key_rot, mixed, resid, branch, cot,
    down, gains, packed, f_w, f_cot, f_normed, hidden_all, both_all, m_block, g_block,
    part, from_core, out_side, from_side, block, send, recv, local,
):
    links = Links(n_dp)
    copies = Copies(send, recv, local)
    cos_full, sin_full = turns[:, :ROPE], turns[:, ROPE:]
    rank = links.side * 2 + links.core
    rows_down, rank_q = down.shape[0], q_down.shape[1]
    quarter = pl.ds(pl.multiple_of(rank * rows_down, 16), rows_down)
    down[:, :rank_q] = q_down[quarter, :]
    kv_rows_down = quarter_of(kv_down_t[...].T, rank)
    pad = down.shape[1] - rank_q - kv_rows_down.shape[1]
    down[:, rank_q:] = jnp.concatenate([kv_rows_down, jnp.zeros((rows_down, pad), BF)], axis=1)
    lanes = gains.shape[1]
    gain_rows = [
        jnp.concatenate([g[...].astype(F32), jnp.zeros((1, lanes - g.shape[1]), F32)], axis=1)
        for g in (gain_attn, gain_q, gain_kv, gain_mlp)
    ]
    gains[...] = jnp.concatenate(gain_rows + [jnp.zeros((12, lanes), F32)], axis=0).astype(BF)
    rows = block.shape[0]
    own_rows = pl.ds(pl.multiple_of(rank * rows, 16), rows)
    cot[...] = cotangent[own_rows, :]
    links.meet(swap=True)
    downs = EveryGather(links, copies, down, f_down, down.shape[1])
    small_gathers = [
        DpGather(links, copies, source, target)
        for source, target in ((gains, f_g), (q_up, f_q), (kv_up, f_kv))
    ]
    o = DpGather(links, copies, o_t, f_o)
    cots = EveryGather(links, copies, cot, f_cot)
    downs.start()
    for work in small_gathers:
        work.start()
    n_high = links.n_high
    downs.first(0)
    for work in small_gathers:
        work.own_low()
    for i in range(1, n_high):
        downs.first(i)
        downs.second(i - 1)
    for i in range(n_high - 1):
        for work in small_gathers:
            work.step(i)
    o.start()
    o.own_low()
    downs.second(n_high - 1)
    for _ in pack_stream(w_gate, w_up, w_down_t, packed):
        pass
    swap = Swap(links, copies, packed, f_w)
    for i in range(n_high):
        downs.third(i)
    for i in range(n_high):
        downs.fourth(i)
    small_gathers[0].finish()

    def gain_of(row, count):
        return jnp.concatenate(
            [f_g[k].astype(F32)[row : row + 1, :count] for k in range(n_dp)], axis=1
        )

    width = o_t.shape[0]
    full_down = f_down[...].reshape(n_dp * width, down.shape[1])
    latent_rows(x, gain_of(0, width), full_down, normed, latents)
    for work in small_gathers[1:]:
        work.finish()
    full_q = f_q[...].reshape(n_dp * q_up.shape[0], q_up.shape[1])
    full_kv = f_kv[...].reshape(n_dp * kv_up.shape[0], kv_up.shape[1])
    o.step(0)
    attend_rows(
        gain_of(1, q_up.shape[0]), gain_of(2, kv_up.shape[0]), full_q, full_kv,
        attention_mask(seg_row, valid_row), cos_full, sin_full,
        latents, q_normed, kv_normed, q_rows, kv_rows, key_rot, mixed,
    )
    for i in range(1, n_high - 1):
        o.step(i)
    cots.start()
    cots.first(0)
    swap.send(range(2, n_dp, 2))
    swap.send(range(1, n_dp, 2))
    o.finish()
    full_o = f_o[...].reshape(n_dp * width, o_t.shape[1])
    attn_part = dot_nt(mixed[...], full_o).astype(BF)
    for side in range(2):
        for core in range(2):
            at = (side * 2 + core) * rows
            part[side, core] = attn_part[at : at + rows]
    over = copies.go(part.at[:, 1 - links.core], from_core, links.over_core())
    over.wait_recv()
    out_side[...] = (
        part[1 - links.side, links.core].astype(F32) + from_core[1 - links.side].astype(F32)
    ).astype(BF)
    over = copies.go(out_side, from_side, links.over_side())
    mine = part[links.side, links.core].astype(F32) + from_core[links.side].astype(F32)
    over.wait_recv()
    attn = RESIDUAL_SCALE * (mine + from_side[...].astype(F32))
    stream = x[own_rows, :].astype(F32) + attn
    branch[...] = attn
    resid[...] = stream
    block[...] = (stream * inverse_rms(stream) * gain_of(3, width)).astype(BF)
    normeds = EveryGather(links, copies, block, f_normed)
    normeds.start()
    normeds.first(0)
    for i in range(n_high + 2):
        if 1 <= i < n_high:
            cots.first(i)
        if 0 <= i - 1 < n_high:
            cots.second(i - 1)
        if 0 <= i - 2:
            cots.third(i - 2)
    normeds.second(0)
    for i in range(n_high):
        cots.fourth(i)
    swap.finish()
    cots.sent()
    normeds.third(0)
    normeds.fourth(0)

    lanes = f_w.shape[2]
    slice_ff = w_gate.shape[1] // n_dp
    wide = both_all.shape[1]
    cut = lanes - hidden_all.shape[1]
    before = 2 * slice_ff - cut
    columns = x.shape[1]
    tokens = 2 * x.shape[0]
    stores = []

    def zeros(count):
        return jnp.zeros((tokens, count), F32)

    def feed_forward_of(high):
        pair = pl.ds(high * 2, 2)
        at = pl.ds(pl.multiple_of(high * tokens, 128), tokens)
        w_in = f_w[:, :, :wide].reshape(columns, wide)
        w_out = f_w[:, :, cut:].reshape(columns, lanes - cut)
        grad_mlp = (RESIDUAL_SCALE * f_cot[pair].astype(F32)).astype(BF)
        f_cot[pair] = grad_mlp
        both = dot(f_normed[pair].reshape(tokens, columns), w_in)
        gate, upper = both[:, :slice_ff], both[:, slice_ff : 2 * slice_ff]
        sigma = jax.nn.sigmoid(gate)
        swish = gate * sigma
        after = lanes - cut - before - slice_ff
        hidden = jnp.concatenate([zeros(before), swish * upper, zeros(after)], axis=1).astype(BF)
        grad_hidden = dot(grad_mlp.reshape(tokens, columns), w_out)[:, before : before + slice_ff]
        grad_both = jnp.concatenate(
            [
                grad_hidden * upper * (sigma * (1.0 + gate * (1.0 - sigma))),
                grad_hidden * swish,
                zeros(wide - 2 * slice_ff),
            ],
            axis=1,
        ).astype(BF)
        hidden_all[at, :] = hidden
        both_all[at, :] = grad_both
        while stores:
            stores.pop().wait()
        m_block[...] = dot_nt(hidden, w_out).astype(BF).reshape(m_block.shape)
        stores.append(copies.near(m_block, m_part.at[pair]))
        g_block[...] = dot_nt(grad_both, w_in).astype(BF).reshape(g_block.shape)
        stores.append(copies.near(g_block, g_part.at[pair]))

    for i in range(1, n_high):
        normeds.first(i)
        if i == 1:
            feed_forward_of(normeds.line.source(0))
        normeds.second(i)
        normeds.third(i)
        if i > 1:
            feed_forward_of(normeds.line.source(i - 1))
        normeds.fourth(i)
    feed_forward_of(normeds.line.source(n_high - 1))
    swap.sent()
    all_tokens = n_dp * x.shape[0]
    for k in range(n_dp):
        at = k * width
        slab_in = dot_tn(
            f_normed[:, :, :, at : at + width].reshape(all_tokens, width), both_all[...]
        )
        slab_out = dot_tn(
            f_cot[:, :, :, at : at + width].reshape(all_tokens, width), hidden_all[...]
        )
        packed[k, :, :cut] = slab_in[:, :cut].astype(BF)
        packed[k, :, cut:wide] = (slab_in[:, cut:] + slab_out[:, : wide - cut]).astype(BF)
        packed[k, :, wide:] = slab_out[:, wide - cut :].astype(BF)
        stores.append(copies.near(packed.at[k], w_grads.at[k]))
    while stores:
        stores.pop().wait()
    copies.finish()


def forward(
    n_dp, x, cotangent, q_down, kv_down_t, gains, q_up, kv_up, o_t, w_gate, w_up, w_down_t,
    segments, valid, turns, down_shape, gain_lanes,
):
    n_high = n_dp // 2
    length, columns = x.shape
    rows = length // 4
    slice_ff = w_gate.shape[1] // n_dp
    lanes = -(-3 * slice_ff // 128) * 128
    wide = -(-2 * slice_ff // 128) * 128
    cut = 2 * slice_ff // 128 * 128
    heads = q_up.shape[1] // (NOPE + ROPE)
    count = 3 * count_every_gather(n_high) + 4 * count_dp_gather(n_high) + n_dp + 1
    block = (rows, columns)

    def over(block, *lead, kind=BF):
        return jax.ShapeDtypeStruct((*lead, *block), kind)

    return pl.pallas_call(
        functools.partial(forward_kernel, n_dp),
        out_shape=(
            over(down_shape, n_dp, 4),
            over(o_t.shape, n_dp),
            over(q_up.shape, n_dp),
            over(kv_up.shape, n_dp),
            over((16, gain_lanes), n_dp),
            over(block, n_dp, 4),
            over(block, n_dp, 4),
            over((w_gate.shape[0], lanes), n_dp),
            over((columns,), length),
            over((down_shape[1],), length, kind=F32),
            over((q_up.shape[0] * n_dp,), length),
            over((kv_up.shape[0] * n_dp,), length),
            over((q_up.shape[1],), length),
            over((kv_up.shape[1],), length),
            over((ROPE,), length),
            over((heads * VD,), length),
            over(block, kind=F32),
            over(block, kind=F32),
            over(block),
        ),
        in_specs=[VMEM] * 17,
        out_specs=[VMEM] * 5 + [ANY] * 3 + [VMEM] * 11,
        scratch_shapes=[
            pltpu.VMEM(down_shape, BF),
            pltpu.VMEM((16, gain_lanes), BF),
            pltpu.VMEM((n_dp, w_gate.shape[0], lanes), BF),
            pltpu.VMEM((n_dp, w_gate.shape[0], lanes), BF),
            pltpu.VMEM((n_dp, 4, *block), BF),
            pltpu.VMEM((n_dp, 4, *block), BF),
            pltpu.VMEM((n_dp * length, lanes - cut), BF),
            pltpu.VMEM((n_dp * length, wide), BF),
            pltpu.VMEM((2, 4, *block), BF),
            pltpu.VMEM((2, 4, *block), BF),
            pltpu.VMEM((2, 2, *block), BF),
            pltpu.VMEM((2, *block), BF),
            pltpu.VMEM(block, BF),
            pltpu.VMEM(block, BF),
            pltpu.VMEM(block, BF),
            *semaphores(count, 8 + 2 * n_high + n_dp),
        ],
        compiler_params=params(7, 62),
        name="forward",
    )(
        x, cotangent, q_down, kv_down_t, *(g[None, :] for g in gains), q_up, kv_up, o_t,
        w_gate, w_up, w_down_t, segments[None, :], valid[None, :], turns,
    )


def feed_forward_kernel(slice_ff, normed, cot, weights, m_part, g_part, grads, sum_in, sum_out):
    step = pl.program_id(0)
    cut = slice_ff * 2 // 128 * 128
    pad = slice_ff * 2 - cut
    w_in, w_out = weights[:, : sum_in.shape[0]], weights[:, cut:]
    rows = normed.shape[0]
    both = dot(normed[...], w_in)
    gate, upper = both[:, :slice_ff], both[:, slice_ff : 2 * slice_ff]
    sigma = jax.nn.sigmoid(gate)
    swish = gate * sigma

    def zeros(count):
        return jnp.zeros((rows, count), F32)

    def placed(hidden):
        rest = w_out.shape[1] - pad - slice_ff
        return jnp.concatenate([zeros(pad), hidden, zeros(rest)], axis=1).astype(BF)

    hidden = placed(swish * upper)
    m_part[...] = dot_nt(hidden, w_out).astype(BF)
    grad_mlp = (RESIDUAL_SCALE * cot[...].astype(F32)).astype(BF)
    grad_hidden = dot(grad_mlp, w_out)[:, pad : pad + slice_ff]
    grad_both = jnp.concatenate(
        [
            grad_hidden * upper * (sigma * (1.0 + gate * (1.0 - sigma))),
            grad_hidden * swish,
            zeros(w_in.shape[1] - 2 * slice_ff),
        ],
        axis=1,
    ).astype(BF)
    g_part[...] = dot_nt(grad_both, w_in).astype(BF)

    @pl.when(step == 0)
    def _():
        sum_in[...] = dot_tn(grad_both, normed[...])
        sum_out[...] = dot_tn(hidden, grad_mlp)

    @pl.when(step > 0)
    def _():
        sum_in[...] += dot_tn(grad_both, normed[...])
        sum_out[...] += dot_tn(hidden, grad_mlp)

    @pl.when(step == pl.num_programs(0) - 1)
    def _():
        mid = sum_in.shape[0]
        if cut:
            grads[:, :cut] = sum_in[:cut].T.astype(BF)
        grads[:, cut:mid] = (sum_in[cut:] + sum_out[: mid - cut]).T.astype(BF)
        grads[:, mid:] = sum_out[mid - cut :].T.astype(BF)


def feed_forward(normed, cot, weights, slice_ff, rows):
    tokens, columns = normed.shape
    lanes = weights.shape[1]
    cut = slice_ff * 2 // 128 * 128
    wide = -(-slice_ff * 2 // 128) * 128
    token_block = pl.BlockSpec((rows, columns), lambda i: (i, 0))
    whole = pl.BlockSpec((columns, lanes), lambda i: (0, 0))
    part = jax.ShapeDtypeStruct((tokens, columns), BF)
    return pl.pallas_call(
        functools.partial(feed_forward_kernel, slice_ff),
        grid=(tokens // rows,),
        out_shape=(part, part, jax.ShapeDtypeStruct((columns, lanes), BF)),
        in_specs=[token_block, token_block, whole],
        out_specs=[token_block, token_block, whole],
        scratch_shapes=[
            pltpu.VMEM((wide, columns), F32),
            pltpu.VMEM((lanes - cut, columns), F32),
        ],
        compiler_params=pltpu.CompilerParams(vmem_limit_bytes=VMEM_BYTES),
        name="feed_forward",
    )(normed, cot, weights)


def attend_back_kernel(
    grad_attn, mixed, o_t, q_rows, kv_rows, key_rot, q_normed, kv_normed, q_up, kv_up,
    seg_row, valid_row, cos_full, sin_full,
    grad_latents, grad_o, grad_q_up, grad_kv_up, grad_q, grad_kv,
):
    rank_q = q_up.shape[0]
    grad_o[...] = dot_tn(grad_attn[...], mixed[...]).astype(BF)
    grad_mixed = dot(grad_attn[...], o_t[...]).astype(BF)
    bias = attention_mask(seg_row, valid_row)
    inv_root = 1.0 / math.sqrt(NOPE + ROPE)
    grad_rot = jnp.zeros((grad_attn.shape[0], ROPE), F32)
    for head in range(q_rows.shape[1] // (NOPE + ROPE)):
        base = head * (NOPE + ROPE)
        start = head * (NOPE + VD)
        query = q_rows[:, base : base + NOPE + ROPE]
        key = jnp.concatenate([kv_rows[:, start : start + NOPE], key_rot[...]], axis=1)
        value = kv_rows[:, start + NOPE : start + NOPE + VD]
        grad = grad_mixed[:, head * VD : head * VD + VD]
        probs = head_probs(query, key, bias, inv_root)
        grad_value = dot_tn(probs.astype(BF), grad)
        grad_probs = dot_nt(grad, value)
        inner = jnp.sum(probs * grad_probs, axis=-1, keepdims=True)
        grad_scores = (probs * (grad_probs - inner)).astype(BF)
        grad_query = dot(grad_scores, key) * inv_root
        grad_key = dot_tn(grad_scores, query) * inv_root
        grad_q[:, base : base + NOPE + ROPE] = jnp.concatenate(
            [grad_query[:, :NOPE], turn(grad_query[:, NOPE:], cos_full[...], -sin_full[...])],
            axis=1,
        ).astype(BF)
        grad_kv[:, start : start + NOPE + VD] = jnp.concatenate(
            [grad_key[:, :NOPE], grad_value], axis=1
        ).astype(BF)
        grad_rot = grad_rot + grad_key[:, NOPE:]
    grad_latents[...] = jnp.zeros_like(grad_latents)
    grad_latents[:, :rank_q] = dot_nt(grad_q[...], q_up[...]).astype(BF)
    grad_latents[:, rank_q : rank_q + KR] = dot_nt(grad_kv[...], kv_up[...]).astype(BF)
    grad_latents[:, rank_q + KR : rank_q + KR + ROPE] = turn(
        grad_rot, cos_full[...], -sin_full[...]
    ).astype(BF)
    grad_q_up[...] = dot_tn(q_normed[...], grad_q[...]).astype(BF)
    grad_kv_up[...] = dot_tn(kv_normed[...], grad_kv[...]).astype(BF)


def attend_back(
    grad_attn, mixed, o_t, q_rows, kv_rows, key_rot, q_normed, kv_normed, q_up, kv_up,
    segments, valid, cos_full, sin_full, columns_down,
):
    length = grad_attn.shape[0]

    def out(shape):
        return jax.ShapeDtypeStruct(shape, BF)

    return pl.pallas_call(
        attend_back_kernel,
        out_shape=(
            out((length, columns_down)),
            out(o_t.shape),
            out(q_up.shape),
            out(kv_up.shape),
        ),
        in_specs=[VMEM] * 14,
        out_specs=[VMEM] * 4,
        scratch_shapes=[pltpu.VMEM(q_rows.shape, BF), pltpu.VMEM(kv_rows.shape, BF)],
        compiler_params=pltpu.CompilerParams(vmem_limit_bytes=VMEM_BYTES),
        name="attend_back",
    )(
        grad_attn, mixed, o_t, q_rows, kv_rows, key_rot, q_normed, kv_normed, q_up, kv_up,
        segments[None, :], valid[None, :], cos_full, sin_full,
    )


class ScatterInto:
    def __init__(self, links, copies, bufs, result):
        self.links, self.copies, self.result = links, copies, result
        self.part, self.from_low, self.from_high = bufs
        self.order = steps_by_distance(links.n_high) + [0]
        self.low_in, self.high_in = {}, {}

    def start(self):
        for k in self.order:
            self.low_in[k] = self.copies.go(
                self.part.at[self.links.ahead(k), 1 - self.links.low],
                self.from_low.at[k],
                self.links.over_low(),
            )

    def steps(self):
        links, part = self.links, self.part
        for k in self.order:
            there = links.ahead(k)
            self.low_in[k].wait_recv()
            part[there, links.low] = (
                part[there, links.low].astype(F32) + self.from_low[k].astype(F32)
            ).astype(BF)
            if k:
                self.high_in[k] = self.copies.go(
                    part.at[there, links.low], self.from_high.at[k - 1], links.device(high=there)
                )

    def finish(self):
        total = self.part[self.links.high, self.links.low].astype(F32)
        for k in steps_by_distance(self.links.n_high):
            self.high_in[k].wait_recv()
            total = total + self.from_high[k - 1].astype(F32)
        self.result[...] = total.astype(self.result.dtype)


def scatter_into_scratch(n_high, shape):
    return [
        pltpu.VMEM((n_high, 2, *shape), BF),
        pltpu.VMEM((n_high, *shape), BF),
        pltpu.VMEM((n_high - 1, *shape), BF),
    ]


def small_stream(links, copies, small, small_in, stats, stats_in, stats_block, small_block, small_full):
    n_high = links.n_high
    low_in = copies.go(
        small.at[:, 1 - links.low], small_in.at[pl.ds(0, n_high)], links.over_low()
    )
    stats_low = copies.go(stats, stats_in.at[0], links.over_low())
    yield
    low_in.wait_recv()
    stats_low.wait_recv()
    for k in range(n_high):
        small_in[k] = small_in[k] + small[k, links.low]
    stats_block[...] = stats[...] + stats_in[0]
    waits = []
    for k in range(1, n_high):
        there = links.ahead(k)
        waits.append(
            copies.go(small_in.at[there], small_in.at[n_high + k - 1], links.device(high=there))
        )
        waits.append(copies.go(stats_block, stats_in.at[k], links.device(high=there)))
    yield
    for wait in waits:
        wait.wait_recv()
    total = small_in[links.high]
    everything = stats_block[...]
    for k in range(1, n_high):
        total = total + small_in[n_high + k - 1]
        everything = everything + stats_in[k]
    small_block[0] = total
    small_block[1] = everything
    yield from tensor_gather(links, copies, small_block, small_full)


def back_kernel(
    n_dp, g_part, m_part, w_part, resid, branch, cot, x, normed, latents, q_normed, kv_normed,
    q_rows, kv_rows, key_rot, mixed, f_down, f_o, f_q, f_kv, f_g, seg_row, valid_row,
    turns,
    block_full, grad_input, d_full, o_sum, q_sum, kv_sum, small_full, w_full,
    attn_full, grad_rows, g_rows, m_rows, grad_q, grad_kv, lat, lat_in, lat_half, lat_side,
    lat_full, d_block, small, small_in, stats, stats_in, stats_block, small_block, *rest,
):
    g_bufs, m_bufs = rest[:8], (rest[0], *rest[8:13])
    d_bufs, o_bufs, q_bufs, kv_bufs = rest[13:16], rest[16:19], rest[19:22], rest[22:25]
    links = Links(n_dp)
    copies = Copies(*rest[25:])
    links.meet(swap=True)
    cos_full, sin_full = turns[:, :ROPE], turns[:, ROPE:]
    length = x.shape[0]
    rank_q, rank_kv = q_normed.shape[1], kv_normed.shape[1]
    width = o_sum.shape[0]

    def gain_of(row, count):
        return jnp.concatenate(
            [f_g[k].astype(F32)[row : row + 1, :count] for k in range(n_dp)], axis=1
        )

    half_columns = x.shape[1] // 256 * 128
    g = EveryScatter(links, copies, g_part, g_bufs, g_rows, half_columns)
    m = EveryScatter(links, copies, m_part, m_bufs, m_rows, 0)
    swap = Swap(links, copies, w_part, w_full)
    high = range(links.n_high)
    g.start()
    swap.send(range(2, n_dp, 2))
    for i in range(links.n_high + 1):
        if i in high:
            g.first(i)
        if i - 1 in high:
            g.second(i - 1)
        if i - 2 in high:
            g.third(i - 2)
    m.start()
    swap.send(range(1, n_dp, 2))
    g.third(links.n_high - 1)
    m.first(0)
    m.first(1)
    g.finish()
    stream = resid[...]
    inv_two = inverse_rms(stream)
    unit_two = stream * inv_two
    gain_mlp = gain_of(3, width)
    grad = cot[...].astype(F32) + norm_back(g_rows[...] * gain_mlp, unit_two, inv_two)
    grad_rows[...] = (RESIDUAL_SCALE * grad).astype(BF)
    t_stream = tensor_gather(links, copies, grad_rows, attn_full)
    next(t_stream)
    m.first(2)
    m.first(3)
    mlp_gain = jnp.sum(g_rows[...] * unit_two, axis=0, keepdims=True)
    bias = attention_mask(seg_row, valid_row)
    for _ in t_stream:
        pass

    grad_attn = attn_full[...].reshape(length, x.shape[1])
    for k in range(n_dp):
        o_bufs[0][k // 2, k % 2] = dot_tn(
            grad_attn[:, k * width : k * width + width], mixed[...]
        ).astype(BF)
    o = ScatterInto(links, copies, o_bufs, o_sum)
    o.start()

    grad_mixed = dot(grad_attn, f_o[...].reshape(n_dp * width, mixed.shape[1])).astype(BF)
    inv_root = 1.0 / math.sqrt(NOPE + ROPE)
    grad_rot = jnp.zeros((length, ROPE), F32)
    for head in range(q_rows.shape[1] // (NOPE + ROPE)):
        base = head * (NOPE + ROPE)
        start = head * (NOPE + VD)
        query = q_rows[:, base : base + NOPE + ROPE]
        key = jnp.concatenate([kv_rows[:, start : start + NOPE], key_rot[...]], axis=1)
        value = kv_rows[:, start + NOPE : start + NOPE + VD]
        grad_head = grad_mixed[:, head * VD : head * VD + VD]
        probs = head_probs(query, key, bias, inv_root)
        grad_value = dot_tn(probs.astype(BF), grad_head)
        grad_probs = dot_nt(grad_head, value)
        inner = jnp.sum(probs * grad_probs, axis=-1, keepdims=True)
        grad_scores = (probs * (grad_probs - inner)).astype(BF)
        grad_query = dot(grad_scores, key) * inv_root
        grad_key = dot_tn(grad_scores, query) * inv_root
        grad_q[:, base : base + NOPE + ROPE] = jnp.concatenate(
            [grad_query[:, :NOPE], turn(grad_query[:, NOPE:], cos_full[...], -sin_full[...])],
            axis=1,
        ).astype(BF)
        grad_kv[:, start : start + NOPE + VD] = jnp.concatenate(
            [grad_key[:, :NOPE], grad_value], axis=1
        ).astype(BF)
        grad_rot = grad_rot + grad_key[:, NOPE:]

    half = length // 2
    lat[...] = jnp.zeros_like(lat)
    full_q = f_q[...].reshape(rank_q, q_rows.shape[1])
    full_kv = f_kv[...].reshape(rank_kv, kv_rows.shape[1])
    grad_turned = turn(grad_rot, cos_full[...], -sin_full[...]).astype(BF)
    for core in range(2):
        at = core * half
        lat[core, :, :rank_q] = dot_nt(grad_q[at : at + half], full_q).astype(BF)
        lat[core, :, rank_q : rank_q + rank_kv] = dot_nt(
            grad_kv[at : at + half], full_kv
        ).astype(BF)
        lat[core, :, rank_q + rank_kv : rank_q + rank_kv + ROPE] = grad_turned[at : at + half]
    over = copies.go(lat.at[1 - links.core], lat_in, links.over_core())
    rows_q = q_sum.shape[0]
    for k in range(n_dp):
        q_bufs[0][k // 2, k % 2] = dot_tn(
            q_normed[:, k * rows_q : k * rows_q + rows_q], grad_q[...]
        ).astype(BF)
    q = ScatterInto(links, copies, q_bufs, q_sum)
    q.start()
    over.wait_recv()
    lat_half[...] = (lat[links.core].astype(F32) + lat_in[...].astype(F32)).astype(BF)
    over = copies.go(lat_half, lat_side, links.over_side())
    rows_kv = kv_sum.shape[0]
    for k in range(n_dp):
        kv_bufs[0][k // 2, k % 2] = dot_tn(
            kv_normed[:, k * rows_kv : k * rows_kv + rows_kv], grad_kv[...]
        ).astype(BF)
    kv = ScatterInto(links, copies, kv_bufs, kv_sum)
    kv.start()
    over.wait_recv()
    lat_full[links.core] = (lat_half[...].astype(F32) + lat_side[...].astype(F32)).astype(BF)
    mine = lat_full.at[links.core]
    over = copies.go(mine, mine, links.over_core())
    q_latent = latents[:, :rank_q]
    inv_q = inverse_rms(q_latent)
    unit_q = q_latent * inv_q
    kv_latent = latents[:, rank_q : rank_q + rank_kv]
    inv_kv = inverse_rms(kv_latent)
    unit_kv = kv_latent * inv_kv
    over.wait_recv()
    lat_sum = lat_full[...].reshape(length, lat.shape[2]).astype(F32)
    grad_q_latent, grad_kv_latent = lat_sum[:, :rank_q], lat_sum[:, rank_q : rank_q + rank_kv]
    q_gain = jnp.sum(grad_q_latent * unit_q, axis=0, keepdims=True)
    kv_gain = jnp.sum(grad_kv_latent * unit_kv, axis=0, keepdims=True)
    grad_down = jnp.concatenate(
        [
            norm_back(grad_q_latent * gain_of(1, rows_q), unit_q, inv_q),
            norm_back(grad_kv_latent * gain_of(2, rows_kv), unit_kv, inv_kv),
            lat_sum[:, rank_q + rank_kv :],
        ],
        axis=1,
    ).astype(BF)

    rows_down = d_block.shape[0]
    m.second(0)
    m.second(1)
    copies.near(normed, g_bufs[0].at[0]).wait()
    normed_rows = g_bufs[0][0].reshape(length, x.shape[1])
    rank = links.side * 2 + links.core
    for k in range(n_dp):
        rows_all = dot_tn(normed_rows[:, k * width : k * width + width], grad_down)
        d_bufs[0][k // 2, k % 2] = quarter_of(rows_all, rank).astype(BF)

    d = ScatterInto(links, copies, d_bufs, d_block)
    d.start()
    o.steps()
    m.second(2)
    m.second(3)
    grad_input[...] = dot_nt(grad_down, f_down[...].reshape(n_dp * width, grad_down.shape[1]))
    q.steps()
    kv.steps()
    for i in high:
        m.third(i)
    d.steps()
    m.finish()
    mlp = RESIDUAL_SCALE * m_rows[...]
    g_rows[...] = resid[...] + mlp
    block_gather = tensor_gather(links, copies, g_rows, block_full)
    next(block_gather)
    valid = jnp.broadcast_to((valid_row[...] == 1).astype(F32), (length, length)).T
    weights = quarter_of(valid, rank)[:, :1]
    lane = lax.broadcasted_iota(jnp.int32, stats.shape, 1)
    sums = [
        jnp.sum(jnp.sum(weights * rows * rows, axis=1, keepdims=True), axis=0, keepdims=True)
        for rows in (resid[...], branch[...], mlp)
    ] + [jnp.sum(weights, axis=0, keepdims=True)]
    packed = jnp.zeros(stats.shape, F32)
    for index, value in enumerate(sums):
        packed = jnp.where(lane == index, value, packed)
    stats[...] = packed
    stream = x[...].astype(F32)
    inv_one = inverse_rms(stream)
    unit_one = stream * inv_one
    attn_gain = jnp.sum(grad_input[...] * unit_one, axis=0, keepdims=True)
    grad_input[...] = grad_attn.astype(F32) * (1.0 / RESIDUAL_SCALE) + norm_back(
        grad_input[...] * gain_of(0, width), unit_one, inv_one
    )

    def piece(vector, k):
        count = vector.shape[1] // n_dp
        cut = vector[:, k * count : k * count + count]
        return jnp.concatenate([cut, jnp.zeros((1, small.shape[3] - count), F32)], axis=1)

    for k in range(n_dp):
        small[k // 2, k % 2] = jnp.concatenate(
            [piece(v, k) for v in (attn_gain, q_gain, kv_gain, mlp_gain)]
            + [jnp.zeros((4, small.shape[3]), F32)],
            axis=0,
        )
    small_rows = small_stream(
        links, copies, small, small_in, stats, stats_in, stats_block, small_block, small_full
    )
    next(small_rows)
    d.finish()
    down_gather = tensor_gather(links, copies, d_block, d_full)
    take_turns(small_rows, down_gather, block_gather)
    o.finish()
    q.finish()
    kv.finish()
    swap.finish()
    copies.finish()


def back(
    n_dp, g_part, m_part, w_part, resid, branch, cot, x, normed, latents, q_normed, kv_normed,
    q_rows, kv_rows, key_rot, mixed, f_down, f_o, f_q, f_kv, f_g, segments, valid, turns,
):
    n_high = n_dp // 2
    rows, columns = resid.shape
    length = x.shape[0]
    lanes = f_g.shape[2]
    half = (length // 2, latents.shape[1])
    shape = (n_high, 2, 2, 2, rows, columns)
    d_shape, o_shape, q_shape, kv_shape = f_down.shape[2:], f_o.shape[1:], f_q.shape[1:], f_kv.shape[1:]
    one = (8, lanes)
    count = 2 * (6 * n_high - 1) + 4 * (2 * n_high - 1) + 4 * 3 + (n_dp - 1) + 2 * n_high + 3

    def out(shape, kind=F32):
        return jax.ShapeDtypeStruct(shape, kind)

    return pl.pallas_call(
        functools.partial(back_kernel, n_dp),
        out_shape=(
            out((4, rows, columns)),
            out((length, columns)),
            out((4, *d_shape), BF),
            out(o_shape),
            out(q_shape),
            out(kv_shape),
            out((4, 2, *one)),
            out(w_part.shape, BF),
        ),
        in_specs=[ANY] * 3 + [VMEM] * 4 + [ANY] + [VMEM] * 15,
        out_specs=[ANY] + [VMEM] * 6 + [ANY],
        scratch_shapes=[
            pltpu.VMEM((4, rows, columns), BF),
            pltpu.VMEM((rows, columns), BF),
            pltpu.VMEM((rows, columns), F32),
            pltpu.VMEM((rows, columns), F32),
            pltpu.VMEM(q_rows.shape, BF),
            pltpu.VMEM(kv_rows.shape, BF),
            pltpu.VMEM((2, *half), BF),
            pltpu.VMEM(half, BF),
            pltpu.VMEM(half, BF),
            pltpu.VMEM(half, BF),
            pltpu.VMEM((2, *half), BF),
            pltpu.VMEM(d_shape, BF),
            pltpu.VMEM((n_high, 2, *one), F32),
            pltpu.VMEM((2 * n_high - 1, *one), F32),
            pltpu.VMEM(one, F32),
            pltpu.VMEM((n_high, *one), F32),
            pltpu.VMEM(one, F32),
            pltpu.VMEM((2, *one), F32),
            *every_scatter_scratch(n_high, rows, columns),
            *every_scatter_scratch(n_high, rows, columns, 0)[1:],
            *scatter_into_scratch(n_high, d_shape),
            *scatter_into_scratch(n_high, o_shape),
            *scatter_into_scratch(n_high, q_shape),
            *scatter_into_scratch(n_high, kv_shape),
            *semaphores(count, 2 * n_high + 6),
        ],
        compiler_params=params(8, 62),
        name="back",
    )(
        g_part.reshape(shape), m_part.reshape(shape), w_part, resid, branch, cot, x,
        normed.reshape(2, 2, rows, columns), latents, q_normed, kv_normed, q_rows, kv_rows, key_rot, mixed, f_down, f_o, f_q, f_kv, f_g,
        segments[None, :], valid[None, :], turns,
    )


def unpack_kernel(
    slice_ff, rank_q, swapped, down, o_in, q_in, kv_in, block_in, input_in, small,
    grad_gate, grad_upper, grad_down_t, grad_o_t, grad_q_down, grad_kv_down_t, grad_q_up, grad_kv_up,
    block_out, grad_input,
    attn_gain, q_gain, kv_gain, mlp_gain, stats,
):
    n_dp = swapped.shape[0]

    def pieces(start):
        return jnp.concatenate(
            [swapped[k, :, start : start + slice_ff] for k in range(n_dp)], axis=1
        ).astype(F32)

    grad_gate[...] = pieces(0)
    grad_upper[...] = pieces(slice_ff)
    grad_down_t[...] = pieces(2 * slice_ff)
    for target, source in (
        (grad_o_t, o_in), (grad_q_up, q_in), (grad_kv_up, kv_in), (block_out, block_in), (grad_input, input_in),
    ):
        target[...] = source[...]
    rows = down[...].reshape(grad_q_down.shape[0], down.shape[2]).astype(F32)
    grad_q_down[...] = rows[:, :rank_q]
    grad_kv_down_t[...] = rows[:, rank_q : rank_q + grad_kv_down_t.shape[0]].T
    gains = small[0, 0]
    for row, gain in ((0, attn_gain), (1, q_gain), (2, kv_gain)):
        gain[...] = gains[row : row + 1, : gain.shape[1]]
    total = small[0, 0] + small[1, 0] + small[2, 0] + small[3, 0]
    mlp_gain[...] = total[3:4, : mlp_gain.shape[1]]
    sums = (small[0, 1] + small[1, 1] + small[2, 1] + small[3, 1])[0:1]
    stats[...] = jnp.sqrt(sums[:, :3] / (sums[:, 3:4] * D))


def unpack(swapped, down, o_t, q_up, kv_up, block, grad_input, small, slice_ff, rank_q, columns_down, gains):
    n_dp, width, _ = swapped.shape

    def out(*shape):
        return jax.ShapeDtypeStruct(shape, F32)

    return pl.pallas_call(
        functools.partial(unpack_kernel, slice_ff, rank_q),
        out_shape=(
            out(width, n_dp * slice_ff),
            out(width, n_dp * slice_ff),
            out(width, n_dp * slice_ff),
            out(*o_t.shape),
            out(width, rank_q),
            out(columns_down - rank_q, width),
            out(*q_up.shape),
            out(*kv_up.shape),
            out(*block.shape),
            out(*grad_input.shape),
            *(out(1, gain.shape[0]) for gain in gains),
            out(1, 3),
        ),
        in_specs=[VMEM] * 8,
        out_specs=[VMEM] * 15,
        compiler_params=pltpu.CompilerParams(vmem_limit_bytes=VMEM_BYTES),
        name="unpack",
    )(swapped, down, o_t, q_up, kv_up, block, grad_input, small)


def per_device(
    layer_input,
    segment_ids,
    valid_mask,
    cotangent,
    attn_gain,
    q_down,
    q_gain,
    q_up,
    kv_down,
    kv_gain,
    kv_up,
    o_proj,
    mlp_gain,
    w_gate,
    w_up,
    w_down,
):
    length = layer_input.shape[0]
    n_dp = lax.axis_size("dp")
    n_tensor = lax.axis_size("tensor")
    share = length // n_tensor
    me = lax.axis_index("tensor")
    width = w_gate.shape[0]
    slice_ff = w_gate.shape[1] // n_dp
    rows_down = width // n_tensor

    def rows_of(values, count):
        return lax.dynamic_slice_in_dim(values, me * count, count, 0)

    rank_q = q_down.shape[1]
    columns_down = rank_q + kv_down.shape[1]
    pad_down = -columns_down % 128
    down_rows = jnp.concatenate(
        [
            rows_of(q_down, rows_down),
            rows_of(kv_down, rows_down),
            jnp.zeros((rows_down, pad_down), BF),
        ],
        axis=1,
    )
    lanes = -(-width // 128) * 128

    def lane_rows(rows, count, kind):
        padded = [jnp.pad(row.astype(kind), (0, lanes - row.shape[0])) for row in rows]
        return jnp.stack(padded + [jnp.zeros((lanes,), kind)] * (count - len(padded)))

    cot_rows = rows_of(cotangent, share)
    x_rows = rows_of(layer_input, share)
    gains_block = lane_rows([attn_gain, q_gain, kv_gain, mlp_gain], 16, BF)
    cosine, sine_table = rope_tables(length, ROPE)
    cos_full = jnp.concatenate([cosine, cosine], axis=1)
    sin_full = jnp.concatenate([-sine_table, sine_table], axis=1)
    fused = n_dp == 8 and rows_down % 16 == 0 and q_up.shape[0] % 16 == 0
    if fused:
        (
            f_down, f_o, f_q, f_kv, f_g, mlp_part, normed_part, grad_packed,
            normed, latents, q_normed, kv_normed, q_rows, kv_rows, key_rot, mixed,
            resid_rows, attn_rows, cot_rows,
        ) = forward(
            n_dp, layer_input, cotangent, q_down, kv_down.T, (attn_gain, q_gain, kv_gain, mlp_gain),
            q_up, kv_up, o_proj.T, w_gate, w_up, w_down.T, segment_ids, valid_mask,
            jnp.concatenate([cos_full, sin_full], axis=1), down_rows.shape, lanes,
        )
    else:
        f_down, f_o, f_q, f_kv, f_g, f_cot = gather_weights(
            n_dp, n_tensor, down_rows, o_proj.T, q_up, kv_up, gains_block, cot_rows
        )
    full_down = f_down.reshape(n_dp * width, columns_down + pad_down)
    full_o = f_o.reshape(n_dp * width, -1)

    def gain_of(row, gain):
        return f_g[:, row, : gain.shape[0]].reshape(-1).astype(F32)

    gain_attn = gain_of(0, attn_gain)
    gain_q = gain_of(1, q_gain)
    gain_kv = gain_of(2, kv_gain)
    gain_mlp = gain_of(3, mlp_gain)
    if not fused:
        packed = jnp.concatenate(
            [
                w_gate.reshape(width, n_dp, slice_ff),
                w_up.reshape(width, n_dp, slice_ff),
                w_down.T.reshape(width, n_dp, slice_ff),
                jnp.zeros((width, n_dp, -3 * slice_ff % 128), BF),
            ],
            axis=2,
        ).transpose(1, 0, 2)
        packed, f_q = lax.optimization_barrier((packed, f_q))
        f_w = swap_dp(packed)
    full_q_up = f_q.reshape(-1, q_up.shape[1])
    full_kv_up = f_kv.reshape(-1, kv_up.shape[1])
    if not fused:
        normed, latents, q_normed, kv_normed, q_rows, kv_rows, key_rot, mixed = attend(
            layer_input, gain_attn, gain_q, gain_kv, full_down, full_q_up, full_kv_up,
            segment_ids, valid_mask, cos_full, sin_full,
        )
        f_normed, resid_rows, attn_rows = attention_residual(
            n_dp, dot_nt(mixed, full_o).astype(BF), x_rows, gain_mlp[None, :]
        )
    if not fused:
        mlp_part, normed_part, grad_packed = feed_forward(
            f_normed.reshape(n_dp * length, -1),
            f_cot.reshape(n_dp * length, -1),
            f_w.reshape(n_dp * width, -1),
            slice_ff,
            length,
        )
    weight_rows = rows_of(valid_mask.astype(F32)[:, None], share)
    if fused:
        f_block, grad_input, s_down, s_o, s_q, s_kv, s_small, swapped = back(
            n_dp, normed_part, mlp_part, grad_packed.reshape(n_dp, width, -1), resid_rows, attn_rows,
            cot_rows, layer_input, normed, latents, q_normed, kv_normed, q_rows, kv_rows,
            key_rot, mixed, f_down, f_o, f_q, f_kv, f_g, segment_ids, valid_mask,
            jnp.concatenate([cos_full, sin_full], axis=1),
        )
        (
            grad_w_gate, grad_w_up, grad_down_t, grad_o_t, grad_q_down, grad_kv_down_t, grad_q_up,
            grad_kv_up, block_full, grad_input, grad_attn_gain, grad_q_gain, grad_kv_gain, grad_mlp_gain, rms_stats,
        ) = unpack(
            swapped, s_down, s_o, s_q, s_kv, f_block.reshape(length, -1), grad_input, s_small,
            slice_ff, rank_q, columns_down,
            (attn_gain, q_gain, kv_gain, mlp_gain),
        )
        return (
            block_full,
            grad_input,
            grad_attn_gain.reshape(-1),
            grad_q_down,
            grad_q_gain.reshape(-1),
            grad_q_up,
            grad_kv_down_t.T,
            grad_kv_gain.reshape(-1),
            grad_kv_up,
            grad_o_t.T,
            grad_mlp_gain.reshape(-1),
            grad_w_gate,
            grad_w_up,
            grad_down_t.T,
            rms_stats.reshape(-1),
        )
    else:
        inv_two = inverse_rms(resid_rows)
        unit_two = resid_rows * inv_two
        swapped = swap_dp(grad_packed.reshape(n_dp, width, -1))
        normed_part, grad_packed = lax.optimization_barrier((normed_part, grad_packed))
        f_attn, grad_normed_two, f_block, mlp_rows = residual_grads(
            n_dp, normed_part, mlp_part, resid_rows, cot_rows, gain_mlp[None, :]
        )
        grad_attn = f_attn.reshape(length, -1)
        block_full = f_block.reshape(length, -1)

        grad_mlp_gain = jnp.sum(grad_normed_two * unit_two, axis=0)

        grad_part, grad_o, grad_q_up, grad_kv_up = attend_back(
            grad_attn, mixed, full_o, q_rows, kv_rows, key_rot, q_normed, kv_normed,
            full_q_up, full_kv_up, segment_ids, valid_mask, cos_full, sin_full,
            columns_down + pad_down,
        )
        grad_part, swapped = lax.optimization_barrier((grad_part, swapped))
        grad_latents = sum_latents(n_dp, grad_part).astype(F32)
        stream = layer_input.astype(F32)
        inv_one = inverse_rms(stream)
        unit_one = stream * inv_one
        q_latent = latents[:, :rank_q]
        inv_q = inverse_rms(q_latent)
        unit_q = q_latent * inv_q
        kv_latent = latents[:, rank_q : rank_q + KR]
        inv_kv = inverse_rms(kv_latent)
        unit_kv = kv_latent * inv_kv
        grad_q_normed = grad_latents[:, :rank_q]
        grad_kv_normed = grad_latents[:, rank_q : rank_q + KR]
        grad_kv_rot = grad_latents[:, rank_q + KR : columns_down]
        grad_q_gain = jnp.sum(grad_q_normed * unit_q, axis=0)
        grad_kv_gain = jnp.sum(grad_kv_normed * unit_kv, axis=0)
        grad_down = jnp.concatenate(
            [
                norm_back(grad_q_normed * gain_q, unit_q, inv_q),
                norm_back(grad_kv_normed * gain_kv, unit_kv, inv_kv),
                grad_kv_rot,
                jnp.zeros((length, pad_down), F32),
            ],
            axis=-1,
        ).astype(BF)
        grad_normed = dot_nt(grad_down, full_down)
        grad_attn_gain = jnp.sum(grad_normed * unit_one, axis=0)
        grad_input = grad_attn.astype(F32) * (1.0 / RESIDUAL_SCALE) + norm_back(
            grad_normed * gain_attn, unit_one, inv_one
        )

        quarter = lax.dynamic_index_in_dim(
            normed.reshape(length, n_dp, n_tensor, rows_down), me, 2, keepdims=False
        ).reshape(length, n_dp * rows_down)
        def by_dp(vector):
            return vector.reshape(n_dp, -1)

        def small_rows(vectors):
            return jnp.stack(
                [jnp.pad(by_dp(v), ((0, 0), (0, lanes - v.shape[0] // n_dp))) for v in vectors]
                + [jnp.zeros((n_dp, lanes), F32)] * (8 - len(vectors)),
                axis=1,
            )

        stats = jnp.stack(
            [
                jnp.sum(weight_rows * resid_rows * resid_rows),
                jnp.sum(weight_rows * attn_rows * attn_rows),
                jnp.sum(weight_rows * mlp_rows * mlp_rows),
                jnp.sum(weight_rows),
            ]
        )
        s_down, s_o, s_q, s_kv, s_small = sum_weight_grads(
            n_dp,
            dot_tn(quarter, grad_down).astype(BF),
            grad_o,
            grad_q_up,
            grad_kv_up,
            small_rows([grad_attn_gain, grad_q_gain, grad_kv_gain, grad_mlp_gain]),
            lane_rows([stats], 8, F32),
        )

    def columns_of(part):
        return part.transpose(1, 0, 2).reshape(width, n_dp * slice_ff).astype(F32)

    grad_w_gate = columns_of(swapped[:, :, :slice_ff])
    grad_w_up = columns_of(swapped[:, :, slice_ff : 2 * slice_ff])
    grad_w_down = columns_of(swapped[:, :, 2 * slice_ff : 3 * slice_ff]).T

    d_down = s_down.reshape(width, -1).astype(F32)
    gains = s_small[me, 0]
    stat_sums = jnp.sum(s_small[:, 1, 0, :4], axis=0)
    rms_stats = jnp.sqrt(stat_sums[:3] / (stat_sums[3] * D))
    return (
        block_full,
        grad_input,
        gains[0, : attn_gain.shape[0]],
        d_down[:, :rank_q],
        gains[1, : q_gain.shape[0]],
        s_q,
        d_down[:, rank_q:columns_down],
        gains[2, : kv_gain.shape[0]],
        s_kv,
        s_o.T,
        jnp.sum(s_small[:, 0, 3], axis=0)[: mlp_gain.shape[0]],
        grad_w_gate,
        grad_w_up,
        grad_w_down,
        rms_stats,
    )


def solution(mesh):
    placed = (
        P("dp", None),
        P("dp"),
        P("dp"),
        P("dp", None),
        P("dp"),
        P("dp", None),
        P("dp"),
        P("dp", "tensor"),
        P("dp", None),
        P("dp"),
        P("dp", "tensor"),
        P("tensor", "dp"),
        P("dp"),
        P("dp", "tensor"),
        P("dp", "tensor"),
        P("tensor", "dp"),
    )
    return jax.shard_map(
        per_device,
        mesh=mesh,
        in_specs=placed,
        out_specs=(
            P("dp", None),
            P("dp", None),
            P("dp"),
            P("dp", None),
            P("dp"),
            P("dp", "tensor"),
            P("dp", None),
            P("dp"),
            P("dp", "tensor"),
            P("tensor", "dp"),
            P("dp"),
            P("dp", "tensor"),
            P("dp", "tensor"),
            P("tensor", "dp"),
            P(),
        ),
        check_vma=False,
    )
```

```python
import functools
import itertools
import math

import jax
import jax.numpy as jnp
from jax import lax
from jax.experimental import pallas as pl
from jax.experimental.pallas import tpu as pltpu
from jax.sharding import PartitionSpec as P

D = 2560
KR = 256
NOPE = 64
ROPE = 32
VD = 64


NORM_EPS = 1e-05
RESIDUAL_SCALE = 1.4 / math.sqrt(62.0)
ROPE_BASE = 10000.0
NEGATIVE = -1e30


def rope_tables(length, rot_dim):
    half_dim = rot_dim // 2
    position = jnp.arange(length, dtype=jnp.float32)
    frequency = jnp.exp(
        -math.log(ROPE_BASE) * 2.0 * jnp.arange(half_dim, dtype=jnp.float32) / rot_dim
    )
    phases = position[:, None] * frequency[None, :]
    return (jnp.cos(phases), jnp.sin(phases))


def inverse_rms(values):
    return lax.rsqrt(jnp.mean(values * values, axis=-1, keepdims=True) + NORM_EPS)


def norm_back(grad_unit, unit, inv_rms):
    return inv_rms * (grad_unit - unit * jnp.mean(grad_unit * unit, axis=-1, keepdims=True))


BF = jnp.bfloat16
F32 = jnp.float32


def dot(left, right):
    return jnp.dot(left, right, preferred_element_type=F32)


def dot_nt(left, right):
    return jnp.einsum("ac,bc->ab", left, right, preferred_element_type=F32)


def dot_tn(left, right):
    return jnp.einsum("ca,cb->ab", left, right, preferred_element_type=F32)


def swap_dp(blocks):
    return lax.all_to_all(blocks, "dp", 0, 0, tiled=True)


MESH = pl.DeviceIdType.MESH
ANY = pl.BlockSpec(memory_space=pl.ANY)
VMEM = pl.BlockSpec(memory_space=pltpu.VMEM)
VMEM_BYTES = 60 * 1024 * 1024


class Links:
    def __init__(self, n_dp):
        self.n_high = n_dp // 2
        dp = lax.axis_index("dp")
        tensor = lax.axis_index("tensor")
        self.high, self.low = dp // 2, dp % 2
        self.side, self.core = tensor // 2, tensor % 2

    def device(self, high=None, low=None, side=None, core=None):
        high = self.high if high is None else high
        low = self.low if low is None else low
        side = self.side if side is None else side
        core = self.core if core is None else core
        return {"dp": high * 2 + low, "tensor": side * 2 + core}

    def behind(self, step):
        return (self.high + self.n_high - step) % self.n_high

    def ahead(self, step):
        return (self.high + step) % self.n_high

    def over_low(self):
        return self.device(low=1 - self.low)

    def over_side(self):
        return self.device(side=1 - self.side)

    def over_core(self):
        return self.device(core=1 - self.core)

    def meet(self, high=True, low=True, side=True, core=True, swap=False):
        barrier = pltpu.get_barrier_semaphore()
        partners = []
        if swap:
            partners += [
                self.device(high=self.ahead(k), low=1 - self.low) for k in range(1, self.n_high)
            ]
        if high:
            partners += [self.device(high=self.ahead(k)) for k in range(1, self.n_high)]
        if low:
            partners.append(self.over_low())
        if side:
            partners.append(self.over_side())
        if core:
            partners.append(self.over_core())
        for partner in partners:
            pl.semaphore_signal(barrier, inc=1, device_id=partner, device_id_type=MESH)
        pl.semaphore_wait(barrier, len(partners))


class Copies:
    def __init__(self, send, recv, local):
        self.send, self.recv, self.local = send, recv, local
        self.count = self.local_count = 0
        self.started = []
        self.maybe = []

    def go(self, source, target, device):
        copy = pltpu.make_async_remote_copy(
            src_ref=source,
            dst_ref=target,
            send_sem=self.send.at[self.count],
            recv_sem=self.recv.at[self.count],
            device_id=device,
            device_id_type=MESH,
        )
        self.count += 1
        copy.start()
        self.started.append(copy)
        return copy

    def sent_maybe(self):
        for condition, copy in self.maybe:
            pl.when(condition)(copy.wait_send)
        self.maybe = []

    def near(self, source, target):
        copy = pltpu.make_async_copy(source, target, self.local.at[self.local_count])
        self.local_count += 1
        copy.start()
        return copy

    def sent(self, copy):
        copy.wait_send()
        self.started = [other for other in self.started if other is not copy]

    def finish(self):
        for copy in self.started:
            copy.wait_send()
        for condition, copy in self.maybe:
            pl.when(condition)(copy.wait_send)


def take_turns(*streams):
    streams = list(streams)
    while streams:
        for stream in list(streams):
            try:
                next(stream)
            except StopIteration:
                streams.remove(stream)


def steps_by_distance(count):
    order, k = [], 1
    while len(order) < count - 1:
        order.append(k)
        if len(order) < count - 1:
            order.append(count - k)
        k += 1
    return order


class Line:
    def __init__(self, links, copies, block, target):
        self.links, self.copies, self.block, self.target = links, copies, block, target
        self.count = links.n_high
        self.first_tag = copies.count
        copies.count += self.count
        inner = steps_by_distance(self.count)
        at_start = (self.count - 1 - links.high) // (self.count - 1)
        at_end = links.high // (self.count - 1)
        self.tags = [0] + [
            at_start * (self.count - i) + at_end * i + (1 - at_start - at_end) * inner[i - 1]
            for i in range(1, self.count)
        ]

    def source(self, i):
        return (self.links.high + self.count - self.tags[i]) % self.count

    def send(self, condition, source, to, tag):
        copy = pltpu.make_async_remote_copy(
            src_ref=source,
            dst_ref=source if source is not self.block else self.target(self.links.high),
            send_sem=self.copies.send.at[self.copies.count],
            recv_sem=self.copies.recv.at[self.first_tag + tag],
            device_id=self.links.device(high=to),
            device_id_type=MESH,
        )
        self.copies.count += 1
        pl.when(condition)(copy.start)
        self.copies.maybe.append((condition, copy))

    def start(self):
        high = self.links.high
        self.send(high < self.count - 1, self.block, (high + 1) % self.count, 1)
        self.send(
            high > 0, self.block, (high + self.count - 1) % self.count, self.count - 1
        )

    def arrived(self, i):
        high, tag = self.links.high, self.tags[i]
        here = self.target(self.source(i))
        pltpu.make_async_remote_copy(
            src_ref=here,
            dst_ref=here,
            send_sem=self.copies.send.at[self.first_tag],
            recv_sem=self.copies.recv.at[self.first_tag + tag],
            device_id=self.links.over_low(),
            device_id_type=MESH,
        ).wait_recv()
        from_left = high >= tag
        onward = (from_left & (high < self.count - 1)) | ((high < tag) & (high > 0))
        way = jnp.where(from_left, 1, self.count - 1)
        self.send(onward, here, (high + way) % self.count, (tag + way) % self.count)


class Direct:
    def __init__(self, links, copies, block, target):
        self.links, self.copies, self.block, self.target = links, copies, block, target
        self.order = [0] + steps_by_distance(links.n_high)

    def source(self, i):
        return self.links.behind(self.order[i])

    def start(self):
        mine = self.target(self.links.high)
        self.arrive = [None] + [
            self.copies.go(self.block, mine, self.links.device(high=self.links.ahead(k)))
            for k in self.order[1:]
        ]

    def arrived(self, i):
        self.arrive[i].wait_recv()


def along_high(links, copies, block, target):
    return (Line if links.n_high == 4 else Direct)(links, copies, block, target)


class EveryGather:
    def __init__(self, links, copies, block, out, cut=None):
        self.links, self.copies, self.block, self.out = links, copies, block, out
        self.columns = out.shape[-1]
        self.cut = self.columns // 256 * 128 if cut is None else cut
        self.line = along_high(
            links, copies, block, lambda high: self.slot(high, links.low, links.side)
        )
        self.over_low, self.over_side = {}, {}
        self.corners = {i: [] for i in range(links.n_high)}
        self.last = {i: [] for i in range(links.n_high)}

    def slot(self, high, low, side):
        return self.out.at[high * 2 + low, side * 2 + self.links.core]

    def start(self):
        links = self.links
        self.own = self.copies.near(self.block, self.slot(links.high, links.low, links.side))
        self.line.start()

    def to_core(self, i, source, target):
        self.last[i].append(self.copies.go(source, target, self.links.over_core()))

    def first(self, i):
        links = self.links
        here = self.slot(self.line.source(i), links.low, links.side)
        if i:
            self.line.arrived(i)
        source = here if i else self.block
        self.over_low[i] = self.copies.go(source, here, links.over_low())
        self.over_side[i] = self.copies.go(source, here, links.over_side())
        self.to_core(i, source, here)

    def second(self, i):
        links, high = self.links, self.line.source(i)
        self.over_low[i].wait_recv()
        here = self.slot(high, 1 - links.low, links.side)
        if self.cut:
            half = pl.ds(0, self.cut)
            part = here.at[:, half]
            self.corners[i].append((self.copies.go(part, part, links.over_side()), half))
        self.to_core(i, here, here)
        self.over_side[i].wait_recv()
        here = self.slot(high, links.low, 1 - links.side)
        if self.cut < self.columns:
            half = pl.ds(self.cut, self.columns - self.cut)
            part = here.at[:, half]
            self.corners[i].append((self.copies.go(part, part, links.over_low()), half))
        self.to_core(i, here, here)

    def third(self, i):
        links = self.links
        here = self.slot(self.line.source(i), 1 - links.low, 1 - links.side)
        for corner, half in self.corners[i]:
            corner.wait_recv()
            part = here.at[:, half]
            self.to_core(i, part, part)

    def fourth(self, i):
        for copy in self.last[i]:
            copy.wait_recv()
        if i == 0:
            self.own.wait()

    def sent(self):
        copies = [*self.over_low.values(), *self.over_side.values()]
        copies += [corner for pairs in self.corners.values() for corner, _ in pairs]
        copies += [copy for last in self.last.values() for copy in last]
        for copy in copies:
            self.copies.sent(copy)
        self.copies.sent_maybe()


def every_gather(links, copies, block, out, cut=None):
    work = EveryGather(links, copies, block, out, cut)
    work.start()
    yield
    for i in range(links.n_high + 2):
        if i < links.n_high:
            work.first(i)
            yield
        if 0 <= i - 1 < links.n_high:
            work.second(i - 1)
            yield
        if 0 <= i - 2:
            work.third(i - 2)
            yield
    for i in range(links.n_high):
        work.fourth(i)


class DpGather:
    def __init__(self, links, copies, block, out):
        self.links, self.copies, self.block, self.out = links, copies, block, out
        self.line = along_high(links, copies, block, lambda high: out.at[high * 2 + links.low])
        self.last = []
        self.mine = out.at[links.high * 2 + links.low]

    def start(self):
        self.own = self.copies.near(self.block, self.mine)
        self.line.start()

    def own_low(self):
        self.last.append(self.copies.go(self.block, self.mine, self.links.over_low()))

    def step(self, i):
        self.line.arrived(i + 1)
        here = self.out.at[self.line.source(i + 1) * 2 + self.links.low]
        self.last.append(self.copies.go(here, here, self.links.over_low()))

    def finish(self):
        for copy in self.last:
            copy.wait_recv()
        self.own.wait()


def dp_gather(links, copies, block, out):
    work = DpGather(links, copies, block, out)
    work.start()
    yield
    work.own_low()
    yield
    for i in range(links.n_high - 1):
        work.step(i)
        yield
    work.finish()


def tensor_gather(links, copies, block, out):
    mine = out.at[links.side * 2 + links.core]
    own = copies.near(block, mine)
    last = [copies.go(block, mine, links.over_core())]
    across = copies.go(block, mine, links.over_side())
    yield
    across.wait_recv()
    here = out.at[(1 - links.side) * 2 + links.core]
    last.append(copies.go(here, here, links.over_core()))
    yield
    for copy in last:
        copy.wait_recv()
    own.wait()


class EveryScatter:
    def __init__(self, links, copies, part, bufs, result, cut):
        self.links, self.copies, self.part, self.result = links, copies, part, result
        self.own, self.chip, *bufs = bufs
        self.low_a, self.side_a = (bufs.pop(0), bufs.pop(0)) if cut else (None, None)
        self.side_b, self.low_b, self.done, self.from_high = bufs
        self.cut = cut
        self.half_a, self.half_b = pl.ds(0, cut), pl.ds(cut, part.shape[-1] - cut)
        self.order = steps_by_distance(links.n_high) + [0]
        self.loads, self.core_in, self.a_in, self.b_in = {}, {}, {}, {}
        self.a_last, self.b_last, self.high_in = {}, {}, {}

    def load(self, i):
        there = self.links.ahead(self.order[i])
        self.loads[i] = self.copies.near(
            self.part.at[there, :, :, self.links.core], self.own.at[i % 2]
        )

    def start(self):
        for i, k in enumerate(self.order):
            self.core_in[k] = self.copies.go(
                self.part.at[self.links.ahead(k), :, :, 1 - self.links.core],
                self.chip.at[k],
                self.links.over_core(),
            )
            if i < 2:
                self.load(i)

    def first(self, i):
        links, copies, chip, k = self.links, self.copies, self.chip, self.order[i]
        self.core_in[k].wait_recv()
        self.loads[i].wait()
        for low in range(2):
            for side in range(2):
                chip[k, low, side] = (
                    self.own[i % 2, low, side].astype(F32) + chip[k, low, side].astype(F32)
                ).astype(BF)
        if i + 2 < links.n_high:
            self.load(i + 2)
        if self.cut:
            self.a_in[k] = copies.go(
                chip.at[k, 1 - links.low, :, :, self.half_a], self.low_a.at[k], links.over_low()
            )
        self.b_in[k] = copies.go(
            chip.at[k, :, 1 - links.side, :, self.half_b], self.side_b.at[k], links.over_side()
        )

    def second(self, i):
        links, copies, chip, k = self.links, self.copies, self.chip, self.order[i]
        low_a, side_b = self.low_a, self.side_b
        if self.cut:
            self.a_in[k].wait_recv()
            for side in range(2):
                low_a[k, side] = (
                    low_a[k, side].astype(F32)
                    + chip[k, links.low, side, :, self.half_a].astype(F32)
                ).astype(BF)
            self.a_last[k] = copies.go(
                low_a.at[k, 1 - links.side], self.side_a.at[k], links.over_side()
            )
        self.b_in[k].wait_recv()
        for low in range(2):
            side_b[k, low] = (
                side_b[k, low].astype(F32) + chip[k, low, links.side, :, self.half_b].astype(F32)
            ).astype(BF)
        self.b_last[k] = copies.go(side_b.at[k, 1 - links.low], self.low_b.at[k], links.over_low())

    def third(self, i):
        links, k = self.links, self.order[i]
        if self.cut:
            self.a_last[k].wait_recv()
            self.done[k, :, self.half_a] = (
                self.side_a[k].astype(F32) + self.low_a[k, links.side].astype(F32)
            ).astype(BF)
        self.b_last[k].wait_recv()
        self.done[k, :, self.half_b] = (
            self.low_b[k].astype(F32) + self.side_b[k, links.low].astype(F32)
        ).astype(BF)
        if k:
            self.high_in[k] = self.copies.go(
                self.done.at[k], self.from_high.at[k - 1], links.device(high=links.ahead(k))
            )

    def finish(self):
        total = self.done[0].astype(F32)
        for k in steps_by_distance(self.links.n_high):
            self.high_in[k].wait_recv()
            total = total + self.from_high[k - 1].astype(F32)
        self.result[...] = total


def every_scatter(links, copies, part, bufs, result):
    work = EveryScatter(links, copies, part, bufs, result, part.shape[-1] // 256 * 128)
    work.start()
    yield
    for i in range(links.n_high + 2):
        if i < links.n_high:
            work.first(i)
            yield
        if 0 <= i - 1 < links.n_high:
            work.second(i - 1)
            yield
        if 0 <= i - 2:
            work.third(i - 2)
            yield
    work.finish()


def every_scatter_scratch(n_high, rows, columns, cut=None):
    cut = columns // 256 * 128 if cut is None else cut
    over_low = [
        pltpu.VMEM((n_high, 2, rows, cut), BF),
        pltpu.VMEM((n_high, rows, cut), BF),
    ]
    return [
        pltpu.VMEM((2, 2, 2, rows, columns), BF),
        pltpu.VMEM((n_high, 2, 2, rows, columns), BF),
        *(over_low if cut else []),
        pltpu.VMEM((n_high, 2, rows, columns - cut), BF),
        pltpu.VMEM((n_high, rows, columns - cut), BF),
        pltpu.VMEM((n_high, rows, columns), BF),
        pltpu.VMEM((n_high - 1, rows, columns), BF),
    ]


def dp_scatter(links, copies, part, bufs, result):
    from_low, done, from_high = bufs
    order = steps_by_distance(links.n_high) + [0]
    low_in, high_in = {}, {}
    for k in order:
        low_in[k] = copies.go(
            part.at[links.ahead(k), 1 - links.low], from_low.at[k], links.over_low()
        )
    yield
    for k in order:
        low_in[k].wait_recv()
        done[k] = (
            part[links.ahead(k), links.low].astype(F32) + from_low[k].astype(F32)
        ).astype(BF)
        if k:
            high_in[k] = copies.go(
                done.at[k], from_high.at[k - 1], links.device(high=links.ahead(k))
            )
        yield
    total = done[0].astype(F32)
    for k in steps_by_distance(links.n_high):
        high_in[k].wait_recv()
        total = total + from_high[k - 1].astype(F32)
    result[...] = total.astype(result.dtype)
    yield


def dp_scatter_scratch(n_high, shape):
    return [
        pltpu.VMEM((n_high, *shape), BF),
        pltpu.VMEM((n_high, *shape), BF),
        pltpu.VMEM((n_high - 1, *shape), BF),
    ]


def semaphores(count, local):
    return [
        pltpu.SemaphoreType.DMA((count,)),
        pltpu.SemaphoreType.DMA((count,)),
        pltpu.SemaphoreType.DMA((local,)),
    ]


def params(number, mebibytes=60):
    return pltpu.CompilerParams(
        collective_id=number, has_side_effects=True, vmem_limit_bytes=mebibytes * 1024 * 1024
    )


def count_every_gather(n_high):
    return 11 * n_high + 1


def count_dp_gather(n_high):
    return 3 * n_high + 1


def weights_kernel(n_dp, down, o_t, q_up, kv_up, gains, cot, f_down, f_o, f_q, f_kv, f_g, f_cot, send, recv, local):
    links = Links(n_dp)
    copies = Copies(send, recv, local)
    links.meet()
    take_turns(
        every_gather(links, copies, down, f_down),
        dp_gather(links, copies, gains, f_g),
        dp_gather(links, copies, q_up, f_q),
        dp_gather(links, copies, kv_up, f_kv),
        dp_gather(links, copies, o_t, f_o),
        every_gather(links, copies, cot, f_cot),
    )
    copies.finish()


def gather_weights(n_dp, n_tensor, down, o_t, q_up, kv_up, gains, cot):
    n_high = n_dp // 2
    count = 2 * count_every_gather(n_high) + 4 * count_dp_gather(n_high)

    def over(block, *lead):
        return jax.ShapeDtypeStruct((*lead, *block.shape), block.dtype)

    return pl.pallas_call(
        functools.partial(weights_kernel, n_dp),
        out_shape=(
            over(down, n_dp, n_tensor),
            over(o_t, n_dp),
            over(q_up, n_dp),
            over(kv_up, n_dp),
            over(gains, n_dp),
            over(cot, n_dp, n_tensor),
        ),
        in_specs=[ANY] * 6,
        out_specs=[ANY] * 6,
        scratch_shapes=semaphores(count, 6),
        compiler_params=params(1),
        name="gather_weights",
    )(down, o_t, q_up, kv_up, gains, cot)


def resid_kernel(n_dp, part, x_rows, gain, full, resid, branch, from_core, out_side, from_side, block, send, recv, local):
    links = Links(n_dp)
    copies = Copies(send, recv, local)
    links.meet()
    arrive = copies.go(part.at[:, 1 - links.core], from_core, links.over_core())
    arrive.wait_recv()
    out_side[...] = (
        part[1 - links.side, links.core].astype(F32) + from_core[1 - links.side].astype(F32)
    ).astype(BF)
    arrive = copies.go(out_side, from_side, links.over_side())
    mine = part[links.side, links.core].astype(F32) + from_core[links.side].astype(F32)
    arrive.wait_recv()
    attn = RESIDUAL_SCALE * (mine + from_side[...].astype(F32))
    stream = x_rows[...].astype(F32) + attn
    branch[...] = attn
    resid[...] = stream
    block[...] = (stream * inverse_rms(stream) * gain[...]).astype(BF)
    take_turns(every_gather(links, copies, block, full))
    copies.finish()


def attention_residual(n_dp, part, x_rows, gain):
    n_tensor = 4
    rows, columns = x_rows.shape
    block = (rows, columns)
    return pl.pallas_call(
        functools.partial(resid_kernel, n_dp),
        out_shape=(
            jax.ShapeDtypeStruct((n_dp, n_tensor, rows, columns), BF),
            jax.ShapeDtypeStruct(block, F32),
            jax.ShapeDtypeStruct(block, F32),
        ),
        in_specs=[VMEM] * 3,
        out_specs=[ANY, VMEM, VMEM],
        scratch_shapes=[
            pltpu.VMEM((2, *block), BF),
            pltpu.VMEM(block, BF),
            pltpu.VMEM(block, BF),
            pltpu.VMEM(block, BF),
            *semaphores(2 + count_every_gather(n_dp // 2), 1),
        ],
        compiler_params=params(2),
        name="attention_residual",
    )(part.reshape(2, 2, rows, columns), x_rows, gain)


def grad_rows_kernel(n_dp, both, *refs):
    links = Links(n_dp)
    copies = Copies(*refs[-3:])
    g_part, resid, cot, gain = refs[:4]
    if both:
        m_part, attn_full, g_rows, block_full, m_rows = refs[4:9]
        scratch = refs[9:-3]
    else:
        attn_full, g_rows = refs[4:6]
        scratch = refs[6:-3]
    links.meet()

    def grad_stream():
        grad_rows = scratch[0]
        yield from every_scatter(links, copies, g_part, scratch[1:9], g_rows)
        stream = resid[...]
        inv = inverse_rms(stream)
        grad = cot[...].astype(F32) + norm_back(g_rows[...] * gain[...], stream * inv, inv)
        grad_rows[...] = (RESIDUAL_SCALE * grad).astype(BF)
        yield from tensor_gather(links, copies, grad_rows, attn_full)

    if both:
        block = block_stream(links, copies, m_part, resid, block_full, m_rows, scratch[9:])
        take_turns(grad_stream(), block)
    else:
        take_turns(grad_stream())
    copies.finish()


def block_stream(links, copies, m_part, resid, block_full, m_rows, scratch):
    block_rows = scratch[0]
    yield from every_scatter(links, copies, m_part, scratch[1:9], m_rows)
    m_rows[...] = RESIDUAL_SCALE * m_rows[...]
    block_rows[...] = resid[...] + m_rows[...]
    yield from tensor_gather(links, copies, block_rows, block_full)


def block_rows_kernel(n_dp, m_part, resid, block_full, m_rows, *rest):
    links = Links(n_dp)
    copies = Copies(*rest[-3:])
    links.meet()
    take_turns(block_stream(links, copies, m_part, resid, block_full, m_rows, rest[:-3]))
    copies.finish()


def residual_grads(n_dp, g_part, m_part, resid, cot, gain):
    n_high = n_dp // 2
    rows, columns = resid.shape
    shape = (n_high, 2, 2, 2, rows, columns)
    g_part, m_part = g_part.reshape(shape), m_part.reshape(shape)
    both = n_high <= 4
    one = jax.ShapeDtypeStruct((rows, columns), F32)
    grad_out = (jax.ShapeDtypeStruct((4, rows, columns), BF), one)
    block_out = (jax.ShapeDtypeStruct((4, rows, columns), F32), one)
    grad_scratch = [
        pltpu.VMEM((rows, columns), BF),
        *every_scatter_scratch(n_high, rows, columns),
    ]
    block_scratch = [
        pltpu.VMEM((rows, columns), F32),
        *every_scatter_scratch(n_high, rows, columns),
    ]
    count, local = 6 * n_high - 1 + 3, n_high + 1
    if both:
        return pl.pallas_call(
            functools.partial(grad_rows_kernel, n_dp, True),
            out_shape=grad_out + block_out,
            in_specs=[ANY, VMEM, VMEM, VMEM, ANY],
            out_specs=[ANY, VMEM, ANY, VMEM],
            scratch_shapes=[*grad_scratch, *block_scratch, *semaphores(2 * count, 2 * local)],
            compiler_params=params(3),
            name="residual_grads",
        )(g_part, resid, cot, gain, m_part)
    grads = pl.pallas_call(
        functools.partial(grad_rows_kernel, n_dp, False),
        out_shape=grad_out,
        in_specs=[ANY, VMEM, VMEM, VMEM],
        out_specs=[ANY, VMEM],
        scratch_shapes=[*grad_scratch, *semaphores(count, local)],
        compiler_params=params(3),
        name="residual_grads",
    )(g_part, resid, cot, gain)
    block = pl.pallas_call(
        functools.partial(block_rows_kernel, n_dp),
        out_shape=block_out,
        in_specs=[ANY, VMEM],
        out_specs=[ANY, VMEM],
        scratch_shapes=[*block_scratch, *semaphores(count, local)],
        compiler_params=params(6),
        name="block_rows",
    )(m_part, resid)
    return (*grads, *block)


def latent_kernel(n_dp, part, full, from_core, half, from_side, send, recv, local):
    links = Links(n_dp)
    copies = Copies(send, recv, local)
    links.meet(high=False, low=False)
    arrive = copies.go(part.at[1 - links.core], from_core, links.over_core())
    arrive.wait_recv()
    half[...] = (part[links.core].astype(F32) + from_core[...].astype(F32)).astype(BF)
    arrive = copies.go(half, from_side, links.over_side())
    arrive.wait_recv()
    full[links.core] = (half[...].astype(F32) + from_side[...].astype(F32)).astype(BF)
    arrive = copies.go(full.at[links.core], full.at[links.core], links.over_core())
    arrive.wait_recv()
    copies.finish()


def sum_latents(n_dp, part):
    rows, columns = part.shape
    half = (rows // 2, columns)
    return pl.pallas_call(
        functools.partial(latent_kernel, n_dp),
        out_shape=jax.ShapeDtypeStruct((2, *half), BF),
        in_specs=[VMEM],
        out_specs=VMEM,
        scratch_shapes=[pltpu.VMEM(half, BF)] * 3 + semaphores(3, 1),
        compiler_params=params(4),
        name="sum_latents",
    )(part.reshape(2, *half)).reshape(rows, columns)


def weight_grads_kernel(n_dp, d_part, o_part, q_part, kv_part, small, stats, d_full, o_sum, q_sum, kv_sum, small_full, *rest):
    d_block, small_block, stats_block = rest[:3]
    bufs = rest[3:15]
    small_in, stats_in = rest[15:17]
    send, recv, local = rest[17:]
    links = Links(n_dp)
    copies = Copies(send, recv, local)
    links.meet()

    def small_stream():
        n_high = links.n_high
        low_in = copies.go(
            small.at[:, 1 - links.low], small_in.at[pl.ds(0, n_high)], links.over_low()
        )
        stats_low = copies.go(stats, stats_in.at[0], links.over_low())
        yield
        low_in.wait_recv()
        stats_low.wait_recv()
        for k in range(n_high):
            small_in[k] = small_in[k] + small[k, links.low]
        stats_block[...] = stats[...] + stats_in[0]
        waits = []
        for k in range(1, n_high):
            there = links.ahead(k)
            waits.append(
                copies.go(
                    small_in.at[there], small_in.at[n_high + k - 1], links.device(high=there)
                )
            )
            waits.append(copies.go(stats_block, stats_in.at[k], links.device(high=there)))
        yield
        for wait in waits:
            wait.wait_recv()
        total = small_in[links.high]
        everything = stats_block[...]
        for k in range(1, n_high):
            total = total + small_in[n_high + k - 1]
            everything = everything + stats_in[k]
        small_block[0] = total
        small_block[1] = everything
        yield from tensor_gather(links, copies, small_block, small_full)

    def down_stream():
        yield from dp_scatter(links, copies, d_part, bufs[:3], d_block)
        yield from tensor_gather(links, copies, d_block, d_full)

    take_turns(
        down_stream(),
        dp_scatter(links, copies, q_part, bufs[6:9], q_sum),
        dp_scatter(links, copies, kv_part, bufs[9:12], kv_sum),
        dp_scatter(links, copies, o_part, bufs[3:6], o_sum),
        small_stream(),
    )
    copies.finish()


def sum_weight_grads(n_dp, down, o_t, q_up, kv_up, small, stats):
    n_high = n_dp // 2

    def parts(array):
        return array.reshape(n_high, 2, array.shape[0] // n_dp, *array.shape[1:])

    down, o_t, q_up, kv_up = parts(down), parts(o_t), parts(q_up), parts(kv_up)
    small = small.reshape(n_high, 2, *small.shape[1:])
    count = 4 * (2 * n_high - 1) + 2 * n_high + 6
    d_shape, o_shape, q_shape, kv_shape = (a.shape[2:] for a in (down, o_t, q_up, kv_up))
    one = stats.shape
    return pl.pallas_call(
        functools.partial(weight_grads_kernel, n_dp),
        out_shape=(
            jax.ShapeDtypeStruct((4, *d_shape), BF),
            jax.ShapeDtypeStruct(o_shape, F32),
            jax.ShapeDtypeStruct(q_shape, F32),
            jax.ShapeDtypeStruct(kv_shape, F32),
            jax.ShapeDtypeStruct((4, 2, *one), F32),
        ),
        in_specs=[VMEM] * 6,
        out_specs=[VMEM] * 5,
        scratch_shapes=[
            pltpu.VMEM(d_shape, BF),
            pltpu.VMEM((2, *one), F32),
            pltpu.VMEM(one, F32),
            *dp_scatter_scratch(n_high, d_shape),
            *dp_scatter_scratch(n_high, o_shape),
            *dp_scatter_scratch(n_high, q_shape),
            *dp_scatter_scratch(n_high, kv_shape),
            pltpu.VMEM((2 * n_high - 1, *one), F32),
            pltpu.VMEM((n_high, *one), F32),
            *semaphores(count, 2),
        ],
        compiler_params=params(5),
        name="sum_weight_grads",
    )(down, o_t, q_up, kv_up, small, stats)


def attention_mask(seg_row, valid_row):
    length = seg_row.shape[1]
    row = lax.broadcasted_iota(jnp.int32, (length, length), 0)
    column = lax.broadcasted_iota(jnp.int32, (length, length), 1)
    segments = jnp.broadcast_to(seg_row[...].astype(F32), (length, length))
    allowed = (
        (segments == segments.T)
        & (column <= row)
        & ((valid_row[...] == 1) | (column == row))
    )
    return jnp.where(allowed, 0.0, NEGATIVE)


def swap_halves(values):
    half = values.shape[1] // 2
    return jnp.concatenate([values[:, half:], values[:, :half]], axis=1)


def turn(values, cos_full, sin_full):
    return values * cos_full + swap_halves(values) * sin_full


def head_probs(query, key, bias, inv_root):
    scores = dot_nt(query, key) * inv_root + bias
    weights = jnp.exp(scores - jnp.max(scores, axis=-1, keepdims=True))
    return weights / jnp.sum(weights, axis=-1, keepdims=True)


def latent_rows(x, gain_attn, down, normed, latents):
    stream = x[...].astype(F32)
    normed[...] = (stream * inverse_rms(stream) * gain_attn).astype(BF)
    latents[...] = dot(normed[...], down)


def attend_rows(
    gain_q, gain_kv, q_up, kv_up, bias, cos_full, sin_full, latents, q_normed, kv_normed, q_rows, kv_rows, key_rot, mixed,
):
    rank_q = gain_q.shape[1]
    q_latent = latents[:, :rank_q]
    q_normed[...] = (q_latent * inverse_rms(q_latent) * gain_q).astype(BF)
    kv_latent = latents[:, rank_q : rank_q + KR]
    kv_normed[...] = (kv_latent * inverse_rms(kv_latent) * gain_kv).astype(BF)
    turned = turn(latents[:, rank_q + KR : rank_q + KR + ROPE], cos_full[...], sin_full[...])
    key_rot[...] = turned.astype(BF)
    kv_rows[...] = dot(kv_normed[...], kv_up).astype(BF)
    q_heads = dot(q_normed[...], q_up)
    inv_root = 1.0 / math.sqrt(NOPE + ROPE)
    for head in range(q_rows.shape[1] // (NOPE + ROPE)):
        base = head * (NOPE + ROPE)
        query = jnp.concatenate(
            [
                q_heads[:, base : base + NOPE],
                turn(
                    q_heads[:, base + NOPE : base + NOPE + ROPE], cos_full[...], sin_full[...]
                ),
            ],
            axis=1,
        ).astype(BF)
        q_rows[:, base : base + NOPE + ROPE] = query
        start = head * (NOPE + VD)
        key = jnp.concatenate([kv_rows[:, start : start + NOPE], key_rot[...]], axis=1)
        value = kv_rows[:, start + NOPE : start + NOPE + VD]
        probs = head_probs(query, key, bias, inv_root).astype(BF)
        mixed[:, head * VD : head * VD + VD] = dot(probs, value).astype(BF)


def attend_kernel(
    x, gain_attn, gain_q, gain_kv, down, q_up, kv_up, seg_row, valid_row, cos_full, sin_full,
    normed, *outs,
):
    latent_rows(x, gain_attn[...], down[...], normed, outs[0])
    attend_rows(
        gain_q[...], gain_kv[...], q_up[...], kv_up[...], attention_mask(seg_row, valid_row),
        cos_full, sin_full, *outs,
    )


def attend(x, gain_attn, gain_q, gain_kv, down, q_up, kv_up, segments, valid, cos_full, sin_full):
    length = x.shape[0]
    heads = q_up.shape[1] // (NOPE + ROPE)

    def rows(columns, kind):
        return jax.ShapeDtypeStruct((length, columns), kind)

    return pl.pallas_call(
        attend_kernel,
        out_shape=(
            rows(x.shape[1], BF),
            rows(down.shape[1], F32),
            rows(q_up.shape[0], BF),
            rows(kv_up.shape[0], BF),
            rows(q_up.shape[1], BF),
            rows(kv_up.shape[1], BF),
            rows(ROPE, BF),
            rows(heads * VD, BF),
        ),
        in_specs=[VMEM] * 11,
        out_specs=[VMEM] * 8,
        compiler_params=pltpu.CompilerParams(vmem_limit_bytes=VMEM_BYTES),
        name="attend",
    )(
        x,
        gain_attn[None, :],
        gain_q[None, :],
        gain_kv[None, :],
        down,
        q_up,
        kv_up,
        segments[None, :],
        valid[None, :],
        cos_full,
        sin_full,
    )


def later(stream, turns):
    for _ in range(turns):
        yield
    yield from stream


class Swap:
    def __init__(self, links, copies, blocks, out):
        self.me = links.high * 2 + links.low
        self.copies, self.blocks, self.out = copies, blocks, out
        self.own = copies.near(blocks.at[self.me], out.at[self.me])
        self.arrive = []

    def send(self, steps):
        n_dp = self.blocks.shape[0]
        for k in steps:
            there = (self.me + k) % n_dp
            self.arrive.append(
                self.copies.go(self.blocks.at[there], self.out.at[self.me], {"dp": there})
            )

    def finish(self):
        for copy in self.arrive:
            copy.wait_recv()
        self.own.wait()

    def sent(self):
        for copy in self.arrive:
            self.copies.sent(copy)


def pack_stream(w_gate, w_up, w_down_t, packed):
    n_dp, width, lanes = packed.shape
    slice_ff = w_gate.shape[1] // n_dp
    for k in range(n_dp):
        at = k * slice_ff
        packed[k] = jnp.concatenate(
            [
                w_gate[:, at : at + slice_ff],
                w_up[:, at : at + slice_ff],
                w_down_t[:, at : at + slice_ff],
                jnp.zeros((width, lanes - 3 * slice_ff), BF),
            ],
            axis=1,
        )
        yield


def quarter_of(values, rank):
    rows = values.shape[0] // 4
    mine = values[:rows]
    for other in range(1, 4):
        mine = jnp.where(rank == other, values[other * rows : other * rows + rows], mine)
    return mine


def forward_kernel(
    n_dp, x, cotangent, q_down, kv_down_t, gain_attn, gain_q, gain_kv, gain_mlp, q_up, kv_up, o_t,
    w_gate, w_up, w_down_t, seg_row, valid_row, turns,
    d_out, o_out, q_out, kv_out, f_g, m_part, g_part, w_grads,
    normed, latents, q_normed, kv_normed, q_rows, kv_rows, key_rot, mixed, resid, branch, cot,
    f_down, f_o, f_q, f_kv, down, gains, packed, f_w, f_cot, f_normed, hidden_all, both_all, m_block, g_block,
    part, from_core, out_side, from_side, block, send, recv, local,
):
    links = Links(n_dp)
    copies = Copies(send, recv, local)
    cos_full, sin_full = turns[:, :ROPE], turns[:, ROPE:]
    rank = links.side * 2 + links.core
    rows_down, rank_q = down.shape[0], q_down.shape[1]
    quarter = pl.ds(pl.multiple_of(rank * rows_down, 16), rows_down)
    down[:, :rank_q] = q_down[quarter, :]
    kv_rows_down = quarter_of(kv_down_t[...].T, rank)
    pad = down.shape[1] - rank_q - kv_rows_down.shape[1]
    down[:, rank_q:] = jnp.concatenate([kv_rows_down, jnp.zeros((rows_down, pad), BF)], axis=1)
    lanes = gains.shape[1]
    gain_rows = [
        jnp.concatenate([g[...].astype(F32), jnp.zeros((1, lanes - g.shape[1]), F32)], axis=1)
        for g in (gain_attn, gain_q, gain_kv, gain_mlp)
    ]
    gains[...] = jnp.concatenate(gain_rows + [jnp.zeros((12, lanes), F32)], axis=0).astype(BF)
    rows = block.shape[0]
    own_rows = pl.ds(pl.multiple_of(rank * rows, 16), rows)
    cot[...] = cotangent[own_rows, :]
    links.meet(swap=True)
    downs = EveryGather(links, copies, down, f_down, down.shape[1])
    small_gathers = [
        DpGather(links, copies, source, target)
        for source, target in ((gains, f_g), (q_up, f_q), (kv_up, f_kv))
    ]
    o = DpGather(links, copies, o_t, f_o)
    cots = EveryGather(links, copies, cot, f_cot)
    downs.start()
    for work in small_gathers:
        work.start()
    n_high = links.n_high
    downs.first(0)
    for work in small_gathers:
        work.own_low()
    for i in range(1, n_high):
        downs.first(i)
        downs.second(i - 1)
    for i in range(n_high - 1):
        for work in small_gathers:
            work.step(i)
    o.start()
    o.own_low()
    downs.second(n_high - 1)
    for _ in pack_stream(w_gate, w_up, w_down_t, packed):
        pass
    swap = Swap(links, copies, packed, f_w)
    for i in range(n_high):
        downs.third(i)
    for i in range(n_high):
        downs.fourth(i)
    small_gathers[0].finish()

    def gain_of(row, count):
        return jnp.concatenate(
            [f_g[k].astype(F32)[row : row + 1, :count] for k in range(n_dp)], axis=1
        )

    width = o_t.shape[0]
    full_down = f_down[...].reshape(n_dp * width, down.shape[1])
    latent_rows(x, gain_of(0, width), full_down, normed, latents)
    for work in small_gathers[1:]:
        work.finish()
    full_q = f_q[...].reshape(n_dp * q_up.shape[0], q_up.shape[1])
    full_kv = f_kv[...].reshape(n_dp * kv_up.shape[0], kv_up.shape[1])
    keeps = [
        copies.near(source, target)
        for source, target in ((f_down, d_out), (f_q, q_out), (f_kv, kv_out))
    ]
    o.step(0)
    attend_rows(
        gain_of(1, q_up.shape[0]), gain_of(2, kv_up.shape[0]), full_q, full_kv,
        attention_mask(seg_row, valid_row), cos_full, sin_full,
        latents, q_normed, kv_normed, q_rows, kv_rows, key_rot, mixed,
    )
    for i in range(1, n_high - 1):
        o.step(i)
    cots.start()
    cots.first(0)
    swap.send(range(2, n_dp, 2))
    swap.send(range(1, n_dp, 2))
    o.finish()
    keeps.append(copies.near(f_o, o_out))
    full_o = f_o[...].reshape(n_dp * width, o_t.shape[1])
    attn_part = dot_nt(mixed[...], full_o).astype(BF)
    for side in range(2):
        for core in range(2):
            at = (side * 2 + core) * rows
            part[side, core] = attn_part[at : at + rows]
    over = copies.go(part.at[:, 1 - links.core], from_core, links.over_core())
    over.wait_recv()
    out_side[...] = (
        part[1 - links.side, links.core].astype(F32) + from_core[1 - links.side].astype(F32)
    ).astype(BF)
    over = copies.go(out_side, from_side, links.over_side())
    mine = part[links.side, links.core].astype(F32) + from_core[links.side].astype(F32)
    over.wait_recv()
    attn = RESIDUAL_SCALE * (mine + from_side[...].astype(F32))
    stream = x[own_rows, :].astype(F32) + attn
    branch[...] = attn
    resid[...] = stream
    block[...] = (stream * inverse_rms(stream) * gain_of(3, width)).astype(BF)
    normeds = EveryGather(links, copies, block, f_normed)
    normeds.start()
    normeds.first(0)
    for i in range(n_high + 2):
        if 1 <= i < n_high:
            cots.first(i)
        if 0 <= i - 1 < n_high:
            cots.second(i - 1)
        if 0 <= i - 2:
            cots.third(i - 2)
    normeds.second(0)
    for i in range(n_high):
        cots.fourth(i)
    swap.finish()
    cots.sent()
    normeds.third(0)
    normeds.fourth(0)

    lanes = f_w.shape[2]
    slice_ff = w_gate.shape[1] // n_dp
    wide = both_all.shape[1]
    cut = lanes - hidden_all.shape[1]
    before = 2 * slice_ff - cut
    columns = x.shape[1]
    tokens = 2 * x.shape[0]
    stores = []

    def zeros(count):
        return jnp.zeros((tokens, count), F32)

    def feed_forward_of(high):
        pair = pl.ds(high * 2, 2)
        at = pl.ds(pl.multiple_of(high * tokens, 128), tokens)
        w_in = f_w[:, :, :wide].reshape(columns, wide)
        w_out = f_w[:, :, cut:].reshape(columns, lanes - cut)
        grad_mlp = (RESIDUAL_SCALE * f_cot[pair].astype(F32)).astype(BF)
        f_cot[pair] = grad_mlp
        both = dot(f_normed[pair].reshape(tokens, columns), w_in)
        gate, upper = both[:, :slice_ff], both[:, slice_ff : 2 * slice_ff]
        sigma = jax.nn.sigmoid(gate)
        swish = gate * sigma
        after = lanes - cut - before - slice_ff
        hidden = jnp.concatenate([zeros(before), swish * upper, zeros(after)], axis=1).astype(BF)
        grad_hidden = dot(grad_mlp.reshape(tokens, columns), w_out)[:, before : before + slice_ff]
        grad_both = jnp.concatenate(
            [
                grad_hidden * upper * (sigma * (1.0 + gate * (1.0 - sigma))),
                grad_hidden * swish,
                zeros(wide - 2 * slice_ff),
            ],
            axis=1,
        ).astype(BF)
        hidden_all[at, :] = hidden
        both_all[at, :] = grad_both
        while stores:
            stores.pop().wait()
        m_block[...] = dot_nt(hidden, w_out).astype(BF).reshape(m_block.shape)
        stores.append(copies.near(m_block, m_part.at[pair]))
        g_block[...] = dot_nt(grad_both, w_in).astype(BF).reshape(g_block.shape)
        stores.append(copies.near(g_block, g_part.at[pair]))

    for i in range(1, n_high):
        normeds.first(i)
        if i == 1:
            feed_forward_of(normeds.line.source(0))
        normeds.second(i)
        normeds.third(i)
        if i > 1:
            feed_forward_of(normeds.line.source(i - 1))
        normeds.fourth(i)
    feed_forward_of(normeds.line.source(n_high - 1))
    swap.sent()
    all_tokens = n_dp * x.shape[0]
    for k in range(n_dp):
        at = k * width
        slab_in = dot_tn(
            f_normed[:, :, :, at : at + width].reshape(all_tokens, width), both_all[...]
        )
        slab_out = dot_tn(
            f_cot[:, :, :, at : at + width].reshape(all_tokens, width), hidden_all[...]
        )
        packed[k, :, :cut] = slab_in[:, :cut].astype(BF)
        packed[k, :, cut:wide] = (slab_in[:, cut:] + slab_out[:, : wide - cut]).astype(BF)
        packed[k, :, wide:] = slab_out[:, wide - cut :].astype(BF)
        stores.append(copies.near(packed.at[k], w_grads.at[k]))
    while stores:
        stores.pop().wait()
    for keep in keeps:
        keep.wait()
    copies.finish()


def forward(
    n_dp, x, cotangent, q_down, kv_down_t, gains, q_up, kv_up, o_t, w_gate, w_up, w_down_t,
    segments, valid, turns, down_shape, gain_lanes,
):
    n_high = n_dp // 2
    length, columns = x.shape
    rows = length // 4
    slice_ff = w_gate.shape[1] // n_dp
    lanes = -(-3 * slice_ff // 128) * 128
    wide = -(-2 * slice_ff // 128) * 128
    cut = 2 * slice_ff // 128 * 128
    heads = q_up.shape[1] // (NOPE + ROPE)
    count = 3 * count_every_gather(n_high) + 4 * count_dp_gather(n_high) + n_dp + 1
    block = (rows, columns)

    def over(block, *lead, kind=BF):
        return jax.ShapeDtypeStruct((*lead, *block), kind)

    return pl.pallas_call(
        functools.partial(forward_kernel, n_dp),
        out_shape=(
            over(down_shape, n_dp, 4),
            over(o_t.shape, n_dp),
            over(q_up.shape, n_dp),
            over(kv_up.shape, n_dp),
            over((16, gain_lanes), n_dp),
            over(block, n_dp, 4),
            over(block, n_dp, 4),
            over((w_gate.shape[0], lanes), n_dp),
            over((columns,), length),
            over((down_shape[1],), length, kind=F32),
            over((q_up.shape[0] * n_dp,), length),
            over((kv_up.shape[0] * n_dp,), length),
            over((q_up.shape[1],), length),
            over((kv_up.shape[1],), length),
            over((ROPE,), length),
            over((heads * VD,), length),
            over(block, kind=F32),
            over(block, kind=F32),
            over(block),
        ),
        in_specs=[VMEM] * 17,
        out_specs=[ANY] * 4 + [VMEM] + [ANY] * 3 + [VMEM] * 11,
        scratch_shapes=[
            pltpu.VMEM((n_dp, 4, *down_shape), BF),
            pltpu.VMEM((n_dp, *o_t.shape), BF),
            pltpu.VMEM((n_dp, *q_up.shape), BF),
            pltpu.VMEM((n_dp, *kv_up.shape), BF),
            pltpu.VMEM(down_shape, BF),
            pltpu.VMEM((16, gain_lanes), BF),
            pltpu.VMEM((n_dp, w_gate.shape[0], lanes), BF),
            pltpu.VMEM((n_dp, w_gate.shape[0], lanes), BF),
            pltpu.VMEM((n_dp, 4, *block), BF),
            pltpu.VMEM((n_dp, 4, *block), BF),
            pltpu.VMEM((n_dp * length, lanes - cut), BF),
            pltpu.VMEM((n_dp * length, wide), BF),
            pltpu.VMEM((2, 4, *block), BF),
            pltpu.VMEM((2, 4, *block), BF),
            pltpu.VMEM((2, 2, *block), BF),
            pltpu.VMEM((2, *block), BF),
            pltpu.VMEM(block, BF),
            pltpu.VMEM(block, BF),
            pltpu.VMEM(block, BF),
            *semaphores(count, 12 + 2 * n_high + n_dp),
        ],
        compiler_params=params(7, 62),
        name="forward",
    )(
        x, cotangent, q_down, kv_down_t, *(g[None, :] for g in gains), q_up, kv_up, o_t,
        w_gate, w_up, w_down_t, segments[None, :], valid[None, :], turns,
    )


def feed_forward_kernel(slice_ff, normed, cot, weights, m_part, g_part, grads, sum_in, sum_out):
    step = pl.program_id(0)
    cut = slice_ff * 2 // 128 * 128
    pad = slice_ff * 2 - cut
    w_in, w_out = weights[:, : sum_in.shape[0]], weights[:, cut:]
    rows = normed.shape[0]
    both = dot(normed[...], w_in)
    gate, upper = both[:, :slice_ff], both[:, slice_ff : 2 * slice_ff]
    sigma = jax.nn.sigmoid(gate)
    swish = gate * sigma

    def zeros(count):
        return jnp.zeros((rows, count), F32)

    def placed(hidden):
        rest = w_out.shape[1] - pad - slice_ff
        return jnp.concatenate([zeros(pad), hidden, zeros(rest)], axis=1).astype(BF)

    hidden = placed(swish * upper)
    m_part[...] = dot_nt(hidden, w_out).astype(BF)
    grad_mlp = (RESIDUAL_SCALE * cot[...].astype(F32)).astype(BF)
    grad_hidden = dot(grad_mlp, w_out)[:, pad : pad + slice_ff]
    grad_both = jnp.concatenate(
        [
            grad_hidden * upper * (sigma * (1.0 + gate * (1.0 - sigma))),
            grad_hidden * swish,
            zeros(w_in.shape[1] - 2 * slice_ff),
        ],
        axis=1,
    ).astype(BF)
    g_part[...] = dot_nt(grad_both, w_in).astype(BF)

    @pl.when(step == 0)
    def _():
        sum_in[...] = dot_tn(grad_both, normed[...])
        sum_out[...] = dot_tn(hidden, grad_mlp)

    @pl.when(step > 0)
    def _():
        sum_in[...] += dot_tn(grad_both, normed[...])
        sum_out[...] += dot_tn(hidden, grad_mlp)

    @pl.when(step == pl.num_programs(0) - 1)
    def _():
        mid = sum_in.shape[0]
        if cut:
            grads[:, :cut] = sum_in[:cut].T.astype(BF)
        grads[:, cut:mid] = (sum_in[cut:] + sum_out[: mid - cut]).T.astype(BF)
        grads[:, mid:] = sum_out[mid - cut :].T.astype(BF)


def feed_forward(normed, cot, weights, slice_ff, rows):
    tokens, columns = normed.shape
    lanes = weights.shape[1]
    cut = slice_ff * 2 // 128 * 128
    wide = -(-slice_ff * 2 // 128) * 128
    token_block = pl.BlockSpec((rows, columns), lambda i: (i, 0))
    whole = pl.BlockSpec((columns, lanes), lambda i: (0, 0))
    part = jax.ShapeDtypeStruct((tokens, columns), BF)
    return pl.pallas_call(
        functools.partial(feed_forward_kernel, slice_ff),
        grid=(tokens // rows,),
        out_shape=(part, part, jax.ShapeDtypeStruct((columns, lanes), BF)),
        in_specs=[token_block, token_block, whole],
        out_specs=[token_block, token_block, whole],
        scratch_shapes=[
            pltpu.VMEM((wide, columns), F32),
            pltpu.VMEM((lanes - cut, columns), F32),
        ],
        compiler_params=pltpu.CompilerParams(vmem_limit_bytes=VMEM_BYTES),
        name="feed_forward",
    )(normed, cot, weights)


def attend_back_kernel(
    grad_attn, mixed, o_t, q_rows, kv_rows, key_rot, q_normed, kv_normed, q_up, kv_up,
    seg_row, valid_row, cos_full, sin_full,
    grad_latents, grad_o, grad_q_up, grad_kv_up, grad_q, grad_kv,
):
    rank_q = q_up.shape[0]
    grad_o[...] = dot_tn(grad_attn[...], mixed[...]).astype(BF)
    grad_mixed = dot(grad_attn[...], o_t[...]).astype(BF)
    bias = attention_mask(seg_row, valid_row)
    inv_root = 1.0 / math.sqrt(NOPE + ROPE)
    grad_rot = jnp.zeros((grad_attn.shape[0], ROPE), F32)
    for head in range(q_rows.shape[1] // (NOPE + ROPE)):
        base = head * (NOPE + ROPE)
        start = head * (NOPE + VD)
        query = q_rows[:, base : base + NOPE + ROPE]
        key = jnp.concatenate([kv_rows[:, start : start + NOPE], key_rot[...]], axis=1)
        value = kv_rows[:, start + NOPE : start + NOPE + VD]
        grad = grad_mixed[:, head * VD : head * VD + VD]
        probs = head_probs(query, key, bias, inv_root)
        grad_value = dot_tn(probs.astype(BF), grad)
        grad_probs = dot_nt(grad, value)
        inner = jnp.sum(probs * grad_probs, axis=-1, keepdims=True)
        grad_scores = (probs * (grad_probs - inner)).astype(BF)
        grad_query = dot(grad_scores, key) * inv_root
        grad_key = dot_tn(grad_scores, query) * inv_root
        grad_q[:, base : base + NOPE + ROPE] = jnp.concatenate(
            [grad_query[:, :NOPE], turn(grad_query[:, NOPE:], cos_full[...], -sin_full[...])],
            axis=1,
        ).astype(BF)
        grad_kv[:, start : start + NOPE + VD] = jnp.concatenate(
            [grad_key[:, :NOPE], grad_value], axis=1
        ).astype(BF)
        grad_rot = grad_rot + grad_key[:, NOPE:]
    grad_latents[...] = jnp.zeros_like(grad_latents)
    grad_latents[:, :rank_q] = dot_nt(grad_q[...], q_up[...]).astype(BF)
    grad_latents[:, rank_q : rank_q + KR] = dot_nt(grad_kv[...], kv_up[...]).astype(BF)
    grad_latents[:, rank_q + KR : rank_q + KR + ROPE] = turn(
        grad_rot, cos_full[...], -sin_full[...]
    ).astype(BF)
    grad_q_up[...] = dot_tn(q_normed[...], grad_q[...]).astype(BF)
    grad_kv_up[...] = dot_tn(kv_normed[...], grad_kv[...]).astype(BF)


def attend_back(
    grad_attn, mixed, o_t, q_rows, kv_rows, key_rot, q_normed, kv_normed, q_up, kv_up,
    segments, valid, cos_full, sin_full, columns_down,
):
    length = grad_attn.shape[0]

    def out(shape):
        return jax.ShapeDtypeStruct(shape, BF)

    return pl.pallas_call(
        attend_back_kernel,
        out_shape=(
            out((length, columns_down)),
            out(o_t.shape),
            out(q_up.shape),
            out(kv_up.shape),
        ),
        in_specs=[VMEM] * 14,
        out_specs=[VMEM] * 4,
        scratch_shapes=[pltpu.VMEM(q_rows.shape, BF), pltpu.VMEM(kv_rows.shape, BF)],
        compiler_params=pltpu.CompilerParams(vmem_limit_bytes=VMEM_BYTES),
        name="attend_back",
    )(
        grad_attn, mixed, o_t, q_rows, kv_rows, key_rot, q_normed, kv_normed, q_up, kv_up,
        segments[None, :], valid[None, :], cos_full, sin_full,
    )


class ScatterInto:
    def __init__(self, links, copies, bufs, result):
        self.links, self.copies, self.result = links, copies, result
        self.part, self.from_low, self.from_high = bufs
        self.order = steps_by_distance(links.n_high) + [0]
        self.low_in, self.high_in = {}, {}

    def start(self):
        for k in self.order:
            self.low_in[k] = self.copies.go(
                self.part.at[self.links.ahead(k), 1 - self.links.low],
                self.from_low.at[k],
                self.links.over_low(),
            )

    def steps(self):
        links, part = self.links, self.part
        for k in self.order:
            there = links.ahead(k)
            self.low_in[k].wait_recv()
            part[there, links.low] = (
                part[there, links.low].astype(F32) + self.from_low[k].astype(F32)
            ).astype(BF)
            if k:
                self.high_in[k] = self.copies.go(
                    part.at[there, links.low], self.from_high.at[k - 1], links.device(high=there)
                )

    def finish(self):
        total = self.part[self.links.high, self.links.low].astype(F32)
        for k in steps_by_distance(self.links.n_high):
            self.high_in[k].wait_recv()
            total = total + self.from_high[k - 1].astype(F32)
        self.result[...] = total.astype(self.result.dtype)


def scatter_into_scratch(n_high, shape):
    return [
        pltpu.VMEM((n_high, 2, *shape), BF),
        pltpu.VMEM((n_high, *shape), BF),
        pltpu.VMEM((n_high - 1, *shape), BF),
    ]


def small_stream(links, copies, small, small_in, stats, stats_in, stats_block, small_block, small_full):
    n_high = links.n_high
    low_in = copies.go(
        small.at[:, 1 - links.low], small_in.at[pl.ds(0, n_high)], links.over_low()
    )
    stats_low = copies.go(stats, stats_in.at[0], links.over_low())
    yield
    low_in.wait_recv()
    stats_low.wait_recv()
    for k in range(n_high):
        small_in[k] = small_in[k] + small[k, links.low]
    stats_block[...] = stats[...] + stats_in[0]
    waits = []
    for k in range(1, n_high):
        there = links.ahead(k)
        waits.append(
            copies.go(small_in.at[there], small_in.at[n_high + k - 1], links.device(high=there))
        )
        waits.append(copies.go(stats_block, stats_in.at[k], links.device(high=there)))
    yield
    for wait in waits:
        wait.wait_recv()
    total = small_in[links.high]
    everything = stats_block[...]
    for k in range(1, n_high):
        total = total + small_in[n_high + k - 1]
        everything = everything + stats_in[k]
    small_block[0] = total
    small_block[1] = everything
    yield from tensor_gather(links, copies, small_block, small_full)


def back_kernel(
    n_dp, g_part, m_part, w_part, resid, branch, cot, x, normed, latents, q_normed, kv_normed,
    q_rows, kv_rows, key_rot, mixed, d_in, o_in, q_in, kv_in, f_g, seg_row, valid_row,
    turns,
    block_full, grad_input, d_full, o_sum, q_sum, kv_sum, small_full, w_full,
    f_down, f_o, f_q, f_kv, attn_full, grad_rows, g_rows, m_rows, grad_q, grad_kv, lat, lat_in, lat_half, lat_side,
    lat_full, d_block, small, small_in, stats, stats_in, stats_block, small_block, *rest,
):
    g_bufs, m_bufs = rest[:8], (rest[0], *rest[8:13])
    d_bufs, o_bufs, q_bufs, kv_bufs = rest[13:16], rest[16:19], rest[19:22], rest[22:25]
    links = Links(n_dp)
    copies = Copies(*rest[25:])
    links.meet(swap=True)
    cos_full, sin_full = turns[:, :ROPE], turns[:, ROPE:]
    length = x.shape[0]
    rank_q, rank_kv = q_normed.shape[1], kv_normed.shape[1]
    width = o_sum.shape[0]

    def gain_of(row, count):
        return jnp.concatenate(
            [f_g[k].astype(F32)[row : row + 1, :count] for k in range(n_dp)], axis=1
        )

    half_columns = x.shape[1] // 256 * 128
    g = EveryScatter(links, copies, g_part, g_bufs, g_rows, half_columns)
    m = EveryScatter(links, copies, m_part, m_bufs, m_rows, 0)
    swap = Swap(links, copies, w_part, w_full)
    high = range(links.n_high)
    g.start()
    loads = [
        copies.near(source, target)
        for source, target in ((d_in, f_down), (o_in, f_o), (q_in, f_q), (kv_in, f_kv))
    ]
    swap.send(range(2, n_dp, 2))
    for i in range(links.n_high + 1):
        if i in high:
            g.first(i)
        if i - 1 in high:
            g.second(i - 1)
        if i - 2 in high:
            g.third(i - 2)
    m.start()
    swap.send(range(1, n_dp, 2))
    g.third(links.n_high - 1)
    m.first(0)
    m.first(1)
    g.finish()
    stream = resid[...]
    inv_two = inverse_rms(stream)
    unit_two = stream * inv_two
    gain_mlp = gain_of(3, width)
    grad = cot[...].astype(F32) + norm_back(g_rows[...] * gain_mlp, unit_two, inv_two)
    grad_rows[...] = (RESIDUAL_SCALE * grad).astype(BF)
    t_stream = tensor_gather(links, copies, grad_rows, attn_full)
    next(t_stream)
    m.first(2)
    m.first(3)
    mlp_gain = jnp.sum(g_rows[...] * unit_two, axis=0, keepdims=True)
    bias = attention_mask(seg_row, valid_row)
    for _ in t_stream:
        pass

    for load in loads:
        load.wait()
    grad_attn = attn_full[...].reshape(length, x.shape[1])
    for k in range(n_dp):
        o_bufs[0][k // 2, k % 2] = dot_tn(
            grad_attn[:, k * width : k * width + width], mixed[...]
        ).astype(BF)
    o = ScatterInto(links, copies, o_bufs, o_sum)
    o.start()

    grad_mixed = dot(grad_attn, f_o[...].reshape(n_dp * width, mixed.shape[1])).astype(BF)
    inv_root = 1.0 / math.sqrt(NOPE + ROPE)
    grad_rot = jnp.zeros((length, ROPE), F32)
    for head in range(q_rows.shape[1] // (NOPE + ROPE)):
        base = head * (NOPE + ROPE)
        start = head * (NOPE + VD)
        query = q_rows[:, base : base + NOPE + ROPE]
        key = jnp.concatenate([kv_rows[:, start : start + NOPE], key_rot[...]], axis=1)
        value = kv_rows[:, start + NOPE : start + NOPE + VD]
        grad_head = grad_mixed[:, head * VD : head * VD + VD]
        probs = head_probs(query, key, bias, inv_root)
        grad_value = dot_tn(probs.astype(BF), grad_head)
        grad_probs = dot_nt(grad_head, value)
        inner = jnp.sum(probs * grad_probs, axis=-1, keepdims=True)
        grad_scores = (probs * (grad_probs - inner)).astype(BF)
        grad_query = dot(grad_scores, key) * inv_root
        grad_key = dot_tn(grad_scores, query) * inv_root
        grad_q[:, base : base + NOPE + ROPE] = jnp.concatenate(
            [grad_query[:, :NOPE], turn(grad_query[:, NOPE:], cos_full[...], -sin_full[...])],
            axis=1,
        ).astype(BF)
        grad_kv[:, start : start + NOPE + VD] = jnp.concatenate(
            [grad_key[:, :NOPE], grad_value], axis=1
        ).astype(BF)
        grad_rot = grad_rot + grad_key[:, NOPE:]

    half = length // 2
    lat[...] = jnp.zeros_like(lat)
    full_q = f_q[...].reshape(rank_q, q_rows.shape[1])
    full_kv = f_kv[...].reshape(rank_kv, kv_rows.shape[1])
    grad_turned = turn(grad_rot, cos_full[...], -sin_full[...]).astype(BF)
    for core in range(2):
        at = core * half
        lat[core, :, :rank_q] = dot_nt(grad_q[at : at + half], full_q).astype(BF)
        lat[core, :, rank_q : rank_q + rank_kv] = dot_nt(
            grad_kv[at : at + half], full_kv
        ).astype(BF)
        lat[core, :, rank_q + rank_kv : rank_q + rank_kv + ROPE] = grad_turned[at : at + half]
    over = copies.go(lat.at[1 - links.core], lat_in, links.over_core())
    rows_q = q_sum.shape[0]
    for k in range(n_dp):
        q_bufs[0][k // 2, k % 2] = dot_tn(
            q_normed[:, k * rows_q : k * rows_q + rows_q], grad_q[...]
        ).astype(BF)
    q = ScatterInto(links, copies, q_bufs, q_sum)
    q.start()
    over.wait_recv()
    lat_half[...] = (lat[links.core].astype(F32) + lat_in[...].astype(F32)).astype(BF)
    over = copies.go(lat_half, lat_side, links.over_side())
    rows_kv = kv_sum.shape[0]
    for k in range(n_dp):
        kv_bufs[0][k // 2, k % 2] = dot_tn(
            kv_normed[:, k * rows_kv : k * rows_kv + rows_kv], grad_kv[...]
        ).astype(BF)
    kv = ScatterInto(links, copies, kv_bufs, kv_sum)
    kv.start()
    over.wait_recv()
    lat_full[links.core] = (lat_half[...].astype(F32) + lat_side[...].astype(F32)).astype(BF)
    mine = lat_full.at[links.core]
    over = copies.go(mine, mine, links.over_core())
    q_latent = latents[:, :rank_q]
    inv_q = inverse_rms(q_latent)
    unit_q = q_latent * inv_q
    kv_latent = latents[:, rank_q : rank_q + rank_kv]
    inv_kv = inverse_rms(kv_latent)
    unit_kv = kv_latent * inv_kv
    over.wait_recv()
    lat_sum = lat_full[...].reshape(length, lat.shape[2]).astype(F32)
    grad_q_latent, grad_kv_latent = lat_sum[:, :rank_q], lat_sum[:, rank_q : rank_q + rank_kv]
    q_gain = jnp.sum(grad_q_latent * unit_q, axis=0, keepdims=True)
    kv_gain = jnp.sum(grad_kv_latent * unit_kv, axis=0, keepdims=True)
    grad_down = jnp.concatenate(
        [
            norm_back(grad_q_latent * gain_of(1, rows_q), unit_q, inv_q),
            norm_back(grad_kv_latent * gain_of(2, rows_kv), unit_kv, inv_kv),
            lat_sum[:, rank_q + rank_kv :],
        ],
        axis=1,
    ).astype(BF)

    rows_down = d_block.shape[0]
    m.second(0)
    m.second(1)
    copies.near(normed, g_bufs[0].at[0]).wait()
    normed_rows = g_bufs[0][0].reshape(length, x.shape[1])
    rank = links.side * 2 + links.core
    for k in range(n_dp):
        rows_all = dot_tn(normed_rows[:, k * width : k * width + width], grad_down)
        d_bufs[0][k // 2, k % 2] = quarter_of(rows_all, rank).astype(BF)

    d = ScatterInto(links, copies, d_bufs, d_block)
    d.start()
    o.steps()
    m.second(2)
    m.second(3)
    grad_input[...] = dot_nt(grad_down, f_down[...].reshape(n_dp * width, grad_down.shape[1]))
    q.steps()
    kv.steps()
    for i in high:
        m.third(i)
    d.steps()
    m.finish()
    mlp = RESIDUAL_SCALE * m_rows[...]
    g_rows[...] = resid[...] + mlp
    block_gather = tensor_gather(links, copies, g_rows, block_full)
    next(block_gather)
    valid = jnp.broadcast_to((valid_row[...] == 1).astype(F32), (length, length)).T
    weights = quarter_of(valid, rank)[:, :1]
    lane = lax.broadcasted_iota(jnp.int32, stats.shape, 1)
    sums = [
        jnp.sum(jnp.sum(weights * rows * rows, axis=1, keepdims=True), axis=0, keepdims=True)
        for rows in (resid[...], branch[...], mlp)
    ] + [jnp.sum(weights, axis=0, keepdims=True)]
    packed = jnp.zeros(stats.shape, F32)
    for index, value in enumerate(sums):
        packed = jnp.where(lane == index, value, packed)
    stats[...] = packed
    stream = x[...].astype(F32)
    inv_one = inverse_rms(stream)
    unit_one = stream * inv_one
    attn_gain = jnp.sum(grad_input[...] * unit_one, axis=0, keepdims=True)
    grad_input[...] = grad_attn.astype(F32) * (1.0 / RESIDUAL_SCALE) + norm_back(
        grad_input[...] * gain_of(0, width), unit_one, inv_one
    )

    def piece(vector, k):
        count = vector.shape[1] // n_dp
        cut = vector[:, k * count : k * count + count]
        return jnp.concatenate([cut, jnp.zeros((1, small.shape[3] - count), F32)], axis=1)

    for k in range(n_dp):
        small[k // 2, k % 2] = jnp.concatenate(
            [piece(v, k) for v in (attn_gain, q_gain, kv_gain, mlp_gain)]
            + [jnp.zeros((4, small.shape[3]), F32)],
            axis=0,
        )
    small_rows = small_stream(
        links, copies, small, small_in, stats, stats_in, stats_block, small_block, small_full
    )
    next(small_rows)
    d.finish()
    down_gather = tensor_gather(links, copies, d_block, d_full)
    take_turns(small_rows, down_gather, block_gather)
    o.finish()
    q.finish()
    kv.finish()
    swap.finish()
    copies.finish()


def back(
    n_dp, g_part, m_part, w_part, resid, branch, cot, x, normed, latents, q_normed, kv_normed,
    q_rows, kv_rows, key_rot, mixed, f_down, f_o, f_q, f_kv, f_g, segments, valid, turns,
):
    n_high = n_dp // 2
    rows, columns = resid.shape
    length = x.shape[0]
    lanes = f_g.shape[2]
    half = (length // 2, latents.shape[1])
    shape = (n_high, 2, 2, 2, rows, columns)
    d_shape, o_shape, q_shape, kv_shape = f_down.shape[2:], f_o.shape[1:], f_q.shape[1:], f_kv.shape[1:]
    one = (8, lanes)
    count = 2 * (6 * n_high - 1) + 4 * (2 * n_high - 1) + 4 * 3 + (n_dp - 1) + 2 * n_high + 3

    def out(shape, kind=F32):
        return jax.ShapeDtypeStruct(shape, kind)

    return pl.pallas_call(
        functools.partial(back_kernel, n_dp),
        out_shape=(
            out((4, rows, columns)),
            out((length, columns)),
            out((4, *d_shape), BF),
            out(o_shape),
            out(q_shape),
            out(kv_shape),
            out((4, 2, *one)),
            out(w_part.shape, BF),
        ),
        in_specs=[ANY] * 3 + [VMEM] * 4 + [ANY] + [VMEM] * 7 + [ANY] * 4 + [VMEM] * 4,
        out_specs=[ANY] + [VMEM] * 6 + [ANY],
        scratch_shapes=[
            *(pltpu.VMEM(full.shape, BF) for full in (f_down, f_o, f_q, f_kv)),
            pltpu.VMEM((4, rows, columns), BF),
            pltpu.VMEM((rows, columns), BF),
            pltpu.VMEM((rows, columns), F32),
            pltpu.VMEM((rows, columns), F32),
            pltpu.VMEM(q_rows.shape, BF),
            pltpu.VMEM(kv_rows.shape, BF),
            pltpu.VMEM((2, *half), BF),
            pltpu.VMEM(half, BF),
            pltpu.VMEM(half, BF),
            pltpu.VMEM(half, BF),
            pltpu.VMEM((2, *half), BF),
            pltpu.VMEM(d_shape, BF),
            pltpu.VMEM((n_high, 2, *one), F32),
            pltpu.VMEM((2 * n_high - 1, *one), F32),
            pltpu.VMEM(one, F32),
            pltpu.VMEM((n_high, *one), F32),
            pltpu.VMEM(one, F32),
            pltpu.VMEM((2, *one), F32),
            *every_scatter_scratch(n_high, rows, columns),
            *every_scatter_scratch(n_high, rows, columns, 0)[1:],
            *scatter_into_scratch(n_high, d_shape),
            *scatter_into_scratch(n_high, o_shape),
            *scatter_into_scratch(n_high, q_shape),
            *scatter_into_scratch(n_high, kv_shape),
            *semaphores(count, 2 * n_high + 10),
        ],
        compiler_params=params(8, 62),
        name="back",
    )(
        g_part.reshape(shape), m_part.reshape(shape), w_part, resid, branch, cot, x,
        normed.reshape(2, 2, rows, columns), latents, q_normed, kv_normed, q_rows, kv_rows, key_rot, mixed, f_down, f_o, f_q, f_kv, f_g,
        segments[None, :], valid[None, :], turns,
    )


def unpack_kernel(
    slice_ff, rank_q, swapped, down, o_in, q_in, kv_in, block_in, input_in, small,
    grad_gate, grad_upper, grad_down_t, grad_o_t, grad_q_down, grad_kv_down_t, grad_q_up, grad_kv_up,
    block_out, grad_input,
    attn_gain, q_gain, kv_gain, mlp_gain, stats,
):
    n_dp = swapped.shape[0]

    def pieces(start):
        return jnp.concatenate(
            [swapped[k, :, start : start + slice_ff] for k in range(n_dp)], axis=1
        ).astype(F32)

    grad_gate[...] = pieces(0)
    grad_upper[...] = pieces(slice_ff)
    grad_down_t[...] = pieces(2 * slice_ff)
    for target, source in (
        (grad_o_t, o_in), (grad_q_up, q_in), (grad_kv_up, kv_in), (block_out, block_in), (grad_input, input_in),
    ):
        target[...] = source[...]
    rows = down[...].reshape(grad_q_down.shape[0], down.shape[2]).astype(F32)
    grad_q_down[...] = rows[:, :rank_q]
    grad_kv_down_t[...] = rows[:, rank_q : rank_q + grad_kv_down_t.shape[0]].T
    gains = small[0, 0]
    for row, gain in ((0, attn_gain), (1, q_gain), (2, kv_gain)):
        gain[...] = gains[row : row + 1, : gain.shape[1]]
    total = small[0, 0] + small[1, 0] + small[2, 0] + small[3, 0]
    mlp_gain[...] = total[3:4, : mlp_gain.shape[1]]
    sums = (small[0, 1] + small[1, 1] + small[2, 1] + small[3, 1])[0:1]
    stats[...] = jnp.sqrt(sums[:, :3] / (sums[:, 3:4] * D))


def unpack(swapped, down, o_t, q_up, kv_up, block, grad_input, small, slice_ff, rank_q, columns_down, gains):
    n_dp, width, _ = swapped.shape

    def out(*shape):
        return jax.ShapeDtypeStruct(shape, F32)

    return pl.pallas_call(
        functools.partial(unpack_kernel, slice_ff, rank_q),
        out_shape=(
            out(width, n_dp * slice_ff),
            out(width, n_dp * slice_ff),
            out(width, n_dp * slice_ff),
            out(*o_t.shape),
            out(width, rank_q),
            out(columns_down - rank_q, width),
            out(*q_up.shape),
            out(*kv_up.shape),
            out(*block.shape),
            out(*grad_input.shape),
            *(out(1, gain.shape[0]) for gain in gains),
            out(1, 3),
        ),
        in_specs=[VMEM] * 8,
        out_specs=[VMEM] * 15,
        compiler_params=pltpu.CompilerParams(vmem_limit_bytes=VMEM_BYTES),
        name="unpack",
    )(swapped, down, o_t, q_up, kv_up, block, grad_input, small)


def per_device(
    layer_input,
    segment_ids,
    valid_mask,
    cotangent,
    attn_gain,
    q_down,
    q_gain,
    q_up,
    kv_down,
    kv_gain,
    kv_up,
    o_proj,
    mlp_gain,
    w_gate,
    w_up,
    w_down,
):
    length = layer_input.shape[0]
    n_dp = lax.axis_size("dp")
    n_tensor = lax.axis_size("tensor")
    share = length // n_tensor
    me = lax.axis_index("tensor")
    width = w_gate.shape[0]
    slice_ff = w_gate.shape[1] // n_dp
    rows_down = width // n_tensor

    def rows_of(values, count):
        return lax.dynamic_slice_in_dim(values, me * count, count, 0)

    rank_q = q_down.shape[1]
    columns_down = rank_q + kv_down.shape[1]
    pad_down = -columns_down % 128
    down_rows = jnp.concatenate(
        [
            rows_of(q_down, rows_down),
            rows_of(kv_down, rows_down),
            jnp.zeros((rows_down, pad_down), BF),
        ],
        axis=1,
    )
    lanes = -(-width // 128) * 128

    def lane_rows(rows, count, kind):
        padded = [jnp.pad(row.astype(kind), (0, lanes - row.shape[0])) for row in rows]
        return jnp.stack(padded + [jnp.zeros((lanes,), kind)] * (count - len(padded)))

    cot_rows = rows_of(cotangent, share)
    x_rows = rows_of(layer_input, share)
    gains_block = lane_rows([attn_gain, q_gain, kv_gain, mlp_gain], 16, BF)
    cosine, sine_table = rope_tables(length, ROPE)
    cos_full = jnp.concatenate([cosine, cosine], axis=1)
    sin_full = jnp.concatenate([-sine_table, sine_table], axis=1)
    fused = n_dp == 8 and rows_down % 16 == 0 and q_up.shape[0] % 16 == 0
    if fused:
        (
            f_down, f_o, f_q, f_kv, f_g, mlp_part, normed_part, grad_packed,
            normed, latents, q_normed, kv_normed, q_rows, kv_rows, key_rot, mixed,
            resid_rows, attn_rows, cot_rows,
        ) = forward(
            n_dp, layer_input, cotangent, q_down, kv_down.T, (attn_gain, q_gain, kv_gain, mlp_gain),
            q_up, kv_up, o_proj.T, w_gate, w_up, w_down.T, segment_ids, valid_mask,
            jnp.concatenate([cos_full, sin_full], axis=1), down_rows.shape, lanes,
        )
    else:
        f_down, f_o, f_q, f_kv, f_g, f_cot = gather_weights(
            n_dp, n_tensor, down_rows, o_proj.T, q_up, kv_up, gains_block, cot_rows
        )
    full_down = f_down.reshape(n_dp * width, columns_down + pad_down)
    full_o = f_o.reshape(n_dp * width, -1)

    def gain_of(row, gain):
        return f_g[:, row, : gain.shape[0]].reshape(-1).astype(F32)

    gain_attn = gain_of(0, attn_gain)
    gain_q = gain_of(1, q_gain)
    gain_kv = gain_of(2, kv_gain)
    gain_mlp = gain_of(3, mlp_gain)
    if not fused:
        packed = jnp.concatenate(
            [
                w_gate.reshape(width, n_dp, slice_ff),
                w_up.reshape(width, n_dp, slice_ff),
                w_down.T.reshape(width, n_dp, slice_ff),
                jnp.zeros((width, n_dp, -3 * slice_ff % 128), BF),
            ],
            axis=2,
        ).transpose(1, 0, 2)
        packed, f_q = lax.optimization_barrier((packed, f_q))
        f_w = swap_dp(packed)
    full_q_up = f_q.reshape(-1, q_up.shape[1])
    full_kv_up = f_kv.reshape(-1, kv_up.shape[1])
    if not fused:
        normed, latents, q_normed, kv_normed, q_rows, kv_rows, key_rot, mixed = attend(
            layer_input, gain_attn, gain_q, gain_kv, full_down, full_q_up, full_kv_up,
            segment_ids, valid_mask, cos_full, sin_full,
        )
        f_normed, resid_rows, attn_rows = attention_residual(
            n_dp, dot_nt(mixed, full_o).astype(BF), x_rows, gain_mlp[None, :]
        )
    if not fused:
        mlp_part, normed_part, grad_packed = feed_forward(
            f_normed.reshape(n_dp * length, -1),
            f_cot.reshape(n_dp * length, -1),
            f_w.reshape(n_dp * width, -1),
            slice_ff,
            length,
        )
    weight_rows = rows_of(valid_mask.astype(F32)[:, None], share)
    if fused:
        f_block, grad_input, s_down, s_o, s_q, s_kv, s_small, swapped = back(
            n_dp, normed_part, mlp_part, grad_packed.reshape(n_dp, width, -1), resid_rows, attn_rows,
            cot_rows, layer_input, normed, latents, q_normed, kv_normed, q_rows, kv_rows,
            key_rot, mixed, f_down, f_o, f_q, f_kv, f_g, segment_ids, valid_mask,
            jnp.concatenate([cos_full, sin_full], axis=1),
        )
        (
            grad_w_gate, grad_w_up, grad_down_t, grad_o_t, grad_q_down, grad_kv_down_t, grad_q_up,
            grad_kv_up, block_full, grad_input, grad_attn_gain, grad_q_gain, grad_kv_gain, grad_mlp_gain, rms_stats,
        ) = unpack(
            swapped, s_down, s_o, s_q, s_kv, f_block.reshape(length, -1), grad_input, s_small,
            slice_ff, rank_q, columns_down,
            (attn_gain, q_gain, kv_gain, mlp_gain),
        )
        return (
            block_full,
            grad_input,
            grad_attn_gain.reshape(-1),
            grad_q_down,
            grad_q_gain.reshape(-1),
            grad_q_up,
            grad_kv_down_t.T,
            grad_kv_gain.reshape(-1),
            grad_kv_up,
            grad_o_t.T,
            grad_mlp_gain.reshape(-1),
            grad_w_gate,
            grad_w_up,
            grad_down_t.T,
            rms_stats.reshape(-1),
        )
    else:
        inv_two = inverse_rms(resid_rows)
        unit_two = resid_rows * inv_two
        swapped = swap_dp(grad_packed.reshape(n_dp, width, -1))
        normed_part, grad_packed = lax.optimization_barrier((normed_part, grad_packed))
        f_attn, grad_normed_two, f_block, mlp_rows = residual_grads(
            n_dp, normed_part, mlp_part, resid_rows, cot_rows, gain_mlp[None, :]
        )
        grad_attn = f_attn.reshape(length, -1)
        block_full = f_block.reshape(length, -1)

        grad_mlp_gain = jnp.sum(grad_normed_two * unit_two, axis=0)

        grad_part, grad_o, grad_q_up, grad_kv_up = attend_back(
            grad_attn, mixed, full_o, q_rows, kv_rows, key_rot, q_normed, kv_normed,
            full_q_up, full_kv_up, segment_ids, valid_mask, cos_full, sin_full,
            columns_down + pad_down,
        )
        grad_part, swapped = lax.optimization_barrier((grad_part, swapped))
        grad_latents = sum_latents(n_dp, grad_part).astype(F32)
        stream = layer_input.astype(F32)
        inv_one = inverse_rms(stream)
        unit_one = stream * inv_one
        q_latent = latents[:, :rank_q]
        inv_q = inverse_rms(q_latent)
        unit_q = q_latent * inv_q
        kv_latent = latents[:, rank_q : rank_q + KR]
        inv_kv = inverse_rms(kv_latent)
        unit_kv = kv_latent * inv_kv
        grad_q_normed = grad_latents[:, :rank_q]
        grad_kv_normed = grad_latents[:, rank_q : rank_q + KR]
        grad_kv_rot = grad_latents[:, rank_q + KR : columns_down]
        grad_q_gain = jnp.sum(grad_q_normed * unit_q, axis=0)
        grad_kv_gain = jnp.sum(grad_kv_normed * unit_kv, axis=0)
        grad_down = jnp.concatenate(
            [
                norm_back(grad_q_normed * gain_q, unit_q, inv_q),
                norm_back(grad_kv_normed * gain_kv, unit_kv, inv_kv),
                grad_kv_rot,
                jnp.zeros((length, pad_down), F32),
            ],
            axis=-1,
        ).astype(BF)
        grad_normed = dot_nt(grad_down, full_down)
        grad_attn_gain = jnp.sum(grad_normed * unit_one, axis=0)
        grad_input = grad_attn.astype(F32) * (1.0 / RESIDUAL_SCALE) + norm_back(
            grad_normed * gain_attn, unit_one, inv_one
        )

        quarter = lax.dynamic_index_in_dim(
            normed.reshape(length, n_dp, n_tensor, rows_down), me, 2, keepdims=False
        ).reshape(length, n_dp * rows_down)
        def by_dp(vector):
            return vector.reshape(n_dp, -1)

        def small_rows(vectors):
            return jnp.stack(
                [jnp.pad(by_dp(v), ((0, 0), (0, lanes - v.shape[0] // n_dp))) for v in vectors]
                + [jnp.zeros((n_dp, lanes), F32)] * (8 - len(vectors)),
                axis=1,
            )

        stats = jnp.stack(
            [
                jnp.sum(weight_rows * resid_rows * resid_rows),
                jnp.sum(weight_rows * attn_rows * attn_rows),
                jnp.sum(weight_rows * mlp_rows * mlp_rows),
                jnp.sum(weight_rows),
            ]
        )
        s_down, s_o, s_q, s_kv, s_small = sum_weight_grads(
            n_dp,
            dot_tn(quarter, grad_down).astype(BF),
            grad_o,
            grad_q_up,
            grad_kv_up,
            small_rows([grad_attn_gain, grad_q_gain, grad_kv_gain, grad_mlp_gain]),
            lane_rows([stats], 8, F32),
        )

    def columns_of(part):
        return part.transpose(1, 0, 2).reshape(width, n_dp * slice_ff).astype(F32)

    grad_w_gate = columns_of(swapped[:, :, :slice_ff])
    grad_w_up = columns_of(swapped[:, :, slice_ff : 2 * slice_ff])
    grad_w_down = columns_of(swapped[:, :, 2 * slice_ff : 3 * slice_ff]).T

    d_down = s_down.reshape(width, -1).astype(F32)
    gains = s_small[me, 0]
    stat_sums = jnp.sum(s_small[:, 1, 0, :4], axis=0)
    rms_stats = jnp.sqrt(stat_sums[:3] / (stat_sums[3] * D))
    return (
        block_full,
        grad_input,
        gains[0, : attn_gain.shape[0]],
        d_down[:, :rank_q],
        gains[1, : q_gain.shape[0]],
        s_q,
        d_down[:, rank_q:columns_down],
        gains[2, : kv_gain.shape[0]],
        s_kv,
        s_o.T,
        jnp.sum(s_small[:, 0, 3], axis=0)[: mlp_gain.shape[0]],
        grad_w_gate,
        grad_w_up,
        grad_w_down,
        rms_stats,
    )


def solution(mesh):
    placed = (
        P("dp", None),
        P("dp"),
        P("dp"),
        P("dp", None),
        P("dp"),
        P("dp", None),
        P("dp"),
        P("dp", "tensor"),
        P("dp", None),
        P("dp"),
        P("dp", "tensor"),
        P("tensor", "dp"),
        P("dp"),
        P("dp", "tensor"),
        P("dp", "tensor"),
        P("tensor", "dp"),
    )
    return jax.shard_map(
        per_device,
        mesh=mesh,
        in_specs=placed,
        out_specs=(
            P("dp", None),
            P("dp", None),
            P("dp"),
            P("dp", None),
            P("dp"),
            P("dp", "tensor"),
            P("dp", None),
            P("dp"),
            P("dp", "tensor"),
            P("tensor", "dp"),
            P("dp"),
            P("dp", "tensor"),
            P("dp", "tensor"),
            P("tensor", "dp"),
            P(),
        ),
        check_vma=False,
    )
```

```python
import functools
import itertools
import math

import jax
import jax.numpy as jnp
from jax import lax
from jax.experimental import pallas as pl
from jax.experimental.pallas import tpu as pltpu
from jax.sharding import PartitionSpec as P

D = 2560
KR = 256
NOPE = 64
ROPE = 32
VD = 64


NORM_EPS = 1e-05
RESIDUAL_SCALE = 1.4 / math.sqrt(62.0)
ROPE_BASE = 10000.0
NEGATIVE = -1e30


def rope_tables(length, rot_dim):
    half_dim = rot_dim // 2
    position = jnp.arange(length, dtype=jnp.float32)
    frequency = jnp.exp(
        -math.log(ROPE_BASE) * 2.0 * jnp.arange(half_dim, dtype=jnp.float32) / rot_dim
    )
    phases = position[:, None] * frequency[None, :]
    return (jnp.cos(phases), jnp.sin(phases))


def inverse_rms(values):
    return lax.rsqrt(jnp.mean(values * values, axis=-1, keepdims=True) + NORM_EPS)


def norm_back(grad_unit, unit, inv_rms):
    return inv_rms * (grad_unit - unit * jnp.mean(grad_unit * unit, axis=-1, keepdims=True))


BF = jnp.bfloat16
F32 = jnp.float32


def dot(left, right):
    return jnp.dot(left, right, preferred_element_type=F32)


def dot_nt(left, right):
    return jnp.einsum("ac,bc->ab", left, right, preferred_element_type=F32)


def dot_tn(left, right):
    return jnp.einsum("ca,cb->ab", left, right, preferred_element_type=F32)


def swap_dp(blocks):
    return lax.all_to_all(blocks, "dp", 0, 0, tiled=True)


MESH = pl.DeviceIdType.MESH
ANY = pl.BlockSpec(memory_space=pl.ANY)
VMEM = pl.BlockSpec(memory_space=pltpu.VMEM)
VMEM_BYTES = 60 * 1024 * 1024


class Links:
    def __init__(self, n_dp):
        self.n_high = n_dp // 2
        dp = lax.axis_index("dp")
        tensor = lax.axis_index("tensor")
        self.high, self.low = dp // 2, dp % 2
        self.side, self.core = tensor // 2, tensor % 2

    def device(self, high=None, low=None, side=None, core=None):
        high = self.high if high is None else high
        low = self.low if low is None else low
        side = self.side if side is None else side
        core = self.core if core is None else core
        return {"dp": high * 2 + low, "tensor": side * 2 + core}

    def behind(self, step):
        return (self.high + self.n_high - step) % self.n_high

    def ahead(self, step):
        return (self.high + step) % self.n_high

    def over_low(self):
        return self.device(low=1 - self.low)

    def over_side(self):
        return self.device(side=1 - self.side)

    def over_core(self):
        return self.device(core=1 - self.core)

    def meet(self, high=True, low=True, side=True, core=True, swap=False):
        barrier = pltpu.get_barrier_semaphore()
        partners = []
        if swap:
            partners += [
                self.device(high=self.ahead(k), low=1 - self.low) for k in range(1, self.n_high)
            ]
        if high:
            partners += [self.device(high=self.ahead(k)) for k in range(1, self.n_high)]
        if low:
            partners.append(self.over_low())
        if side:
            partners.append(self.over_side())
        if core:
            partners.append(self.over_core())
        for partner in partners:
            pl.semaphore_signal(barrier, inc=1, device_id=partner, device_id_type=MESH)
        pl.semaphore_wait(barrier, len(partners))


class Copies:
    def __init__(self, send, recv, local):
        self.send, self.recv, self.local = send, recv, local
        self.count = self.local_count = 0
        self.started = []
        self.maybe = []

    def go(self, source, target, device):
        copy = pltpu.make_async_remote_copy(
            src_ref=source,
            dst_ref=target,
            send_sem=self.send.at[self.count],
            recv_sem=self.recv.at[self.count],
            device_id=device,
            device_id_type=MESH,
        )
        self.count += 1
        copy.start()
        self.started.append(copy)
        return copy

    def sent_maybe(self):
        for condition, copy in self.maybe:
            pl.when(condition)(copy.wait_send)
        self.maybe = []

    def near(self, source, target):
        copy = pltpu.make_async_copy(source, target, self.local.at[self.local_count])
        self.local_count += 1
        copy.start()
        return copy

    def sent(self, copy):
        copy.wait_send()
        self.started = [other for other in self.started if other is not copy]

    def finish(self):
        for copy in self.started:
            copy.wait_send()
        for condition, copy in self.maybe:
            pl.when(condition)(copy.wait_send)


def take_turns(*streams):
    streams = list(streams)
    while streams:
        for stream in list(streams):
            try:
                next(stream)
            except StopIteration:
                streams.remove(stream)


def steps_by_distance(count):
    order, k = [], 1
    while len(order) < count - 1:
        order.append(k)
        if len(order) < count - 1:
            order.append(count - k)
        k += 1
    return order


class Line:
    def __init__(self, links, copies, block, target):
        self.links, self.copies, self.block, self.target = links, copies, block, target
        self.count = links.n_high
        self.first_tag = copies.count
        copies.count += self.count
        inner = steps_by_distance(self.count)
        at_start = (self.count - 1 - links.high) // (self.count - 1)
        at_end = links.high // (self.count - 1)
        self.tags = [0] + [
            at_start * (self.count - i) + at_end * i + (1 - at_start - at_end) * inner[i - 1]
            for i in range(1, self.count)
        ]

    def source(self, i):
        return (self.links.high + self.count - self.tags[i]) % self.count

    def send(self, condition, source, to, tag):
        copy = pltpu.make_async_remote_copy(
            src_ref=source,
            dst_ref=source if source is not self.block else self.target(self.links.high),
            send_sem=self.copies.send.at[self.copies.count],
            recv_sem=self.copies.recv.at[self.first_tag + tag],
            device_id=self.links.device(high=to),
            device_id_type=MESH,
        )
        self.copies.count += 1
        pl.when(condition)(copy.start)
        self.copies.maybe.append((condition, copy))

    def start(self):
        high = self.links.high
        self.send(high < self.count - 1, self.block, (high + 1) % self.count, 1)
        self.send(
            high > 0, self.block, (high + self.count - 1) % self.count, self.count - 1
        )

    def arrived(self, i):
        high, tag = self.links.high, self.tags[i]
        here = self.target(self.source(i))
        pltpu.make_async_remote_copy(
            src_ref=here,
            dst_ref=here,
            send_sem=self.copies.send.at[self.first_tag],
            recv_sem=self.copies.recv.at[self.first_tag + tag],
            device_id=self.links.over_low(),
            device_id_type=MESH,
        ).wait_recv()
        from_left = high >= tag
        onward = (from_left & (high < self.count - 1)) | ((high < tag) & (high > 0))
        way = jnp.where(from_left, 1, self.count - 1)
        self.send(onward, here, (high + way) % self.count, (tag + way) % self.count)


class Direct:
    def __init__(self, links, copies, block, target):
        self.links, self.copies, self.block, self.target = links, copies, block, target
        self.order = [0] + steps_by_distance(links.n_high)

    def source(self, i):
        return self.links.behind(self.order[i])

    def start(self):
        mine = self.target(self.links.high)
        self.arrive = [None] + [
            self.copies.go(self.block, mine, self.links.device(high=self.links.ahead(k)))
            for k in self.order[1:]
        ]

    def arrived(self, i):
        self.arrive[i].wait_recv()


def along_high(links, copies, block, target):
    return (Line if links.n_high == 4 else Direct)(links, copies, block, target)


class EveryGather:
    def __init__(self, links, copies, block, out, cut=None):
        self.links, self.copies, self.block, self.out = links, copies, block, out
        self.columns = out.shape[-1]
        self.cut = self.columns // 256 * 128 if cut is None else cut
        self.line = along_high(
            links, copies, block, lambda high: self.slot(high, links.low, links.side)
        )
        self.over_low, self.over_side = {}, {}
        self.corners = {i: [] for i in range(links.n_high)}
        self.last = {i: [] for i in range(links.n_high)}

    def slot(self, high, low, side):
        return self.out.at[high * 2 + low, side * 2 + self.links.core]

    def start(self):
        links = self.links
        self.own = self.copies.near(self.block, self.slot(links.high, links.low, links.side))
        self.line.start()

    def to_core(self, i, source, target):
        self.last[i].append(self.copies.go(source, target, self.links.over_core()))

    def first(self, i):
        links = self.links
        here = self.slot(self.line.source(i), links.low, links.side)
        if i:
            self.line.arrived(i)
        source = here if i else self.block
        self.over_low[i] = self.copies.go(source, here, links.over_low())
        self.over_side[i] = self.copies.go(source, here, links.over_side())
        self.to_core(i, source, here)

    def second(self, i):
        links, high = self.links, self.line.source(i)
        self.over_low[i].wait_recv()
        here = self.slot(high, 1 - links.low, links.side)
        if self.cut:
            half = pl.ds(0, self.cut)
            part = here.at[:, half]
            self.corners[i].append((self.copies.go(part, part, links.over_side()), half))
        self.to_core(i, here, here)
        self.over_side[i].wait_recv()
        here = self.slot(high, links.low, 1 - links.side)
        if self.cut < self.columns:
            half = pl.ds(self.cut, self.columns - self.cut)
            part = here.at[:, half]
            self.corners[i].append((self.copies.go(part, part, links.over_low()), half))
        self.to_core(i, here, here)

    def third(self, i):
        links = self.links
        here = self.slot(self.line.source(i), 1 - links.low, 1 - links.side)
        for corner, half in self.corners[i]:
            corner.wait_recv()
            part = here.at[:, half]
            self.to_core(i, part, part)

    def fourth(self, i):
        for copy in self.last[i]:
            copy.wait_recv()
        if i == 0:
            self.own.wait()

    def sent(self):
        copies = [*self.over_low.values(), *self.over_side.values()]
        copies += [corner for pairs in self.corners.values() for corner, _ in pairs]
        copies += [copy for last in self.last.values() for copy in last]
        for copy in copies:
            self.copies.sent(copy)
        self.copies.sent_maybe()


def every_gather(links, copies, block, out, cut=None):
    work = EveryGather(links, copies, block, out, cut)
    work.start()
    yield
    for i in range(links.n_high + 2):
        if i < links.n_high:
            work.first(i)
            yield
        if 0 <= i - 1 < links.n_high:
            work.second(i - 1)
            yield
        if 0 <= i - 2:
            work.third(i - 2)
            yield
    for i in range(links.n_high):
        work.fourth(i)


class DpGather:
    def __init__(self, links, copies, block, out):
        self.links, self.copies, self.block, self.out = links, copies, block, out
        self.line = along_high(links, copies, block, lambda high: out.at[high * 2 + links.low])
        self.last = []
        self.mine = out.at[links.high * 2 + links.low]

    def start(self):
        self.own = self.copies.near(self.block, self.mine)
        self.line.start()

    def own_low(self):
        self.last.append(self.copies.go(self.block, self.mine, self.links.over_low()))

    def step(self, i):
        self.line.arrived(i + 1)
        here = self.out.at[self.line.source(i + 1) * 2 + self.links.low]
        self.last.append(self.copies.go(here, here, self.links.over_low()))

    def finish(self):
        for copy in self.last:
            copy.wait_recv()
        self.own.wait()


def dp_gather(links, copies, block, out):
    work = DpGather(links, copies, block, out)
    work.start()
    yield
    work.own_low()
    yield
    for i in range(links.n_high - 1):
        work.step(i)
        yield
    work.finish()


def tensor_gather(links, copies, block, out):
    mine = out.at[links.side * 2 + links.core]
    own = copies.near(block, mine)
    last = [copies.go(block, mine, links.over_core())]
    across = copies.go(block, mine, links.over_side())
    yield
    across.wait_recv()
    here = out.at[(1 - links.side) * 2 + links.core]
    last.append(copies.go(here, here, links.over_core()))
    yield
    for copy in last:
        copy.wait_recv()
    own.wait()


class EveryScatter:
    def __init__(self, links, copies, part, bufs, result, cut):
        self.links, self.copies, self.part, self.result = links, copies, part, result
        self.own, self.chip, *bufs = bufs
        self.low_a, self.side_a = (bufs.pop(0), bufs.pop(0)) if cut else (None, None)
        self.side_b, self.low_b, self.done, self.from_high = bufs
        self.cut = cut
        self.half_a, self.half_b = pl.ds(0, cut), pl.ds(cut, part.shape[-1] - cut)
        self.order = steps_by_distance(links.n_high) + [0]
        self.loads, self.core_in, self.a_in, self.b_in = {}, {}, {}, {}
        self.a_last, self.b_last, self.high_in = {}, {}, {}

    def load(self, i):
        there = self.links.ahead(self.order[i])
        self.loads[i] = self.copies.near(
            self.part.at[there, :, :, self.links.core], self.own.at[i % 2]
        )

    def start(self):
        for i, k in enumerate(self.order):
            self.core_in[k] = self.copies.go(
                self.part.at[self.links.ahead(k), :, :, 1 - self.links.core],
                self.chip.at[k],
                self.links.over_core(),
            )
            if i < 2:
                self.load(i)

    def first(self, i):
        links, copies, chip, k = self.links, self.copies, self.chip, self.order[i]
        self.core_in[k].wait_recv()
        self.loads[i].wait()
        for low in range(2):
            for side in range(2):
                chip[k, low, side] = (
                    self.own[i % 2, low, side].astype(F32) + chip[k, low, side].astype(F32)
                ).astype(BF)
        if i + 2 < links.n_high:
            self.load(i + 2)
        if self.cut:
            self.a_in[k] = copies.go(
                chip.at[k, 1 - links.low, :, :, self.half_a], self.low_a.at[k], links.over_low()
            )
        self.b_in[k] = copies.go(
            chip.at[k, :, 1 - links.side, :, self.half_b], self.side_b.at[k], links.over_side()
        )

    def second(self, i):
        links, copies, chip, k = self.links, self.copies, self.chip, self.order[i]
        low_a, side_b = self.low_a, self.side_b
        if self.cut:
            self.a_in[k].wait_recv()
            for side in range(2):
                low_a[k, side] = (
                    low_a[k, side].astype(F32)
                    + chip[k, links.low, side, :, self.half_a].astype(F32)
                ).astype(BF)
            self.a_last[k] = copies.go(
                low_a.at[k, 1 - links.side], self.side_a.at[k], links.over_side()
            )
        self.b_in[k].wait_recv()
        for low in range(2):
            side_b[k, low] = (
                side_b[k, low].astype(F32) + chip[k, low, links.side, :, self.half_b].astype(F32)
            ).astype(BF)
        self.b_last[k] = copies.go(side_b.at[k, 1 - links.low], self.low_b.at[k], links.over_low())

    def third(self, i):
        links, k = self.links, self.order[i]
        if self.cut:
            self.a_last[k].wait_recv()
            self.done[k, :, self.half_a] = (
                self.side_a[k].astype(F32) + self.low_a[k, links.side].astype(F32)
            ).astype(BF)
        self.b_last[k].wait_recv()
        self.done[k, :, self.half_b] = (
            self.low_b[k].astype(F32) + self.side_b[k, links.low].astype(F32)
        ).astype(BF)
        if k:
            self.high_in[k] = self.copies.go(
                self.done.at[k], self.from_high.at[k - 1], links.device(high=links.ahead(k))
            )

    def finish(self):
        total = self.done[0].astype(F32)
        for k in steps_by_distance(self.links.n_high):
            self.high_in[k].wait_recv()
            total = total + self.from_high[k - 1].astype(F32)
        self.result[...] = total


def every_scatter(links, copies, part, bufs, result):
    work = EveryScatter(links, copies, part, bufs, result, part.shape[-1] // 256 * 128)
    work.start()
    yield
    for i in range(links.n_high + 2):
        if i < links.n_high:
            work.first(i)
            yield
        if 0 <= i - 1 < links.n_high:
            work.second(i - 1)
            yield
        if 0 <= i - 2:
            work.third(i - 2)
            yield
    work.finish()


def every_scatter_scratch(n_high, rows, columns, cut=None):
    cut = columns // 256 * 128 if cut is None else cut
    over_low = [
        pltpu.VMEM((n_high, 2, rows, cut), BF),
        pltpu.VMEM((n_high, rows, cut), BF),
    ]
    return [
        pltpu.VMEM((2, 2, 2, rows, columns), BF),
        pltpu.VMEM((n_high, 2, 2, rows, columns), BF),
        *(over_low if cut else []),
        pltpu.VMEM((n_high, 2, rows, columns - cut), BF),
        pltpu.VMEM((n_high, rows, columns - cut), BF),
        pltpu.VMEM((n_high, rows, columns), BF),
        pltpu.VMEM((n_high - 1, rows, columns), BF),
    ]


def dp_scatter(links, copies, part, bufs, result):
    from_low, done, from_high = bufs
    order = steps_by_distance(links.n_high) + [0]
    low_in, high_in = {}, {}
    for k in order:
        low_in[k] = copies.go(
            part.at[links.ahead(k), 1 - links.low], from_low.at[k], links.over_low()
        )
    yield
    for k in order:
        low_in[k].wait_recv()
        done[k] = (
            part[links.ahead(k), links.low].astype(F32) + from_low[k].astype(F32)
        ).astype(BF)
        if k:
            high_in[k] = copies.go(
                done.at[k], from_high.at[k - 1], links.device(high=links.ahead(k))
            )
        yield
    total = done[0].astype(F32)
    for k in steps_by_distance(links.n_high):
        high_in[k].wait_recv()
        total = total + from_high[k - 1].astype(F32)
    result[...] = total.astype(result.dtype)
    yield


def dp_scatter_scratch(n_high, shape):
    return [
        pltpu.VMEM((n_high, *shape), BF),
        pltpu.VMEM((n_high, *shape), BF),
        pltpu.VMEM((n_high - 1, *shape), BF),
    ]


def semaphores(count, local):
    return [
        pltpu.SemaphoreType.DMA((count,)),
        pltpu.SemaphoreType.DMA((count,)),
        pltpu.SemaphoreType.DMA((local,)),
    ]


def params(number, mebibytes=60):
    return pltpu.CompilerParams(
        collective_id=number, has_side_effects=True, vmem_limit_bytes=mebibytes * 1024 * 1024
    )


def count_every_gather(n_high):
    return 11 * n_high + 1


def count_dp_gather(n_high):
    return 3 * n_high + 1


def weights_kernel(n_dp, down, o_t, q_up, kv_up, gains, cot, f_down, f_o, f_q, f_kv, f_g, f_cot, send, recv, local):
    links = Links(n_dp)
    copies = Copies(send, recv, local)
    links.meet()
    take_turns(
        every_gather(links, copies, down, f_down),
        dp_gather(links, copies, gains, f_g),
        dp_gather(links, copies, q_up, f_q),
        dp_gather(links, copies, kv_up, f_kv),
        dp_gather(links, copies, o_t, f_o),
        every_gather(links, copies, cot, f_cot),
    )
    copies.finish()


def gather_weights(n_dp, n_tensor, down, o_t, q_up, kv_up, gains, cot):
    n_high = n_dp // 2
    count = 2 * count_every_gather(n_high) + 4 * count_dp_gather(n_high)

    def over(block, *lead):
        return jax.ShapeDtypeStruct((*lead, *block.shape), block.dtype)

    return pl.pallas_call(
        functools.partial(weights_kernel, n_dp),
        out_shape=(
            over(down, n_dp, n_tensor),
            over(o_t, n_dp),
            over(q_up, n_dp),
            over(kv_up, n_dp),
            over(gains, n_dp),
            over(cot, n_dp, n_tensor),
        ),
        in_specs=[ANY] * 6,
        out_specs=[ANY] * 6,
        scratch_shapes=semaphores(count, 6),
        compiler_params=params(1),
        name="gather_weights",
    )(down, o_t, q_up, kv_up, gains, cot)


def resid_kernel(n_dp, part, x_rows, gain, full, resid, branch, from_core, out_side, from_side, block, send, recv, local):
    links = Links(n_dp)
    copies = Copies(send, recv, local)
    links.meet()
    arrive = copies.go(part.at[:, 1 - links.core], from_core, links.over_core())
    arrive.wait_recv()
    out_side[...] = (
        part[1 - links.side, links.core].astype(F32) + from_core[1 - links.side].astype(F32)
    ).astype(BF)
    arrive = copies.go(out_side, from_side, links.over_side())
    mine = part[links.side, links.core].astype(F32) + from_core[links.side].astype(F32)
    arrive.wait_recv()
    attn = RESIDUAL_SCALE * (mine + from_side[...].astype(F32))
    stream = x_rows[...].astype(F32) + attn
    branch[...] = attn
    resid[...] = stream
    block[...] = (stream * inverse_rms(stream) * gain[...]).astype(BF)
    take_turns(every_gather(links, copies, block, full))
    copies.finish()


def attention_residual(n_dp, part, x_rows, gain):
    n_tensor = 4
    rows, columns = x_rows.shape
    block = (rows, columns)
    return pl.pallas_call(
        functools.partial(resid_kernel, n_dp),
        out_shape=(
            jax.ShapeDtypeStruct((n_dp, n_tensor, rows, columns), BF),
            jax.ShapeDtypeStruct(block, F32),
            jax.ShapeDtypeStruct(block, F32),
        ),
        in_specs=[VMEM] * 3,
        out_specs=[ANY, VMEM, VMEM],
        scratch_shapes=[
            pltpu.VMEM((2, *block), BF),
            pltpu.VMEM(block, BF),
            pltpu.VMEM(block, BF),
            pltpu.VMEM(block, BF),
            *semaphores(2 + count_every_gather(n_dp // 2), 1),
        ],
        compiler_params=params(2),
        name="attention_residual",
    )(part.reshape(2, 2, rows, columns), x_rows, gain)


def grad_rows_kernel(n_dp, both, *refs):
    links = Links(n_dp)
    copies = Copies(*refs[-3:])
    g_part, resid, cot, gain = refs[:4]
    if both:
        m_part, attn_full, g_rows, block_full, m_rows = refs[4:9]
        scratch = refs[9:-3]
    else:
        attn_full, g_rows = refs[4:6]
        scratch = refs[6:-3]
    links.meet()

    def grad_stream():
        grad_rows = scratch[0]
        yield from every_scatter(links, copies, g_part, scratch[1:9], g_rows)
        stream = resid[...]
        inv = inverse_rms(stream)
        grad = cot[...].astype(F32) + norm_back(g_rows[...] * gain[...], stream * inv, inv)
        grad_rows[...] = (RESIDUAL_SCALE * grad).astype(BF)
        yield from tensor_gather(links, copies, grad_rows, attn_full)

    if both:
        block = block_stream(links, copies, m_part, resid, block_full, m_rows, scratch[9:])
        take_turns(grad_stream(), block)
    else:
        take_turns(grad_stream())
    copies.finish()


def block_stream(links, copies, m_part, resid, block_full, m_rows, scratch):
    block_rows = scratch[0]
    yield from every_scatter(links, copies, m_part, scratch[1:9], m_rows)
    m_rows[...] = RESIDUAL_SCALE * m_rows[...]
    block_rows[...] = resid[...] + m_rows[...]
    yield from tensor_gather(links, copies, block_rows, block_full)


def block_rows_kernel(n_dp, m_part, resid, block_full, m_rows, *rest):
    links = Links(n_dp)
    copies = Copies(*rest[-3:])
    links.meet()
    take_turns(block_stream(links, copies, m_part, resid, block_full, m_rows, rest[:-3]))
    copies.finish()


def residual_grads(n_dp, g_part, m_part, resid, cot, gain):
    n_high = n_dp // 2
    rows, columns = resid.shape
    shape = (n_high, 2, 2, 2, rows, columns)
    g_part, m_part = g_part.reshape(shape), m_part.reshape(shape)
    both = n_high <= 4
    one = jax.ShapeDtypeStruct((rows, columns), F32)
    grad_out = (jax.ShapeDtypeStruct((4, rows, columns), BF), one)
    block_out = (jax.ShapeDtypeStruct((4, rows, columns), F32), one)
    grad_scratch = [
        pltpu.VMEM((rows, columns), BF),
        *every_scatter_scratch(n_high, rows, columns),
    ]
    block_scratch = [
        pltpu.VMEM((rows, columns), F32),
        *every_scatter_scratch(n_high, rows, columns),
    ]
    count, local = 6 * n_high - 1 + 3, n_high + 1
    if both:
        return pl.pallas_call(
            functools.partial(grad_rows_kernel, n_dp, True),
            out_shape=grad_out + block_out,
            in_specs=[ANY, VMEM, VMEM, VMEM, ANY],
            out_specs=[ANY, VMEM, ANY, VMEM],
            scratch_shapes=[*grad_scratch, *block_scratch, *semaphores(2 * count, 2 * local)],
            compiler_params=params(3),
            name="residual_grads",
        )(g_part, resid, cot, gain, m_part)
    grads = pl.pallas_call(
        functools.partial(grad_rows_kernel, n_dp, False),
        out_shape=grad_out,
        in_specs=[ANY, VMEM, VMEM, VMEM],
        out_specs=[ANY, VMEM],
        scratch_shapes=[*grad_scratch, *semaphores(count, local)],
        compiler_params=params(3),
        name="residual_grads",
    )(g_part, resid, cot, gain)
    block = pl.pallas_call(
        functools.partial(block_rows_kernel, n_dp),
        out_shape=block_out,
        in_specs=[ANY, VMEM],
        out_specs=[ANY, VMEM],
        scratch_shapes=[*block_scratch, *semaphores(count, local)],
        compiler_params=params(6),
        name="block_rows",
    )(m_part, resid)
    return (*grads, *block)


def latent_kernel(n_dp, part, full, from_core, half, from_side, send, recv, local):
    links = Links(n_dp)
    copies = Copies(send, recv, local)
    links.meet(high=False, low=False)
    arrive = copies.go(part.at[1 - links.core], from_core, links.over_core())
    arrive.wait_recv()
    half[...] = (part[links.core].astype(F32) + from_core[...].astype(F32)).astype(BF)
    arrive = copies.go(half, from_side, links.over_side())
    arrive.wait_recv()
    full[links.core] = (half[...].astype(F32) + from_side[...].astype(F32)).astype(BF)
    arrive = copies.go(full.at[links.core], full.at[links.core], links.over_core())
    arrive.wait_recv()
    copies.finish()


def sum_latents(n_dp, part):
    rows, columns = part.shape
    half = (rows // 2, columns)
    return pl.pallas_call(
        functools.partial(latent_kernel, n_dp),
        out_shape=jax.ShapeDtypeStruct((2, *half), BF),
        in_specs=[VMEM],
        out_specs=VMEM,
        scratch_shapes=[pltpu.VMEM(half, BF)] * 3 + semaphores(3, 1),
        compiler_params=params(4),
        name="sum_latents",
    )(part.reshape(2, *half)).reshape(rows, columns)


def weight_grads_kernel(n_dp, d_part, o_part, q_part, kv_part, small, stats, d_full, o_sum, q_sum, kv_sum, small_full, *rest):
    d_block, small_block, stats_block = rest[:3]
    bufs = rest[3:15]
    small_in, stats_in = rest[15:17]
    send, recv, local = rest[17:]
    links = Links(n_dp)
    copies = Copies(send, recv, local)
    links.meet()

    def small_stream():
        n_high = links.n_high
        low_in = copies.go(
            small.at[:, 1 - links.low], small_in.at[pl.ds(0, n_high)], links.over_low()
        )
        stats_low = copies.go(stats, stats_in.at[0], links.over_low())
        yield
        low_in.wait_recv()
        stats_low.wait_recv()
        for k in range(n_high):
            small_in[k] = small_in[k] + small[k, links.low]
        stats_block[...] = stats[...] + stats_in[0]
        waits = []
        for k in range(1, n_high):
            there = links.ahead(k)
            waits.append(
                copies.go(
                    small_in.at[there], small_in.at[n_high + k - 1], links.device(high=there)
                )
            )
            waits.append(copies.go(stats_block, stats_in.at[k], links.device(high=there)))
        yield
        for wait in waits:
            wait.wait_recv()
        total = small_in[links.high]
        everything = stats_block[...]
        for k in range(1, n_high):
            total = total + small_in[n_high + k - 1]
            everything = everything + stats_in[k]
        small_block[0] = total
        small_block[1] = everything
        yield from tensor_gather(links, copies, small_block, small_full)

    def down_stream():
        yield from dp_scatter(links, copies, d_part, bufs[:3], d_block)
        yield from tensor_gather(links, copies, d_block, d_full)

    take_turns(
        down_stream(),
        dp_scatter(links, copies, q_part, bufs[6:9], q_sum),
        dp_scatter(links, copies, kv_part, bufs[9:12], kv_sum),
        dp_scatter(links, copies, o_part, bufs[3:6], o_sum),
        small_stream(),
    )
    copies.finish()


def sum_weight_grads(n_dp, down, o_t, q_up, kv_up, small, stats):
    n_high = n_dp // 2

    def parts(array):
        return array.reshape(n_high, 2, array.shape[0] // n_dp, *array.shape[1:])

    down, o_t, q_up, kv_up = parts(down), parts(o_t), parts(q_up), parts(kv_up)
    small = small.reshape(n_high, 2, *small.shape[1:])
    count = 4 * (2 * n_high - 1) + 2 * n_high + 6
    d_shape, o_shape, q_shape, kv_shape = (a.shape[2:] for a in (down, o_t, q_up, kv_up))
    one = stats.shape
    return pl.pallas_call(
        functools.partial(weight_grads_kernel, n_dp),
        out_shape=(
            jax.ShapeDtypeStruct((4, *d_shape), BF),
            jax.ShapeDtypeStruct(o_shape, F32),
            jax.ShapeDtypeStruct(q_shape, F32),
            jax.ShapeDtypeStruct(kv_shape, F32),
            jax.ShapeDtypeStruct((4, 2, *one), F32),
        ),
        in_specs=[VMEM] * 6,
        out_specs=[VMEM] * 5,
        scratch_shapes=[
            pltpu.VMEM(d_shape, BF),
            pltpu.VMEM((2, *one), F32),
            pltpu.VMEM(one, F32),
            *dp_scatter_scratch(n_high, d_shape),
            *dp_scatter_scratch(n_high, o_shape),
            *dp_scatter_scratch(n_high, q_shape),
            *dp_scatter_scratch(n_high, kv_shape),
            pltpu.VMEM((2 * n_high - 1, *one), F32),
            pltpu.VMEM((n_high, *one), F32),
            *semaphores(count, 2),
        ],
        compiler_params=params(5),
        name="sum_weight_grads",
    )(down, o_t, q_up, kv_up, small, stats)


def attention_mask(seg_row, valid_row):
    length = seg_row.shape[1]
    row = lax.broadcasted_iota(jnp.int32, (length, length), 0)
    column = lax.broadcasted_iota(jnp.int32, (length, length), 1)
    segments = jnp.broadcast_to(seg_row[...].astype(F32), (length, length))
    allowed = (
        (segments == segments.T)
        & (column <= row)
        & ((valid_row[...] == 1) | (column == row))
    )
    return jnp.where(allowed, 0.0, NEGATIVE)


def swap_halves(values):
    half = values.shape[1] // 2
    return jnp.concatenate([values[:, half:], values[:, :half]], axis=1)


def turn(values, cos_full, sin_full):
    return values * cos_full + swap_halves(values) * sin_full


def head_probs(query, key, bias, inv_root):
    scores = dot_nt(query, key) * inv_root + bias
    weights = jnp.exp(scores - jnp.max(scores, axis=-1, keepdims=True))
    return weights / jnp.sum(weights, axis=-1, keepdims=True)


def latent_rows(x, gain_attn, down, normed, latents):
    stream = x[...].astype(F32)
    normed[...] = (stream * inverse_rms(stream) * gain_attn).astype(BF)
    latents[...] = dot(normed[...], down)


def attend_rows(
    gain_q, gain_kv, q_up, kv_up, bias, cos_full, sin_full, latents, q_normed, kv_normed, q_rows, kv_rows, key_rot, mixed,
):
    rank_q = gain_q.shape[1]
    q_latent = latents[:, :rank_q]
    q_normed[...] = (q_latent * inverse_rms(q_latent) * gain_q).astype(BF)
    kv_latent = latents[:, rank_q : rank_q + KR]
    kv_normed[...] = (kv_latent * inverse_rms(kv_latent) * gain_kv).astype(BF)
    turned = turn(latents[:, rank_q + KR : rank_q + KR + ROPE], cos_full[...], sin_full[...])
    key_rot[...] = turned.astype(BF)
    kv_rows[...] = dot(kv_normed[...], kv_up).astype(BF)
    q_heads = dot(q_normed[...], q_up)
    inv_root = 1.0 / math.sqrt(NOPE + ROPE)
    for head in range(q_rows.shape[1] // (NOPE + ROPE)):
        base = head * (NOPE + ROPE)
        query = jnp.concatenate(
            [
                q_heads[:, base : base + NOPE],
                turn(
                    q_heads[:, base + NOPE : base + NOPE + ROPE], cos_full[...], sin_full[...]
                ),
            ],
            axis=1,
        ).astype(BF)
        q_rows[:, base : base + NOPE + ROPE] = query
        start = head * (NOPE + VD)
        key = jnp.concatenate([kv_rows[:, start : start + NOPE], key_rot[...]], axis=1)
        value = kv_rows[:, start + NOPE : start + NOPE + VD]
        probs = head_probs(query, key, bias, inv_root).astype(BF)
        mixed[:, head * VD : head * VD + VD] = dot(probs, value).astype(BF)


def attend_kernel(
    x, gain_attn, gain_q, gain_kv, down, q_up, kv_up, seg_row, valid_row, cos_full, sin_full,
    normed, *outs,
):
    latent_rows(x, gain_attn[...], down[...], normed, outs[0])
    attend_rows(
        gain_q[...], gain_kv[...], q_up[...], kv_up[...], attention_mask(seg_row, valid_row),
        cos_full, sin_full, *outs,
    )


def attend(x, gain_attn, gain_q, gain_kv, down, q_up, kv_up, segments, valid, cos_full, sin_full):
    length = x.shape[0]
    heads = q_up.shape[1] // (NOPE + ROPE)

    def rows(columns, kind):
        return jax.ShapeDtypeStruct((length, columns), kind)

    return pl.pallas_call(
        attend_kernel,
        out_shape=(
            rows(x.shape[1], BF),
            rows(down.shape[1], F32),
            rows(q_up.shape[0], BF),
            rows(kv_up.shape[0], BF),
            rows(q_up.shape[1], BF),
            rows(kv_up.shape[1], BF),
            rows(ROPE, BF),
            rows(heads * VD, BF),
        ),
        in_specs=[VMEM] * 11,
        out_specs=[VMEM] * 8,
        compiler_params=pltpu.CompilerParams(vmem_limit_bytes=VMEM_BYTES),
        name="attend",
    )(
        x,
        gain_attn[None, :],
        gain_q[None, :],
        gain_kv[None, :],
        down,
        q_up,
        kv_up,
        segments[None, :],
        valid[None, :],
        cos_full,
        sin_full,
    )


def later(stream, turns):
    for _ in range(turns):
        yield
    yield from stream


class Swap:
    def __init__(self, links, copies, blocks, out):
        self.me = links.high * 2 + links.low
        self.copies, self.blocks, self.out = copies, blocks, out
        self.own = copies.near(blocks.at[self.me], out.at[self.me])
        self.arrive = []

    def send(self, steps):
        n_dp = self.blocks.shape[0]
        for k in steps:
            there = (self.me + k) % n_dp
            self.arrive.append(
                self.copies.go(self.blocks.at[there], self.out.at[self.me], {"dp": there})
            )

    def finish(self):
        for copy in self.arrive:
            copy.wait_recv()
        self.own.wait()

    def sent(self):
        for copy in self.arrive:
            self.copies.sent(copy)


def pack_stream(w_gate, w_up, w_down_t, packed):
    n_dp, width, lanes = packed.shape
    slice_ff = w_gate.shape[1] // n_dp
    for k in range(n_dp):
        at = k * slice_ff
        packed[k] = jnp.concatenate(
            [
                w_gate[:, at : at + slice_ff],
                w_up[:, at : at + slice_ff],
                w_down_t[:, at : at + slice_ff],
                jnp.zeros((width, lanes - 3 * slice_ff), BF),
            ],
            axis=1,
        )
        yield


def quarter_of(values, rank):
    rows = values.shape[0] // 4
    mine = values[:rows]
    for other in range(1, 4):
        mine = jnp.where(rank == other, values[other * rows : other * rows + rows], mine)
    return mine


def forward_kernel(
    n_dp, x, cotangent, q_down, kv_down_t, gain_attn, gain_q, gain_kv, gain_mlp, q_up, kv_up, o_t,
    w_gate, w_up, w_down_t, seg_row, valid_row, turns,
    d_out, o_out, q_out, kv_out, f_g, m_part, g_part, w_grads,
    normed, latents, q_normed, kv_normed, q_rows, kv_rows, key_rot, mixed, resid, branch, cot,
    f_down, f_o, f_q, f_kv, down, gains, packed, f_w, f_cot, f_normed, hidden_all, both_all, m_block, g_block,
    part, from_core, out_side, from_side, block, send, recv, local,
):
    links = Links(n_dp)
    copies = Copies(send, recv, local)
    cos_full, sin_full = turns[:, :ROPE], turns[:, ROPE:]
    rank = links.side * 2 + links.core
    rows_down, rank_q = down.shape[0], q_down.shape[1]
    quarter = pl.ds(pl.multiple_of(rank * rows_down, 16), rows_down)
    down[:, :rank_q] = q_down[quarter, :]
    kv_rows_down = quarter_of(kv_down_t[...].T, rank)
    pad = down.shape[1] - rank_q - kv_rows_down.shape[1]
    down[:, rank_q:] = jnp.concatenate([kv_rows_down, jnp.zeros((rows_down, pad), BF)], axis=1)
    lanes = gains.shape[1]
    gain_rows = [
        jnp.concatenate([g[...].astype(F32), jnp.zeros((1, lanes - g.shape[1]), F32)], axis=1)
        for g in (gain_attn, gain_q, gain_kv, gain_mlp)
    ]
    gains[...] = jnp.concatenate(gain_rows + [jnp.zeros((12, lanes), F32)], axis=0).astype(BF)
    rows = block.shape[0]
    own_rows = pl.ds(pl.multiple_of(rank * rows, 16), rows)
    cot[...] = cotangent[own_rows, :]
    links.meet(swap=True)
    downs = EveryGather(links, copies, down, f_down)
    small_gathers = [
        DpGather(links, copies, source, target)
        for source, target in ((gains, f_g), (q_up, f_q), (kv_up, f_kv))
    ]
    o = DpGather(links, copies, o_t, f_o)
    cots = EveryGather(links, copies, cot, f_cot)
    downs.start()
    for work in small_gathers:
        work.start()
    n_high = links.n_high
    downs.first(0)
    for work in small_gathers:
        work.own_low()
    for i in range(1, n_high):
        downs.first(i)
        downs.second(i - 1)
    for i in range(n_high - 1):
        for work in small_gathers:
            work.step(i)
    o.start()
    o.own_low()
    downs.second(n_high - 1)
    for _ in pack_stream(w_gate, w_up, w_down_t, packed):
        pass
    swap = Swap(links, copies, packed, f_w)
    for i in range(n_high):
        downs.third(i)
    for i in range(n_high):
        downs.fourth(i)
    small_gathers[0].finish()

    def gain_of(row, count):
        return jnp.concatenate(
            [f_g[k].astype(F32)[row : row + 1, :count] for k in range(n_dp)], axis=1
        )

    width = o_t.shape[0]
    full_down = f_down[...].reshape(n_dp * width, down.shape[1])
    latent_rows(x, gain_of(0, width), full_down, normed, latents)
    for work in small_gathers[1:]:
        work.finish()
    full_q = f_q[...].reshape(n_dp * q_up.shape[0], q_up.shape[1])
    full_kv = f_kv[...].reshape(n_dp * kv_up.shape[0], kv_up.shape[1])
    keeps = [
        copies.near(source, target)
        for source, target in ((f_down, d_out), (f_q, q_out), (f_kv, kv_out))
    ]
    o.step(0)
    attend_rows(
        gain_of(1, q_up.shape[0]), gain_of(2, kv_up.shape[0]), full_q, full_kv,
        attention_mask(seg_row, valid_row), cos_full, sin_full,
        latents, q_normed, kv_normed, q_rows, kv_rows, key_rot, mixed,
    )
    for i in range(1, n_high - 1):
        o.step(i)
    cots.start()
    cots.first(0)
    swap.send(range(2, n_dp, 2))
    swap.send(range(1, n_dp, 2))
    o.finish()
    keeps.append(copies.near(f_o, o_out))
    full_o = f_o[...].reshape(n_dp * width, o_t.shape[1])
    attn_part = dot_nt(mixed[...], full_o).astype(BF)
    for side in range(2):
        for core in range(2):
            at = (side * 2 + core) * rows
            part[side, core] = attn_part[at : at + rows]
    over = copies.go(part.at[:, 1 - links.core], from_core, links.over_core())
    over.wait_recv()
    out_side[...] = (
        part[1 - links.side, links.core].astype(F32) + from_core[1 - links.side].astype(F32)
    ).astype(BF)
    over = copies.go(out_side, from_side, links.over_side())
    mine = part[links.side, links.core].astype(F32) + from_core[links.side].astype(F32)
    over.wait_recv()
    attn = RESIDUAL_SCALE * (mine + from_side[...].astype(F32))
    stream = x[own_rows, :].astype(F32) + attn
    branch[...] = attn
    resid[...] = stream
    block[...] = (stream * inverse_rms(stream) * gain_of(3, width)).astype(BF)
    normeds = EveryGather(links, copies, block, f_normed)
    normeds.start()
    normeds.first(0)
    for i in range(n_high + 2):
        if 1 <= i < n_high:
            cots.first(i)
        if 0 <= i - 1 < n_high:
            cots.second(i - 1)
        if 0 <= i - 2:
            cots.third(i - 2)
    normeds.second(0)
    for i in range(n_high):
        cots.fourth(i)
    swap.finish()
    cots.sent()
    normeds.third(0)
    normeds.fourth(0)

    lanes = f_w.shape[2]
    slice_ff = w_gate.shape[1] // n_dp
    wide = both_all.shape[1]
    cut = lanes - hidden_all.shape[1]
    before = 2 * slice_ff - cut
    columns = x.shape[1]
    tokens = 2 * x.shape[0]
    stores = []

    def zeros(count):
        return jnp.zeros((tokens, count), F32)

    def feed_forward_of(high):
        pair = pl.ds(high * 2, 2)
        at = pl.ds(pl.multiple_of(high * tokens, 128), tokens)
        w_in = f_w[:, :, :wide].reshape(columns, wide)
        w_out = f_w[:, :, cut:].reshape(columns, lanes - cut)
        grad_mlp = (RESIDUAL_SCALE * f_cot[pair].astype(F32)).astype(BF)
        f_cot[pair] = grad_mlp
        both = dot(f_normed[pair].reshape(tokens, columns), w_in)
        gate, upper = both[:, :slice_ff], both[:, slice_ff : 2 * slice_ff]
        sigma = jax.nn.sigmoid(gate)
        swish = gate * sigma
        after = lanes - cut - before - slice_ff
        hidden = jnp.concatenate([zeros(before), swish * upper, zeros(after)], axis=1).astype(BF)
        grad_hidden = dot(grad_mlp.reshape(tokens, columns), w_out)[:, before : before + slice_ff]
        grad_both = jnp.concatenate(
            [
                grad_hidden * upper * (sigma * (1.0 + gate * (1.0 - sigma))),
                grad_hidden * swish,
                zeros(wide - 2 * slice_ff),
            ],
            axis=1,
        ).astype(BF)
        hidden_all[at, :] = hidden
        both_all[at, :] = grad_both
        while stores:
            stores.pop().wait()
        m_block[...] = dot_nt(hidden, w_out).astype(BF).reshape(m_block.shape)
        stores.append(copies.near(m_block, m_part.at[pair]))
        g_block[...] = dot_nt(grad_both, w_in).astype(BF).reshape(g_block.shape)
        stores.append(copies.near(g_block, g_part.at[pair]))

    for i in range(1, n_high):
        normeds.first(i)
        if i == 1:
            feed_forward_of(normeds.line.source(0))
        normeds.second(i)
        normeds.third(i)
        if i > 1:
            feed_forward_of(normeds.line.source(i - 1))
        normeds.fourth(i)
    feed_forward_of(normeds.line.source(n_high - 1))
    swap.sent()
    all_tokens = n_dp * x.shape[0]
    for k in range(n_dp):
        at = k * width
        slab_in = dot_tn(
            f_normed[:, :, :, at : at + width].reshape(all_tokens, width), both_all[...]
        )
        slab_out = dot_tn(
            f_cot[:, :, :, at : at + width].reshape(all_tokens, width), hidden_all[...]
        )
        packed[k, :, :cut] = slab_in[:, :cut].astype(BF)
        packed[k, :, cut:wide] = (slab_in[:, cut:] + slab_out[:, : wide - cut]).astype(BF)
        packed[k, :, wide:] = slab_out[:, wide - cut :].astype(BF)
        stores.append(copies.near(packed.at[k], w_grads.at[k]))
    while stores:
        stores.pop().wait()
    for keep in keeps:
        keep.wait()
    copies.finish()


def forward(
    n_dp, x, cotangent, q_down, kv_down_t, gains, q_up, kv_up, o_t, w_gate, w_up, w_down_t,
    segments, valid, turns, down_shape, gain_lanes,
):
    n_high = n_dp // 2
    length, columns = x.shape
    rows = length // 4
    slice_ff = w_gate.shape[1] // n_dp
    lanes = -(-3 * slice_ff // 128) * 128
    wide = -(-2 * slice_ff // 128) * 128
    cut = 2 * slice_ff // 128 * 128
    heads = q_up.shape[1] // (NOPE + ROPE)
    count = 3 * count_every_gather(n_high) + 4 * count_dp_gather(n_high) + n_dp + 1
    block = (rows, columns)

    def over(block, *lead, kind=BF):
        return jax.ShapeDtypeStruct((*lead, *block), kind)

    return pl.pallas_call(
        functools.partial(forward_kernel, n_dp),
        out_shape=(
            over(down_shape, n_dp, 4),
            over(o_t.shape, n_dp),
            over(q_up.shape, n_dp),
            over(kv_up.shape, n_dp),
            over((16, gain_lanes), n_dp),
            over(block, n_dp, 4),
            over(block, n_dp, 4),
            over((w_gate.shape[0], lanes), n_dp),
            over((columns,), length),
            over((down_shape[1],), length, kind=F32),
            over((q_up.shape[0] * n_dp,), length),
            over((kv_up.shape[0] * n_dp,), length),
            over((q_up.shape[1],), length),
            over((kv_up.shape[1],), length),
            over((ROPE,), length),
            over((heads * VD,), length),
            over(block, kind=F32),
            over(block, kind=F32),
            over(block),
        ),
        in_specs=[VMEM] * 17,
        out_specs=[ANY] * 4 + [VMEM] + [ANY] * 3 + [VMEM] * 11,
        scratch_shapes=[
            pltpu.VMEM((n_dp, 4, *down_shape), BF),
            pltpu.VMEM((n_dp, *o_t.shape), BF),
            pltpu.VMEM((n_dp, *q_up.shape), BF),
            pltpu.VMEM((n_dp, *kv_up.shape), BF),
            pltpu.VMEM(down_shape, BF),
            pltpu.VMEM((16, gain_lanes), BF),
            pltpu.VMEM((n_dp, w_gate.shape[0], lanes), BF),
            pltpu.VMEM((n_dp, w_gate.shape[0], lanes), BF),
            pltpu.VMEM((n_dp, 4, *block), BF),
            pltpu.VMEM((n_dp, 4, *block), BF),
            pltpu.VMEM((n_dp * length, lanes - cut), BF),
            pltpu.VMEM((n_dp * length, wide), BF),
            pltpu.VMEM((2, 4, *block), BF),
            pltpu.VMEM((2, 4, *block), BF),
            pltpu.VMEM((2, 2, *block), BF),
            pltpu.VMEM((2, *block), BF),
            pltpu.VMEM(block, BF),
            pltpu.VMEM(block, BF),
            pltpu.VMEM(block, BF),
            *semaphores(count, 12 + 2 * n_high + n_dp),
        ],
        compiler_params=params(7, 62),
        name="forward",
    )(
        x, cotangent, q_down, kv_down_t, *(g[None, :] for g in gains), q_up, kv_up, o_t,
        w_gate, w_up, w_down_t, segments[None, :], valid[None, :], turns,
    )


def feed_forward_kernel(slice_ff, normed, cot, weights, m_part, g_part, grads, sum_in, sum_out):
    step = pl.program_id(0)
    cut = slice_ff * 2 // 128 * 128
    pad = slice_ff * 2 - cut
    w_in, w_out = weights[:, : sum_in.shape[0]], weights[:, cut:]
    rows = normed.shape[0]
    both = dot(normed[...], w_in)
    gate, upper = both[:, :slice_ff], both[:, slice_ff : 2 * slice_ff]
    sigma = jax.nn.sigmoid(gate)
    swish = gate * sigma

    def zeros(count):
        return jnp.zeros((rows, count), F32)

    def placed(hidden):
        rest = w_out.shape[1] - pad - slice_ff
        return jnp.concatenate([zeros(pad), hidden, zeros(rest)], axis=1).astype(BF)

    hidden = placed(swish * upper)
    m_part[...] = dot_nt(hidden, w_out).astype(BF)
    grad_mlp = (RESIDUAL_SCALE * cot[...].astype(F32)).astype(BF)
    grad_hidden = dot(grad_mlp, w_out)[:, pad : pad + slice_ff]
    grad_both = jnp.concatenate(
        [
            grad_hidden * upper * (sigma * (1.0 + gate * (1.0 - sigma))),
            grad_hidden * swish,
            zeros(w_in.shape[1] - 2 * slice_ff),
        ],
        axis=1,
    ).astype(BF)
    g_part[...] = dot_nt(grad_both, w_in).astype(BF)

    @pl.when(step == 0)
    def _():
        sum_in[...] = dot_tn(grad_both, normed[...])
        sum_out[...] = dot_tn(hidden, grad_mlp)

    @pl.when(step > 0)
    def _():
        sum_in[...] += dot_tn(grad_both, normed[...])
        sum_out[...] += dot_tn(hidden, grad_mlp)

    @pl.when(step == pl.num_programs(0) - 1)
    def _():
        mid = sum_in.shape[0]
        if cut:
            grads[:, :cut] = sum_in[:cut].T.astype(BF)
        grads[:, cut:mid] = (sum_in[cut:] + sum_out[: mid - cut]).T.astype(BF)
        grads[:, mid:] = sum_out[mid - cut :].T.astype(BF)


def feed_forward(normed, cot, weights, slice_ff, rows):
    tokens, columns = normed.shape
    lanes = weights.shape[1]
    cut = slice_ff * 2 // 128 * 128
    wide = -(-slice_ff * 2 // 128) * 128
    token_block = pl.BlockSpec((rows, columns), lambda i: (i, 0))
    whole = pl.BlockSpec((columns, lanes), lambda i: (0, 0))
    part = jax.ShapeDtypeStruct((tokens, columns), BF)
    return pl.pallas_call(
        functools.partial(feed_forward_kernel, slice_ff),
        grid=(tokens // rows,),
        out_shape=(part, part, jax.ShapeDtypeStruct((columns, lanes), BF)),
        in_specs=[token_block, token_block, whole],
        out_specs=[token_block, token_block, whole],
        scratch_shapes=[
            pltpu.VMEM((wide, columns), F32),
            pltpu.VMEM((lanes - cut, columns), F32),
        ],
        compiler_params=pltpu.CompilerParams(vmem_limit_bytes=VMEM_BYTES),
        name="feed_forward",
    )(normed, cot, weights)


def attend_back_kernel(
    grad_attn, mixed, o_t, q_rows, kv_rows, key_rot, q_normed, kv_normed, q_up, kv_up,
    seg_row, valid_row, cos_full, sin_full,
    grad_latents, grad_o, grad_q_up, grad_kv_up, grad_q, grad_kv,
):
    rank_q = q_up.shape[0]
    grad_o[...] = dot_tn(grad_attn[...], mixed[...]).astype(BF)
    grad_mixed = dot(grad_attn[...], o_t[...]).astype(BF)
    bias = attention_mask(seg_row, valid_row)
    inv_root = 1.0 / math.sqrt(NOPE + ROPE)
    grad_rot = jnp.zeros((grad_attn.shape[0], ROPE), F32)
    for head in range(q_rows.shape[1] // (NOPE + ROPE)):
        base = head * (NOPE + ROPE)
        start = head * (NOPE + VD)
        query = q_rows[:, base : base + NOPE + ROPE]
        key = jnp.concatenate([kv_rows[:, start : start + NOPE], key_rot[...]], axis=1)
        value = kv_rows[:, start + NOPE : start + NOPE + VD]
        grad = grad_mixed[:, head * VD : head * VD + VD]
        probs = head_probs(query, key, bias, inv_root)
        grad_value = dot_tn(probs.astype(BF), grad)
        grad_probs = dot_nt(grad, value)
        inner = jnp.sum(probs * grad_probs, axis=-1, keepdims=True)
        grad_scores = (probs * (grad_probs - inner)).astype(BF)
        grad_query = dot(grad_scores, key) * inv_root
        grad_key = dot_tn(grad_scores, query) * inv_root
        grad_q[:, base : base + NOPE + ROPE] = jnp.concatenate(
            [grad_query[:, :NOPE], turn(grad_query[:, NOPE:], cos_full[...], -sin_full[...])],
            axis=1,
        ).astype(BF)
        grad_kv[:, start : start + NOPE + VD] = jnp.concatenate(
            [grad_key[:, :NOPE], grad_value], axis=1
        ).astype(BF)
        grad_rot = grad_rot + grad_key[:, NOPE:]
    grad_latents[...] = jnp.zeros_like(grad_latents)
    grad_latents[:, :rank_q] = dot_nt(grad_q[...], q_up[...]).astype(BF)
    grad_latents[:, rank_q : rank_q + KR] = dot_nt(grad_kv[...], kv_up[...]).astype(BF)
    grad_latents[:, rank_q + KR : rank_q + KR + ROPE] = turn(
        grad_rot, cos_full[...], -sin_full[...]
    ).astype(BF)
    grad_q_up[...] = dot_tn(q_normed[...], grad_q[...]).astype(BF)
    grad_kv_up[...] = dot_tn(kv_normed[...], grad_kv[...]).astype(BF)


def attend_back(
    grad_attn, mixed, o_t, q_rows, kv_rows, key_rot, q_normed, kv_normed, q_up, kv_up,
    segments, valid, cos_full, sin_full, columns_down,
):
    length = grad_attn.shape[0]

    def out(shape):
        return jax.ShapeDtypeStruct(shape, BF)

    return pl.pallas_call(
        attend_back_kernel,
        out_shape=(
            out((length, columns_down)),
            out(o_t.shape),
            out(q_up.shape),
            out(kv_up.shape),
        ),
        in_specs=[VMEM] * 14,
        out_specs=[VMEM] * 4,
        scratch_shapes=[pltpu.VMEM(q_rows.shape, BF), pltpu.VMEM(kv_rows.shape, BF)],
        compiler_params=pltpu.CompilerParams(vmem_limit_bytes=VMEM_BYTES),
        name="attend_back",
    )(
        grad_attn, mixed, o_t, q_rows, kv_rows, key_rot, q_normed, kv_normed, q_up, kv_up,
        segments[None, :], valid[None, :], cos_full, sin_full,
    )


class ScatterInto:
    def __init__(self, links, copies, bufs, result):
        self.links, self.copies, self.result = links, copies, result
        self.part, self.from_low, self.from_high = bufs
        self.order = steps_by_distance(links.n_high) + [0]
        self.low_in, self.high_in = {}, {}

    def start(self):
        for k in self.order:
            self.low_in[k] = self.copies.go(
                self.part.at[self.links.ahead(k), 1 - self.links.low],
                self.from_low.at[k],
                self.links.over_low(),
            )

    def steps(self):
        links, part = self.links, self.part
        for k in self.order:
            there = links.ahead(k)
            self.low_in[k].wait_recv()
            part[there, links.low] = (
                part[there, links.low].astype(F32) + self.from_low[k].astype(F32)
            ).astype(BF)
            if k:
                self.high_in[k] = self.copies.go(
                    part.at[there, links.low], self.from_high.at[k - 1], links.device(high=there)
                )

    def finish(self):
        total = self.part[self.links.high, self.links.low].astype(F32)
        for k in steps_by_distance(self.links.n_high):
            self.high_in[k].wait_recv()
            total = total + self.from_high[k - 1].astype(F32)
        self.result[...] = total.astype(self.result.dtype)


def scatter_into_scratch(n_high, shape):
    return [
        pltpu.VMEM((n_high, 2, *shape), BF),
        pltpu.VMEM((n_high, *shape), BF),
        pltpu.VMEM((n_high - 1, *shape), BF),
    ]


def small_stream(links, copies, small, small_in, stats, stats_in, stats_block, small_block, small_full):
    n_high = links.n_high
    low_in = copies.go(
        small.at[:, 1 - links.low], small_in.at[pl.ds(0, n_high)], links.over_low()
    )
    stats_low = copies.go(stats, stats_in.at[0], links.over_low())
    yield
    low_in.wait_recv()
    stats_low.wait_recv()
    for k in range(n_high):
        small_in[k] = small_in[k] + small[k, links.low]
    stats_block[...] = stats[...] + stats_in[0]
    waits = []
    for k in range(1, n_high):
        there = links.ahead(k)
        waits.append(
            copies.go(small_in.at[there], small_in.at[n_high + k - 1], links.device(high=there))
        )
        waits.append(copies.go(stats_block, stats_in.at[k], links.device(high=there)))
    yield
    for wait in waits:
        wait.wait_recv()
    total = small_in[links.high]
    everything = stats_block[...]
    for k in range(1, n_high):
        total = total + small_in[n_high + k - 1]
        everything = everything + stats_in[k]
    small_block[0] = total
    small_block[1] = everything
    yield from tensor_gather(links, copies, small_block, small_full)


def back_kernel(
    n_dp, g_part, m_part, w_part, resid, branch, cot, x, normed, latents, q_normed, kv_normed,
    q_rows, kv_rows, key_rot, mixed, d_in, o_in, q_in, kv_in, f_g, seg_row, valid_row,
    turns,
    block_full, grad_input, d_full, o_sum, q_sum, kv_sum, small_full, w_full,
    f_down, f_o, f_q, f_kv, attn_full, grad_rows, g_rows, m_rows, grad_q, grad_kv, lat, lat_in, lat_half, lat_side,
    lat_full, d_block, small, small_in, stats, stats_in, stats_block, small_block, *rest,
):
    g_bufs, m_bufs = rest[:8], (rest[0], *rest[8:13])
    d_bufs, o_bufs, q_bufs, kv_bufs = rest[13:16], rest[16:19], rest[19:22], rest[22:25]
    links = Links(n_dp)
    copies = Copies(*rest[25:])
    links.meet(swap=True)
    cos_full, sin_full = turns[:, :ROPE], turns[:, ROPE:]
    length = x.shape[0]
    rank_q, rank_kv = q_normed.shape[1], kv_normed.shape[1]
    width = o_sum.shape[0]

    def gain_of(row, count):
        return jnp.concatenate(
            [f_g[k].astype(F32)[row : row + 1, :count] for k in range(n_dp)], axis=1
        )

    half_columns = x.shape[1] // 256 * 128
    g = EveryScatter(links, copies, g_part, g_bufs, g_rows, half_columns)
    m = EveryScatter(links, copies, m_part, m_bufs, m_rows, 0)
    swap = Swap(links, copies, w_part, w_full)
    high = range(links.n_high)
    g.start()
    loads = [
        copies.near(source, target)
        for source, target in ((d_in, f_down), (o_in, f_o), (q_in, f_q), (kv_in, f_kv))
    ]
    swap.send(range(2, n_dp, 2))
    for i in range(links.n_high + 1):
        if i in high:
            g.first(i)
        if i - 1 in high:
            g.second(i - 1)
        if i - 2 in high:
            g.third(i - 2)
    m.start()
    swap.send(range(1, n_dp, 2))
    g.third(links.n_high - 1)
    m.first(0)
    m.first(1)
    g.finish()
    stream = resid[...]
    inv_two = inverse_rms(stream)
    unit_two = stream * inv_two
    gain_mlp = gain_of(3, width)
    grad = cot[...].astype(F32) + norm_back(g_rows[...] * gain_mlp, unit_two, inv_two)
    grad_rows[...] = (RESIDUAL_SCALE * grad).astype(BF)
    t_stream = tensor_gather(links, copies, grad_rows, attn_full)
    next(t_stream)
    m.first(2)
    m.first(3)
    mlp_gain = jnp.sum(g_rows[...] * unit_two, axis=0, keepdims=True)
    bias = attention_mask(seg_row, valid_row)
    for _ in t_stream:
        pass

    for load in loads:
        load.wait()
    grad_attn = attn_full[...].reshape(length, x.shape[1])
    for k in range(n_dp):
        o_bufs[0][k // 2, k % 2] = dot_tn(
            grad_attn[:, k * width : k * width + width], mixed[...]
        ).astype(BF)
    o = ScatterInto(links, copies, o_bufs, o_sum)
    o.start()

    grad_mixed = dot(grad_attn, f_o[...].reshape(n_dp * width, mixed.shape[1])).astype(BF)
    inv_root = 1.0 / math.sqrt(NOPE + ROPE)
    grad_rot = jnp.zeros((length, ROPE), F32)
    for head in range(q_rows.shape[1] // (NOPE + ROPE)):
        base = head * (NOPE + ROPE)
        start = head * (NOPE + VD)
        query = q_rows[:, base : base + NOPE + ROPE]
        key = jnp.concatenate([kv_rows[:, start : start + NOPE], key_rot[...]], axis=1)
        value = kv_rows[:, start + NOPE : start + NOPE + VD]
        grad_head = grad_mixed[:, head * VD : head * VD + VD]
        probs = head_probs(query, key, bias, inv_root)
        grad_value = dot_tn(probs.astype(BF), grad_head)
        grad_probs = dot_nt(grad_head, value)
        inner = jnp.sum(probs * grad_probs, axis=-1, keepdims=True)
        grad_scores = (probs * (grad_probs - inner)).astype(BF)
        grad_query = dot(grad_scores, key) * inv_root
        grad_key = dot_tn(grad_scores, query) * inv_root
        grad_q[:, base : base + NOPE + ROPE] = jnp.concatenate(
            [grad_query[:, :NOPE], turn(grad_query[:, NOPE:], cos_full[...], -sin_full[...])],
            axis=1,
        ).astype(BF)
        grad_kv[:, start : start + NOPE + VD] = jnp.concatenate(
            [grad_key[:, :NOPE], grad_value], axis=1
        ).astype(BF)
        grad_rot = grad_rot + grad_key[:, NOPE:]

    half = length // 2
    lat[...] = jnp.zeros_like(lat)
    full_q = f_q[...].reshape(rank_q, q_rows.shape[1])
    full_kv = f_kv[...].reshape(rank_kv, kv_rows.shape[1])
    grad_turned = turn(grad_rot, cos_full[...], -sin_full[...]).astype(BF)
    for core in range(2):
        at = core * half
        lat[core, :, :rank_q] = dot_nt(grad_q[at : at + half], full_q).astype(BF)
        lat[core, :, rank_q : rank_q + rank_kv] = dot_nt(
            grad_kv[at : at + half], full_kv
        ).astype(BF)
        lat[core, :, rank_q + rank_kv : rank_q + rank_kv + ROPE] = grad_turned[at : at + half]
    over = copies.go(lat.at[1 - links.core], lat_in, links.over_core())
    rows_q = q_sum.shape[0]
    for k in range(n_dp):
        q_bufs[0][k // 2, k % 2] = dot_tn(
            q_normed[:, k * rows_q : k * rows_q + rows_q], grad_q[...]
        ).astype(BF)
    q = ScatterInto(links, copies, q_bufs, q_sum)
    q.start()
    over.wait_recv()
    lat_half[...] = (lat[links.core].astype(F32) + lat_in[...].astype(F32)).astype(BF)
    over = copies.go(lat_half, lat_side, links.over_side())
    rows_kv = kv_sum.shape[0]
    for k in range(n_dp):
        kv_bufs[0][k // 2, k % 2] = dot_tn(
            kv_normed[:, k * rows_kv : k * rows_kv + rows_kv], grad_kv[...]
        ).astype(BF)
    kv = ScatterInto(links, copies, kv_bufs, kv_sum)
    kv.start()
    over.wait_recv()
    lat_full[links.core] = (lat_half[...].astype(F32) + lat_side[...].astype(F32)).astype(BF)
    mine = lat_full.at[links.core]
    over = copies.go(mine, mine, links.over_core())
    q_latent = latents[:, :rank_q]
    inv_q = inverse_rms(q_latent)
    unit_q = q_latent * inv_q
    kv_latent = latents[:, rank_q : rank_q + rank_kv]
    inv_kv = inverse_rms(kv_latent)
    unit_kv = kv_latent * inv_kv
    over.wait_recv()
    lat_sum = lat_full[...].reshape(length, lat.shape[2]).astype(F32)
    grad_q_latent, grad_kv_latent = lat_sum[:, :rank_q], lat_sum[:, rank_q : rank_q + rank_kv]
    q_gain = jnp.sum(grad_q_latent * unit_q, axis=0, keepdims=True)
    kv_gain = jnp.sum(grad_kv_latent * unit_kv, axis=0, keepdims=True)
    grad_down = jnp.concatenate(
        [
            norm_back(grad_q_latent * gain_of(1, rows_q), unit_q, inv_q),
            norm_back(grad_kv_latent * gain_of(2, rows_kv), unit_kv, inv_kv),
            lat_sum[:, rank_q + rank_kv :],
        ],
        axis=1,
    ).astype(BF)

    rows_down = d_block.shape[0]
    m.second(0)
    m.second(1)
    copies.near(normed, g_bufs[0].at[0]).wait()
    normed_rows = g_bufs[0][0].reshape(length, x.shape[1])
    rank = links.side * 2 + links.core
    for k in range(n_dp):
        rows_all = dot_tn(normed_rows[:, k * width : k * width + width], grad_down)
        d_bufs[0][k // 2, k % 2] = quarter_of(rows_all, rank).astype(BF)

    d = ScatterInto(links, copies, d_bufs, d_block)
    d.start()
    o.steps()
    m.second(2)
    m.second(3)
    grad_input[...] = dot_nt(grad_down, f_down[...].reshape(n_dp * width, grad_down.shape[1]))
    q.steps()
    kv.steps()
    for i in high:
        m.third(i)
    d.steps()
    m.finish()
    mlp = RESIDUAL_SCALE * m_rows[...]
    g_rows[...] = resid[...] + mlp
    block_gather = tensor_gather(links, copies, g_rows, block_full)
    next(block_gather)
    valid = jnp.broadcast_to((valid_row[...] == 1).astype(F32), (length, length)).T
    weights = quarter_of(valid, rank)[:, :1]
    lane = lax.broadcasted_iota(jnp.int32, stats.shape, 1)
    sums = [
        jnp.sum(jnp.sum(weights * rows * rows, axis=1, keepdims=True), axis=0, keepdims=True)
        for rows in (resid[...], branch[...], mlp)
    ] + [jnp.sum(weights, axis=0, keepdims=True)]
    packed = jnp.zeros(stats.shape, F32)
    for index, value in enumerate(sums):
        packed = jnp.where(lane == index, value, packed)
    stats[...] = packed
    stream = x[...].astype(F32)
    inv_one = inverse_rms(stream)
    unit_one = stream * inv_one
    attn_gain = jnp.sum(grad_input[...] * unit_one, axis=0, keepdims=True)
    grad_input[...] = grad_attn.astype(F32) * (1.0 / RESIDUAL_SCALE) + norm_back(
        grad_input[...] * gain_of(0, width), unit_one, inv_one
    )

    def piece(vector, k):
        count = vector.shape[1] // n_dp
        cut = vector[:, k * count : k * count + count]
        return jnp.concatenate([cut, jnp.zeros((1, small.shape[3] - count), F32)], axis=1)

    for k in range(n_dp):
        small[k // 2, k % 2] = jnp.concatenate(
            [piece(v, k) for v in (attn_gain, q_gain, kv_gain, mlp_gain)]
            + [jnp.zeros((4, small.shape[3]), F32)],
            axis=0,
        )
    small_rows = small_stream(
        links, copies, small, small_in, stats, stats_in, stats_block, small_block, small_full
    )
    next(small_rows)
    d.finish()
    down_gather = tensor_gather(links, copies, d_block, d_full)
    take_turns(small_rows, down_gather, block_gather)
    o.finish()
    q.finish()
    kv.finish()
    swap.finish()
    copies.finish()


def back(
    n_dp, g_part, m_part, w_part, resid, branch, cot, x, normed, latents, q_normed, kv_normed,
    q_rows, kv_rows, key_rot, mixed, f_down, f_o, f_q, f_kv, f_g, segments, valid, turns,
):
    n_high = n_dp // 2
    rows, columns = resid.shape
    length = x.shape[0]
    lanes = f_g.shape[2]
    half = (length // 2, latents.shape[1])
    shape = (n_high, 2, 2, 2, rows, columns)
    d_shape, o_shape, q_shape, kv_shape = f_down.shape[2:], f_o.shape[1:], f_q.shape[1:], f_kv.shape[1:]
    one = (8, lanes)
    count = 2 * (6 * n_high - 1) + 4 * (2 * n_high - 1) + 4 * 3 + (n_dp - 1) + 2 * n_high + 3

    def out(shape, kind=F32):
        return jax.ShapeDtypeStruct(shape, kind)

    return pl.pallas_call(
        functools.partial(back_kernel, n_dp),
        out_shape=(
            out((4, rows, columns)),
            out((length, columns)),
            out((4, *d_shape), BF),
            out(o_shape),
            out(q_shape),
            out(kv_shape),
            out((4, 2, *one)),
            out(w_part.shape, BF),
        ),
        in_specs=[ANY] * 3 + [VMEM] * 4 + [ANY] + [VMEM] * 7 + [ANY] * 4 + [VMEM] * 4,
        out_specs=[ANY] + [VMEM] * 6 + [ANY],
        scratch_shapes=[
            *(pltpu.VMEM(full.shape, BF) for full in (f_down, f_o, f_q, f_kv)),
            pltpu.VMEM((4, rows, columns), BF),
            pltpu.VMEM((rows, columns), BF),
            pltpu.VMEM((rows, columns), F32),
            pltpu.VMEM((rows, columns), F32),
            pltpu.VMEM(q_rows.shape, BF),
            pltpu.VMEM(kv_rows.shape, BF),
            pltpu.VMEM((2, *half), BF),
            pltpu.VMEM(half, BF),
            pltpu.VMEM(half, BF),
            pltpu.VMEM(half, BF),
            pltpu.VMEM((2, *half), BF),
            pltpu.VMEM(d_shape, BF),
            pltpu.VMEM((n_high, 2, *one), F32),
            pltpu.VMEM((2 * n_high - 1, *one), F32),
            pltpu.VMEM(one, F32),
            pltpu.VMEM((n_high, *one), F32),
            pltpu.VMEM(one, F32),
            pltpu.VMEM((2, *one), F32),
            *every_scatter_scratch(n_high, rows, columns),
            *every_scatter_scratch(n_high, rows, columns, 0)[1:],
            *scatter_into_scratch(n_high, d_shape),
            *scatter_into_scratch(n_high, o_shape),
            *scatter_into_scratch(n_high, q_shape),
            *scatter_into_scratch(n_high, kv_shape),
            *semaphores(count, 2 * n_high + 10),
        ],
        compiler_params=params(8, 62),
        name="back",
    )(
        g_part.reshape(shape), m_part.reshape(shape), w_part, resid, branch, cot, x,
        normed.reshape(2, 2, rows, columns), latents, q_normed, kv_normed, q_rows, kv_rows, key_rot, mixed, f_down, f_o, f_q, f_kv, f_g,
        segments[None, :], valid[None, :], turns,
    )


def unpack_kernel(
    slice_ff, rank_q, swapped, down, o_in, q_in, kv_in, block_in, input_in, small,
    grad_gate, grad_upper, grad_down_t, grad_o_t, grad_q_down, grad_kv_down_t, grad_q_up, grad_kv_up,
    block_out, grad_input,
    attn_gain, q_gain, kv_gain, mlp_gain, stats,
):
    n_dp = swapped.shape[0]

    def pieces(start):
        return jnp.concatenate(
            [swapped[k, :, start : start + slice_ff] for k in range(n_dp)], axis=1
        ).astype(F32)

    grad_gate[...] = pieces(0)
    grad_upper[...] = pieces(slice_ff)
    grad_down_t[...] = pieces(2 * slice_ff)
    for target, source in (
        (grad_o_t, o_in), (grad_q_up, q_in), (grad_kv_up, kv_in), (block_out, block_in), (grad_input, input_in),
    ):
        target[...] = source[...]
    rows = down[...].reshape(grad_q_down.shape[0], down.shape[2]).astype(F32)
    grad_q_down[...] = rows[:, :rank_q]
    grad_kv_down_t[...] = rows[:, rank_q : rank_q + grad_kv_down_t.shape[0]].T
    gains = small[0, 0]
    for row, gain in ((0, attn_gain), (1, q_gain), (2, kv_gain)):
        gain[...] = gains[row : row + 1, : gain.shape[1]]
    total = small[0, 0] + small[1, 0] + small[2, 0] + small[3, 0]
    mlp_gain[...] = total[3:4, : mlp_gain.shape[1]]
    sums = (small[0, 1] + small[1, 1] + small[2, 1] + small[3, 1])[0:1]
    stats[...] = jnp.sqrt(sums[:, :3] / (sums[:, 3:4] * D))


def unpack(swapped, down, o_t, q_up, kv_up, block, grad_input, small, slice_ff, rank_q, columns_down, gains):
    n_dp, width, _ = swapped.shape

    def out(*shape):
        return jax.ShapeDtypeStruct(shape, F32)

    return pl.pallas_call(
        functools.partial(unpack_kernel, slice_ff, rank_q),
        out_shape=(
            out(width, n_dp * slice_ff),
            out(width, n_dp * slice_ff),
            out(width, n_dp * slice_ff),
            out(*o_t.shape),
            out(width, rank_q),
            out(columns_down - rank_q, width),
            out(*q_up.shape),
            out(*kv_up.shape),
            out(*block.shape),
            out(*grad_input.shape),
            *(out(1, gain.shape[0]) for gain in gains),
            out(1, 3),
        ),
        in_specs=[VMEM] * 8,
        out_specs=[VMEM] * 15,
        compiler_params=pltpu.CompilerParams(vmem_limit_bytes=VMEM_BYTES),
        name="unpack",
    )(swapped, down, o_t, q_up, kv_up, block, grad_input, small)


def per_device(
    layer_input,
    segment_ids,
    valid_mask,
    cotangent,
    attn_gain,
    q_down,
    q_gain,
    q_up,
    kv_down,
    kv_gain,
    kv_up,
    o_proj,
    mlp_gain,
    w_gate,
    w_up,
    w_down,
):
    length = layer_input.shape[0]
    n_dp = lax.axis_size("dp")
    n_tensor = lax.axis_size("tensor")
    share = length // n_tensor
    me = lax.axis_index("tensor")
    width = w_gate.shape[0]
    slice_ff = w_gate.shape[1] // n_dp
    rows_down = width // n_tensor

    def rows_of(values, count):
        return lax.dynamic_slice_in_dim(values, me * count, count, 0)

    rank_q = q_down.shape[1]
    columns_down = rank_q + kv_down.shape[1]
    pad_down = -columns_down % 128
    down_rows = jnp.concatenate(
        [
            rows_of(q_down, rows_down),
            rows_of(kv_down, rows_down),
            jnp.zeros((rows_down, pad_down), BF),
        ],
        axis=1,
    )
    lanes = -(-width // 128) * 128

    def lane_rows(rows, count, kind):
        padded = [jnp.pad(row.astype(kind), (0, lanes - row.shape[0])) for row in rows]
        return jnp.stack(padded + [jnp.zeros((lanes,), kind)] * (count - len(padded)))

    cot_rows = rows_of(cotangent, share)
    x_rows = rows_of(layer_input, share)
    gains_block = lane_rows([attn_gain, q_gain, kv_gain, mlp_gain], 16, BF)
    cosine, sine_table = rope_tables(length, ROPE)
    cos_full = jnp.concatenate([cosine, cosine], axis=1)
    sin_full = jnp.concatenate([-sine_table, sine_table], axis=1)
    fused = n_dp == 8 and rows_down % 16 == 0 and q_up.shape[0] % 16 == 0
    if fused:
        (
            f_down, f_o, f_q, f_kv, f_g, mlp_part, normed_part, grad_packed,
            normed, latents, q_normed, kv_normed, q_rows, kv_rows, key_rot, mixed,
            resid_rows, attn_rows, cot_rows,
        ) = forward(
            n_dp, layer_input, cotangent, q_down, kv_down.T, (attn_gain, q_gain, kv_gain, mlp_gain),
            q_up, kv_up, o_proj.T, w_gate, w_up, w_down.T, segment_ids, valid_mask,
            jnp.concatenate([cos_full, sin_full], axis=1), down_rows.shape, lanes,
        )
    else:
        f_down, f_o, f_q, f_kv, f_g, f_cot = gather_weights(
            n_dp, n_tensor, down_rows, o_proj.T, q_up, kv_up, gains_block, cot_rows
        )
    full_down = f_down.reshape(n_dp * width, columns_down + pad_down)
    full_o = f_o.reshape(n_dp * width, -1)

    def gain_of(row, gain):
        return f_g[:, row, : gain.shape[0]].reshape(-1).astype(F32)

    gain_attn = gain_of(0, attn_gain)
    gain_q = gain_of(1, q_gain)
    gain_kv = gain_of(2, kv_gain)
    gain_mlp = gain_of(3, mlp_gain)
    if not fused:
        packed = jnp.concatenate(
            [
                w_gate.reshape(width, n_dp, slice_ff),
                w_up.reshape(width, n_dp, slice_ff),
                w_down.T.reshape(width, n_dp, slice_ff),
                jnp.zeros((width, n_dp, -3 * slice_ff % 128), BF),
            ],
            axis=2,
        ).transpose(1, 0, 2)
        packed, f_q = lax.optimization_barrier((packed, f_q))
        f_w = swap_dp(packed)
    full_q_up = f_q.reshape(-1, q_up.shape[1])
    full_kv_up = f_kv.reshape(-1, kv_up.shape[1])
    if not fused:
        normed, latents, q_normed, kv_normed, q_rows, kv_rows, key_rot, mixed = attend(
            layer_input, gain_attn, gain_q, gain_kv, full_down, full_q_up, full_kv_up,
            segment_ids, valid_mask, cos_full, sin_full,
        )
        f_normed, resid_rows, attn_rows = attention_residual(
            n_dp, dot_nt(mixed, full_o).astype(BF), x_rows, gain_mlp[None, :]
        )
    if not fused:
        mlp_part, normed_part, grad_packed = feed_forward(
            f_normed.reshape(n_dp * length, -1),
            f_cot.reshape(n_dp * length, -1),
            f_w.reshape(n_dp * width, -1),
            slice_ff,
            length,
        )
    weight_rows = rows_of(valid_mask.astype(F32)[:, None], share)
    if fused:
        f_block, grad_input, s_down, s_o, s_q, s_kv, s_small, swapped = back(
            n_dp, normed_part, mlp_part, grad_packed.reshape(n_dp, width, -1), resid_rows, attn_rows,
            cot_rows, layer_input, normed, latents, q_normed, kv_normed, q_rows, kv_rows,
            key_rot, mixed, f_down, f_o, f_q, f_kv, f_g, segment_ids, valid_mask,
            jnp.concatenate([cos_full, sin_full], axis=1),
        )
        (
            grad_w_gate, grad_w_up, grad_down_t, grad_o_t, grad_q_down, grad_kv_down_t, grad_q_up,
            grad_kv_up, block_full, grad_input, grad_attn_gain, grad_q_gain, grad_kv_gain, grad_mlp_gain, rms_stats,
        ) = unpack(
            swapped, s_down, s_o, s_q, s_kv, f_block.reshape(length, -1), grad_input, s_small,
            slice_ff, rank_q, columns_down,
            (attn_gain, q_gain, kv_gain, mlp_gain),
        )
        return (
            block_full,
            grad_input,
            grad_attn_gain.reshape(-1),
            grad_q_down,
            grad_q_gain.reshape(-1),
            grad_q_up,
            grad_kv_down_t.T,
            grad_kv_gain.reshape(-1),
            grad_kv_up,
            grad_o_t.T,
            grad_mlp_gain.reshape(-1),
            grad_w_gate,
            grad_w_up,
            grad_down_t.T,
            rms_stats.reshape(-1),
        )
    else:
        inv_two = inverse_rms(resid_rows)
        unit_two = resid_rows * inv_two
        swapped = swap_dp(grad_packed.reshape(n_dp, width, -1))
        normed_part, grad_packed = lax.optimization_barrier((normed_part, grad_packed))
        f_attn, grad_normed_two, f_block, mlp_rows = residual_grads(
            n_dp, normed_part, mlp_part, resid_rows, cot_rows, gain_mlp[None, :]
        )
        grad_attn = f_attn.reshape(length, -1)
        block_full = f_block.reshape(length, -1)

        grad_mlp_gain = jnp.sum(grad_normed_two * unit_two, axis=0)

        grad_part, grad_o, grad_q_up, grad_kv_up = attend_back(
            grad_attn, mixed, full_o, q_rows, kv_rows, key_rot, q_normed, kv_normed,
            full_q_up, full_kv_up, segment_ids, valid_mask, cos_full, sin_full,
            columns_down + pad_down,
        )
        grad_part, swapped = lax.optimization_barrier((grad_part, swapped))
        grad_latents = sum_latents(n_dp, grad_part).astype(F32)
        stream = layer_input.astype(F32)
        inv_one = inverse_rms(stream)
        unit_one = stream * inv_one
        q_latent = latents[:, :rank_q]
        inv_q = inverse_rms(q_latent)
        unit_q = q_latent * inv_q
        kv_latent = latents[:, rank_q : rank_q + KR]
        inv_kv = inverse_rms(kv_latent)
        unit_kv = kv_latent * inv_kv
        grad_q_normed = grad_latents[:, :rank_q]
        grad_kv_normed = grad_latents[:, rank_q : rank_q + KR]
        grad_kv_rot = grad_latents[:, rank_q + KR : columns_down]
        grad_q_gain = jnp.sum(grad_q_normed * unit_q, axis=0)
        grad_kv_gain = jnp.sum(grad_kv_normed * unit_kv, axis=0)
        grad_down = jnp.concatenate(
            [
                norm_back(grad_q_normed * gain_q, unit_q, inv_q),
                norm_back(grad_kv_normed * gain_kv, unit_kv, inv_kv),
                grad_kv_rot,
                jnp.zeros((length, pad_down), F32),
            ],
            axis=-1,
        ).astype(BF)
        grad_normed = dot_nt(grad_down, full_down)
        grad_attn_gain = jnp.sum(grad_normed * unit_one, axis=0)
        grad_input = grad_attn.astype(F32) * (1.0 / RESIDUAL_SCALE) + norm_back(
            grad_normed * gain_attn, unit_one, inv_one
        )

        quarter = lax.dynamic_index_in_dim(
            normed.reshape(length, n_dp, n_tensor, rows_down), me, 2, keepdims=False
        ).reshape(length, n_dp * rows_down)
        def by_dp(vector):
            return vector.reshape(n_dp, -1)

        def small_rows(vectors):
            return jnp.stack(
                [jnp.pad(by_dp(v), ((0, 0), (0, lanes - v.shape[0] // n_dp))) for v in vectors]
                + [jnp.zeros((n_dp, lanes), F32)] * (8 - len(vectors)),
                axis=1,
            )

        stats = jnp.stack(
            [
                jnp.sum(weight_rows * resid_rows * resid_rows),
                jnp.sum(weight_rows * attn_rows * attn_rows),
                jnp.sum(weight_rows * mlp_rows * mlp_rows),
                jnp.sum(weight_rows),
            ]
        )
        s_down, s_o, s_q, s_kv, s_small = sum_weight_grads(
            n_dp,
            dot_tn(quarter, grad_down).astype(BF),
            grad_o,
            grad_q_up,
            grad_kv_up,
            small_rows([grad_attn_gain, grad_q_gain, grad_kv_gain, grad_mlp_gain]),
            lane_rows([stats], 8, F32),
        )

    def columns_of(part):
        return part.transpose(1, 0, 2).reshape(width, n_dp * slice_ff).astype(F32)

    grad_w_gate = columns_of(swapped[:, :, :slice_ff])
    grad_w_up = columns_of(swapped[:, :, slice_ff : 2 * slice_ff])
    grad_w_down = columns_of(swapped[:, :, 2 * slice_ff : 3 * slice_ff]).T

    d_down = s_down.reshape(width, -1).astype(F32)
    gains = s_small[me, 0]
    stat_sums = jnp.sum(s_small[:, 1, 0, :4], axis=0)
    rms_stats = jnp.sqrt(stat_sums[:3] / (stat_sums[3] * D))
    return (
        block_full,
        grad_input,
        gains[0, : attn_gain.shape[0]],
        d_down[:, :rank_q],
        gains[1, : q_gain.shape[0]],
        s_q,
        d_down[:, rank_q:columns_down],
        gains[2, : kv_gain.shape[0]],
        s_kv,
        s_o.T,
        jnp.sum(s_small[:, 0, 3], axis=0)[: mlp_gain.shape[0]],
        grad_w_gate,
        grad_w_up,
        grad_w_down,
        rms_stats,
    )


def solution(mesh):
    placed = (
        P("dp", None),
        P("dp"),
        P("dp"),
        P("dp", None),
        P("dp"),
        P("dp", None),
        P("dp"),
        P("dp", "tensor"),
        P("dp", None),
        P("dp"),
        P("dp", "tensor"),
        P("tensor", "dp"),
        P("dp"),
        P("dp", "tensor"),
        P("dp", "tensor"),
        P("tensor", "dp"),
    )
    return jax.shard_map(
        per_device,
        mesh=mesh,
        in_specs=placed,
        out_specs=(
            P("dp", None),
            P("dp", None),
            P("dp"),
            P("dp", None),
            P("dp"),
            P("dp", "tensor"),
            P("dp", None),
            P("dp"),
            P("dp", "tensor"),
            P("tensor", "dp"),
            P("dp"),
            P("dp", "tensor"),
            P("dp", "tensor"),
            P("tensor", "dp"),
            P(),
        ),
        check_vma=False,
    )
```
